32 devices in a mesh: seq: 2 (over x), ctx: 8 (over z, y), wt: 2 (over core).
Axes of the slice: x: 2, y: 2, z: 4, core: 2. Of those that a mesh axis runs over, the one named last changes fastest.
Arguments:
- tokens: bfloat16 [8, 1024, 1280], P('seq', 'ctx'), may hold values from -6 to 6
- segments: int32 [8, 1024], P('seq', 'ctx'), may hold values from 0 to 2, as said below
- adapter_index: int32 [8], P('seq'), may hold values from 0 to 7, each once
- w_attn_in: bfloat16 [3, 1280, 1280], P(None, None, 'wt'), may hold values from -0.15625 to 0.15625
- w_attn_out: bfloat16 [1280, 1280], P('wt'), may hold values from -0.15625 to 0.15625
- w_gate_up: bfloat16 [2, 1280, 5120], P(None, None, 'wt'), may hold values from -0.15625 to 0.15625
- w_down: bfloat16 [5120, 1280], P('wt'), may hold values from -0.078125 to 0.078125
- qk_scale: float32 [1280], P('wt'), may hold values from 1 to 2
- mix_rates: float32 [2, 1280], replicated, may hold values from 0.2 to 0.8
- mlp_scales: float32 [2, 5120], P(None, 'wt'), may hold values from 0.5 to 2
- a_model: bfloat16 [8, 5, 16, 1280], replicated, may hold values from -0.15625 to 0.15625
- b_model: bfloat16 [8, 2, 16, 1280], replicated, may hold values from -0.75 to 0.75
- a_heads: bfloat16 [8, 16, 20, 64], P(None, None, 'wt'), may hold values from -0.15625 to 0.15625
- b_heads: bfloat16 [8, 3, 16, 20, 64], P(None, None, None, 'wt'), may hold values from -0.75 to 0.75
- a_hidden: bfloat16 [8, 16, 40, 128], P(None, None, 'wt'), may hold values from -0.078125 to 0.078125
- b_hidden: bfloat16 [8, 2, 16, 40, 128], P(None, None, None, 'wt'), may hold values from -0.75 to 0.75
- cotangent: bfloat16 [8, 1024, 1280], P('seq', 'ctx'), may hold values from -6 to 6
Outputs:
- layer_out: bfloat16 [8, 1024, 1280], P('seq', 'ctx')
- input_grad: float32 [8, 1024, 1280], P('seq', 'ctx')
- grad_a_model: float32 [8, 5, 16, 1280], P(None, None, None, ('seq', 'ctx', 'wt'))
- grad_b_model: float32 [8, 2, 16, 1280], P(None, None, None, ('seq', 'ctx'))
- grad_a_heads: float32 [8, 16, 20, 64], P(None, None, 'wt', ('seq', 'ctx'))
- grad_b_heads: float32 [8, 3, 16, 20, 64], P(None, None, None, 'wt', ('seq', 'ctx'))
- grad_a_hidden: float32 [8, 16, 40, 128], P(None, None, 'wt', ('seq', 'ctx'))
- grad_b_hidden: float32 [8, 2, 16, 40, 128], P(None, None, None, 'wt', ('seq', 'ctx'))
The draws below stay inside these ranges and needn't reach their ends.
Inputs may be any that keep to these rules, and one draw needn't show every extreme that they name: `segments`: segment numbers never fall along a sequence. Sequences come in groups of 8 / 2 consecutive ones; in each group exactly one sequence is a single document of all 1024 tokens (segment 0 throughout), and each other sequence packs exactly 3 documents of 51 to 512 tokens, the longest of exactly 512 tokens. `adapter_index`: each adapter serves exactly one sequence.
All inputs are finite; a program needn't handle non-finite values.
Results may differ from the reference program's by a relative error of at most 0.023.
Values may be sent and summed in bfloat16 or wider, within the bound.
No kernel may reach another device: no remote copies, remote signals or barrier semaphores. Data moves between devices by JAX's collectives and lax.ppermute only.
A program may use at most 512 MiB of HBM per device.

```python
import math
import jax
import jax.numpy as jnp
from jax import lax

D = 1280
HEADS = 20
HEAD_DIM = 64
FF = 5120
RANK = 16
ADAPTERS = 8
FW = 128
FG = 40
LEN = 1024
DOCS = 3
DOC_MOST = 512
DOC_LEAST = 51
N_SEQ = 2


def draw_segments(key, part):
    sub_keys = jax.random.split(jax.random.fold_in(key, 17), ADAPTERS)
    others_count = DOCS - 1
    spare_tokens = LEN - DOC_MOST
    extra_tokens = spare_tokens - others_count * DOC_LEAST
    base_size = DOC_LEAST + extra_tokens // others_count
    remainder = extra_tokens % others_count
    jitter = max(0, min(extra_tokens // others_count, DOC_MOST - base_size - remainder))
    group_size = ADAPTERS // N_SEQ

    def draw_single(single_key):
        move_key, turn_key = jax.random.split(single_key)
        shifts_by = jax.random.randint(move_key, (others_count,), 0, jitter + 1).astype(jnp.int32)
        first_flag = (jnp.arange(others_count, dtype=jnp.int32) == 0).astype(jnp.int32)
        others = base_size + shifts_by - jnp.roll(shifts_by, 1) + remainder * first_flag
        doc_sizes = jnp.concatenate([jnp.full((1,), DOC_MOST, jnp.int32), others.astype(jnp.int32)])
        rotation = jax.random.randint(turn_key, (), 0, DOCS)
        doc_sizes = jnp.roll(doc_sizes, rotation)
        doc_ends = jnp.cumsum(doc_sizes)
        position = jnp.arange(LEN, dtype=jnp.int32)
        return jnp.sum((position[:, None] >= doc_ends[None, :-1]).astype(jnp.int32), axis=1)
    packed = jax.vmap(draw_single)(sub_keys)
    chosen = jax.random.randint(jax.random.fold_in(key, 29), (N_SEQ,), 0, group_size).astype(jnp.int32)
    seq_number = jnp.arange(ADAPTERS, dtype=jnp.int32)
    group_of = seq_number // group_size
    whole_flag = seq_number % group_size == jnp.sum(jnp.where(group_of[:, None] == jnp.arange(N_SEQ, dtype=jnp.int32)[None, :], chosen[None, :], 0), axis=1)
    return jnp.where(whole_flag[:, None], jnp.zeros_like(packed), packed).astype(jnp.int32)


def block_scale(own_key, shape, cuts, low, high):
    def one(dim, shards_of):
        steps = jax.random.uniform(jax.random.fold_in(jax.random.fold_in(own_key, 6), dim), (shards_of,), jnp.float32, low / len(cuts), high / len(cuts))
        return jnp.repeat(jnp.exp(steps), shape[dim] // shards_of).reshape((-1,) + (1,) * (len(shape) - dim - 1))

    level = one(*cuts[0])
    for cut in cuts[1:]:
        level = level * one(*cut)
    return level


def gaussian(stream_key, extent, scale, most, cuts=(), held_as=jnp.bfloat16):
    result = jax.random.normal(stream_key, extent, jnp.float32) * scale
    if len(cuts) > 0:
        result = block_scale(stream_key, extent, cuts, -0.22, 0.18) * result
    return jnp.clip(result, min=-most, max=most).astype(held_as)


def setup_inputs(seed: int = 0) -> dict:
    key_of = jax.random.split(jax.random.key(seed), 18)
    return {
        "tokens": gaussian(key_of[0], (ADAPTERS, LEN, D), 1.0, 6.0, ((0, 2), (1, 8))),
        "segments": draw_segments(jax.random.fold_in(key_of[17], 71), 0),
        "adapter_index": jax.random.permutation(key_of[2], ADAPTERS).astype(jnp.int32),
        "w_attn_in": gaussian(key_of[3], (3, D, D), D ** -0.5, 0.15625, ((2, 2),)),
        "w_attn_out": gaussian(key_of[4], (D, D), D ** -0.5, 0.15625, ((0, 2),)),
        "w_gate_up": gaussian(key_of[5], (2, D, FF), D ** -0.5, 0.15625, ((2, 2),)),
        "w_down": gaussian(key_of[6], (FF, D), FF ** -0.5, 0.078125, ((0, 2),)),
        "qk_scale": jnp.clip(jnp.exp(math.log(2.0) - 0.6931472 * jax.random.uniform(key_of[7], (D,), jnp.float32) ** block_scale(key_of[7], (D,), ((0, 2),), -0.2, 0.2)), 1.0, 2.0),
        "mix_rates": jnp.clip(jax.random.uniform(key_of[8], (2, D), jnp.float32, 0.2, 0.8), 0.2, 0.8),
        "mlp_scales": jnp.clip(jnp.exp(math.log(2.0) - 1.3862944 * jax.random.uniform(key_of[9], (2, FF), jnp.float32) ** block_scale(key_of[9], (2, FF), ((1, 2),), -0.2, 0.2)), 0.5, 2.0),
        "a_model": gaussian(key_of[10], (ADAPTERS, 5, RANK, D), D ** -0.5, 0.15625),
        "b_model": gaussian(key_of[11], (ADAPTERS, 2, RANK, D), (4 * RANK) ** -0.5, 0.75),
        "a_heads": gaussian(key_of[12], (ADAPTERS, RANK, HEADS, HEAD_DIM), D ** -0.5, 0.15625, ((2, 2),)),
        "b_heads": gaussian(key_of[13], (ADAPTERS, 3, RANK, HEADS, HEAD_DIM), (4 * RANK) ** -0.5, 0.75, ((3, 2),)),
        "a_hidden": gaussian(key_of[14], (ADAPTERS, RANK, FG, FW), FF ** -0.5, 0.078125, ((2, 2),)),
        "b_hidden": gaussian(key_of[15], (ADAPTERS, 2, RANK, FG, FW), (4 * RANK) ** -0.5, 0.75, ((3, 2),)),
        "cotangent": gaussian(key_of[16], (ADAPTERS, LEN, D), 1.0, 6.0, ((0, 2), (1, 8))),
    }


@jax.custom_vjp
def low(v):
    return lax.optimization_barrier(v.astype(jnp.bfloat16)).astype(jnp.float32)

@jax.custom_vjp
def low_back(v):
    return v

def low_keep(v):
    return (low(v), None)

def low_pass(kept, grad):
    return (grad,)

def back_keep(v):
    return (v, None)

def back_low(kept, grad):
    return (low(grad),)
low.defvjp(low_keep, low_pass)
low_back.defvjp(back_keep, back_low)
highest = lax.Precision.HIGHEST
epsilon = 1e-06
masked_value = -1e+30

def matmul(left, right):
    return jnp.dot(left, right, precision=highest)

def normalize(values):
    return values * lax.rsqrt(lax.optimization_barrier(jnp.mean(values * values, axis=-1, keepdims=True)) + epsilon)

def angles(positions, half_dim):
    frequency = 10000.0 ** (-jnp.arange(half_dim, dtype=jnp.float32) / half_dim)
    turn_angle = positions.astype(jnp.float32)[:, None] * frequency[None, :]
    return (jnp.cos(turn_angle), jnp.sin(turn_angle))

def rotate(values, cosine_table, sine_table):
    half_dim = values.shape[-1] // 2
    lower_half = values[..., :half_dim]
    upper_half = values[..., half_dim:]
    cosine_part = cosine_table[:, None, :]
    sine_part = sine_table[:, None, :]
    return jnp.concatenate([lower_half * cosine_part - upper_half * sine_part, lower_half * sine_part + upper_half * cosine_part], axis=-1)

def head_prep(raw, cosine_table, sine_table, scale, head_dim):
    reshaped = raw.reshape(raw.shape[:-1] + (raw.shape[-1] // head_dim, head_dim))
    return normalize(rotate(reshaped, cosine_table, sine_table)).reshape(raw.shape) * scale

def mix_state(state, branch, rate):
    return normalize(state + rate * (normalize(branch) - state))

def swiglu(gate, up_value, scales):
    return up_value * scales[0] * jax.nn.silu(gate * scales[1])

def attend_rows(query_rows, row_offset, keys, values, row_segments, key_segments):
    scores = low_back(jnp.einsum('qhd,khd->hqk', query_rows, keys, precision=highest) * 0.125)
    query_pos = row_offset + jnp.arange(query_rows.shape[0], dtype=jnp.int32)
    key_pos = jnp.arange(keys.shape[0], dtype=jnp.int32)
    allowed = (key_pos[None, :] <= query_pos[:, None]) & (row_segments[:, None] == key_segments[None, :])
    weights = jax.nn.softmax(jnp.where(allowed[None], scores, masked_value), axis=-1)
    return jnp.einsum('hqk,khd->qhd', low(weights), values, precision=highest)

def apply_layer(state, segment_ids, frozen, factors):
    w_attn_in, w_attn_out, w_gate_up, w_down, qk_scale, mix_rates, mlp_scales = frozen
    a_model, b_model, a_heads, b_heads, a_hidden, b_hidden = factors
    length = state.shape[0]
    cosine_table, sine_table = angles(jnp.arange(length, dtype=jnp.int32), HEAD_DIM // 2)
    low_qkv = [low(low_back(matmul(state, a_model[member].T))) for member in range(3)]
    raw_qkv = [low_back(matmul(state, w_attn_in[member]) + matmul(low_qkv[member], b_heads[member])) for member in range(3)]
    queries = low(head_prep(raw_qkv[0], cosine_table, sine_table, qk_scale, HEAD_DIM)).reshape(length, HEADS, HEAD_DIM)
    keys = low(head_prep(raw_qkv[1], cosine_table, sine_table, qk_scale, HEAD_DIM)).reshape(length, HEADS, HEAD_DIM)
    values = low(raw_qkv[2]).reshape(length, HEADS, HEAD_DIM)
    row_block = min(length, 512)

    def one_block(block_index):
        row_offset = block_index * row_block
        query_rows = lax.dynamic_slice_in_dim(queries, row_offset, row_block, 0)
        row_segments = lax.dynamic_slice_in_dim(segment_ids, row_offset, row_block, 0)
        return attend_rows(query_rows, row_offset, keys, values, row_segments, segment_ids)
    attended = lax.map(jax.checkpoint(one_block), jnp.arange(length // row_block, dtype=jnp.int32)).reshape(length, D)
    attn_low = low(low_back(attended))
    low_out = low(low_back(matmul(attn_low, a_heads.T)))
    attn_raw = low_back(matmul(attn_low, w_attn_out) + matmul(low_out, b_model[0]))
    middle = mix_state(state, attn_raw, mix_rates[0])
    middle_low = low(middle)
    low_gate = low(low_back(matmul(middle_low, a_model[3].T)))
    low_up = low(low_back(matmul(middle_low, a_model[4].T)))
    gate = low_back(matmul(middle_low, w_gate_up[0]) + matmul(low_gate, b_hidden[0]))
    up_value = low_back(matmul(middle_low, w_gate_up[1]) + matmul(low_up, b_hidden[1]))
    hidden = low(swiglu(gate, up_value, mlp_scales))
    low_down = low(low_back(matmul(hidden, a_hidden.T)))
    down_raw = low_back(matmul(hidden, w_down) + matmul(low_down, b_model[1]))
    return mix_state(middle, down_raw, mix_rates[1])

def reference(tokens, segments, adapter_index, w_attn_in, w_attn_out, w_gate_up, w_down, qk_scale, mix_rates, mlp_scales, a_model, b_model, a_heads, b_heads, a_hidden, b_hidden, cotangent):
    frozen = tuple((member_array.astype(jnp.float32) for member_array in (w_attn_in, w_attn_out, w_gate_up, w_down, qk_scale, mix_rates, mlp_scales)))
    factors = (a_model.astype(jnp.float32), b_model.astype(jnp.float32), a_heads.astype(jnp.float32).reshape(ADAPTERS, RANK, D), b_heads.astype(jnp.float32).reshape(ADAPTERS, 3, RANK, D), a_hidden.astype(jnp.float32).reshape(ADAPTERS, RANK, FF), b_hidden.astype(jnp.float32).reshape(ADAPTERS, 2, RANK, FF))

    def forward(state_all, am_table, bm_table, ah_table, bh_table, ad_table, bd_table):
        tables = (am_table, bm_table, ah_table, bh_table, ad_table, bd_table)

        def advance(running, per_seq):
            state, segment_ids, chosen = per_seq
            picked = tuple((table[chosen] for table in tables))
            return (running, apply_layer(state, segment_ids, frozen, picked))
        unused, outputs = lax.scan(jax.checkpoint(advance), jnp.zeros((), jnp.float32), (state_all, segments, adapter_index))
        return outputs
    outputs, pullback = jax.vjp(forward, tokens.astype(jnp.float32), *factors)
    gradients = pullback(cotangent.astype(jnp.float32))
    return (outputs.astype(jnp.bfloat16), gradients[0], gradients[1], gradients[2], gradients[3].reshape(ADAPTERS, RANK, HEADS, HEAD_DIM), gradients[4].reshape(ADAPTERS, 3, RANK, HEADS, HEAD_DIM), gradients[5].reshape(ADAPTERS, RANK, FG, FW), gradients[6].reshape(ADAPTERS, 2, RANK, FG, FW))
```

```python
import functools

import jax
import jax.numpy as jnp
from jax import lax
from jax.experimental import pallas as pl
from jax.experimental.pallas import tpu as pltpu
from jax.sharding import PartitionSpec as P

epsilon = 1e-06
f32 = jnp.float32
bf16 = jnp.bfloat16
VMEM_LIMIT = 56 * 1024 * 1024
log2e = 1.4426950408889634


def dot(left, right, contract):
    return lax.dot_general(left, right, (contract, ((), ())), preferred_element_type=f32)


def nn(left, right):
    return dot(left, right, ((1,), (0,)))


def nt(left, right):
    return dot(left, right, ((1,), (1,)))


def tn(left, right):
    return dot(left, right, ((0,), (0,)))


def normalize(values):
    return values * lax.rsqrt(jnp.mean(values * values, axis=-1, keepdims=True) + epsilon)


def mix_state(state, branch, rate):
    return normalize(state + rate * (normalize(branch) - state))


def swiglu(gate, up_value, scales):
    return up_value * scales[0] * jax.nn.silu(gate * scales[1])


def lane_iota(shape):
    return lax.broadcasted_iota(jnp.int32, shape, len(shape) - 1)


def swap_halves(tile, half):
    lower = lane_iota(tile.shape) % (2 * half) < half
    return jnp.where(lower, pltpu.roll(tile, 128 - half, 1), pltpu.roll(tile, half, 1))


def head_sums(tile, head_dim):
    rows = lax.broadcasted_iota(jnp.int32, (128, 128), 0) // head_dim
    cols = lax.broadcasted_iota(jnp.int32, (128, 128), 1) // head_dim
    ones = jnp.where(rows == cols, 1.0, 0.0).astype(bf16)
    high = tile.astype(bf16)
    rest = (tile - high.astype(f32)).astype(bf16)
    return nn(high, ones) + nn(rest, ones)


def prep_tile(raw, cosine, sine, scale, head_dim):
    mean = head_sums(raw * raw, head_dim) * (1.0 / head_dim)
    inverse = lax.rsqrt(mean + epsilon)
    turned = raw * cosine + swap_halves(raw, head_dim // 2) * sine
    return (turned * inverse * scale).astype(bf16), inverse


def prep_tile_back(grad, low, inverse, cosine, sine, scale, head_dim):
    unit = low.astype(f32) / scale
    grad_unit = grad * scale
    mean = head_sums(grad_unit * unit, head_dim) * (1.0 / head_dim)
    grad_turned = inverse * (grad_unit - unit * mean)
    return grad_turned * cosine - swap_halves(grad_turned, head_dim // 2) * sine


def qkv_kernel(
    dims, place, h_ref, w_ref, a_ref, b_ref, cos_ref, sin_ref, scale_ref,
    q_ref, k_ref, v_ref, u_ref, qi_ref, ki_ref,
):
    chunk, head_dim, rank = dims
    width = w_ref.shape[2]
    own = pl.ds(pl.multiple_of(place[0] * chunk, chunk), chunk)
    h = h_ref[...]
    low = nt(h, a_ref[...]).astype(bf16)
    u_ref[...] = low
    keys = nn(h, w_ref[1]) + nn(low[:, rank : 2 * rank], b_ref[1])
    cosine = cos_ref[...]
    sine = sin_ref[...]
    for tile in range(width // 128):
        cols = slice(tile * 128, tile * 128 + 128)
        k_ref[:, cols], ki_ref[:, cols] = prep_tile(
            keys[:, cols], cosine, sine, scale_ref[:, cols], head_dim
        )
    v_ref[...] = (nn(h, w_ref[2]) + nn(low[:, 2 * rank :], b_ref[2])).astype(bf16)
    h_own = h_ref[own, :]
    low_own = nt(h_own, a_ref[:rank, :]).astype(bf16)
    queries = nn(h_own, w_ref[0]) + nn(low_own, b_ref[0])
    cosine = cos_ref[own, :]
    sine = sin_ref[own, :]
    for tile in range(width // 128):
        cols = slice(tile * 128, tile * 128 + 128)
        q_ref[:, cols], qi_ref[:, cols] = prep_tile(
            queries[:, cols], cosine, sine, scale_ref[:, cols], head_dim
        )


def run_qkv(place, h_full, w, a, b, cos, sin, scale, chunks, chunk, head_dim):
    rows, model = h_full.shape
    width = w.shape[2]
    rank = b.shape[1]
    block = rows // chunks
    whole = lambda *shape: pl.BlockSpec(shape, lambda i, s: (0,) * len(shape))
    row = lambda size, cols: pl.BlockSpec((size, cols), lambda i, s: (i, 0))
    return pl.pallas_call(
        functools.partial(qkv_kernel, (chunk, head_dim, rank)),
        grid_spec=pltpu.PrefetchScalarGridSpec(
            num_scalar_prefetch=1,
            grid=(chunks,),
            in_specs=[
                row(block, model),
                whole(3, model, width),
                whole(3 * rank, model),
                whole(3, rank, width),
                row(block, 128),
                row(block, 128),
                whole(1, width),
            ],
            out_specs=[
                row(chunk, width),
                row(block, width),
                row(block, width),
                row(block, 3 * rank),
                row(chunk, width),
                row(block, width),
            ],
        ),
        out_shape=[
            jax.ShapeDtypeStruct((chunks * chunk, width), bf16),
            jax.ShapeDtypeStruct((rows, width), bf16),
            jax.ShapeDtypeStruct((rows, width), bf16),
            jax.ShapeDtypeStruct((rows, 3 * rank), bf16),
            jax.ShapeDtypeStruct((chunks * chunk, width), f32),
            jax.ShapeDtypeStruct((rows, width), f32),
        ],
        compiler_params=pltpu.CompilerParams(vmem_limit_bytes=VMEM_LIMIT),
        name="qkv",
    )(place, h_full, w, a, b, cos, sin, scale)


def spread_pair(tile, head_dim):
    lower = lane_iota(tile.shape) < head_dim
    zero = jnp.zeros_like(tile)
    return jnp.concatenate([jnp.where(lower, tile, zero), jnp.where(lower, zero, tile)], axis=0)


def allowed_mask(first, last, key_start, rows, diagonal):
    keys = key_start + lax.broadcasted_iota(jnp.int32, (rows, first.shape[1]), 0)
    mask = keys >= first
    if diagonal:
        mask = mask & (keys <= last)
    return mask


def query_bounds(start_ref, m, place, group, chunk):
    first = start_ref[:, m * chunk : (m + 1) * chunk]
    last = (m * group + place) * chunk + lane_iota((1, chunk))
    return jnp.concatenate([first, first], axis=1), jnp.concatenate([last, last], axis=1)


def attend_kernel(dims, place, start_ref, q_ref, k_ref, v_ref, o_ref, of_ref, inv_ref, vt_ref):
    chunks, chunk, group, head_dim = dims
    block = group * chunk
    vt_ref[...] = v_ref[...].T
    for m in range(chunks):
        own = slice(m * chunk, (m + 1) * chunk)
        pair = spread_pair(q_ref[own, :], head_dim)
        first, last = query_bounds(start_ref, m, place[0], group, chunk)
        total = jnp.zeros((1, 2 * chunk), f32)
        gathered = jnp.zeros((128, 2 * chunk), f32)
        for b in range(m + 1):
            at = slice(b * block, (b + 1) * block)
            scores = nt(k_ref[at, :], pair)
            mask = allowed_mask(first, last, b * block, block, b == m)
            weights = jnp.where(mask, jnp.exp2(scores * (0.125 * log2e)), 0.0)
            total = total + jnp.sum(weights, axis=0, keepdims=True)
            gathered = gathered + nn(vt_ref[:, at], weights.astype(bf16))
        inverse = 1.0 / total
        gathered = gathered * inverse
        upper = lax.broadcasted_iota(jnp.int32, (128, chunk), 0) < head_dim
        final = jnp.where(upper, gathered[:, :chunk], gathered[:, chunk:])
        of_ref[0, :, own] = final
        o_ref[own, :] = final.T.astype(bf16)
        inv_ref[0, m : m + 1, :] = inverse


def run_attend(place, start, q, k, v, chunks, chunk, group, head_dim):
    rows, width = q.shape
    keys = k.shape[0]
    pairs = width // 128
    col = lambda size: pl.BlockSpec((size, 128), lambda p, s: (0, p))
    return pl.pallas_call(
        functools.partial(attend_kernel, (chunks, chunk, group, head_dim)),
        grid_spec=pltpu.PrefetchScalarGridSpec(
            num_scalar_prefetch=1,
            grid=(pairs,),
            in_specs=[
                pl.BlockSpec((1, rows), lambda p, s: (0, 0)),
                col(rows),
                col(keys),
                col(keys),
            ],
            out_specs=[
                col(rows),
                pl.BlockSpec((1, 128, rows), lambda p, s: (p, 0, 0)),
                pl.BlockSpec((1, chunks, 2 * chunk), lambda p, s: (p, 0, 0)),
            ],
            scratch_shapes=[pltpu.VMEM((128, keys), bf16)],
        ),
        out_shape=[
            jax.ShapeDtypeStruct((rows, width), bf16),
            jax.ShapeDtypeStruct((pairs, 128, rows), f32),
            jax.ShapeDtypeStruct((pairs, chunks, 2 * chunk), f32),
        ],
        compiler_params=pltpu.CompilerParams(vmem_limit_bytes=VMEM_LIMIT),
        name="attend",
    )(place, start, q, k, v)


def attend_back_kernel(
    dims, place, start_ref, q_ref, k_ref, v_ref, g_ref, of_ref, inv_ref, qi_ref, ki_ref,
    cos_ref, sin_ref, scale_ref, gq_ref, gk_ref, gv_ref, kt_ref, gqt_ref,
):
    chunks, chunk, group, head_dim = dims
    block = group * chunk
    kt_ref[...] = k_ref[...].T
    scale = scale_ref[...]
    pairs_q, pairs_g, deltas, bounds = [], [], [], []
    for m in range(chunks):
        own = slice(m * chunk, (m + 1) * chunk)
        pairs_q.append(spread_pair(q_ref[own, :], head_dim))
        grad = g_ref[own, :]
        pairs_g.append(spread_pair(grad, head_dim))
        products = grad.astype(f32).T * of_ref[0, :, own]
        deltas.append(
            jnp.concatenate(
                [
                    jnp.sum(products[:head_dim], axis=0, keepdims=True),
                    jnp.sum(products[head_dim:], axis=0, keepdims=True),
                ],
                axis=1,
            )
        )
        bounds.append(query_bounds(start_ref, m, place[0], group, chunk))
    for b in range(chunks):
        at = slice(b * block, (b + 1) * block)
        grad_key = jnp.zeros((block, 128), f32)
        grad_value = jnp.zeros((block, 128), f32)
        for m in range(b, chunks):
            first, last = bounds[m]
            scores = nt(k_ref[at, :], pairs_q[m])
            mask = allowed_mask(first, last, b * block, block, b == m)
            weights = jnp.exp2(scores * (0.125 * log2e)) * inv_ref[0, m : m + 1, :]
            weights = jnp.where(mask, weights, 0.0)
            grad_value = grad_value + nn(weights.astype(bf16), pairs_g[m])
            grad_weights = nt(v_ref[at, :], pairs_g[m])
            grad_scores = (weights * (grad_weights - deltas[m])).astype(bf16)
            grad_key = grad_key + nn(grad_scores, pairs_q[m])
            part = nn(kt_ref[:, at], grad_scores)
            if b == 0:
                gqt_ref[m] = part
            else:
                gqt_ref[m] += part
        gv_ref[at, :] = grad_value.astype(bf16)
        gk_ref[at, :] = prep_tile_back(
            grad_key * 0.125, k_ref[at, :], ki_ref[at, :], cos_ref[at, :], sin_ref[at, :],
            scale, head_dim,
        ).astype(bf16)
    upper = lax.broadcasted_iota(jnp.int32, (128, chunk), 0) < head_dim
    for m in range(chunks):
        own = slice(m * chunk, (m + 1) * chunk)
        both = gqt_ref[m]
        grad = jnp.where(upper, both[:, :chunk], both[:, chunk:]).T * 0.125
        rows = pl.ds(pl.multiple_of((m * group + place[0]) * chunk, chunk), chunk)
        gq_ref[own, :] = prep_tile_back(
            grad, q_ref[own, :], qi_ref[own, :], cos_ref[rows, :], sin_ref[rows, :],
            scale, head_dim,
        ).astype(bf16)


def run_attend_back(
    place, start, q, k, v, grad, o_full, inverse, q_inv, k_inv, cos, sin, scale,
    chunks, chunk, group, head_dim,
):
    rows, width = q.shape
    keys = k.shape[0]
    pairs = width // 128
    col = lambda size: pl.BlockSpec((size, 128), lambda p, s: (0, p))
    whole = pl.BlockSpec((keys, 128), lambda p, s: (0, 0))
    return pl.pallas_call(
        functools.partial(attend_back_kernel, (chunks, chunk, group, head_dim)),
        grid_spec=pltpu.PrefetchScalarGridSpec(
            num_scalar_prefetch=1,
            grid=(pairs,),
            in_specs=[
                pl.BlockSpec((1, rows), lambda p, s: (0, 0)),
                col(rows),
                col(keys),
                col(keys),
                col(rows),
                pl.BlockSpec((1, 128, rows), lambda p, s: (p, 0, 0)),
                pl.BlockSpec((1, chunks, 2 * chunk), lambda p, s: (p, 0, 0)),
                col(rows),
                col(keys),
                whole,
                whole,
                col(1),
            ],
            out_specs=[col(rows), col(keys), col(keys)],
            scratch_shapes=[
                pltpu.VMEM((128, keys), bf16),
                pltpu.VMEM((chunks, 128, 2 * chunk), f32),
            ],
        ),
        out_shape=[
            jax.ShapeDtypeStruct((rows, width), bf16),
            jax.ShapeDtypeStruct((keys, width), bf16),
            jax.ShapeDtypeStruct((keys, width), bf16),
        ],
        compiler_params=pltpu.CompilerParams(vmem_limit_bytes=VMEM_LIMIT),
        name="attend_back",
    )(place, start, q, k, v, grad, o_full, inverse, q_inv, k_inv, cos, sin, scale)


def pick(array, index):
    return lax.dynamic_index_in_dim(array, index, 0, keepdims=False)


def body(
    tokens, segments, adapter_index, w_attn_in, w_attn_out, w_gate_up, w_down, qk_scale,
    mix_rates, mlp_scales, a_model, b_model, a_heads, b_heads, a_hidden, b_hidden, cotangent,
):
    slabs, chunk, model = tokens.shape
    n_seq = lax.axis_size("seq")
    n_ctx = lax.axis_size("ctx")
    group = n_ctx // slabs
    local_width = w_attn_out.shape[0]
    local_hidden = w_down.shape[0]
    head_dim = a_heads.shape[-1]
    local_heads = local_width // head_dim
    rank = a_model.shape[2]
    adapters = a_model.shape[0]
    row_width = a_hidden.shape[-1]
    half = model // 2
    place = lax.axis_index("ctx")
    slab = place // group
    inner = place % group
    core = lax.axis_index("wt")
    owners = n_seq * n_ctx
    rows = slabs * chunk
    length = rows * group

    def to_slab(array, shift):
        pairs = [(c, (c + shift * group) % n_ctx) for c in range(n_ctx)]
        return lax.ppermute(array, "ctx", pairs)

    def within_slab(array, shift):
        pairs = [(c, c - c % group + (c % group + shift) % group) for c in range(n_ctx)]
        return lax.ppermute(array, "ctx", pairs)

    def other_core(array):
        return lax.ppermute(array, "wt", [(0, 1), (1, 0)])

    def both_halves(mine):
        other = other_core(mine)
        return jnp.where(
            core == 0,
            jnp.concatenate([mine, other], axis=-1),
            jnp.concatenate([other, mine], axis=-1),
        )

    def half_cols(array, which):
        return lax.dynamic_slice_in_dim(array, which * half, half, array.ndim - 1)

    def exchange_slabs(pieces):
        result = lax.dynamic_update_index_in_dim(
            jnp.zeros_like(pieces), pick(pieces, slab), slab, 0
        )
        for shift in range(1, slabs):
            got = to_slab(pick(pieces, (slab + shift) % slabs), shift)
            result = lax.dynamic_update_index_in_dim(result, got, (slab - shift) % slabs, 0)
        return result

    def gather_inner(own):
        result = lax.dynamic_update_index_in_dim(
            jnp.zeros((group,) + own.shape, own.dtype), own, inner, 0
        )
        for shift in range(1, group):
            got = within_slab(own, shift)
            result = lax.dynamic_update_index_in_dim(result, got, (inner - shift) % group, 0)
        return result

    own_half = exchange_slabs(half_cols(tokens, core))
    full_half = jnp.moveaxis(gather_inner(own_half), 0, 1)
    h_full = both_halves(full_half.reshape(length, half))
    h_own = pick(
        jnp.moveaxis(h_full.reshape(slabs, group, chunk, model), 1, 0), inner
    ).reshape(rows, model)
    own_seg = exchange_slabs(segments)
    full_seg = jnp.moveaxis(gather_inner(own_seg), 0, 1).reshape(1, length)
    start = jnp.sum(
        (full_seg < own_seg.reshape(rows, 1)).astype(jnp.int32), axis=1
    ).reshape(1, rows)
    g_out = both_halves(exchange_slabs(half_cols(cotangent, core))).reshape(rows, model)

    adapter = pick(adapter_index, slab)
    am = pick(a_model, adapter)
    bm = pick(b_model, adapter)
    ah = pick(a_heads, adapter).reshape(rank, local_width)
    bh = pick(b_heads, adapter).reshape(3, rank, local_width)
    ad = pick(a_hidden, adapter).reshape(rank, local_hidden)
    bd = pick(b_hidden, adapter).reshape(2, rank, local_hidden)

    frequency = 10000.0 ** (-jnp.arange(head_dim // 2, dtype=f32) / (head_dim // 2))
    turn = jnp.arange(length, dtype=jnp.int32).astype(f32)[:, None] * frequency[None, :]
    cos = jnp.tile(jnp.cos(turn), (1, 256 // head_dim))
    sine = jnp.sin(turn)
    sin = jnp.tile(jnp.concatenate([-sine, sine], axis=1), (1, 128 // head_dim))
    scale = qk_scale[None, :]
    inner_arg = inner[None].astype(jnp.int32)

    q, k, v, low_qkv, q_inv, k_inv = run_qkv(
        inner_arg, h_full, w_attn_in, am[:3].reshape(3 * rank, model), bh, cos, sin, scale,
        slabs, chunk, head_dim,
    )
    attn_low, o_full, inverse = run_attend(
        inner_arg, start, q, k, v, slabs, chunk, group, head_dim
    )
    h_own32 = h_own.astype(f32)
    attn_part = nn(attn_low, w_attn_out)
    low_out_part = nt(attn_low, ah)
    attn_sum = attn_part + other_core(attn_part)
    low_out = (low_out_part + other_core(low_out_part)).astype(bf16)
    attn_raw = attn_sum + nn(low_out, bm[0])

    def first_mix(state, branch):
        return mix_state(state, branch, mix_rates[0])

    middle, first_pull = jax.vjp(first_mix, h_own32, attn_raw)
    middle_low = middle.astype(bf16)
    low_gate = nt(middle_low, am[3]).astype(bf16)
    low_up = nt(middle_low, am[4]).astype(bf16)
    gate = nn(middle_low, w_gate_up[0]) + nn(low_gate, bd[0])
    up_value = nn(middle_low, w_gate_up[1]) + nn(low_up, bd[1])

    def feed(gate, up_value):
        return swiglu(gate, up_value, mlp_scales)

    hidden, feed_pull = jax.vjp(feed, gate, up_value)
    hidden_low = hidden.astype(bf16)
    down_part = nn(hidden_low, w_down)
    low_down_part = nt(hidden_low, ad)
    low_down = (low_down_part + other_core(low_down_part)).astype(bf16)
    down_raw = down_part + other_core(down_part) + nn(low_down, bm[1])

    def second_mix(state, branch):
        return mix_state(state, branch, mix_rates[1])

    layer_out, second_pull = jax.vjp(second_mix, middle, down_raw)
    out_half = half_cols(layer_out.astype(bf16), core).reshape(slabs, chunk, half)
    layer_out_own = both_halves(exchange_slabs(out_half))

    grad_mid_res, grad_down = second_pull(g_out.astype(f32))
    grad_down_b = grad_down.astype(bf16)
    grad_bm_down = tn(low_down, grad_down_b)
    grad_low_down = nt(grad_down_b, bm[1]).astype(bf16)
    grad_ad = tn(grad_low_down, hidden_low)
    grad_hidden = nt(grad_down_b, w_down) + nn(grad_low_down, ad)
    grad_gate, grad_up = feed_pull(grad_hidden)
    grad_gate = grad_gate.astype(bf16)
    grad_up = grad_up.astype(bf16)
    grad_bd = jnp.stack([tn(low_gate, grad_gate), tn(low_up, grad_up)])
    grad_low_gate = nt(grad_gate, bd[0]).astype(bf16)
    grad_low_up = nt(grad_up, bd[1]).astype(bf16)
    grad_am_gu = jnp.stack([tn(grad_low_gate, middle_low), tn(grad_low_up, middle_low)])
    middle_part = (
        nt(grad_gate, w_gate_up[0])
        + nt(grad_up, w_gate_up[1])
        + nn(grad_low_gate, am[3])
        + nn(grad_low_up, am[4])
    )
    grad_middle = grad_mid_res + middle_part + other_core(middle_part)
    grad_input_res, grad_attn = first_pull(grad_middle)
    grad_attn_b = grad_attn.astype(bf16)
    grad_bm_attn = tn(low_out, grad_attn_b)
    grad_low_out = nt(grad_attn_b, bm[0]).astype(bf16)
    grad_ah = tn(grad_low_out, attn_low)
    grad_attended = (nt(grad_attn_b, w_attn_out) + nn(grad_low_out, ah)).astype(bf16)

    grad_q, grad_k, grad_v = run_attend_back(
        inner_arg, start, q, k, v, grad_attended, o_full, inverse, q_inv, k_inv, cos, sin,
        scale, slabs, chunk, group, head_dim,
    )

    def own_rows(array):
        parts = jnp.moveaxis(array.reshape(slabs, group, chunk, array.shape[-1]), 1, 0)
        return pick(parts, inner).reshape(rows, array.shape[-1])

    low_q = own_rows(low_qkv[:, :rank])
    low_k = low_qkv[:, rank : 2 * rank]
    low_v = low_qkv[:, 2 * rank :]
    grad_bh = jnp.stack([tn(low_q, grad_q), tn(low_k, grad_k), tn(low_v, grad_v)])
    grad_low_q = nt(grad_q, bh[0]).astype(bf16)
    grad_low_k = nt(grad_k, bh[1]).astype(bf16)
    grad_low_v = nt(grad_v, bh[2]).astype(bf16)
    grad_am_qkv = jnp.stack(
        [tn(grad_low_q, h_own), tn(grad_low_k, h_full), tn(grad_low_v, h_full)]
    )
    input_kv = (
        nt(grad_k, w_attn_in[1])
        + nt(grad_v, w_attn_in[2])
        + nn(grad_low_k, am[1])
        + nn(grad_low_v, am[2])
    )
    input_q = nt(grad_q, w_attn_in[0]) + nn(grad_low_q, am[0])

    kv_parts = jnp.moveaxis(input_kv.reshape(slabs, group, chunk, model), 1, 0)
    mine = half_cols(kv_parts, core)
    theirs = half_cols(kv_parts, 1 - core).astype(bf16)
    kv_sum = mine + other_core(theirs).astype(f32)
    input_half = (
        half_cols(input_q, core)
        + other_core(half_cols(input_q, 1 - core).astype(bf16)).astype(f32)
        + half_cols(grad_input_res, core)
        + pick(kv_sum, inner).reshape(rows, half)
    )
    for shift in range(1, group):
        sent = pick(kv_sum, (inner + shift) % group).reshape(rows, half).astype(bf16)
        input_half = input_half + within_slab(sent, shift).astype(f32)
    input_half = input_half.astype(bf16).reshape(slabs, chunk, half)
    input_grad = both_halves(exchange_slabs(input_half)).astype(f32)

    def pieces(array, lead, split):
        return array

    def by_owner(array, unit):
        lead = array.shape[:-1]
        units = array.shape[-1] // unit
        shaped = array.reshape(lead + (units, owners, unit // owners))
        return jnp.moveaxis(shaped, -2, 0).reshape(owners, -1)

    grad_am = jnp.concatenate([grad_am_qkv, grad_am_gu], axis=0)
    am_split = grad_am.reshape(5, rank, owners, 2, model // (2 * owners))
    am_split = jnp.transpose(am_split, (3, 2, 0, 1, 4)).reshape(2, owners, -1)
    am_sum = pick(am_split, core) + other_core(pick(am_split, 1 - core).astype(bf16)).astype(f32)
    flat = jnp.concatenate(
        [
            am_sum,
            by_owner(jnp.stack([grad_bm_attn, grad_bm_down]), model),
            by_owner(grad_ah, head_dim),
            by_owner(grad_bh, head_dim),
            by_owner(grad_ad, row_width),
            by_owner(grad_bd, row_width),
        ],
        axis=1,
    )
    sizes = flat.shape[1]
    by_inner = jnp.moveaxis(flat.reshape(n_seq, slabs, group, sizes), 2, 0)
    table = pick(by_inner, inner)
    for shift in range(1, group):
        sent = pick(by_inner, (inner + shift) % group).astype(bf16)
        table = table + within_slab(sent, shift).astype(f32)
    table = jnp.moveaxis(table, 1, 0).astype(bf16)
    table = exchange_slabs(table)
    seq_place = lax.axis_index("seq")
    by_seq = jnp.moveaxis(table, 1, 0)
    collected = jnp.zeros_like(by_seq)
    indices = jnp.zeros((n_seq,) + adapter_index.shape, jnp.int32)
    collected = lax.dynamic_update_index_in_dim(collected, pick(by_seq, seq_place), seq_place, 0)
    indices = lax.dynamic_update_index_in_dim(indices, adapter_index, seq_place, 0)
    for shift in range(1, n_seq):
        pairs = [(c, (c + shift) % n_seq) for c in range(n_seq)]
        got = lax.ppermute(pick(by_seq, (seq_place + shift) % n_seq), "seq", pairs)
        got_index = lax.ppermute(adapter_index, "seq", pairs)
        collected = lax.dynamic_update_index_in_dim(
            collected, got, (seq_place - shift) % n_seq, 0
        )
        indices = lax.dynamic_update_index_in_dim(
            indices, got_index, (seq_place - shift) % n_seq, 0
        )
    onehot = (
        jnp.arange(adapters, dtype=jnp.int32)[:, None] == indices.reshape(1, -1)
    ).astype(bf16)
    owned = nn(onehot, collected.reshape(n_seq * slabs, sizes))
    shapes = [
        (5, rank, model // (2 * owners)),
        (2, rank, model // owners),
        (rank, local_heads, head_dim // owners),
        (3, rank, local_heads, head_dim // owners),
        (rank, local_hidden // row_width, row_width // owners),
        (2, rank, local_hidden // row_width, row_width // owners),
    ]
    outputs = []
    at = 0
    for shape in shapes:
        count = 1
        for extent in shape:
            count *= extent
        outputs.append(owned[:, at : at + count].reshape((adapters,) + shape))
        at += count
    return (layer_out_own, input_grad, *outputs)


def solution(mesh):
    return jax.shard_map(
        body,
        mesh=mesh,
        in_specs=(
            P("seq", "ctx", None),
            P("seq", "ctx"),
            P("seq"),
            P(None, None, "wt"),
            P("wt", None),
            P(None, None, "wt"),
            P("wt", None),
            P("wt"),
            P(),
            P(None, "wt"),
            P(),
            P(),
            P(None, None, "wt", None),
            P(None, None, None, "wt", None),
            P(None, None, "wt", None),
            P(None, None, None, "wt", None),
            P("seq", "ctx", None),
        ),
        out_specs=(
            P("seq", "ctx", None),
            P("seq", "ctx", None),
            P(None, None, None, ("seq", "ctx", "wt")),
            P(None, None, None, ("seq", "ctx")),
            P(None, None, "wt", ("seq", "ctx")),
            P(None, None, None, "wt", ("seq", "ctx")),
            P(None, None, "wt", ("seq", "ctx")),
            P(None, None, None, "wt", ("seq", "ctx")),
        ),
        check_vma=False,
    )
```

```python
import functools

import jax
import jax.numpy as jnp
from jax import lax
from jax.experimental import pallas as pl
from jax.experimental.pallas import tpu as pltpu
from jax.sharding import PartitionSpec as P

epsilon = 1e-06
f32 = jnp.float32
bf16 = jnp.bfloat16
i32 = jnp.int32
VMEM_LIMIT = 58 * 1024 * 1024
log2e = 1.4426950408889634
LANES = 128


def dot(left, right, contract):
    return lax.dot_general(left, right, (contract, ((), ())), preferred_element_type=f32)


def nn(left, right):
    return dot(left, right, ((1,), (0,)))


def nt(left, right):
    return dot(left, right, ((1,), (1,)))


def tn(left, right):
    return dot(left, right, ((0,), (0,)))


def lane_iota(shape):
    return lax.broadcasted_iota(i32, shape, len(shape) - 1)


def row_iota(shape):
    return lax.broadcasted_iota(i32, shape, 0)


def row_mean(values):
    return jnp.mean(values, axis=-1, keepdims=True)


def inverse_rms(values):
    return lax.rsqrt(row_mean(values * values) + epsilon)


def at_rows(index, size):
    return pl.ds(pl.multiple_of(index * size, size), size)


def by_rows(total, size, step):
    lax.fori_loop(0, total // size, lambda i, c: (step(at_rows(i, size)), c)[1], 0)


def swap_halves(tile, half):
    lower = lane_iota(tile.shape) % (2 * half) < half
    return jnp.where(lower, pltpu.roll(tile, LANES - half, 1), pltpu.roll(tile, half, 1))


def head_sums(tile, head_dim):
    same = row_iota((LANES, LANES)) // head_dim == lane_iota((LANES, LANES)) // head_dim
    ones = jnp.where(same, 1.0, 0.0).astype(bf16)
    high = tile.astype(bf16)
    rest = (tile - high.astype(f32)).astype(bf16)
    return nn(high, ones) + nn(rest, ones)


def prep_tile(raw, cosine, sine, scale, head_dim):
    mean = head_sums(raw * raw, head_dim) * (1.0 / head_dim)
    inverse = lax.rsqrt(mean + epsilon)
    turned = raw * cosine + swap_halves(raw, head_dim // 2) * sine
    return (turned * inverse * scale).astype(bf16), inverse


def prep_tile_back(grad, low, inverse, cosine, sine, scale, head_dim):
    unit = low.astype(f32) / scale
    grad_unit = grad * scale
    mean = head_sums(grad_unit * unit, head_dim) * (1.0 / head_dim)
    grad_turned = inverse * (grad_unit - unit * mean)
    return (grad_turned * cosine - swap_halves(grad_turned, head_dim // 2) * sine).astype(bf16)


def spread_pair(tile, head_dim):
    lower = lane_iota(tile.shape) < head_dim
    zero = jnp.zeros_like(tile)
    return jnp.concatenate([jnp.where(lower, tile, zero), jnp.where(lower, zero, tile)], axis=0)


def allowed_mask(first, last, key_start, rows, diagonal):
    keys = key_start + row_iota((rows, first.shape[1]))
    mask = keys >= first
    if diagonal:
        mask = mask & (keys <= last)
    return mask


def query_bounds(start_ref, m, place, group, chunk):
    first = start_ref[:, m * chunk : (m + 1) * chunk]
    last = (m * group + place) * chunk + lane_iota((1, chunk))
    return jnp.concatenate([first, first], axis=1), jnp.concatenate([last, last], axis=1)


def whole_spec(shape):
    return pl.BlockSpec(shape, lambda *a: (0,) * len(shape))


def col_spec(size, width=LANES):
    return pl.BlockSpec((size, width), lambda p, s: (0, p))


def params():
    return pltpu.CompilerParams(vmem_limit_bytes=VMEM_LIMIT)


def attend_kernel(dims, place, *refs):
    slabs, chunk, group, head_dim, rank, half = dims
    count = 1 + (slabs - 1) * 2 + (group - 1) * slabs * 2
    pieces = refs[:count]
    (
        start_ref, w_ref, a_ref, b_ref, cos_ref, sin_ref, scale_ref, wout_ref, ah_ref,
        h_ref, own_ref, u_ref, q_ref, k_ref, v_ref, qi_ref, ki_ref, o_ref, of_ref, inv_ref,
        msg_ref, vt_ref, acc_ref,
    ) = refs[count:]
    inner, slab, core = place[0], place[1], place[2]
    block = group * chunk
    length = slabs * block
    rows = slabs * chunk
    model = 2 * half
    step = pl.program_id(0)

    @pl.when(step == 0)
    def _():
        mine = pl.ds(pl.multiple_of(core * half, half), half)
        other = pl.ds(pl.multiple_of((1 - core) * half, half), half)
        h_ref[at_rows(slab * group + inner, chunk), :] = pieces[0][0]
        own_ref[at_rows(slab, chunk), :] = pieces[0][0]
        at = 1
        for shift in range(1, slabs):
            source = lax.rem(slab - shift + slabs, slabs)
            rows_at = at_rows(source * group + inner, chunk)
            h_ref[rows_at, mine] = pieces[at][...]
            h_ref[rows_at, other] = pieces[at + 1][...]
            own_ref[at_rows(source, chunk), mine] = pieces[at][...]
            own_ref[at_rows(source, chunk), other] = pieces[at + 1][...]
            at += 2
        for turn in range(1, group):
            peer = lax.rem(inner - turn + group, group)
            for shift in range(slabs):
                source = lax.rem(slab - shift + slabs, slabs)
                rows_at = at_rows(source * group + peer, chunk)
                h_ref[rows_at, mine] = pieces[at][...]
                h_ref[rows_at, other] = pieces[at + 1][...]
                at += 2

        def low_rows(sl):
            u_ref[sl, :] = nt(h_ref[sl, :], a_ref[...]).astype(bf16)

        by_rows(length, 512, low_rows)
        acc_ref[...] = jnp.zeros_like(acc_ref)

    scale = scale_ref[...]
    w_kv = jnp.concatenate([w_ref[1], w_ref[2]], axis=1)

    def keys_rows(sl):
        both = nn(h_ref[sl, :], w_kv)
        low = u_ref[sl, :]
        raw = both[:, :LANES] + nn(low[:, rank : 2 * rank], b_ref[1])
        k_ref[sl, :], ki_ref[sl, :] = prep_tile(
            raw, cos_ref[sl, :], sin_ref[sl, :], scale, head_dim
        )
        v_ref[sl, :] = (both[:, LANES:] + nn(low[:, 2 * rank :], b_ref[2])).astype(bf16)

    by_rows(length, 512, keys_rows)
    queries = nn(own_ref[...], w_ref[0])
    for m in range(slabs):
        own = slice(m * chunk, (m + 1) * chunk)
        there = at_rows(m * group + inner, chunk)
        raw = queries[own] + nn(u_ref[there, :rank], b_ref[0])
        q_ref[own, :], qi_ref[own, :] = prep_tile(
            raw, cos_ref[there, :], sin_ref[there, :], scale, head_dim
        )
    vt_ref[...] = v_ref[...].T
    for m in range(slabs):
        own = slice(m * chunk, (m + 1) * chunk)
        pair = spread_pair(q_ref[own, :], head_dim)
        first, last = query_bounds(start_ref, m, inner, group, chunk)
        total = jnp.zeros((1, 2 * chunk), f32)
        gathered = jnp.zeros((LANES, 2 * chunk), f32)
        for b in range(m + 1):
            at = slice(b * block, (b + 1) * block)
            scores = nt(k_ref[at, :], pair)
            mask = allowed_mask(first, last, b * block, block, b == m)
            weights = jnp.where(mask, jnp.exp2(scores * (0.125 * log2e)), 0.0)
            total = total + jnp.sum(weights, axis=0, keepdims=True)
            gathered = gathered + nn(vt_ref[:, at], weights.astype(bf16))
        inverse = 1.0 / total
        gathered = gathered * inverse
        upper = row_iota((LANES, chunk)) < head_dim
        final = jnp.where(upper, gathered[:, :chunk], gathered[:, chunk:])
        of_ref[0, :, own] = final
        o_ref[own, :] = final.T.astype(bf16)
        inv_ref[0, m : m + 1, :] = inverse
    low_o = o_ref[...]
    acc_ref[:, :model] += nn(low_o, wout_ref[...])
    acc_ref[:, model:] += nt(low_o, ah_ref[...])

    @pl.when(step == pl.num_programs(0) - 1)
    def _():
        msg_ref[...] = acc_ref[...].astype(bf16)


def run_attend(place, tokens, pieces, start, w, a, b, cos, sin, scale, wout, ah, group, head_dim):
    slabs, chunk, model = tokens.shape
    width = w.shape[2]
    rank = b.shape[1]
    half = model // 2
    rows = slabs * chunk
    length = rows * group
    pairs = width // LANES
    in_specs = [pl.BlockSpec((1, chunk, model), lambda p, s: (s[1], 0, 0))]
    in_specs += [whole_spec((chunk, half))] * len(pieces)
    in_specs += [
        whole_spec((1, rows)),
        pl.BlockSpec((3, model, LANES), lambda p, s: (0, 0, p)),
        whole_spec((3 * rank, model)),
        pl.BlockSpec((3, rank, LANES), lambda p, s: (0, 0, p)),
        whole_spec((length, LANES)),
        whole_spec((length, LANES)),
        col_spec(1),
        pl.BlockSpec((LANES, model), lambda p, s: (p, 0)),
        col_spec(LANES),
    ]
    out = [
        ((length, model), bf16, whole_spec((length, model))),
        ((rows, model), bf16, whole_spec((rows, model))),
        ((length, 3 * rank), bf16, whole_spec((length, 3 * rank))),
        ((rows, width), bf16, col_spec(rows)),
        ((length, width), bf16, col_spec(length)),
        ((length, width), bf16, col_spec(length)),
        ((rows, width), f32, col_spec(rows)),
        ((length, width), f32, col_spec(length)),
        ((rows, width), bf16, col_spec(rows)),
        ((pairs, LANES, rows), f32, pl.BlockSpec((1, LANES, rows), lambda p, s: (p, 0, 0))),
        (
            (pairs, slabs, 2 * chunk),
            f32,
            pl.BlockSpec((1, slabs, 2 * chunk), lambda p, s: (p, 0, 0)),
        ),
        ((rows, model + LANES), bf16, whole_spec((rows, model + LANES))),
    ]
    return pl.pallas_call(
        functools.partial(attend_kernel, (slabs, chunk, group, head_dim, rank, half)),
        grid_spec=pltpu.PrefetchScalarGridSpec(
            num_scalar_prefetch=1,
            grid=(pairs,),
            in_specs=in_specs,
            out_specs=[o[2] for o in out],
            scratch_shapes=[
                pltpu.VMEM((LANES, length), bf16),
                pltpu.VMEM((rows, model + LANES), f32),
            ],
        ),
        out_shape=[jax.ShapeDtypeStruct(o[0], o[1]) for o in out],
        compiler_params=params(),
        name="attend",
    )(place, tokens, *pieces, start, w, a, b, cos, sin, scale, wout, ah)


def feed_kernel(
    dims, mine_ref, other_ref, h_ref, bo_ref, rate_ref, a_ref, wgu_ref, bgu_ref, wd_ref, ad_ref,
    scales_ref, mid_ref, u_ref, gate_ref, up_ref, msg_ref, low_ref, acc_ref,
):
    rank, model = dims
    rows = h_ref.shape[0]
    step = pl.program_id(0)

    @pl.when(step == 0)
    def _():
        def mix(sl):
            both = mine_ref[sl, :].astype(f32) + other_ref[sl, :].astype(f32)
            low = both[:, model : model + rank].astype(bf16)
            raw = both[:, :model] + nn(low, bo_ref[...])
            unit = raw * inverse_rms(raw)
            state = h_ref[sl, :].astype(f32)
            mixed = state + rate_ref[0:1, :] * (unit - state)
            mixed = mixed * inverse_rms(mixed)
            mid_ref[sl, :] = mixed
            low_ref[sl, :] = mixed.astype(bf16)

        by_rows(rows, 64, mix)
        u_ref[...] = nt(low_ref[...], a_ref[...]).astype(bf16)
        acc_ref[...] = jnp.zeros_like(acc_ref)

    low = low_ref[...]
    u = u_ref[...]
    gate = nn(low, wgu_ref[0]) + nn(u[:, :rank], bgu_ref[0])
    up = nn(low, wgu_ref[1]) + nn(u[:, rank:], bgu_ref[1])
    gate_ref[...] = gate.astype(bf16)
    up_ref[...] = up.astype(bf16)
    turned = gate * scales_ref[1:2, :]
    hidden = (up * scales_ref[0:1, :] * (turned / (1.0 + jnp.exp(-turned)))).astype(bf16)
    acc_ref[:, :model] += nn(hidden, wd_ref[...])
    acc_ref[:, model:] += nt(hidden, ad_ref[...])

    @pl.when(step == pl.num_programs(0) - 1)
    def _():
        msg_ref[...] = acc_ref[...].astype(bf16)


def run_feed(mine, other, h_own, bo, rates, a, wgu, bgu, wd, ad, scales, block):
    rows, model = h_own.shape
    hidden = wd.shape[0]
    rank = bo.shape[0]
    out = [
        ((rows, model), f32, whole_spec((rows, model))),
        ((rows, 2 * rank), bf16, whole_spec((rows, 2 * rank))),
        ((rows, hidden), bf16, pl.BlockSpec((rows, block), lambda f: (0, f))),
        ((rows, hidden), bf16, pl.BlockSpec((rows, block), lambda f: (0, f))),
        ((rows, model + LANES), bf16, whole_spec((rows, model + LANES))),
    ]
    return pl.pallas_call(
        functools.partial(feed_kernel, (rank, model)),
        grid=(hidden // block,),
        in_specs=[
            whole_spec((rows, model + LANES)),
            whole_spec((rows, model + LANES)),
            whole_spec((rows, model)),
            whole_spec((rank, model)),
            whole_spec((2, model)),
            whole_spec((2 * rank, model)),
            pl.BlockSpec((2, model, block), lambda f: (0, 0, f)),
            pl.BlockSpec((2, rank, block), lambda f: (0, 0, f)),
            pl.BlockSpec((block, model), lambda f: (f, 0)),
            pl.BlockSpec((LANES, block), lambda f: (0, f)),
            pl.BlockSpec((2, block), lambda f: (0, f)),
        ],
        out_specs=[o[2] for o in out],
        out_shape=[jax.ShapeDtypeStruct(o[0], o[1]) for o in out],
        scratch_shapes=[
            pltpu.VMEM((rows, model), bf16),
            pltpu.VMEM((rows, model + LANES), f32),
        ],
        compiler_params=params(),
        name="feed",
    )(mine, other, h_own, bo, rates, a, wgu, bgu, wd, ad, scales)


def owner_index(place, group, slabs, n_seq):
    inner, slab, seq = place
    return seq * slabs * group + slab * group + inner


def pad_lanes(tile):
    return jnp.pad(tile, ((0, 0), (0, LANES - tile.shape[1])))


def feed_back_kernel(
    dims, place, mine_ref, other_ref, mid_ref, g_own_ref, g_mine_ref, g_other_ref, bd_ref,
    rate_ref, a_ref, u_ref, gate_ref, up_ref, wgu_ref, bgu_ref, wd_ref, ad_ref, scales_ref,
    out_ref, res_ref, msg_ref, table_ref,
    gd_ref, gdt_ref, ut_ref, udt_ref, gud_ref, gudt_ref, low_ref, acc_ref, gu_ref, hid_ref,
    g_ref, lo_ref,
):
    slabs, chunk, group, n_seq, rank, model, row_width, hidden_rows = dims
    rows = slabs * chunk
    half = model // 2
    step = pl.program_id(0)
    slab, core = place[1], place[2]
    block = gate_ref.shape[1]

    @pl.when(step == 0)
    def _():
        mine = pl.ds(pl.multiple_of(core * half, half), half)
        other = pl.ds(pl.multiple_of((1 - core) * half, half), half)
        g_ref[at_rows(slab, chunk), :] = g_own_ref[0]
        for shift in range(1, slabs):
            source = at_rows(lax.rem(slab - shift + slabs, slabs), chunk)
            g_ref[source, mine] = g_mine_ref[shift - 1]
            g_ref[source, other] = g_other_ref[shift - 1]

        def mix(sl):
            both = mine_ref[sl, :].astype(f32) + other_ref[sl, :].astype(f32)
            low = both[:, model : model + rank].astype(bf16)
            hid_ref[sl, :] = low
            raw = both[:, :model] + nn(low, bd_ref[...])
            raw_inv = inverse_rms(raw)
            unit = raw * raw_inv
            state = mid_ref[sl, :]
            low_ref[sl, :] = state.astype(bf16)
            rate = rate_ref[1:2, :]
            mixed = state + rate * (unit - state)
            mixed_inv = inverse_rms(mixed)
            out = mixed * mixed_inv
            lo_ref[sl, :] = out.astype(bf16)
            grad = g_ref[sl, :].astype(f32)
            grad_mixed = mixed_inv * (grad - out * row_mean(grad * out))
            res_ref[sl, :] = (1.0 - rate) * grad_mixed
            grad_unit = rate * grad_mixed
            gd_ref[sl, :] = (raw_inv * (grad_unit - unit * row_mean(grad_unit * unit))).astype(bf16)

        by_rows(rows, 64, mix)
        out_ref[...] = lo_ref[:, mine].reshape(slabs, chunk, half)
        ut_ref[...] = u_ref[...].T
        udt_ref[...] = hid_ref[...].T
        low_gud = nt(gd_ref[...], bd_ref[...]).astype(bf16)
        gud_ref[...] = low_gud
        gudt_ref[...] = low_gud.T
        acc_ref[...] = jnp.zeros_like(acc_ref)
        gu_ref[...] = jnp.zeros_like(gu_ref)

    grad_hidden = nt(gd_ref[...], wd_ref[...]) + nn(gud_ref[...], ad_ref[...])
    gate = gate_ref[...].astype(f32)
    up = up_ref[...].astype(f32)
    up_scale = scales_ref[0:1, :]
    gate_scale = scales_ref[1:2, :]
    turned = gate * gate_scale
    sigmoid = 1.0 / (1.0 + jnp.exp(-turned))
    silu = turned * sigmoid
    up_scaled = up * up_scale
    hidden = (up_scaled * silu).astype(bf16)
    grad_up = (grad_hidden * up_scale * silu).astype(bf16)
    slope = sigmoid * (1.0 + turned * (1.0 - sigmoid)) * gate_scale
    grad_gate = (grad_hidden * up_scaled * slope).astype(bf16)
    acc_ref[...] += nt(grad_gate, wgu_ref[0]) + nt(grad_up, wgu_ref[1])
    gu_ref[:, :rank] += nt(grad_gate, bgu_ref[0])
    gu_ref[:, rank:] += nt(grad_up, bgu_ref[1])
    ut = ut_ref[...]
    parts = jnp.concatenate(
        [nn(gudt_ref[...], hidden), nn(ut[:rank], grad_gate), nn(ut[rank:], grad_up)], axis=0
    ).astype(bf16)
    tiles = block // row_width
    for tile in range(tiles):
        gdt_ref[step * tiles + tile] = parts[:, tile * row_width : (tile + 1) * row_width]

    @pl.when(step == pl.num_programs(0) - 1)
    def _():
        low_gu = gu_ref[...].astype(bf16)
        msg_ref[...] = (acc_ref[...] + nn(low_gu, a_ref[...])).astype(bf16)
        low = low_ref[...]
        model_rows = jnp.concatenate(
            [nn(low_gu.T, low), nn(udt_ref[...], gd_ref[...])], axis=0
        ).astype(bf16).astype(f32)
        ranks = 3 * rank
        units = ranks * hidden_rows
        padded = (units + LANES - 1) // LANES * LANES
        flat = gdt_ref[...].reshape(units, row_width)
        lanes = lane_iota((1, padded))
        target = lanes % hidden_rows * ranks + lanes // hidden_rows
        target = jnp.where(lanes < units, target, -1)
        moved = jnp.where(row_iota((units, padded)) == target, 1.0, 0.0).astype(bf16)
        turned_rows = tn(flat, moved)
        owners = n_seq * slabs * group
        cols = model // owners
        units_each = row_width // owners
        for y in range(group):
            for z in range(slabs):
                for x in range(n_seq):
                    d = owner_index((y, z, x), group, slabs, n_seq)
                    head = pad_lanes(model_rows[:, d * cols : (d + 1) * cols])
                    mine = turned_rows[d * units_each : (d + 1) * units_each]
                    tail = [
                        mine[:, t * LANES : (t + 1) * LANES] for t in range(padded // LANES)
                    ]
                    table_ref[y, z, x] = jnp.concatenate([head] + tail, axis=0).astype(bf16)


def run_feed_back(
    place, mine, other, mid, cotangent, g_mine, g_other, bd_model, rates, a, u, gate, up, wgu,
    bgu, wd, ad, scales, block, group, n_seq, row_width,
):
    slabs, chunk, model = cotangent.shape
    rows = slabs * chunk
    half = model // 2
    hidden = wd.shape[0]
    rank = bd_model.shape[0]
    hidden_rows = hidden // row_width
    owners = n_seq * slabs * group
    padded = (3 * rank * hidden_rows + LANES - 1) // LANES * LANES
    table_rows = 3 * rank + row_width // owners * (padded // LANES)
    out = [
        ((slabs, chunk, half), bf16),
        ((rows, model), f32),
        ((rows, model), bf16),
        ((group, slabs, n_seq, table_rows, LANES), bf16),
    ]
    return pl.pallas_call(
        functools.partial(
            feed_back_kernel,
            (slabs, chunk, group, n_seq, rank, model, row_width, hidden_rows),
        ),
        grid_spec=pltpu.PrefetchScalarGridSpec(
            num_scalar_prefetch=1,
            grid=(hidden // block,),
            in_specs=[
                whole_spec((rows, model + LANES)),
                whole_spec((rows, model + LANES)),
                whole_spec((rows, model)),
                pl.BlockSpec((1, chunk, model), lambda f, s: (s[1], 0, 0)),
                whole_spec((slabs - 1, chunk, half)),
                whole_spec((slabs - 1, chunk, half)),
                whole_spec((rank, model)),
                whole_spec((2, model)),
                whole_spec((2 * rank, model)),
                whole_spec((rows, 2 * rank)),
                col_spec(rows, block),
                col_spec(rows, block),
                pl.BlockSpec((2, model, block), lambda f, s: (0, 0, f)),
                pl.BlockSpec((2, rank, block), lambda f, s: (0, 0, f)),
                pl.BlockSpec((block, model), lambda f, s: (f, 0)),
                col_spec(rank, block),
                col_spec(2, block),
            ],
            out_specs=[whole_spec(o[0]) for o in out],
            scratch_shapes=[
                pltpu.VMEM((rows, model), bf16),
                pltpu.VMEM((hidden_rows, 3 * rank, row_width), bf16),
                pltpu.VMEM((2 * rank, rows), bf16),
                pltpu.VMEM((rank, rows), bf16),
                pltpu.VMEM((rows, rank), bf16),
                pltpu.VMEM((rank, rows), bf16),
                pltpu.VMEM((rows, model), bf16),
                pltpu.VMEM((rows, model), f32),
                pltpu.VMEM((rows, 2 * rank), f32),
                pltpu.VMEM((rows, rank), bf16),
                pltpu.VMEM((rows, model), bf16),
                pltpu.VMEM((rows, model), bf16),
            ],
        ),
        out_shape=[jax.ShapeDtypeStruct(o[0], o[1]) for o in out],
        compiler_params=params(),
        name="feed_back",
    )(
        place, mine, other, mid, cotangent, g_mine, g_other, bd_model, rates, a, u, gate, up,
        wgu, bgu, wd, ad, scales,
    )


def attend_back_kernel(
    dims, place, res_ref, gm_ref, go_ref, mid_ref, h_ref, am_ref, ao_ref, rate_ref, bo_ref,
    wout_ref, ah_ref, start_ref, q_ref, k_ref, v_ref, o_ref, of_ref, inv_ref, qi_ref, ki_ref,
    cos_ref, sin_ref, scale_ref,
    gq_ref, gk_ref, gv_ref, gres_ref, gbo_ref, gah_ref,
    kt_ref, gqt_ref, ga_ref, guo_ref, guot_ref, uo_ref,
):
    slabs, chunk, group, head_dim, rank, model = dims
    block = group * chunk
    rows = slabs * chunk
    inner = place[0]
    step = pl.program_id(0)

    @pl.when(step == 0)
    def _():
        def mix(sl):
            grad = res_ref[sl, :] + gm_ref[sl, :].astype(f32) + go_ref[sl, :].astype(f32)
            both = am_ref[sl, :].astype(f32) + ao_ref[sl, :].astype(f32)
            low = both[:, model : model + rank].astype(bf16)
            uo_ref[sl, :] = low
            raw = both[:, :model] + nn(low, bo_ref[...])
            raw_inv = inverse_rms(raw)
            unit = raw * raw_inv
            state = h_ref[sl, :].astype(f32)
            rate = rate_ref[0:1, :]
            mixed = state + rate * (unit - state)
            mixed_inv = inverse_rms(mixed)
            out = mid_ref[sl, :]
            grad_mixed = mixed_inv * (grad - out * row_mean(grad * out))
            gres_ref[sl, :] = (1.0 - rate) * grad_mixed
            grad_unit = rate * grad_mixed
            ga_ref[sl, :] = (raw_inv * (grad_unit - unit * row_mean(grad_unit * unit))).astype(bf16)

        by_rows(rows, 64, mix)
        gbo_ref[...] = nn(uo_ref[...].T, ga_ref[...])
        low_g = nt(ga_ref[...], bo_ref[...]).astype(bf16)
        guo_ref[...] = low_g
        guot_ref[...] = low_g.T

    kt_ref[...] = k_ref[...].T
    scale = scale_ref[...]
    grad_o = (nt(ga_ref[...], wout_ref[...]) + nn(guo_ref[...], ah_ref[...])).astype(bf16)
    gah_ref[...] = nn(guot_ref[...], o_ref[...])
    pairs_q, pairs_g, deltas, bounds = [], [], [], []
    for m in range(slabs):
        own = slice(m * chunk, (m + 1) * chunk)
        pairs_q.append(spread_pair(q_ref[own, :], head_dim))
        grad = grad_o[own]
        pairs_g.append(spread_pair(grad, head_dim))
        products = grad.astype(f32).T * of_ref[0, :, own]
        deltas.append(
            jnp.concatenate(
                [
                    jnp.sum(products[:head_dim], axis=0, keepdims=True),
                    jnp.sum(products[head_dim:], axis=0, keepdims=True),
                ],
                axis=1,
            )
        )
        bounds.append(query_bounds(start_ref, m, inner, group, chunk))
    for b in range(slabs):
        at = slice(b * block, (b + 1) * block)
        grad_key = jnp.zeros((block, LANES), f32)
        grad_value = jnp.zeros((block, LANES), f32)
        for m in range(b, slabs):
            first, last = bounds[m]
            scores = nt(k_ref[at, :], pairs_q[m])
            mask = allowed_mask(first, last, b * block, block, b == m)
            weights = jnp.exp2(scores * (0.125 * log2e)) * inv_ref[0, m : m + 1, :]
            weights = jnp.where(mask, weights, 0.0)
            grad_value = grad_value + nn(weights.astype(bf16), pairs_g[m])
            grad_weights = nt(v_ref[at, :], pairs_g[m])
            grad_scores = (weights * (grad_weights - deltas[m])).astype(bf16)
            grad_key = grad_key + nn(grad_scores, pairs_q[m])
            part = nn(kt_ref[:, at], grad_scores)
            if b == 0:
                gqt_ref[m] = part
            else:
                gqt_ref[m] += part
        gv_ref[at, :] = grad_value.astype(bf16)
        gk_ref[at, :] = prep_tile_back(
            grad_key * 0.125, k_ref[at, :], ki_ref[at, :], cos_ref[at, :], sin_ref[at, :],
            scale, head_dim,
        )
    upper = row_iota((LANES, chunk)) < head_dim
    for m in range(slabs):
        own = slice(m * chunk, (m + 1) * chunk)
        both = gqt_ref[m]
        grad = jnp.where(upper, both[:, :chunk], both[:, chunk:]).T * 0.125
        there = at_rows(m * group + inner, chunk)
        gq_ref[own, :] = prep_tile_back(
            grad, q_ref[own, :], qi_ref[own, :], cos_ref[there, :], sin_ref[there, :],
            scale, head_dim,
        )


def run_attend_back(
    place, res, gm, go, mid, h_own, am, ao, rates, bo, wout, ah, start, q, k, v, o, of, inv,
    qi, ki, cos, sin, scale, slabs, group, head_dim,
):
    rows, model = h_own.shape
    chunk = rows // slabs
    width = q.shape[1]
    length = k.shape[0]
    rank = bo.shape[0]
    pairs = width // LANES
    full = whole_spec((rows, model))
    out = [
        ((rows, width), bf16, col_spec(rows)),
        ((length, width), bf16, col_spec(length)),
        ((length, width), bf16, col_spec(length)),
        ((rows, model), f32, full),
        ((rank, model), f32, whole_spec((rank, model))),
        ((rank, width), f32, col_spec(rank)),
    ]
    return pl.pallas_call(
        functools.partial(attend_back_kernel, (slabs, chunk, group, head_dim, rank, model)),
        grid_spec=pltpu.PrefetchScalarGridSpec(
            num_scalar_prefetch=1,
            grid=(pairs,),
            in_specs=[
                full,
                full,
                full,
                full,
                full,
                whole_spec((rows, model + LANES)),
                whole_spec((rows, model + LANES)),
                whole_spec((2, model)),
                whole_spec((rank, model)),
                pl.BlockSpec((LANES, model), lambda p, s: (p, 0)),
                col_spec(rank),
                whole_spec((1, rows)),
                col_spec(rows),
                col_spec(length),
                col_spec(length),
                col_spec(rows),
                pl.BlockSpec((1, LANES, rows), lambda p, s: (p, 0, 0)),
                pl.BlockSpec((1, slabs, 2 * chunk), lambda p, s: (p, 0, 0)),
                col_spec(rows),
                col_spec(length),
                whole_spec((length, LANES)),
                whole_spec((length, LANES)),
                col_spec(1),
            ],
            out_specs=[o_[2] for o_ in out],
            scratch_shapes=[
                pltpu.VMEM((LANES, length), bf16),
                pltpu.VMEM((slabs, LANES, 2 * chunk), f32),
                pltpu.VMEM((rows, model), bf16),
                pltpu.VMEM((rows, rank), bf16),
                pltpu.VMEM((rank, rows), bf16),
                pltpu.VMEM((rows, rank), bf16),
            ],
        ),
        out_shape=[jax.ShapeDtypeStruct(o_[0], o_[1]) for o_ in out],
        compiler_params=params(),
        name="attend_back",
    )(
        place, res, gm, go, mid, h_own, am, ao, rates, bo, wout, ah, start, q, k, v, o, of,
        inv, qi, ki, cos, sin, scale,
    )


def others_kernel(dims, place, gk_ref, gv_ref, w_ref, a_ref, b_ref, keep_ref, send_ref, acc_ref):
    slabs, chunk, rank, model = dims
    half = model // 2
    core = place[2]
    width = gk_ref.shape[-1]
    gk = gk_ref[...].reshape(slabs * chunk, width)
    gv = gv_ref[...].reshape(slabs * chunk, width)
    low_k = nt(gk, b_ref[1]).astype(bf16)
    low_v = nt(gv, b_ref[2]).astype(bf16)
    acc_ref[...] = (
        nt(gk, w_ref[1])
        + nt(gv, w_ref[2])
        + nn(low_k, a_ref[rank : 2 * rank, :])
        + nn(low_v, a_ref[2 * rank :, :])
    )
    keep_ref[0] = acc_ref[:, pl.ds(pl.multiple_of(core * half, half), half)]
    send_ref[0] = acc_ref[:, pl.ds(pl.multiple_of((1 - core) * half, half), half)].astype(bf16)


def run_others(place, gk, gv, w, a, b, slabs, group):
    length, width = gk.shape
    chunk = length // (slabs * group)
    rows = slabs * chunk
    model = w.shape[1]
    half = model // 2
    rank = b.shape[1]
    shaped = (slabs, group, chunk, width)
    peer = pl.BlockSpec(
        (slabs, 1, chunk, width), lambda g, s: (0, lax.rem(s[0] + 1 + g, group), 0, 0)
    )
    return pl.pallas_call(
        functools.partial(others_kernel, (slabs, chunk, rank, model)),
        grid_spec=pltpu.PrefetchScalarGridSpec(
            num_scalar_prefetch=1,
            grid=(group - 1,),
            in_specs=[
                peer,
                peer,
                whole_spec((3, model, width)),
                whole_spec((3 * rank, model)),
                whole_spec((3, rank, width)),
            ],
            out_specs=[pl.BlockSpec((1, rows, half), lambda g, s: (g, 0, 0))] * 2,
            scratch_shapes=[pltpu.VMEM((rows, model), f32)],
        ),
        out_shape=[
            jax.ShapeDtypeStruct((group - 1, rows, half), f32),
            jax.ShapeDtypeStruct((group - 1, rows, half), bf16),
        ],
        compiler_params=params(),
        name="others",
    )(place, gk.reshape(shaped), gv.reshape(shaped), w, a, b)


def own_kernel(
    dims, place, gq_ref, gk_ref, gv_ref, gko_ref, gvo_ref, w_ref, a_ref, b_ref, u_ref, h_ref,
    hown_ref, res_ref, gbo_ref, gah_ref, keep_ref, send_ref, table_ref, acc_ref, uq_ref,
):
    slabs, chunk, group, n_seq, rank, model, head_dim = dims
    half = model // 2
    rows = slabs * chunk
    inner, core = place[0], place[2]
    width = gq_ref.shape[1]
    heads = width // head_dim
    gq = gq_ref[...]
    gko = gko_ref[...].reshape(rows, width)
    gvo = gvo_ref[...].reshape(rows, width)
    low_q = nt(gq, b_ref[0]).astype(bf16)
    low_k = nt(gk_ref[...], b_ref[1]).astype(bf16)
    low_v = nt(gv_ref[...], b_ref[2]).astype(bf16)
    acc_ref[...] = (
        nt(gq, w_ref[0])
        + nt(gko, w_ref[1])
        + nt(gvo, w_ref[2])
        + nn(low_q, a_ref[:rank, :])
        + nn(nt(gko, b_ref[1]).astype(bf16), a_ref[rank : 2 * rank, :])
        + nn(nt(gvo, b_ref[2]).astype(bf16), a_ref[2 * rank :, :])
    )
    mine = pl.ds(pl.multiple_of(core * half, half), half)
    keep_ref[...] = acc_ref[:, mine] + res_ref[:, mine]
    send_ref[...] = acc_ref[:, pl.ds(pl.multiple_of((1 - core) * half, half), half)].astype(bf16)

    for m in range(slabs):
        uq_ref[m * chunk : (m + 1) * chunk, :] = u_ref[at_rows(m * group + inner, chunk), :]
    h = h_ref[...]
    model_rows = jnp.concatenate(
        [
            nn(low_q.T, hown_ref[...]),
            nn(low_k.T, h),
            nn(low_v.T, h),
            gbo_ref[...],
        ],
        axis=0,
    ).astype(bf16).astype(f32)
    ut = u_ref[...].T
    uqt = uq_ref[...].T
    head_rows = jnp.concatenate(
        [
            gah_ref[...],
            nn(uqt[:rank], gq),
            nn(ut[rank : 2 * rank], gk_ref[...]),
            nn(ut[2 * rank :], gv_ref[...]),
        ],
        axis=0,
    ).astype(bf16)
    owners = n_seq * slabs * group
    cols = model // owners
    each = head_dim // owners
    units = heads * each
    spots = lax.broadcasted_iota(i32, (width, 1), 0)
    owner = spots // units
    inside = spots % units
    source = inside // each * head_dim + owner * each + inside % each
    moved = jnp.where(lane_iota((width, width)) == source, 1.0, 0.0).astype(bf16)
    turned = nt(moved, head_rows)
    gap = table_ref.shape[3] - 4 * rank - units
    for y in range(group):
        for z in range(slabs):
            for x in range(n_seq):
                d = owner_index((y, z, x), group, slabs, n_seq)
                parts = [
                    pad_lanes(model_rows[:, d * cols : (d + 1) * cols]),
                    pad_lanes(turned[d * units : (d + 1) * units]),
                ]
                if gap:
                    parts.append(jnp.zeros((gap, LANES), f32))
                table_ref[y, z, x] = jnp.concatenate(parts, axis=0).astype(bf16)


def run_own(place, gq, gk, gv, w, a, b, u, h, h_own, res, gbo, gah, slabs, group, n_seq, head_dim):
    length, width = gk.shape
    rows, model = h_own.shape
    chunk = rows // slabs
    half = model // 2
    rank = b.shape[1]
    heads = width // head_dim
    owners = n_seq * slabs * group
    units = heads * (head_dim // owners)
    table_rows = (4 * rank + units + 7) // 8 * 8
    shaped = (slabs, group, chunk, width)
    peer = pl.BlockSpec((slabs, 1, chunk, width), lambda g, s: (0, s[0], 0, 0))
    out = [
        ((rows, half), f32),
        ((rows, half), bf16),
        ((group, slabs, n_seq, table_rows, LANES), bf16),
    ]
    return pl.pallas_call(
        functools.partial(own_kernel, (slabs, chunk, group, n_seq, rank, model, head_dim)),
        grid_spec=pltpu.PrefetchScalarGridSpec(
            num_scalar_prefetch=1,
            grid=(1,),
            in_specs=[
                whole_spec((rows, width)),
                whole_spec((length, width)),
                whole_spec((length, width)),
                peer,
                peer,
                whole_spec((3, model, width)),
                whole_spec((3 * rank, model)),
                whole_spec((3, rank, width)),
                whole_spec((length, 3 * rank)),
                whole_spec((length, model)),
                whole_spec((rows, model)),
                whole_spec((rows, model)),
                whole_spec((rank, model)),
                whole_spec((rank, width)),
            ],
            out_specs=[whole_spec(o[0]) for o in out],
            scratch_shapes=[
                pltpu.VMEM((rows, model), f32),
                pltpu.VMEM((rows, 3 * rank), bf16),
            ],
        ),
        out_shape=[jax.ShapeDtypeStruct(o[0], o[1]) for o in out],
        compiler_params=params(),
        name="own",
    )(
        place, gq, gk, gv, gk.reshape(shaped), gv.reshape(shaped), w, a, b, u, h, h_own, res,
        gbo, gah,
    )


def join_kernel(slabs, place, mine_ref, other_ref, out_ref):
    half = mine_ref.shape[-1]
    core, slab = place[2], place[1]
    for shift in range(slabs):
        source = lax.rem(slab - shift + slabs, slabs)
        out_ref[source, :, pl.ds(pl.multiple_of(core * half, half), half)] = mine_ref[
            shift
        ].astype(out_ref.dtype)
        out_ref[source, :, pl.ds(pl.multiple_of((1 - core) * half, half), half)] = other_ref[
            shift
        ].astype(out_ref.dtype)


def run_join(place, mine, other, dtype):
    slabs, chunk, half = mine.shape
    return pl.pallas_call(
        functools.partial(join_kernel, slabs),
        grid_spec=pltpu.PrefetchScalarGridSpec(
            num_scalar_prefetch=1,
            grid=(1,),
            in_specs=[whole_spec(mine.shape)] * 2,
            out_specs=whole_spec((slabs, chunk, 2 * half)),
        ),
        out_shape=jax.ShapeDtypeStruct((slabs, chunk, 2 * half), dtype),
        compiler_params=params(),
        name="join",
    )(place, mine, other)


def unpack_early_kernel(dims, place, index, mine_ref, other_ref, am_ref, bm_ref, ad_ref, bd_ref):
    n_seq, slabs, rank, cols, each, hidden_rows, tiles = dims
    core = place[2]
    for s in range(n_seq):
        for r in range(slabs):
            adapter = index[s, r]
            block = mine_ref[s, r].astype(f32)
            both = block[: 2 * rank] + other_ref[s, r, : 2 * rank].astype(f32)
            left = both[:, : cols // 2]
            right = both[:, cols // 2 : cols]
            am_ref[adapter] = jnp.where(core == 0, left, right).reshape(2, rank, cols // 2)
            bm_ref[adapter] = block[2 * rank : 3 * rank, :cols]
            base = 3 * rank
            wide = jnp.concatenate(
                [block[base + t * each : base + (t + 1) * each] for t in range(tiles)], axis=1
            )
            for k in range(rank):
                ad_ref[adapter, k] = wide[:, k * hidden_rows : (k + 1) * hidden_rows]
            for j in range(2):
                for k in range(rank):
                    at = ((j + 1) * rank + k) * hidden_rows
                    bd_ref[adapter, j, k] = wide[:, at : at + hidden_rows]


def run_unpack_early(place, index, mine, other, adapters, rank, cols, each, hidden_rows):
    n_seq, slabs = mine.shape[:2]
    tiles = (mine.shape[2] - 3 * rank) // each
    shapes = [
        (adapters, 2, rank, cols // 2),
        (adapters, rank, cols),
        (adapters, rank, each, hidden_rows),
        (adapters, 2, rank, each, hidden_rows),
    ]
    return pl.pallas_call(
        functools.partial(
            unpack_early_kernel, (n_seq, slabs, rank, cols, each, hidden_rows, tiles)
        ),
        grid_spec=pltpu.PrefetchScalarGridSpec(
            num_scalar_prefetch=2,
            grid=(1,),
            in_specs=[whole_spec(mine.shape)] * 2,
            out_specs=[whole_spec(s) for s in shapes],
        ),
        out_shape=[jax.ShapeDtypeStruct(s, f32) for s in shapes],
        compiler_params=params(),
        name="unpack_early",
    )(place, index, mine, other)


def unpack_late_kernel(
    dims, place, index, mine_ref, other_ref, am_gu_ref, bm_down_ref, am_ref, bm_ref, ah_ref,
    bh_ref,
):
    n_seq, slabs, rank, cols, heads, each = dims
    core = place[2]
    for s in range(n_seq):
        for r in range(slabs):
            adapter = index[s, r]
            block = mine_ref[s, r].astype(f32)
            both = block[: 3 * rank] + other_ref[s, r, : 3 * rank].astype(f32)
            left = both[:, : cols // 2]
            right = both[:, cols // 2 : cols]
            am_ref[adapter, 0:3] = jnp.where(core == 0, left, right).reshape(3, rank, cols // 2)
            am_ref[adapter, 3:5] = am_gu_ref[adapter]
            bm_ref[adapter, 0] = block[3 * rank : 4 * rank, :cols]
            bm_ref[adapter, 1] = bm_down_ref[adapter]
            units = block[4 * rank : 4 * rank + heads * each]
            for n in range(heads):
                piece = units[n * each : (n + 1) * each]
                ah_ref[adapter, n] = piece[:, :rank]
                for j in range(3):
                    bh_ref[adapter, j, n] = piece[:, (j + 1) * rank : (j + 2) * rank]


def run_unpack_late(place, index, mine, other, am_gu, bm_down, heads, each):
    n_seq, slabs = mine.shape[:2]
    adapters, _, rank, narrow = am_gu.shape
    cols = bm_down.shape[2]
    shapes = [
        (adapters, 5, rank, narrow),
        (adapters, 2, rank, cols),
        (adapters, heads, each, rank),
        (adapters, 3, heads, each, rank),
    ]
    return pl.pallas_call(
        functools.partial(unpack_late_kernel, (n_seq, slabs, rank, cols, heads, each)),
        grid_spec=pltpu.PrefetchScalarGridSpec(
            num_scalar_prefetch=2,
            grid=(1,),
            in_specs=[
                whole_spec(mine.shape),
                whole_spec(other.shape),
                whole_spec(am_gu.shape),
                whole_spec(bm_down.shape),
            ],
            out_specs=[whole_spec(s) for s in shapes],
        ),
        out_shape=[jax.ShapeDtypeStruct(s, f32) for s in shapes],
        compiler_params=params(),
        name="unpack_late",
    )(place, index, mine, other, am_gu, bm_down)


def pick(array, index):
    return lax.dynamic_index_in_dim(array, index, 0, keepdims=False)


def body(
    tokens, segments, adapter_index, w_attn_in, w_attn_out, w_gate_up, w_down, qk_scale,
    mix_rates, mlp_scales, a_model, b_model, a_heads, b_heads, a_hidden, b_hidden, cotangent,
):
    slabs, chunk, model = tokens.shape
    n_seq = lax.axis_size("seq")
    n_ctx = lax.axis_size("ctx")
    group = n_ctx // slabs
    local_width = w_attn_out.shape[0]
    local_hidden = w_down.shape[0]
    head_dim = a_heads.shape[-1]
    local_heads = local_width // head_dim
    rank = a_model.shape[2]
    adapters = a_model.shape[0]
    row_width = a_hidden.shape[-1]
    half = model // 2
    ctx_place = lax.axis_index("ctx")
    slab = ctx_place // group
    inner = ctx_place % group
    core = lax.axis_index("wt")
    seq_place = lax.axis_index("seq")
    owners = n_seq * n_ctx
    rows = slabs * chunk
    length = rows * group
    place = jnp.stack([inner, slab, core, seq_place]).astype(i32)

    def to_slab(array, shift):
        pairs = [(c, (c + shift * group) % n_ctx) for c in range(n_ctx)]
        return lax.ppermute(array, "ctx", pairs)

    def within_slab(array, shift):
        pairs = [(c, c - c % group + (c % group + shift) % group) for c in range(n_ctx)]
        return lax.ppermute(array, "ctx", pairs)

    def to_seq(array, shift):
        return lax.ppermute(array, "seq", [(c, (c + shift) % n_seq) for c in range(n_seq)])

    def other_core(array):
        return lax.ppermute(array, "wt", [(0, 1), (1, 0)])

    def half_piece(array, index, which):
        return lax.dynamic_slice(array, (index, 0, which * half), (1, chunk, half))[0]

    own_piece = half_piece(tokens, slab, core)
    got = [own_piece] + [
        to_slab(half_piece(tokens, (slab + shift) % slabs, core), shift)
        for shift in range(1, slabs)
    ]
    pieces = []
    for shift in range(1, slabs):
        pieces += [got[shift], other_core(got[shift])]
    for turn in range(1, group):
        for shift in range(slabs):
            peer = within_slab(got[shift], turn)
            pieces += [peer, other_core(peer)]

    own_seg = lax.dynamic_update_index_in_dim(segments, pick(segments, slab), slab, 0)
    for shift in range(1, slabs):
        seg = to_slab(pick(segments, (slab + shift) % slabs), shift)
        own_seg = lax.dynamic_update_index_in_dim(own_seg, seg, (slab - shift) % slabs, 0)
    below = lambda seg: jnp.sum(
        (seg.reshape(1, rows) < own_seg.reshape(rows, 1)).astype(i32), axis=1
    )
    start = below(own_seg)
    for turn in range(1, group):
        start = start + below(within_slab(own_seg, turn))
    start = start.reshape(1, rows)

    g_mine = [
        to_slab(half_piece(cotangent, (slab + shift) % slabs, core), shift)
        for shift in range(1, slabs)
    ]
    g_mine = jnp.stack(g_mine)
    g_other = other_core(g_mine)

    adapter = pick(adapter_index, slab)
    am = pick(a_model, adapter)
    bm = pick(b_model, adapter)
    ah = pick(a_heads, adapter).reshape(rank, local_width)
    bh = pick(b_heads, adapter).reshape(3, rank, local_width)
    ad = pick(a_hidden, adapter).reshape(rank, local_hidden)
    bd = pick(b_hidden, adapter).reshape(2, rank, local_hidden)
    am_qkv = am[:3].reshape(3 * rank, model)
    am_gu = am[3:].reshape(2 * rank, model)
    ah_pad = jnp.pad(ah, ((0, LANES - rank), (0, 0)))
    ad_pad = jnp.pad(ad, ((0, LANES - rank), (0, 0)))

    frequency = 10000.0 ** (-jnp.arange(head_dim // 2, dtype=f32) / (head_dim // 2))
    turn = jnp.arange(length, dtype=i32).astype(f32)[:, None] * frequency[None, :]
    cos = jnp.tile(jnp.cos(turn), (1, 2 * LANES // head_dim))
    sine = jnp.sin(turn)
    sin = jnp.tile(jnp.concatenate([-sine, sine], axis=1), (1, LANES // head_dim))
    scale = qk_scale[None, :]

    h_full, h_own, u, q, k, v, qi, ki, o, of, inv, attn_msg = run_attend(
        place, tokens, pieces, start, w_attn_in, am_qkv, bh, cos, sin, scale, w_attn_out,
        ah_pad, group, head_dim,
    )
    attn_other = other_core(attn_msg)
    mid, u_gu, gate, up, down_msg = run_feed(
        attn_msg, attn_other, h_own, bm[0], mix_rates, am_gu, w_gate_up, bd, w_down, ad_pad,
        mlp_scales, 512,
    )
    down_other = other_core(down_msg)
    out_half, mid_res, mid_msg, early = run_feed_back(
        place, down_msg, down_other, mid, cotangent, g_mine, g_other, bm[1], mix_rates, am_gu,
        u_gu, gate, up, w_gate_up, bd, w_down, ad, mlp_scales, 512, group, n_seq, row_width,
    )
    mid_other = other_core(mid_msg)

    out_mine = jnp.stack(
        [pick(out_half, slab)]
        + [
            to_slab(pick(out_half, (slab + shift) % slabs), shift)
            for shift in range(1, slabs)
        ]
    )
    layer_out = run_join(place, out_mine, other_core(out_mine), bf16)

    index = [adapter_index]
    for shift in range(1, n_seq):
        index.append(to_seq(adapter_index, shift))
    order = (slab - jnp.arange(slabs, dtype=i32)) % slabs
    index = jnp.stack(index)[:, order]

    def send_home(table):
        total = pick(table, inner).astype(f32)
        for turn in range(1, group):
            total = total + within_slab(pick(table, (inner + turn) % group), turn).astype(f32)
        total = total.astype(bf16)
        got = [pick(total, slab)]
        for shift in range(1, slabs):
            got.append(to_slab(pick(total, (slab + shift) % slabs), shift))
        got = jnp.stack(got)
        result = [lax.dynamic_index_in_dim(got, seq_place, 1, keepdims=False)]
        for shift in range(1, n_seq):
            sent = lax.dynamic_index_in_dim(
                got, (seq_place + shift) % n_seq, 1, keepdims=False
            )
            result.append(to_seq(sent, shift))
        return jnp.stack(result)

    early = send_home(early)
    grad_am_gu, grad_bm_down, grad_ad, grad_bd = run_unpack_early(
        place, index, early, other_core(early[:, :, : 2 * rank]), adapters, rank,
        model // owners, row_width // owners, local_hidden // row_width,
    )

    gq, gk, gv, h_res, gbo, gah = run_attend_back(
        place, mid_res, mid_msg, mid_other, mid, h_own, attn_msg, attn_other, mix_rates, bm[0],
        w_attn_out, ah, start, q, k, v, o, of, inv, qi, ki, cos, sin, scale, slabs, group,
        head_dim,
    )
    keep, send = run_others(place, gk, gv, w_attn_in, am_qkv, bh, slabs, group)
    others = (keep + other_core(send).astype(f32)).astype(bf16)
    own_keep, own_send, late = run_own(
        place, gq, gk, gv, w_attn_in, am_qkv, bh, u, h_full, h_own, h_res, gbo, gah, slabs,
        group, n_seq, head_dim,
    )
    own_got = other_core(own_send)
    others = others.reshape(group - 1, slabs, chunk, half)
    own_keep = own_keep.reshape(slabs, chunk, half)
    own_got = own_got.reshape(slabs, chunk, half)
    result = [None] * slabs
    for shift in [2, 1, 3, 0] if slabs == 4 else list(range(slabs)):
        target = (slab + shift) % slabs
        total = pick(own_keep, target) + pick(own_got, target).astype(f32)
        for turn in range(1, group):
            got = within_slab(pick(others[turn - 1], target), turn)
            total = total + got.astype(f32)
        total = total.astype(bf16)
        result[shift] = to_slab(total, shift) if shift else total
    result = jnp.stack(result)
    input_grad = run_join(place, result, other_core(result), f32)

    late = send_home(late)
    grad_am, grad_bm, grad_ah, grad_bh = run_unpack_late(
        place, index, late, other_core(late[:, :, : 3 * rank]), grad_am_gu, grad_bm_down,
        local_heads, head_dim // owners,
    )
    return (
        layer_out,
        input_grad,
        grad_am,
        grad_bm,
        jnp.transpose(grad_ah, (0, 3, 1, 2)),
        jnp.transpose(grad_bh, (0, 1, 4, 2, 3)),
        jnp.transpose(grad_ad, (0, 1, 3, 2)),
        jnp.transpose(grad_bd, (0, 1, 2, 4, 3)),
    )


def solution(mesh):
    return jax.shard_map(
        body,
        mesh=mesh,
        in_specs=(
            P("seq", "ctx", None),
            P("seq", "ctx"),
            P("seq"),
            P(None, None, "wt"),
            P("wt", None),
            P(None, None, "wt"),
            P("wt", None),
            P("wt"),
            P(),
            P(None, "wt"),
            P(),
            P(),
            P(None, None, "wt", None),
            P(None, None, None, "wt", None),
            P(None, None, "wt", None),
            P(None, None, None, "wt", None),
            P("seq", "ctx", None),
        ),
        out_specs=(
            P("seq", "ctx", None),
            P("seq", "ctx", None),
            P(None, None, None, ("seq", "ctx", "wt")),
            P(None, None, None, ("seq", "ctx")),
            P(None, None, "wt", ("seq", "ctx")),
            P(None, None, None, "wt", ("seq", "ctx")),
            P(None, None, "wt", ("seq", "ctx")),
            P(None, None, None, "wt", ("seq", "ctx")),
        ),
        check_vma=False,
    )
```

```python
import functools

import jax
import jax.numpy as jnp
from jax import lax
from jax.experimental import pallas as pl
from jax.experimental.pallas import tpu as pltpu
from jax.sharding import PartitionSpec as P

epsilon = 1e-06
f32 = jnp.float32
bf16 = jnp.bfloat16
i32 = jnp.int32
VMEM_LIMIT = 58 * 1024 * 1024
log2e = 1.4426950408889634
LANES = 128


def dot(left, right, contract):
    return lax.dot_general(left, right, (contract, ((), ())), preferred_element_type=f32)


def nn(left, right):
    return dot(left, right, ((1,), (0,)))


def nt(left, right):
    return dot(left, right, ((1,), (1,)))


def tn(left, right):
    return dot(left, right, ((0,), (0,)))


def lane_iota(shape):
    return lax.broadcasted_iota(i32, shape, len(shape) - 1)


def row_iota(shape):
    return lax.broadcasted_iota(i32, shape, 0)


def row_mean(values):
    return jnp.mean(values, axis=-1, keepdims=True)


def inverse_rms(values):
    return lax.rsqrt(row_mean(values * values) + epsilon)


def at_rows(index, size):
    return pl.ds(pl.multiple_of(index * size, size), size)


def by_rows(total, size, step):
    lax.fori_loop(0, total // size, lambda i, c: (step(at_rows(i, size)), c)[1], 0)


def swap_halves(tile, half):
    lower = lane_iota(tile.shape) % (2 * half) < half
    return jnp.where(lower, pltpu.roll(tile, LANES - half, 1), pltpu.roll(tile, half, 1))


def head_sums(tile, head_dim):
    same = row_iota((LANES, LANES)) // head_dim == lane_iota((LANES, LANES)) // head_dim
    ones = jnp.where(same, 1.0, 0.0).astype(bf16)
    high = tile.astype(bf16)
    rest = (tile - high.astype(f32)).astype(bf16)
    return nn(high, ones) + nn(rest, ones)


def prep_tile(raw, cosine, sine, scale, head_dim):
    mean = head_sums(raw * raw, head_dim) * (1.0 / head_dim)
    inverse = lax.rsqrt(mean + epsilon)
    turned = raw * cosine + swap_halves(raw, head_dim // 2) * sine
    return (turned * inverse * scale).astype(bf16), inverse


def prep_tile_back(grad, low, inverse, cosine, sine, scale, head_dim):
    unit = low.astype(f32) / scale
    grad_unit = grad * scale
    mean = head_sums(grad_unit * unit, head_dim) * (1.0 / head_dim)
    grad_turned = inverse * (grad_unit - unit * mean)
    return (grad_turned * cosine - swap_halves(grad_turned, head_dim // 2) * sine).astype(bf16)


def spread_pair(tile, head_dim):
    lower = lane_iota(tile.shape) < head_dim
    zero = jnp.zeros_like(tile)
    return jnp.concatenate([jnp.where(lower, tile, zero), jnp.where(lower, zero, tile)], axis=0)


def allowed_mask(first, last, key_start, rows, diagonal):
    keys = key_start + row_iota((rows, first.shape[1]))
    mask = keys >= first
    if diagonal:
        mask = mask & (keys <= last)
    return mask


def query_bounds(start_ref, m, place, group, chunk):
    first = start_ref[m : m + 1, :]
    last = (m * group + place) * chunk + lane_iota((1, chunk))
    return jnp.concatenate([first, first], axis=1), jnp.concatenate([last, last], axis=1)


def whole_spec(shape):
    return pl.BlockSpec(shape, lambda *a: (0,) * len(shape))


def col_spec(size, width=LANES):
    return pl.BlockSpec((size, width), lambda p, s: (0, p))


def params():
    return pltpu.CompilerParams(vmem_limit_bytes=VMEM_LIMIT)


def cost(flops, moved, transcendentals=0):
    return pl.CostEstimate(
        flops=int(flops), bytes_accessed=int(moved), transcendentals=int(transcendentals)
    )


def attend_kernel(dims, place, *refs):
    slabs, chunk, group, head_dim, rank, half = dims
    count = 2 + (slabs - 1) * 2 + (group - 1) * slabs * 2
    pieces = refs[:count]
    (
        w_ref, a_ref, b_ref, cos_ref, sin_ref, scale_ref, wout_ref, ah_ref,
        h_ref, own_ref, u_ref, q_ref, k_ref, v_ref, qi_ref, ki_ref, o_ref, of_ref, inv_ref,
        msg_ref, start_ref, vt_ref, acc_ref, seg_ref,
    ) = refs[count:]
    inner, slab, core = place[0], place[1], place[2]
    block = group * chunk
    length = slabs * block
    rows = slabs * chunk
    model = 2 * half
    step = pl.program_id(0)

    @pl.when(step == 0)
    def _():
        mine = pl.ds(pl.multiple_of(core * half, half), half)
        other = pl.ds(pl.multiple_of((1 - core) * half, half), half)
        h_ref[at_rows(slab * group + inner, chunk), :] = pieces[0][0]
        own_ref[at_rows(slab, chunk), :] = pieces[0][0]
        seg_ref[...] = jnp.zeros_like(seg_ref)

        def keep_segments(where, piece):
            tail = piece[chunk:, :chunk].astype(f32)
            seg_ref[pl.ds(where, 1), :] = tail[0:1]

        keep_segments(slab * group + inner, pieces[1])
        at = 2
        for shift in range(1, slabs):
            source = lax.rem(slab - shift + slabs, slabs)
            rows_at = at_rows(source * group + inner, chunk)
            h_ref[rows_at, mine] = pieces[at][:chunk, :]
            h_ref[rows_at, other] = pieces[at + 1][:chunk, :]
            own_ref[at_rows(source, chunk), mine] = pieces[at][:chunk, :]
            own_ref[at_rows(source, chunk), other] = pieces[at + 1][:chunk, :]
            keep_segments(source * group + inner, pieces[at])
            at += 2
        for turn in range(1, group):
            peer = lax.rem(inner - turn + group, group)
            for shift in range(slabs):
                source = lax.rem(slab - shift + slabs, slabs)
                rows_at = at_rows(source * group + peer, chunk)
                h_ref[rows_at, mine] = pieces[at][:chunk, :]
                h_ref[rows_at, other] = pieces[at + 1][:chunk, :]
                keep_segments(source * group + peer, pieces[at])
                at += 2
        columns = seg_ref[...].T
        for m in range(slabs):
            line = seg_ref[pl.ds(m * group + inner, 1), :]
            below = jnp.zeros((chunk, chunk), f32)
            for c in range(slabs * group):
                below = below + jnp.where(columns[:, c : c + 1] < line, 1.0, 0.0)
            start_ref[m : m + 1, :] = jnp.sum(below, axis=0, keepdims=True).astype(i32)

        def low_rows(sl):
            u_ref[sl, :] = nt(h_ref[sl, :], a_ref[...]).astype(bf16)

        by_rows(length, 512, low_rows)
        acc_ref[...] = jnp.zeros_like(acc_ref)

    scale = scale_ref[...]
    w_kv = jnp.concatenate([w_ref[1], w_ref[2]], axis=1)

    def keys_rows(sl):
        both = nn(h_ref[sl, :], w_kv)
        low = u_ref[sl, :]
        raw = both[:, :LANES] + nn(low[:, rank : 2 * rank], b_ref[1])
        k_ref[sl, :], ki_ref[sl, :] = prep_tile(
            raw, cos_ref[sl, :], sin_ref[sl, :], scale, head_dim
        )
        v_ref[sl, :] = (both[:, LANES:] + nn(low[:, 2 * rank :], b_ref[2])).astype(bf16)

    by_rows(length, 512, keys_rows)
    queries = nn(own_ref[...], w_ref[0])
    for m in range(slabs):
        own = slice(m * chunk, (m + 1) * chunk)
        there = at_rows(m * group + inner, chunk)
        raw = queries[own] + nn(u_ref[there, :rank], b_ref[0])
        q_ref[own, :], qi_ref[own, :] = prep_tile(
            raw, cos_ref[there, :], sin_ref[there, :], scale, head_dim
        )
    vt_ref[...] = v_ref[...].T
    for m in range(slabs):
        own = slice(m * chunk, (m + 1) * chunk)
        pair = spread_pair(q_ref[own, :], head_dim)
        first, last = query_bounds(start_ref, m, inner, group, chunk)
        total = jnp.zeros((1, 2 * chunk), f32)
        gathered = jnp.zeros((LANES, 2 * chunk), f32)
        for b in range(m + 1):
            at = slice(b * block, (b + 1) * block)
            scores = nt(k_ref[at, :], pair)
            mask = allowed_mask(first, last, b * block, block, b == m)
            weights = jnp.where(mask, jnp.exp2(scores * (0.125 * log2e)), 0.0)
            total = total + jnp.sum(weights, axis=0, keepdims=True)
            gathered = gathered + nn(vt_ref[:, at], weights.astype(bf16))
        inverse = 1.0 / total
        gathered = gathered * inverse
        upper = row_iota((LANES, chunk)) < head_dim
        final = jnp.where(upper, gathered[:, :chunk], gathered[:, chunk:])
        of_ref[0, :, own] = final
        o_ref[own, :] = final.T.astype(bf16)
        inv_ref[0, m : m + 1, :] = inverse
    low_o = o_ref[...]
    acc_ref[:, :model] += nn(low_o, wout_ref[...])
    acc_ref[:, model:] += nt(low_o, ah_ref[...])

    @pl.when(step == pl.num_programs(0) - 1)
    def _():
        msg_ref[...] = acc_ref[...].astype(bf16)


def run_attend(place, tokens, pieces, w, a, b, cos, sin, scale, wout, ah, group, head_dim):
    slabs, chunk, model = tokens.shape
    width = w.shape[2]
    rank = b.shape[1]
    half = model // 2
    rows = slabs * chunk
    length = rows * group
    pairs = width // LANES
    in_specs = [pl.BlockSpec((1, chunk, model), lambda p, s: (s[1], 0, 0))]
    in_specs += [whole_spec(piece.shape) for piece in pieces]
    in_specs += [
        pl.BlockSpec((3, model, LANES), lambda p, s: (0, 0, p)),
        whole_spec((3 * rank, model)),
        pl.BlockSpec((3, rank, LANES), lambda p, s: (0, 0, p)),
        whole_spec((length, LANES)),
        whole_spec((length, LANES)),
        col_spec(1),
        pl.BlockSpec((LANES, model), lambda p, s: (p, 0)),
        col_spec(LANES),
    ]
    out = [
        ((length, model), bf16, whole_spec((length, model))),
        ((rows, model), bf16, whole_spec((rows, model))),
        ((length, 3 * rank), bf16, whole_spec((length, 3 * rank))),
        ((rows, width), bf16, col_spec(rows)),
        ((length, width), bf16, col_spec(length)),
        ((length, width), bf16, col_spec(length)),
        ((rows, width), f32, col_spec(rows)),
        ((length, width), f32, col_spec(length)),
        ((rows, width), bf16, col_spec(rows)),
        ((pairs, LANES, rows), f32, pl.BlockSpec((1, LANES, rows), lambda p, s: (p, 0, 0))),
        (
            (pairs, slabs, 2 * chunk),
            f32,
            pl.BlockSpec((1, slabs, 2 * chunk), lambda p, s: (p, 0, 0)),
        ),
        ((rows, model + LANES), bf16, whole_spec((rows, model + LANES))),
        ((slabs, chunk), i32, whole_spec((slabs, chunk))),
    ]
    return pl.pallas_call(
        functools.partial(attend_kernel, (slabs, chunk, group, head_dim, rank, half)),
        grid_spec=pltpu.PrefetchScalarGridSpec(
            num_scalar_prefetch=1,
            grid=(pairs,),
            in_specs=in_specs,
            out_specs=[o[2] for o in out],
            scratch_shapes=[
                pltpu.VMEM((LANES, length), bf16),
                pltpu.VMEM((rows, model + LANES), f32),
                pltpu.VMEM((chunk, chunk), f32),
            ],
        ),
        out_shape=[jax.ShapeDtypeStruct(o[0], o[1]) for o in out],
        compiler_params=params(),
        cost_estimate=cost(3e10, 4e7),
        name="attend",
    )(place, tokens, *pieces, w, a, b, cos, sin, scale, wout, ah)


def feed_kernel(
    dims, mine_ref, other_ref, h_ref, bo_ref, rate_ref, a_ref, wgu_ref, bgu_ref, wd_ref, ad_ref,
    scales_ref, mid_ref, u_ref, gate_ref, up_ref, msg_ref, low_ref, acc_ref,
):
    rank, model = dims
    rows = h_ref.shape[0]
    step = pl.program_id(0)

    @pl.when(step == 0)
    def _():
        def mix(sl):
            both = mine_ref[sl, :].astype(f32) + other_ref[sl, :].astype(f32)
            low = both[:, model : model + rank].astype(bf16)
            raw = both[:, :model] + nn(low, bo_ref[...])
            unit = raw * inverse_rms(raw)
            state = h_ref[sl, :].astype(f32)
            mixed = state + rate_ref[0:1, :] * (unit - state)
            mixed = mixed * inverse_rms(mixed)
            mid_ref[sl, :] = mixed
            low_ref[sl, :] = mixed.astype(bf16)

        by_rows(rows, 64, mix)
        u_ref[...] = nt(low_ref[...], a_ref[...]).astype(bf16)
        acc_ref[...] = jnp.zeros_like(acc_ref)

    low = low_ref[...]
    u = u_ref[...]
    gate = nn(low, wgu_ref[0]) + nn(u[:, :rank], bgu_ref[0])
    up = nn(low, wgu_ref[1]) + nn(u[:, rank:], bgu_ref[1])
    gate_ref[...] = gate.astype(bf16)
    up_ref[...] = up.astype(bf16)
    turned = gate * scales_ref[1:2, :]
    hidden = (up * scales_ref[0:1, :] * (turned / (1.0 + jnp.exp(-turned)))).astype(bf16)
    acc_ref[:, :model] += nn(hidden, wd_ref[...])
    acc_ref[:, model:] += nt(hidden, ad_ref[...])

    @pl.when(step == pl.num_programs(0) - 1)
    def _():
        msg_ref[...] = acc_ref[...].astype(bf16)


def run_feed(mine, other, h_own, bo, rates, a, wgu, bgu, wd, ad, scales, block):
    rows, model = h_own.shape
    hidden = wd.shape[0]
    rank = bo.shape[0]
    out = [
        ((rows, model), f32, whole_spec((rows, model))),
        ((rows, 2 * rank), bf16, whole_spec((rows, 2 * rank))),
        ((rows, hidden), bf16, pl.BlockSpec((rows, block), lambda f: (0, f))),
        ((rows, hidden), bf16, pl.BlockSpec((rows, block), lambda f: (0, f))),
        ((rows, model + LANES), bf16, whole_spec((rows, model + LANES))),
    ]
    return pl.pallas_call(
        functools.partial(feed_kernel, (rank, model)),
        grid=(hidden // block,),
        in_specs=[
            whole_spec((rows, model + LANES)),
            whole_spec((rows, model + LANES)),
            whole_spec((rows, model)),
            whole_spec((rank, model)),
            whole_spec((2, model)),
            whole_spec((2 * rank, model)),
            pl.BlockSpec((2, model, block), lambda f: (0, 0, f)),
            pl.BlockSpec((2, rank, block), lambda f: (0, 0, f)),
            pl.BlockSpec((block, model), lambda f: (f, 0)),
            pl.BlockSpec((LANES, block), lambda f: (0, f)),
            pl.BlockSpec((2, block), lambda f: (0, f)),
        ],
        out_specs=[o[2] for o in out],
        out_shape=[jax.ShapeDtypeStruct(o[0], o[1]) for o in out],
        scratch_shapes=[
            pltpu.VMEM((rows, model), bf16),
            pltpu.VMEM((rows, model + LANES), f32),
        ],
        compiler_params=params(),
        cost_estimate=cost(2.4e10, 3e7),
        name="feed",
    )(mine, other, h_own, bo, rates, a, wgu, bgu, wd, ad, scales)


def owner_index(place, group, slabs, n_seq):
    inner, slab, seq = place
    return seq * slabs * group + slab * group + inner


def pad_lanes(tile):
    return jnp.pad(tile, ((0, 0), (0, LANES - tile.shape[1])))


def feed_back_kernel(
    dims, place, mine_ref, other_ref, mid_ref, g_own_ref, g_mine_ref, g_other_ref, bd_ref,
    rate_ref, a_ref, u_ref, gate_ref, up_ref, wgu_ref, bgu_ref, wd_ref, ad_ref, scales_ref,
    out_ref, res_ref, msg_ref, table_ref,
    gd_ref, gdt_ref, ut_ref, udt_ref, gud_ref, gudt_ref, low_ref, acc_ref, gu_ref, hid_ref,
    g_ref, lo_ref,
):
    slabs, chunk, group, n_seq, rank, model, row_width, hidden_rows = dims
    rows = slabs * chunk
    half = model // 2
    step = pl.program_id(0)
    slab, core = place[1], place[2]
    block = gate_ref.shape[1]

    @pl.when(step == 0)
    def _():
        mine = pl.ds(pl.multiple_of(core * half, half), half)
        other = pl.ds(pl.multiple_of((1 - core) * half, half), half)
        g_ref[at_rows(slab, chunk), :] = g_own_ref[0]
        for shift in range(1, slabs):
            source = at_rows(lax.rem(slab - shift + slabs, slabs), chunk)
            g_ref[source, mine] = g_mine_ref[shift - 1]
            g_ref[source, other] = g_other_ref[shift - 1]

        def mix(sl):
            both = mine_ref[sl, :].astype(f32) + other_ref[sl, :].astype(f32)
            low = both[:, model : model + rank].astype(bf16)
            hid_ref[sl, :] = low
            raw = both[:, :model] + nn(low, bd_ref[...])
            raw_inv = inverse_rms(raw)
            unit = raw * raw_inv
            state = mid_ref[sl, :]
            low_ref[sl, :] = state.astype(bf16)
            rate = rate_ref[1:2, :]
            mixed = state + rate * (unit - state)
            mixed_inv = inverse_rms(mixed)
            out = mixed * mixed_inv
            lo_ref[sl, :] = out.astype(bf16)
            grad = g_ref[sl, :].astype(f32)
            grad_mixed = mixed_inv * (grad - out * row_mean(grad * out))
            res_ref[sl, :] = (1.0 - rate) * grad_mixed
            grad_unit = rate * grad_mixed
            gd_ref[sl, :] = (raw_inv * (grad_unit - unit * row_mean(grad_unit * unit))).astype(bf16)

        by_rows(rows, 64, mix)
        out_ref[...] = lo_ref[:, mine].reshape(slabs, chunk, half)
        ut_ref[...] = u_ref[...].T
        udt_ref[...] = hid_ref[...].T
        low_gud = nt(gd_ref[...], bd_ref[...]).astype(bf16)
        gud_ref[...] = low_gud
        gudt_ref[...] = low_gud.T
        acc_ref[...] = jnp.zeros_like(acc_ref)
        gu_ref[...] = jnp.zeros_like(gu_ref)

    grad_hidden = nt(gd_ref[...], wd_ref[...]) + nn(gud_ref[...], ad_ref[...])
    gate = gate_ref[...].astype(f32)
    up = up_ref[...].astype(f32)
    up_scale = scales_ref[0:1, :]
    gate_scale = scales_ref[1:2, :]
    turned = gate * gate_scale
    sigmoid = 1.0 / (1.0 + jnp.exp(-turned))
    silu = turned * sigmoid
    up_scaled = up * up_scale
    hidden = (up_scaled * silu).astype(bf16)
    grad_up = (grad_hidden * up_scale * silu).astype(bf16)
    slope = sigmoid * (1.0 + turned * (1.0 - sigmoid)) * gate_scale
    grad_gate = (grad_hidden * up_scaled * slope).astype(bf16)
    acc_ref[...] += nt(grad_gate, wgu_ref[0]) + nt(grad_up, wgu_ref[1])
    gu_ref[:, :rank] += nt(grad_gate, bgu_ref[0])
    gu_ref[:, rank:] += nt(grad_up, bgu_ref[1])
    ut = ut_ref[...]
    parts = jnp.concatenate(
        [nn(gudt_ref[...], hidden), nn(ut[:rank], grad_gate), nn(ut[rank:], grad_up)], axis=0
    ).astype(bf16)
    tiles = block // row_width
    for tile in range(tiles):
        gdt_ref[step * tiles + tile] = parts[:, tile * row_width : (tile + 1) * row_width]

    @pl.when(step == pl.num_programs(0) - 1)
    def _():
        low_gu = gu_ref[...].astype(bf16)
        msg_ref[...] = (acc_ref[...] + nn(low_gu, a_ref[...])).astype(bf16)
        low = low_ref[...]
        model_rows = jnp.concatenate(
            [nn(low_gu.T, low), nn(udt_ref[...], gd_ref[...])], axis=0
        ).astype(bf16).astype(f32)
        ranks = 3 * rank
        units = ranks * hidden_rows
        padded = (units + LANES - 1) // LANES * LANES
        flat = gdt_ref[...].reshape(units, row_width)
        lanes = lane_iota((1, padded))
        target = lanes % hidden_rows * ranks + lanes // hidden_rows
        target = jnp.where(lanes < units, target, -1)
        moved = jnp.where(row_iota((units, padded)) == target, 1.0, 0.0).astype(bf16)
        turned_rows = tn(flat, moved)
        owners = n_seq * slabs * group
        cols = model // owners
        units_each = row_width // owners
        for y in range(group):
            for z in range(slabs):
                for x in range(n_seq):
                    d = owner_index((y, z, x), group, slabs, n_seq)
                    head = pad_lanes(model_rows[:, d * cols : (d + 1) * cols])
                    mine = turned_rows[d * units_each : (d + 1) * units_each]
                    tail = [
                        mine[:, t * LANES : (t + 1) * LANES] for t in range(padded // LANES)
                    ]
                    table_ref[y, z, x] = jnp.concatenate([head] + tail, axis=0).astype(bf16)


def run_feed_back(
    place, mine, other, mid, cotangent, g_mine, g_other, bd_model, rates, a, u, gate, up, wgu,
    bgu, wd, ad, scales, block, group, n_seq, row_width,
):
    slabs, chunk, model = cotangent.shape
    rows = slabs * chunk
    half = model // 2
    hidden = wd.shape[0]
    rank = bd_model.shape[0]
    hidden_rows = hidden // row_width
    owners = n_seq * slabs * group
    padded = (3 * rank * hidden_rows + LANES - 1) // LANES * LANES
    table_rows = 3 * rank + row_width // owners * (padded // LANES)
    out = [
        ((slabs, chunk, half), bf16),
        ((rows, model), f32),
        ((rows, model), bf16),
        ((group, slabs, n_seq, table_rows, LANES), bf16),
    ]
    return pl.pallas_call(
        functools.partial(
            feed_back_kernel,
            (slabs, chunk, group, n_seq, rank, model, row_width, hidden_rows),
        ),
        grid_spec=pltpu.PrefetchScalarGridSpec(
            num_scalar_prefetch=1,
            grid=(hidden // block,),
            in_specs=[
                whole_spec((rows, model + LANES)),
                whole_spec((rows, model + LANES)),
                whole_spec((rows, model)),
                pl.BlockSpec((1, chunk, model), lambda f, s: (s[1], 0, 0)),
                whole_spec((slabs - 1, chunk, half)),
                whole_spec((slabs - 1, chunk, half)),
                whole_spec((rank, model)),
                whole_spec((2, model)),
                whole_spec((2 * rank, model)),
                whole_spec((rows, 2 * rank)),
                col_spec(rows, block),
                col_spec(rows, block),
                pl.BlockSpec((2, model, block), lambda f, s: (0, 0, f)),
                pl.BlockSpec((2, rank, block), lambda f, s: (0, 0, f)),
                pl.BlockSpec((block, model), lambda f, s: (f, 0)),
                col_spec(rank, block),
                col_spec(2, block),
            ],
            out_specs=[whole_spec(o[0]) for o in out],
            scratch_shapes=[
                pltpu.VMEM((rows, model), bf16),
                pltpu.VMEM((hidden_rows, 3 * rank, row_width), bf16),
                pltpu.VMEM((2 * rank, rows), bf16),
                pltpu.VMEM((rank, rows), bf16),
                pltpu.VMEM((rows, rank), bf16),
                pltpu.VMEM((rank, rows), bf16),
                pltpu.VMEM((rows, model), bf16),
                pltpu.VMEM((rows, model), f32),
                pltpu.VMEM((rows, 2 * rank), f32),
                pltpu.VMEM((rows, rank), bf16),
                pltpu.VMEM((rows, model), bf16),
                pltpu.VMEM((rows, model), bf16),
            ],
        ),
        out_shape=[jax.ShapeDtypeStruct(o[0], o[1]) for o in out],
        compiler_params=params(),
        cost_estimate=cost(3e10, 4e7),
        name="feed_back",
    )(
        place, mine, other, mid, cotangent, g_mine, g_other, bd_model, rates, a, u, gate, up,
        wgu, bgu, wd, ad, scales,
    )


def attend_back_kernel(
    dims, place, res_ref, gm_ref, go_ref, mid_ref, h_ref, am_ref, ao_ref, rate_ref, bo_ref,
    wout_ref, ah_ref, start_ref, q_ref, k_ref, v_ref, o_ref, of_ref, inv_ref, qi_ref, ki_ref,
    cos_ref, sin_ref, scale_ref,
    gq_ref, gk_ref, gv_ref, gres_ref, gbo_ref, gah_ref,
    kt_ref, gqt_ref, ga_ref, guo_ref, guot_ref, uo_ref,
):
    slabs, chunk, group, head_dim, rank, model = dims
    block = group * chunk
    rows = slabs * chunk
    inner = place[0]
    step = pl.program_id(0)

    @pl.when(step == 0)
    def _():
        def mix(sl):
            grad = res_ref[sl, :] + gm_ref[sl, :].astype(f32) + go_ref[sl, :].astype(f32)
            both = am_ref[sl, :].astype(f32) + ao_ref[sl, :].astype(f32)
            low = both[:, model : model + rank].astype(bf16)
            uo_ref[sl, :] = low
            raw = both[:, :model] + nn(low, bo_ref[...])
            raw_inv = inverse_rms(raw)
            unit = raw * raw_inv
            state = h_ref[sl, :].astype(f32)
            rate = rate_ref[0:1, :]
            mixed = state + rate * (unit - state)
            mixed_inv = inverse_rms(mixed)
            out = mid_ref[sl, :]
            grad_mixed = mixed_inv * (grad - out * row_mean(grad * out))
            gres_ref[sl, :] = (1.0 - rate) * grad_mixed
            grad_unit = rate * grad_mixed
            ga_ref[sl, :] = (raw_inv * (grad_unit - unit * row_mean(grad_unit * unit))).astype(bf16)

        by_rows(rows, 64, mix)
        gbo_ref[...] = nn(uo_ref[...].T, ga_ref[...])
        low_g = nt(ga_ref[...], bo_ref[...]).astype(bf16)
        guo_ref[...] = low_g
        guot_ref[...] = low_g.T

    kt_ref[...] = k_ref[...].T
    scale = scale_ref[...]
    grad_o = (nt(ga_ref[...], wout_ref[...]) + nn(guo_ref[...], ah_ref[...])).astype(bf16)
    gah_ref[...] = nn(guot_ref[...], o_ref[...])
    pairs_q, pairs_g, deltas, bounds = [], [], [], []
    for m in range(slabs):
        own = slice(m * chunk, (m + 1) * chunk)
        pairs_q.append(spread_pair(q_ref[own, :], head_dim))
        grad = grad_o[own]
        pairs_g.append(spread_pair(grad, head_dim))
        products = grad.astype(f32).T * of_ref[0, :, own]
        deltas.append(
            jnp.concatenate(
                [
                    jnp.sum(products[:head_dim], axis=0, keepdims=True),
                    jnp.sum(products[head_dim:], axis=0, keepdims=True),
                ],
                axis=1,
            )
        )
        bounds.append(query_bounds(start_ref, m, inner, group, chunk))
    for b in range(slabs):
        at = slice(b * block, (b + 1) * block)
        grad_key = jnp.zeros((block, LANES), f32)
        grad_value = jnp.zeros((block, LANES), f32)
        for m in range(b, slabs):
            first, last = bounds[m]
            scores = nt(k_ref[at, :], pairs_q[m])
            mask = allowed_mask(first, last, b * block, block, b == m)
            weights = jnp.exp2(scores * (0.125 * log2e)) * inv_ref[0, m : m + 1, :]
            weights = jnp.where(mask, weights, 0.0)
            grad_value = grad_value + nn(weights.astype(bf16), pairs_g[m])
            grad_weights = nt(v_ref[at, :], pairs_g[m])
            grad_scores = (weights * (grad_weights - deltas[m])).astype(bf16)
            grad_key = grad_key + nn(grad_scores, pairs_q[m])
            part = nn(kt_ref[:, at], grad_scores)
            if b == 0:
                gqt_ref[m] = part
            else:
                gqt_ref[m] += part
        gv_ref[at, :] = grad_value.astype(bf16)
        gk_ref[at, :] = prep_tile_back(
            grad_key * 0.125, k_ref[at, :], ki_ref[at, :], cos_ref[at, :], sin_ref[at, :],
            scale, head_dim,
        )
    upper = row_iota((LANES, chunk)) < head_dim
    for m in range(slabs):
        own = slice(m * chunk, (m + 1) * chunk)
        both = gqt_ref[m]
        grad = jnp.where(upper, both[:, :chunk], both[:, chunk:]).T * 0.125
        there = at_rows(m * group + inner, chunk)
        gq_ref[own, :] = prep_tile_back(
            grad, q_ref[own, :], qi_ref[own, :], cos_ref[there, :], sin_ref[there, :],
            scale, head_dim,
        )


def run_attend_back(
    place, res, gm, go, mid, h_own, am, ao, rates, bo, wout, ah, start, q, k, v, o, of, inv,
    qi, ki, cos, sin, scale, slabs, group, head_dim,
):
    rows, model = h_own.shape
    chunk = rows // slabs
    width = q.shape[1]
    length = k.shape[0]
    rank = bo.shape[0]
    pairs = width // LANES
    full = whole_spec((rows, model))
    out = [
        ((rows, width), bf16, col_spec(rows)),
        ((length, width), bf16, col_spec(length)),
        ((length, width), bf16, col_spec(length)),
        ((rows, model), f32, full),
        ((rank, model), f32, whole_spec((rank, model))),
        ((rank, width), f32, col_spec(rank)),
    ]
    return pl.pallas_call(
        functools.partial(attend_back_kernel, (slabs, chunk, group, head_dim, rank, model)),
        grid_spec=pltpu.PrefetchScalarGridSpec(
            num_scalar_prefetch=1,
            grid=(pairs,),
            in_specs=[
                full,
                full,
                full,
                full,
                full,
                whole_spec((rows, model + LANES)),
                whole_spec((rows, model + LANES)),
                whole_spec((2, model)),
                whole_spec((rank, model)),
                pl.BlockSpec((LANES, model), lambda p, s: (p, 0)),
                col_spec(rank),
                whole_spec((slabs, chunk)),
                col_spec(rows),
                col_spec(length),
                col_spec(length),
                col_spec(rows),
                pl.BlockSpec((1, LANES, rows), lambda p, s: (p, 0, 0)),
                pl.BlockSpec((1, slabs, 2 * chunk), lambda p, s: (p, 0, 0)),
                col_spec(rows),
                col_spec(length),
                whole_spec((length, LANES)),
                whole_spec((length, LANES)),
                col_spec(1),
            ],
            out_specs=[o_[2] for o_ in out],
            scratch_shapes=[
                pltpu.VMEM((LANES, length), bf16),
                pltpu.VMEM((slabs, LANES, 2 * chunk), f32),
                pltpu.VMEM((rows, model), bf16),
                pltpu.VMEM((rows, rank), bf16),
                pltpu.VMEM((rank, rows), bf16),
                pltpu.VMEM((rows, rank), bf16),
            ],
        ),
        out_shape=[jax.ShapeDtypeStruct(o_[0], o_[1]) for o_ in out],
        compiler_params=params(),
        cost_estimate=cost(3e10, 4e7),
        name="attend_back",
    )(
        place, res, gm, go, mid, h_own, am, ao, rates, bo, wout, ah, start, q, k, v, o, of,
        inv, qi, ki, cos, sin, scale,
    )


def others_kernel(dims, place, gk_ref, gv_ref, w_ref, a_ref, b_ref, keep_ref, send_ref, acc_ref):
    slabs, chunk, rank, model = dims
    half = model // 2
    core = place[2]
    width = gk_ref.shape[-1]
    gk = gk_ref[...].reshape(slabs * chunk, width)
    gv = gv_ref[...].reshape(slabs * chunk, width)
    low_k = nt(gk, b_ref[1]).astype(bf16)
    low_v = nt(gv, b_ref[2]).astype(bf16)
    acc_ref[...] = (
        nt(gk, w_ref[1])
        + nt(gv, w_ref[2])
        + nn(low_k, a_ref[rank : 2 * rank, :])
        + nn(low_v, a_ref[2 * rank :, :])
    )
    keep_ref[0] = acc_ref[:, pl.ds(pl.multiple_of(core * half, half), half)]
    send_ref[0] = acc_ref[:, pl.ds(pl.multiple_of((1 - core) * half, half), half)].astype(bf16)


def run_others(place, gk, gv, w, a, b, slabs, group):
    length, width = gk.shape
    chunk = length // (slabs * group)
    rows = slabs * chunk
    model = w.shape[1]
    half = model // 2
    rank = b.shape[1]
    shaped = (slabs, group, chunk, width)
    peer = pl.BlockSpec(
        (slabs, 1, chunk, width), lambda g, s: (0, lax.rem(s[0] + 1 + g, group), 0, 0)
    )
    return pl.pallas_call(
        functools.partial(others_kernel, (slabs, chunk, rank, model)),
        grid_spec=pltpu.PrefetchScalarGridSpec(
            num_scalar_prefetch=1,
            grid=(group - 1,),
            in_specs=[
                peer,
                peer,
                whole_spec((3, model, width)),
                whole_spec((3 * rank, model)),
                whole_spec((3, rank, width)),
            ],
            out_specs=[pl.BlockSpec((1, rows, half), lambda g, s: (g, 0, 0))] * 2,
            scratch_shapes=[pltpu.VMEM((rows, model), f32)],
        ),
        out_shape=[
            jax.ShapeDtypeStruct((group - 1, rows, half), f32),
            jax.ShapeDtypeStruct((group - 1, rows, half), bf16),
        ],
        compiler_params=params(),
        cost_estimate=cost(7e9, 1e7),
        name="others",
    )(place, gk.reshape(shaped), gv.reshape(shaped), w, a, b)


def own_kernel(
    dims, place, gq_ref, gk_ref, gv_ref, w_ref, a_ref, b_ref, res_ref, keep_ref, send_ref, acc_ref
):
    slabs, chunk, rank, model = dims
    half = model // 2
    rows = slabs * chunk
    core = place[2]
    width = gq_ref.shape[1]
    gq = gq_ref[...]
    gk = gk_ref[...].reshape(rows, width)
    gv = gv_ref[...].reshape(rows, width)
    acc_ref[...] = (
        nt(gq, w_ref[0])
        + nt(gk, w_ref[1])
        + nt(gv, w_ref[2])
        + nn(nt(gq, b_ref[0]).astype(bf16), a_ref[:rank, :])
        + nn(nt(gk, b_ref[1]).astype(bf16), a_ref[rank : 2 * rank, :])
        + nn(nt(gv, b_ref[2]).astype(bf16), a_ref[2 * rank :, :])
    )
    mine = pl.ds(pl.multiple_of(core * half, half), half)
    keep_ref[...] = acc_ref[:, mine] + res_ref[:, mine]
    send_ref[...] = acc_ref[:, pl.ds(pl.multiple_of((1 - core) * half, half), half)].astype(bf16)


def run_own(place, gq, gk, gv, w, a, b, res, slabs, group):
    length, width = gk.shape
    rows, model = res.shape
    chunk = rows // slabs
    half = model // 2
    rank = b.shape[1]
    shaped = (slabs, group, chunk, width)
    peer = pl.BlockSpec((slabs, 1, chunk, width), lambda g, s: (0, s[0], 0, 0))
    out = [((rows, half), f32), ((rows, half), bf16)]
    return pl.pallas_call(
        functools.partial(own_kernel, (slabs, chunk, rank, model)),
        grid_spec=pltpu.PrefetchScalarGridSpec(
            num_scalar_prefetch=1,
            grid=(1,),
            in_specs=[
                whole_spec((rows, width)),
                peer,
                peer,
                whole_spec((3, model, width)),
                whole_spec((3 * rank, model)),
                whole_spec((3, rank, width)),
                whole_spec((rows, model)),
            ],
            out_specs=[whole_spec(o[0]) for o in out],
            scratch_shapes=[pltpu.VMEM((rows, model), f32)],
        ),
        out_shape=[jax.ShapeDtypeStruct(o[0], o[1]) for o in out],
        compiler_params=params(),
        cost_estimate=cost(7e9, 1e7),
        name="own",
    )(place, gq, gk.reshape(shaped), gv.reshape(shaped), w, a, b, res)


def grads_kernel(
    dims, place, gq_ref, gk_ref, gv_ref, b_ref, u_ref, h_ref, hown_ref, gbo_ref, gah_ref,
    table_ref, uq_ref,
):
    slabs, chunk, group, n_seq, rank, model, head_dim = dims
    inner = place[0]
    width = gq_ref.shape[1]
    heads = width // head_dim
    gq = gq_ref[...]
    low_q = nt(gq, b_ref[0]).astype(bf16)
    low_k = nt(gk_ref[...], b_ref[1]).astype(bf16)
    low_v = nt(gv_ref[...], b_ref[2]).astype(bf16)
    for m in range(slabs):
        uq_ref[m * chunk : (m + 1) * chunk, :] = u_ref[at_rows(m * group + inner, chunk), :]
    h = h_ref[...]
    model_rows = jnp.concatenate(
        [
            nn(low_q.T, hown_ref[...]),
            nn(low_k.T, h),
            nn(low_v.T, h),
            gbo_ref[...],
        ],
        axis=0,
    ).astype(bf16).astype(f32)
    ut = u_ref[...].T
    uqt = uq_ref[...].T
    head_rows = jnp.concatenate(
        [
            gah_ref[...],
            nn(uqt[:rank], gq),
            nn(ut[rank : 2 * rank], gk_ref[...]),
            nn(ut[2 * rank :], gv_ref[...]),
        ],
        axis=0,
    ).astype(bf16)
    owners = n_seq * slabs * group
    cols = model // owners
    each = head_dim // owners
    units = heads * each
    spots = lax.broadcasted_iota(i32, (width, 1), 0)
    owner = spots // units
    inside = spots % units
    source = inside // each * head_dim + owner * each + inside % each
    moved = jnp.where(lane_iota((width, width)) == source, 1.0, 0.0).astype(bf16)
    turned = nt(moved, head_rows)
    gap = table_ref.shape[3] - 4 * rank - units
    for y in range(group):
        for z in range(slabs):
            for x in range(n_seq):
                d = owner_index((y, z, x), group, slabs, n_seq)
                parts = [
                    pad_lanes(model_rows[:, d * cols : (d + 1) * cols]),
                    pad_lanes(turned[d * units : (d + 1) * units]),
                ]
                if gap:
                    parts.append(jnp.zeros((gap, LANES), f32))
                table_ref[y, z, x] = jnp.concatenate(parts, axis=0).astype(bf16)


def run_grads(place, gq, gk, gv, b, u, h, h_own, gbo, gah, slabs, group, n_seq, head_dim):
    length, width = gk.shape
    rows, model = h_own.shape
    chunk = rows // slabs
    rank = b.shape[1]
    heads = width // head_dim
    owners = n_seq * slabs * group
    units = heads * (head_dim // owners)
    table_rows = (4 * rank + units + 7) // 8 * 8
    shape = (group, slabs, n_seq, table_rows, LANES)
    operands = (gq, gk, gv, b, u, h, h_own, gbo, gah)
    return pl.pallas_call(
        functools.partial(grads_kernel, (slabs, chunk, group, n_seq, rank, model, head_dim)),
        grid_spec=pltpu.PrefetchScalarGridSpec(
            num_scalar_prefetch=1,
            grid=(1,),
            in_specs=[whole_spec(operand.shape) for operand in operands],
            out_specs=whole_spec(shape),
            scratch_shapes=[pltpu.VMEM((rows, 3 * rank), bf16)],
        ),
        out_shape=jax.ShapeDtypeStruct(shape, bf16),
        compiler_params=params(),
        cost_estimate=cost(1e10, 1e7),
        name="grads",
    )(place, *operands)


def join_kernel(slabs, place, *refs):
    out_ref = refs[-1]
    half = refs[0].shape[-1]
    core, slab = place[2], place[1]
    for shift in range(slabs):
        source = lax.rem(slab - shift + slabs, slabs)
        for which, ref in ((core, refs[shift]), (1 - core, refs[slabs + shift])):
            out_ref[source, :, pl.ds(pl.multiple_of(which * half, half), half)] = ref[
                ...
            ].astype(out_ref.dtype)


def run_join(place, mine, other, dtype):
    slabs = len(mine)
    chunk, half = mine[0].shape
    return pl.pallas_call(
        functools.partial(join_kernel, slabs),
        grid_spec=pltpu.PrefetchScalarGridSpec(
            num_scalar_prefetch=1,
            grid=(1,),
            in_specs=[whole_spec((chunk, half))] * (2 * slabs),
            out_specs=whole_spec((slabs, chunk, 2 * half)),
        ),
        out_shape=jax.ShapeDtypeStruct((slabs, chunk, 2 * half), dtype),
        compiler_params=params(),
        cost_estimate=cost(1e6, 8e6),
        name="join",
    )(place, *mine, *other)


def unpack_early_kernel(dims, place, index, mine_ref, other_ref, am_ref, bm_ref, ad_ref, bd_ref):
    n_seq, slabs, rank, cols, each, hidden_rows, tiles = dims
    core = place[2]
    for s in range(n_seq):
        for r in range(slabs):
            adapter = index[s, r]
            block = mine_ref[s, r].astype(f32)
            both = block[: 2 * rank] + other_ref[s, r, : 2 * rank].astype(f32)
            left = both[:, : cols // 2]
            right = both[:, cols // 2 : cols]
            am_ref[adapter] = jnp.where(core == 0, left, right).reshape(2, rank, cols // 2)
            bm_ref[adapter] = block[2 * rank : 3 * rank, :cols]
            base = 3 * rank
            wide = jnp.concatenate(
                [block[base + t * each : base + (t + 1) * each] for t in range(tiles)], axis=1
            )
            for k in range(rank):
                ad_ref[adapter, k] = wide[:, k * hidden_rows : (k + 1) * hidden_rows]
            for j in range(2):
                for k in range(rank):
                    at = ((j + 1) * rank + k) * hidden_rows
                    bd_ref[adapter, j, k] = wide[:, at : at + hidden_rows]


def run_unpack_early(place, index, mine, other, adapters, rank, cols, each, hidden_rows):
    n_seq, slabs = mine.shape[:2]
    tiles = (mine.shape[2] - 3 * rank) // each
    shapes = [
        (adapters, 2, rank, cols // 2),
        (adapters, rank, cols),
        (adapters, rank, each, hidden_rows),
        (adapters, 2, rank, each, hidden_rows),
    ]
    return pl.pallas_call(
        functools.partial(
            unpack_early_kernel, (n_seq, slabs, rank, cols, each, hidden_rows, tiles)
        ),
        grid_spec=pltpu.PrefetchScalarGridSpec(
            num_scalar_prefetch=2,
            grid=(1,),
            in_specs=[whole_spec(mine.shape)] * 2,
            out_specs=[whole_spec(s) for s in shapes],
        ),
        out_shape=[jax.ShapeDtypeStruct(s, f32) for s in shapes],
        compiler_params=params(),
        cost_estimate=cost(1e6, 8e6),
        name="unpack_early",
    )(place, index, mine, other)


def unpack_late_kernel(
    dims, place, index, mine_ref, other_ref, am_gu_ref, bm_down_ref, am_ref, bm_ref, ah_ref,
    bh_ref,
):
    n_seq, slabs, rank, cols, heads, each = dims
    core = place[2]
    for s in range(n_seq):
        for r in range(slabs):
            adapter = index[s, r]
            block = mine_ref[s, r].astype(f32)
            both = block[: 3 * rank] + other_ref[s, r, : 3 * rank].astype(f32)
            left = both[:, : cols // 2]
            right = both[:, cols // 2 : cols]
            am_ref[adapter, 0:3] = jnp.where(core == 0, left, right).reshape(3, rank, cols // 2)
            am_ref[adapter, 3:5] = am_gu_ref[adapter]
            bm_ref[adapter, 0] = block[3 * rank : 4 * rank, :cols]
            bm_ref[adapter, 1] = bm_down_ref[adapter]
            units = block[4 * rank : 4 * rank + heads * each]
            for n in range(heads):
                piece = units[n * each : (n + 1) * each]
                ah_ref[adapter, n] = piece[:, :rank]
                for j in range(3):
                    bh_ref[adapter, j, n] = piece[:, (j + 1) * rank : (j + 2) * rank]


def run_unpack_late(place, index, mine, other, am_gu, bm_down, heads, each):
    n_seq, slabs = mine.shape[:2]
    adapters, _, rank, narrow = am_gu.shape
    cols = bm_down.shape[2]
    shapes = [
        (adapters, 5, rank, narrow),
        (adapters, 2, rank, cols),
        (adapters, heads, each, rank),
        (adapters, 3, heads, each, rank),
    ]
    return pl.pallas_call(
        functools.partial(unpack_late_kernel, (n_seq, slabs, rank, cols, heads, each)),
        grid_spec=pltpu.PrefetchScalarGridSpec(
            num_scalar_prefetch=2,
            grid=(1,),
            in_specs=[
                whole_spec(mine.shape),
                whole_spec(other.shape),
                whole_spec(am_gu.shape),
                whole_spec(bm_down.shape),
            ],
            out_specs=[whole_spec(s) for s in shapes],
        ),
        out_shape=[jax.ShapeDtypeStruct(s, f32) for s in shapes],
        compiler_params=params(),
        cost_estimate=cost(1e6, 8e6),
        name="unpack_late",
    )(place, index, mine, other, am_gu, bm_down)


def pick(array, index):
    return lax.dynamic_index_in_dim(array, index, 0, keepdims=False)


def body(
    tokens, segments, adapter_index, w_attn_in, w_attn_out, w_gate_up, w_down, qk_scale,
    mix_rates, mlp_scales, a_model, b_model, a_heads, b_heads, a_hidden, b_hidden, cotangent,
):
    slabs, chunk, model = tokens.shape
    n_seq = lax.axis_size("seq")
    n_ctx = lax.axis_size("ctx")
    group = n_ctx // slabs
    local_width = w_attn_out.shape[0]
    local_hidden = w_down.shape[0]
    head_dim = a_heads.shape[-1]
    local_heads = local_width // head_dim
    rank = a_model.shape[2]
    adapters = a_model.shape[0]
    row_width = a_hidden.shape[-1]
    half = model // 2
    ctx_place = lax.axis_index("ctx")
    slab = ctx_place // group
    inner = ctx_place % group
    core = lax.axis_index("wt")
    seq_place = lax.axis_index("seq")
    owners = n_seq * n_ctx
    rows = slabs * chunk
    length = rows * group
    place = jnp.stack([inner, slab, core, seq_place]).astype(i32)

    def to_slab(array, shift):
        pairs = [(c, (c + shift * group) % n_ctx) for c in range(n_ctx)]
        return lax.ppermute(array, "ctx", pairs)

    def within_slab(array, shift):
        pairs = [(c, c - c % group + (c % group + shift) % group) for c in range(n_ctx)]
        return lax.ppermute(array, "ctx", pairs)

    def to_seq(array, shift):
        return lax.ppermute(array, "seq", [(c, (c + shift) % n_seq) for c in range(n_seq)])

    def other_core(array):
        return lax.ppermute(array, "wt", [(0, 1), (1, 0)])

    def half_piece(array, index, which):
        return lax.dynamic_slice(array, (index, 0, which * half), (1, chunk, half))[0]

    def token_piece(index):
        seg = jnp.pad(pick(segments, index).astype(bf16), (0, half - chunk))
        return jnp.concatenate(
            [half_piece(tokens, index, core), jnp.broadcast_to(seg, (8, half))], axis=0
        )

    tie = lax.optimization_barrier

    adapter = pick(adapter_index, slab)
    am = pick(a_model, adapter)
    bm = pick(b_model, adapter)
    ah = pick(a_heads, adapter).reshape(rank, local_width)
    bh = pick(b_heads, adapter).reshape(3, rank, local_width)
    ad = pick(a_hidden, adapter).reshape(rank, local_hidden)
    bd = pick(b_hidden, adapter).reshape(2, rank, local_hidden)
    am_qkv = am[:3].reshape(3 * rank, model)
    am_gu = am[3:].reshape(2 * rank, model)
    ah_pad = jnp.pad(ah, ((0, LANES - rank), (0, 0)))
    ad_pad = jnp.pad(ad, ((0, LANES - rank), (0, 0)))

    frequency = 10000.0 ** (-jnp.arange(head_dim // 2, dtype=f32) / (head_dim // 2))
    turn = jnp.arange(length, dtype=i32).astype(f32)[:, None] * frequency[None, :]
    cos = jnp.tile(jnp.cos(turn), (1, 2 * LANES // head_dim))
    sine = jnp.sin(turn)
    sin = jnp.tile(jnp.concatenate([-sine, sine], axis=1), (1, LANES // head_dim))
    scale = qk_scale[None, :]

    own_piece = token_piece(slab)
    got = [own_piece] + [
        to_slab(token_piece((slab + shift) % slabs), shift) for shift in range(1, slabs)
    ]
    index = [adapter_index]
    for shift in range(1, n_seq):
        index.append(to_seq(adapter_index, shift))
    got[2], cos, sin, am_qkv, am_gu, bh, ah_pad, ad_pad, ad, ah, bd, bm = tie(
        (got[2], cos, sin, am_qkv, am_gu, bh, ah_pad, ad_pad, ad, ah, bd, bm)
    )
    pieces = [own_piece]
    for shift in range(1, slabs):
        pieces += [got[shift], other_core(got[shift])]
    for turn in range(1, group):
        for shift in range(slabs):
            peer = within_slab(got[shift], turn)
            pieces += [peer, other_core(peer)]
    got, g_send = tie(
        (
            got,
            [half_piece(cotangent, (slab + shift) % slabs, core) for shift in range(1, slabs)],
        )
    )
    g_mine = [to_slab(g_send[shift - 1], shift) for shift in range(1, slabs)]
    pieces, index = tie((pieces, index))

    h_full, h_own, u, q, k, v, qi, ki, o, of, inv, attn_msg, start = run_attend(
        place, tokens, pieces, w_attn_in, am_qkv, bh, cos, sin, scale, w_attn_out,
        ah_pad, group, head_dim,
    )
    g_mine, attn_msg = tie((g_mine, attn_msg))
    attn_other = other_core(attn_msg)
    g_mine = jnp.stack(g_mine)
    attn_other, g_other = tie((attn_other, other_core(g_mine)))
    mid, u_gu, gate, up, down_msg = run_feed(
        attn_msg, attn_other, h_own, bm[0], mix_rates, am_gu, w_gate_up, bd, w_down, ad_pad,
        mlp_scales, 512,
    )
    down_other = other_core(down_msg)
    out_half, mid_res, mid_msg, early = run_feed_back(
        place, down_msg, down_other, mid, cotangent, g_mine, g_other, bm[1], mix_rates, am_gu,
        u_gu, gate, up, w_gate_up, bd, w_down, ad, mlp_scales, 512, group, n_seq, row_width,
    )
    mid_other = other_core(mid_msg)

    order = (slab - jnp.arange(slabs, dtype=i32)) % slabs
    index = jnp.stack(index)[:, order]

    out_mine = [pick(out_half, slab)] + [
        to_slab(pick(out_half, (slab + shift) % slabs), shift) for shift in range(1, slabs)
    ]

    def sum_inner(table):
        return pick(table, inner), [
            within_slab(pick(table, (inner + turn) % group), turn) for turn in range(1, group)
        ]

    def add_inner(own, got):
        total = own.astype(f32)
        for piece in got:
            total = total + piece.astype(f32)
        return total.astype(bf16)

    def over_slabs(total):
        return [pick(total, slab)] + [
            to_slab(pick(total, (slab + shift) % slabs), shift) for shift in range(1, slabs)
        ]

    def over_seqs(got):
        got = jnp.stack(got)
        result = [lax.dynamic_index_in_dim(got, seq_place, 1, keepdims=False)]
        for shift in range(1, n_seq):
            sent = lax.dynamic_index_in_dim(
                got, (seq_place + shift) % n_seq, 1, keepdims=False
            )
            result.append(to_seq(sent, shift))
        return result

    early_own, early_got = sum_inner(early)
    gq, gk, gv, h_res, gbo, gah = run_attend_back(
        place, mid_res, mid_msg, mid_other, mid, h_own, attn_msg, attn_other, mix_rates, bm[0],
        w_attn_out, ah, start, q, k, v, o, of, inv, qi, ki, cos, sin, scale, slabs, group,
        head_dim,
    )
    early_got, out_mine, gk, gv = tie((early_got, out_mine, gk, gv))
    early = over_slabs(add_inner(early_own, early_got))
    out_other = [other_core(piece) for piece in out_mine]
    keep, send = run_others(place, gk, gv, w_attn_in, am_qkv, bh, slabs, group)
    others = (keep + other_core(send).astype(f32)).astype(bf16)
    early, out_other, others, gq = tie((early, out_other, others, gq))
    others_got = [within_slab(others[turn - 1], turn) for turn in range(1, group)]
    early = over_seqs(early)
    late = run_grads(
        place, gq, gk, gv, bh, u, h_full, h_own, gbo, gah, slabs, group, n_seq, head_dim
    )
    early, late = tie((early, late))
    late_own, late_got = sum_inner(late)
    early_other = other_core(jnp.stack(early)[:, :, : 2 * rank])
    late_own, gq = tie((late_own, gq))
    own_keep, own_send = run_own(
        place, gq, gk, gv, w_attn_in, am_qkv, bh, h_res, slabs, group
    )
    late_got, own_send = tie((late_got, own_send))
    own_got = other_core(own_send)
    total = own_keep + own_got.astype(f32)
    for got_part in others_got:
        total = total + got_part.astype(f32)
    total = total.astype(bf16).reshape(slabs, chunk, half)
    result = over_slabs(total)
    late = over_slabs(add_inner(late_own, late_got))
    layer_out = run_join(place, out_mine, out_other, bf16)
    grad_am_gu, grad_bm_down, grad_ad, grad_bd = run_unpack_early(
        place, index, jnp.stack(early), early_other, adapters, rank, model // owners,
        row_width // owners, local_hidden // row_width,
    )
    late = jnp.stack(over_seqs(late))
    input_grad = run_join(place, result, [other_core(piece) for piece in result], f32)
    grad_am, grad_bm, grad_ah, grad_bh = run_unpack_late(
        place, index, late, other_core(late[:, :, : 3 * rank]), grad_am_gu, grad_bm_down,
        local_heads, head_dim // owners,
    )
    return (
        layer_out,
        input_grad,
        grad_am,
        grad_bm,
        jnp.transpose(grad_ah, (0, 3, 1, 2)),
        jnp.transpose(grad_bh, (0, 1, 4, 2, 3)),
        jnp.transpose(grad_ad, (0, 1, 3, 2)),
        jnp.transpose(grad_bd, (0, 1, 2, 4, 3)),
    )


def solution(mesh):
    return jax.shard_map(
        body,
        mesh=mesh,
        in_specs=(
            P("seq", "ctx", None),
            P("seq", "ctx"),
            P("seq"),
            P(None, None, "wt"),
            P("wt", None),
            P(None, None, "wt"),
            P("wt", None),
            P("wt"),
            P(),
            P(None, "wt"),
            P(),
            P(),
            P(None, None, "wt", None),
            P(None, None, None, "wt", None),
            P(None, None, "wt", None),
            P(None, None, None, "wt", None),
            P("seq", "ctx", None),
        ),
        out_specs=(
            P("seq", "ctx", None),
            P("seq", "ctx", None),
            P(None, None, None, ("seq", "ctx", "wt")),
            P(None, None, None, ("seq", "ctx")),
            P(None, None, "wt", ("seq", "ctx")),
            P(None, None, None, "wt", ("seq", "ctx")),
            P(None, None, "wt", ("seq", "ctx")),
            P(None, None, None, "wt", ("seq", "ctx")),
        ),
        check_vma=False,
    )
```

```python
import functools

import jax
import jax.numpy as jnp
from jax import lax
from jax.experimental import pallas as pl
from jax.experimental.pallas import tpu as pltpu
from jax.sharding import PartitionSpec as P

epsilon = 1e-06
f32 = jnp.float32
bf16 = jnp.bfloat16
i32 = jnp.int32
VMEM_LIMIT = 58 * 1024 * 1024
SMALL_LIMIT = 24 * 1024 * 1024
log2e = 1.4426950408889634
LANES = 128


def dot(left, right, contract):
    return lax.dot_general(left, right, (contract, ((), ())), preferred_element_type=f32)


def nn(left, right):
    return dot(left, right, ((1,), (0,)))


def nt(left, right):
    return dot(left, right, ((1,), (1,)))


def tn(left, right):
    return dot(left, right, ((0,), (0,)))


def lane_iota(shape):
    return lax.broadcasted_iota(i32, shape, len(shape) - 1)


def row_iota(shape):
    return lax.broadcasted_iota(i32, shape, 0)


def row_mean(values):
    return jnp.mean(values, axis=-1, keepdims=True)


def inverse_rms(values):
    return lax.rsqrt(row_mean(values * values) + epsilon)


def at_rows(index, size):
    return pl.ds(pl.multiple_of(index * size, size), size)


def by_rows(total, size, step):
    lax.fori_loop(0, total // size, lambda i, c: (step(at_rows(i, size)), c)[1], 0)


def swap_halves(tile, half):
    lower = lane_iota(tile.shape) % (2 * half) < half
    return jnp.where(lower, pltpu.roll(tile, LANES - half, 1), pltpu.roll(tile, half, 1))


def head_sums(tile, head_dim):
    same = row_iota((LANES, LANES)) // head_dim == lane_iota((LANES, LANES)) // head_dim
    ones = jnp.where(same, 1.0, 0.0).astype(bf16)
    return nn(tile.astype(bf16), ones)


def prep_tile(raw, cosine, sine, scale, head_dim):
    mean = head_sums(raw * raw, head_dim) * (1.0 / head_dim)
    inverse = lax.rsqrt(mean + epsilon)
    turned = raw * cosine + swap_halves(raw, head_dim // 2) * sine
    return (turned * inverse * scale).astype(bf16), inverse.astype(bf16)


def prep_tile_back(grad, low, inverse, cosine, sine, scale, head_dim):
    unit = low.astype(f32) / scale
    grad_unit = grad * scale
    mean = head_sums(grad_unit * unit, head_dim) * (1.0 / head_dim)
    grad_turned = inverse.astype(f32) * (grad_unit - unit * mean)
    return (grad_turned * cosine - swap_halves(grad_turned, head_dim // 2) * sine).astype(bf16)


def spread_pair(tile, head_dim):
    lower = lane_iota(tile.shape) < head_dim
    zero = jnp.zeros_like(tile)
    return jnp.concatenate([jnp.where(lower, tile, zero), jnp.where(lower, zero, tile)], axis=0)


def allowed_mask(first, last, key_start, rows, diagonal):
    keys = key_start + row_iota((rows, first.shape[1]))
    mask = keys >= first
    if diagonal:
        mask = mask & (keys <= last)
    return mask


def query_bounds(start_ref, m, place, group, chunk):
    first = start_ref[m : m + 1, :]
    last = (m * group + place) * chunk + lane_iota((1, chunk))
    return jnp.concatenate([first, first], axis=1), jnp.concatenate([last, last], axis=1)


def whole_spec(shape):
    return pl.BlockSpec(shape, lambda *a: (0,) * len(shape))


def col_spec(size, width=LANES):
    return pl.BlockSpec((size, width), lambda p, s: (0, p))


def params(small=False):
    limit = SMALL_LIMIT if small else VMEM_LIMIT
    return pltpu.CompilerParams(vmem_limit_bytes=limit)


def cost(flops, moved, transcendentals=0):
    return pl.CostEstimate(
        flops=int(flops), bytes_accessed=int(moved), transcendentals=int(transcendentals)
    )


def attend_kernel(dims, place, *refs):
    slabs, chunk, group, head_dim, rank, half = dims
    count = 2 + (slabs - 1) * 2 + (group - 1) * slabs * 2
    pieces = refs[:count]
    (
        wq_ref, w_ref, a_ref, b_ref, bq_ref, cos_ref, sin_ref, scale_ref, wout_ref, ah_ref,
        hout_ref, ownout_ref, u_ref, q_ref, k_ref, v_ref, qi_ref, ki_ref, o_ref, inv_ref,
        msg_ref, start_ref, vt_ref, all_ref, seg_ref, h_ref, own_ref, raw_ref,
    ) = refs[count:]
    inner, slab, core = place[0], place[1], place[2]
    block = group * chunk
    length = slabs * block
    rows = slabs * chunk
    model = 2 * half
    step = pl.program_id(0)

    @pl.when(step == 0)
    def _():
        mine = pl.ds(pl.multiple_of(core * half, half), half)
        other = pl.ds(pl.multiple_of((1 - core) * half, half), half)
        h_ref[at_rows(slab * group + inner, chunk), :] = pieces[0][0]
        own_ref[at_rows(slab, chunk), :] = pieces[0][0]
        seg_ref[...] = jnp.zeros_like(seg_ref)

        def keep_segments(where, piece):
            tail = piece[chunk:, :chunk].astype(f32)
            seg_ref[pl.ds(where, 1), :] = tail[0:1]

        keep_segments(slab * group + inner, pieces[1])
        at = 2
        for shift in range(1, slabs):
            source = lax.rem(slab - shift + slabs, slabs)
            rows_at = at_rows(source * group + inner, chunk)
            h_ref[rows_at, mine] = pieces[at][:chunk, :]
            h_ref[rows_at, other] = pieces[at + 1][:chunk, :]
            own_ref[at_rows(source, chunk), mine] = pieces[at][:chunk, :]
            own_ref[at_rows(source, chunk), other] = pieces[at + 1][:chunk, :]
            keep_segments(source * group + inner, pieces[at])
            at += 2
        for turn in range(1, group):
            peer = lax.rem(inner - turn + group, group)
            for shift in range(slabs):
                source = lax.rem(slab - shift + slabs, slabs)
                rows_at = at_rows(source * group + peer, chunk)
                h_ref[rows_at, mine] = pieces[at][:chunk, :]
                h_ref[rows_at, other] = pieces[at + 1][:chunk, :]
                keep_segments(source * group + peer, pieces[at])
                at += 2
        columns = seg_ref[...].T
        for m in range(slabs):
            line = seg_ref[pl.ds(m * group + inner, 1), :]
            below = jnp.zeros((chunk, chunk), f32)
            for c in range(slabs * group):
                below = below + jnp.where(columns[:, c : c + 1] < line, 1.0, 0.0)
            start_ref[m : m + 1, :] = jnp.sum(below, axis=0, keepdims=True).astype(i32)

        def low_rows(sl):
            u_ref[sl, :] = nt(h_ref[sl, :], a_ref[...]).astype(bf16)

        by_rows(length, 512, low_rows)
        for m in range(slabs):
            low = u_ref[at_rows(m * group + inner, chunk), :rank]
            own = slice(m * chunk, (m + 1) * chunk)
            raw_ref[own, :] = nn(low, bq_ref[0])
        raw_ref[...] += nn(own_ref[...], wq_ref[0])

    last_block = lax.min(step, slabs - 1)
    hout_ref[...] = h_ref[at_rows(last_block, block), :]
    ownout_ref[...] = own_ref[at_rows(last_block, chunk), :]
    here = pl.ds(pl.multiple_of(step * LANES, LANES), LANES)
    scale = scale_ref[...]
    w_kv = jnp.concatenate([w_ref[0], w_ref[1]], axis=1)
    none = jnp.zeros((rank, LANES), bf16)
    b_kv = jnp.concatenate(
        [
            jnp.zeros((rank, 2 * LANES), bf16),
            jnp.concatenate([b_ref[0], none], axis=1),
            jnp.concatenate([none, b_ref[1]], axis=1),
        ],
        axis=0,
    )

    def keys_rows(sl):
        both = nn(h_ref[sl, :], w_kv) + nn(u_ref[sl, :], b_kv)
        k_ref[sl, :], ki_ref[sl, :] = prep_tile(
            both[:, :LANES], cos_ref[sl, :], sin_ref[sl, :], scale, head_dim
        )
        v_ref[sl, :] = both[:, LANES:].astype(bf16)

    by_rows(length, 512, keys_rows)
    for m in range(slabs):
        own = slice(m * chunk, (m + 1) * chunk)
        there = at_rows(m * group + inner, chunk)
        q_ref[own, :], qi_ref[own, :] = prep_tile(
            raw_ref[own, here], cos_ref[there, :], sin_ref[there, :], scale, head_dim
        )
    vt_ref[...] = v_ref[...].T
    for m in range(slabs):
        own = slice(m * chunk, (m + 1) * chunk)
        pair = spread_pair(q_ref[own, :], head_dim)
        first, last = query_bounds(start_ref, m, inner, group, chunk)
        total = jnp.zeros((1, 2 * chunk), f32)
        gathered = jnp.zeros((LANES, 2 * chunk), f32)
        for b in range(m + 1):
            at = slice(b * block, (b + 1) * block)
            scores = nt(k_ref[at, :], pair)
            mask = allowed_mask(first, last, b * block, block, b == m)
            weights = jnp.where(mask, jnp.exp2(scores * (0.125 * log2e)), 0.0)
            total = total + jnp.sum(weights, axis=0, keepdims=True)
            gathered = gathered + nn(vt_ref[:, at], weights.astype(bf16))
        inverse = 1.0 / total
        gathered = gathered * inverse
        upper = row_iota((LANES, chunk)) < head_dim
        final = jnp.where(upper, gathered[:, :chunk], gathered[:, chunk:])
        final = final.T.astype(bf16)
        o_ref[own, :] = final
        all_ref[own, here] = final
        inv_ref[0, m : m + 1, :] = inverse

    @pl.when(step == pl.num_programs(0) - 1)
    def _():
        low_o = all_ref[...]
        msg_ref[:, :model] = nn(low_o, wout_ref[...]).astype(bf16)
        msg_ref[:, model:] = nt(low_o, ah_ref[...]).astype(bf16)


def run_attend(place, tokens, pieces, w, a, b, cos, sin, scale, wout, ah, group, head_dim):
    slabs, chunk, model = tokens.shape
    width = w.shape[2]
    rank = b.shape[1]
    half = model // 2
    rows = slabs * chunk
    length = rows * group
    pairs = width // LANES
    in_specs = [pl.BlockSpec((1, chunk, model), lambda p, s: (s[1], 0, 0))]
    in_specs += [whole_spec(piece.shape) for piece in pieces]
    in_specs += [
        whole_spec((1, model, width)),
        pl.BlockSpec(
            (pl.Element(2), pl.Element(model), pl.Element(LANES)),
            lambda p, s: (1, 0, p * LANES),
        ),
        whole_spec((3 * rank, model)),
        pl.BlockSpec(
            (pl.Element(2), pl.Element(rank), pl.Element(LANES)),
            lambda p, s: (1, 0, p * LANES),
        ),
        whole_spec((1, rank, width)),
        whole_spec((length, LANES)),
        whole_spec((length, LANES)),
        col_spec(1),
        whole_spec((width, model)),
        whole_spec((LANES, width)),
    ]
    def step_rows(size):
        return pl.BlockSpec((size, model), lambda p, s: (lax.min(p, slabs - 1), 0))

    out = [
        ((length, model), bf16, step_rows(group * chunk)),
        ((rows, model), bf16, step_rows(chunk)),
        ((length, 3 * rank), bf16, whole_spec((length, 3 * rank))),
        ((rows, width), bf16, col_spec(rows)),
        ((length, width), bf16, col_spec(length)),
        ((length, width), bf16, col_spec(length)),
        ((rows, width), bf16, col_spec(rows)),
        ((length, width), bf16, col_spec(length)),
        ((rows, width), bf16, col_spec(rows)),
        (
            (pairs, slabs, 2 * chunk),
            f32,
            pl.BlockSpec((1, slabs, 2 * chunk), lambda p, s: (p, 0, 0)),
        ),
        ((rows, model + LANES), bf16, whole_spec((rows, model + LANES))),
        ((slabs, chunk), i32, whole_spec((slabs, chunk))),
    ]
    return pl.pallas_call(
        functools.partial(attend_kernel, (slabs, chunk, group, head_dim, rank, half)),
        grid_spec=pltpu.PrefetchScalarGridSpec(
            num_scalar_prefetch=1,
            grid=(pairs,),
            in_specs=in_specs,
            out_specs=[o[2] for o in out],
            scratch_shapes=[
                pltpu.VMEM((LANES, length), bf16),
                pltpu.VMEM((rows, width), bf16),
                pltpu.VMEM((chunk, chunk), f32),
                pltpu.VMEM((length, model), bf16),
                pltpu.VMEM((rows, model), bf16),
                pltpu.VMEM((rows, width), f32),
            ],
        ),
        out_shape=[jax.ShapeDtypeStruct(o[0], o[1]) for o in out],
        compiler_params=params(),
        cost_estimate=cost(3e10, 4e7),
        name="attend",
    )(place, tokens, *pieces, w, w, a, b, b, cos, sin, scale, wout, ah)


def feed_kernel(
    dims, mine_ref, other_ref, h_ref, bo_ref, rate_ref, a_ref, wgu_ref, bgu_ref, wd_ref, ad_ref,
    scales_ref, mid_ref, u_ref, gate_ref, up_ref, msg_ref, low_ref, acc_ref,
):
    rank, model = dims
    rows = h_ref.shape[0]
    step = pl.program_id(0)

    @pl.when(step == 0)
    def _():
        def mix(sl):
            both = mine_ref[sl, :].astype(f32) + other_ref[sl, :].astype(f32)
            low = both[:, model : model + rank].astype(bf16)
            raw = both[:, :model] + nn(low, bo_ref[...])
            unit = raw * inverse_rms(raw)
            state = h_ref[sl, :].astype(f32)
            mixed = state + rate_ref[0:1, :] * (unit - state)
            mixed = mixed * inverse_rms(mixed)
            mid_ref[sl, :] = mixed
            low_ref[sl, :] = mixed.astype(bf16)

        by_rows(rows, 256, mix)
        u_ref[...] = nt(low_ref[...], a_ref[...]).astype(bf16)
        acc_ref[...] = jnp.zeros_like(acc_ref)

    low = low_ref[...]
    u = u_ref[...]
    gate = nn(low, wgu_ref[0]) + nn(u[:, :rank], bgu_ref[0])
    up = nn(low, wgu_ref[1]) + nn(u[:, rank:], bgu_ref[1])
    gate_ref[...] = gate.astype(bf16)
    up_ref[...] = up.astype(bf16)
    turned = gate * scales_ref[1:2, :]
    hidden = (up * scales_ref[0:1, :] * (turned / (1.0 + jnp.exp(-turned)))).astype(bf16)
    acc_ref[:, :model] += nn(hidden, wd_ref[...])
    acc_ref[:, model:] += nt(hidden, ad_ref[...])

    @pl.when(step == pl.num_programs(0) - 1)
    def _():
        msg_ref[...] = acc_ref[...].astype(bf16)


def run_feed(mine, other, h_own, bo, rates, a, wgu, bgu, wd, ad, scales, block):
    rows, model = h_own.shape
    hidden = wd.shape[0]
    rank = bo.shape[0]
    out = [
        ((rows, model), f32, whole_spec((rows, model))),
        ((rows, 2 * rank), bf16, whole_spec((rows, 2 * rank))),
        ((rows, hidden), bf16, pl.BlockSpec((rows, block), lambda f: (0, f))),
        ((rows, hidden), bf16, pl.BlockSpec((rows, block), lambda f: (0, f))),
        ((rows, model + LANES), bf16, whole_spec((rows, model + LANES))),
    ]
    return pl.pallas_call(
        functools.partial(feed_kernel, (rank, model)),
        grid=(hidden // block,),
        in_specs=[
            whole_spec((rows, model + LANES)),
            whole_spec((rows, model + LANES)),
            whole_spec((rows, model)),
            whole_spec((rank, model)),
            whole_spec((2, model)),
            whole_spec((2 * rank, model)),
            pl.BlockSpec((2, model, block), lambda f: (0, 0, f)),
            pl.BlockSpec((2, rank, block), lambda f: (0, 0, f)),
            pl.BlockSpec((block, model), lambda f: (f, 0)),
            pl.BlockSpec((LANES, block), lambda f: (0, f)),
            pl.BlockSpec((2, block), lambda f: (0, f)),
        ],
        out_specs=[o[2] for o in out],
        out_shape=[jax.ShapeDtypeStruct(o[0], o[1]) for o in out],
        scratch_shapes=[
            pltpu.VMEM((rows, model), bf16),
            pltpu.VMEM((rows, model + LANES), f32),
        ],
        compiler_params=params(),
        cost_estimate=cost(2.4e10, 3e7),
        name="feed",
    )(mine, other, h_own, bo, rates, a, wgu, bgu, wd, ad, scales)


def owner_index(place, group, slabs, n_seq):
    inner, slab, seq = place
    return seq * slabs * group + slab * group + inner


def pad_lanes(tile):
    return jnp.pad(tile, ((0, 0), (0, LANES - tile.shape[1])))


def folded_rows(rows, groups):
    return (rows + groups * 8 - 1) // (groups * 8) * 8


def fold(tile, groups):
    size = folded_rows(tile.shape[0], groups)
    tile = jnp.pad(tile, ((0, size * groups - tile.shape[0]), (0, 0)))
    return jnp.concatenate([tile[g * size : (g + 1) * size] for g in range(groups)], axis=1)


def unfold(block):
    groups = block.shape[1] // LANES
    return jnp.concatenate(
        [block[:, g * LANES : (g + 1) * LANES] for g in range(groups)], axis=0
    ).astype(f32)


def feed_back_kernel(
    dims, place, mine_ref, other_ref, mid_ref, g_own_ref, g_mine_ref, g_other_ref, bd_ref,
    rate_ref, a_ref, u_ref, gate_ref, up_ref, wgu_ref, bgu_ref, wd_ref, ad_ref, scales_ref,
    out_ref, res_ref, msg_ref, table_ref,
    gd_ref, gdt_ref, ut_ref, udt_ref, gud_ref, gudt_ref, low_ref, acc_ref, gu_ref, hid_ref,
    g_ref, lo_ref,
):
    slabs, chunk, group, n_seq, rank, model, row_width, hidden_rows = dims
    rows = slabs * chunk
    half = model // 2
    step = pl.program_id(0)
    slab, core = place[1], place[2]
    block = gate_ref.shape[1]

    @pl.when(step == 0)
    def _():
        mine = pl.ds(pl.multiple_of(core * half, half), half)
        other = pl.ds(pl.multiple_of((1 - core) * half, half), half)
        g_ref[at_rows(slab, chunk), :] = g_own_ref[0]
        for shift in range(1, slabs):
            source = at_rows(lax.rem(slab - shift + slabs, slabs), chunk)
            g_ref[source, mine] = g_mine_ref[shift - 1]
            g_ref[source, other] = g_other_ref[shift - 1]

        def mix(sl):
            both = mine_ref[sl, :].astype(f32) + other_ref[sl, :].astype(f32)
            low = both[:, model : model + rank].astype(bf16)
            hid_ref[sl, :] = low
            raw = both[:, :model] + nn(low, bd_ref[...])
            raw_inv = inverse_rms(raw)
            unit = raw * raw_inv
            state = mid_ref[sl, :]
            low_ref[sl, :] = state.astype(bf16)
            rate = rate_ref[1:2, :]
            mixed = state + rate * (unit - state)
            mixed_inv = inverse_rms(mixed)
            out = mixed * mixed_inv
            lo_ref[sl, :] = out.astype(bf16)
            grad = g_ref[sl, :].astype(f32)
            grad_mixed = mixed_inv * (grad - out * row_mean(grad * out))
            res_ref[sl, :] = (1.0 - rate) * grad_mixed
            grad_unit = rate * grad_mixed
            gd_ref[sl, :] = (raw_inv * (grad_unit - unit * row_mean(grad_unit * unit))).astype(bf16)

        by_rows(rows, 256, mix)
        out_ref[...] = lo_ref[:, mine].reshape(slabs, chunk, half)
        ut_ref[...] = u_ref[...].T
        udt_ref[...] = hid_ref[...].T
        low_gud = nt(gd_ref[...], bd_ref[...]).astype(bf16)
        gud_ref[...] = low_gud
        gudt_ref[...] = low_gud.T
        acc_ref[...] = jnp.zeros_like(acc_ref)
        gu_ref[...] = jnp.zeros_like(gu_ref)

    grad_hidden = nt(gd_ref[...], wd_ref[...]) + nn(gud_ref[...], ad_ref[...])
    gate = gate_ref[...].astype(f32)
    up = up_ref[...].astype(f32)
    up_scale = scales_ref[0:1, :]
    gate_scale = scales_ref[1:2, :]
    turned = gate * gate_scale
    sigmoid = 1.0 / (1.0 + jnp.exp(-turned))
    silu = turned * sigmoid
    up_scaled = up * up_scale
    hidden = (up_scaled * silu).astype(bf16)
    grad_up = (grad_hidden * up_scale * silu).astype(bf16)
    slope = sigmoid * (1.0 + turned * (1.0 - sigmoid)) * gate_scale
    grad_gate = (grad_hidden * up_scaled * slope).astype(bf16)
    acc_ref[...] += nt(grad_gate, wgu_ref[0]) + nt(grad_up, wgu_ref[1])
    gu_ref[:, :rank] += nt(grad_gate, bgu_ref[0])
    gu_ref[:, rank:] += nt(grad_up, bgu_ref[1])
    ut = ut_ref[...]
    parts = jnp.concatenate(
        [nn(gudt_ref[...], hidden), nn(ut[:rank], grad_gate), nn(ut[rank:], grad_up)], axis=0
    ).astype(bf16)
    tiles = block // row_width
    for tile in range(tiles):
        gdt_ref[step * tiles + tile] = parts[:, tile * row_width : (tile + 1) * row_width]

    @pl.when(step == pl.num_programs(0) - 1)
    def _():
        low_gu = gu_ref[...].astype(bf16)
        msg_ref[...] = (acc_ref[...] + nn(low_gu, a_ref[...])).astype(bf16)
        low = low_ref[...]
        model_rows = jnp.concatenate(
            [nn(low_gu.T, low), nn(udt_ref[...], gd_ref[...])], axis=0
        ).astype(bf16).astype(f32)
        ranks = 3 * rank
        units = ranks * hidden_rows
        padded = (units + LANES - 1) // LANES * LANES
        flat = gdt_ref[...].reshape(units, row_width)
        lanes = lane_iota((1, padded))
        target = lanes % hidden_rows * ranks + lanes // hidden_rows
        target = jnp.where(lanes < units, target, -1)
        moved = jnp.where(row_iota((units, padded)) == target, 1.0, 0.0).astype(bf16)
        turned_rows = tn(flat, moved)
        owners = n_seq * slabs * group
        cols = model // owners
        units_each = row_width // owners
        for y in range(group):
            for z in range(slabs):
                for x in range(n_seq):
                    d = owner_index((y, z, x), group, slabs, n_seq)
                    head = pad_lanes(model_rows[:, d * cols : (d + 1) * cols])
                    mine = turned_rows[d * units_each : (d + 1) * units_each]
                    tail = [
                        mine[:, t * LANES : (t + 1) * LANES] for t in range(padded // LANES)
                    ]
                    packed = jnp.concatenate([head] + tail, axis=0)
                    table_ref[y, z, x] = fold(packed, half // LANES).astype(bf16)


def run_feed_back(
    place, mine, other, mid, cotangent, g_mine, g_other, bd_model, rates, a, u, gate, up, wgu,
    bgu, wd, ad, scales, block, group, n_seq, row_width,
):
    slabs, chunk, model = cotangent.shape
    rows = slabs * chunk
    half = model // 2
    hidden = wd.shape[0]
    rank = bd_model.shape[0]
    hidden_rows = hidden // row_width
    owners = n_seq * slabs * group
    padded = (3 * rank * hidden_rows + LANES - 1) // LANES * LANES
    table_rows = 3 * rank + row_width // owners * (padded // LANES)
    out = [
        ((slabs, chunk, half), bf16),
        ((rows, model), f32),
        ((rows, model), bf16),
        ((group, slabs, n_seq, folded_rows(table_rows, half // LANES), half), bf16),
    ]
    return pl.pallas_call(
        functools.partial(
            feed_back_kernel,
            (slabs, chunk, group, n_seq, rank, model, row_width, hidden_rows),
        ),
        grid_spec=pltpu.PrefetchScalarGridSpec(
            num_scalar_prefetch=1,
            grid=(hidden // block,),
            in_specs=[
                whole_spec((rows, model + LANES)),
                whole_spec((rows, model + LANES)),
                whole_spec((rows, model)),
                pl.BlockSpec((1, chunk, model), lambda f, s: (s[1], 0, 0)),
                whole_spec((slabs - 1, chunk, half)),
                whole_spec((slabs - 1, chunk, half)),
                whole_spec((rank, model)),
                whole_spec((2, model)),
                whole_spec((2 * rank, model)),
                whole_spec((rows, 2 * rank)),
                col_spec(rows, block),
                col_spec(rows, block),
                pl.BlockSpec((2, model, block), lambda f, s: (0, 0, f)),
                pl.BlockSpec((2, rank, block), lambda f, s: (0, 0, f)),
                pl.BlockSpec((block, model), lambda f, s: (f, 0)),
                col_spec(rank, block),
                col_spec(2, block),
            ],
            out_specs=[whole_spec(o[0]) for o in out],
            scratch_shapes=[
                pltpu.VMEM((rows, model), bf16),
                pltpu.VMEM((hidden_rows, 3 * rank, row_width), bf16),
                pltpu.VMEM((2 * rank, rows), bf16),
                pltpu.VMEM((rank, rows), bf16),
                pltpu.VMEM((rows, rank), bf16),
                pltpu.VMEM((rank, rows), bf16),
                pltpu.VMEM((rows, model), bf16),
                pltpu.VMEM((rows, model), f32),
                pltpu.VMEM((rows, 2 * rank), f32),
                pltpu.VMEM((rows, rank), bf16),
                pltpu.VMEM((rows, model), bf16),
                pltpu.VMEM((rows, model), bf16),
            ],
        ),
        out_shape=[jax.ShapeDtypeStruct(o[0], o[1]) for o in out],
        compiler_params=params(),
        cost_estimate=cost(3e10, 4e7),
        name="feed_back",
    )(
        place, mine, other, mid, cotangent, g_mine, g_other, bd_model, rates, a, u, gate, up,
        wgu, bgu, wd, ad, scales,
    )


def attend_back_kernel(
    dims, place, res_ref, gm_ref, go_ref, mid_ref, h_ref, am_ref, ao_ref, rate_ref, bo_ref,
    wout_ref, ah_ref, start_ref, q_ref, k_ref, v_ref, o_ref, inv_ref, qi_ref, ki_ref,
    cos_ref, sin_ref, scale_ref,
    gq_ref, gk_ref, gv_ref, gres_ref, gbo_ref, gah_ref,
    kt_ref, gqt_ref, ga_ref, guo_ref, guot_ref, uo_ref,
):
    slabs, chunk, group, head_dim, rank, model = dims
    block = group * chunk
    rows = slabs * chunk
    inner = place[0]
    step = pl.program_id(0)

    @pl.when(step == 0)
    def _():
        def mix(sl):
            grad = res_ref[sl, :] + gm_ref[sl, :].astype(f32) + go_ref[sl, :].astype(f32)
            both = am_ref[sl, :].astype(f32) + ao_ref[sl, :].astype(f32)
            low = both[:, model : model + rank].astype(bf16)
            uo_ref[sl, :] = low
            raw = both[:, :model] + nn(low, bo_ref[...])
            raw_inv = inverse_rms(raw)
            unit = raw * raw_inv
            state = h_ref[sl, :].astype(f32)
            rate = rate_ref[0:1, :]
            mixed = state + rate * (unit - state)
            mixed_inv = inverse_rms(mixed)
            out = mid_ref[sl, :]
            grad_mixed = mixed_inv * (grad - out * row_mean(grad * out))
            gres_ref[sl, :] = (1.0 - rate) * grad_mixed
            grad_unit = rate * grad_mixed
            ga_ref[sl, :] = (raw_inv * (grad_unit - unit * row_mean(grad_unit * unit))).astype(bf16)

        by_rows(rows, 256, mix)
        gbo_ref[...] = nn(uo_ref[...].T, ga_ref[...])
        low_g = nt(ga_ref[...], bo_ref[...]).astype(bf16)
        guo_ref[...] = low_g
        guot_ref[...] = low_g.T

    kt_ref[...] = k_ref[...].T
    scale = scale_ref[...]
    grad_o = (nt(ga_ref[...], wout_ref[...]) + nn(guo_ref[...], ah_ref[...])).astype(bf16)
    gah_ref[...] = nn(guot_ref[...], o_ref[...])
    pairs_q, pairs_g, deltas, bounds = [], [], [], []
    for m in range(slabs):
        own = slice(m * chunk, (m + 1) * chunk)
        pairs_q.append(spread_pair(q_ref[own, :], head_dim))
        grad = grad_o[own]
        pairs_g.append(spread_pair(grad, head_dim))
        products = (grad.astype(f32) * o_ref[own, :].astype(f32)).T
        deltas.append(
            jnp.concatenate(
                [
                    jnp.sum(products[:head_dim], axis=0, keepdims=True),
                    jnp.sum(products[head_dim:], axis=0, keepdims=True),
                ],
                axis=1,
            )
        )
        bounds.append(query_bounds(start_ref, m, inner, group, chunk))
    for b in range(slabs):
        at = slice(b * block, (b + 1) * block)
        grad_key = jnp.zeros((block, LANES), f32)
        grad_value = jnp.zeros((block, LANES), f32)
        for m in range(b, slabs):
            first, last = bounds[m]
            scores = nt(k_ref[at, :], pairs_q[m])
            mask = allowed_mask(first, last, b * block, block, b == m)
            weights = jnp.exp2(scores * (0.125 * log2e)) * inv_ref[0, m : m + 1, :]
            weights = jnp.where(mask, weights, 0.0)
            grad_value = grad_value + nn(weights.astype(bf16), pairs_g[m])
            grad_weights = nt(v_ref[at, :], pairs_g[m])
            grad_scores = (weights * (grad_weights - deltas[m])).astype(bf16)
            grad_key = grad_key + nn(grad_scores, pairs_q[m])
            part = nn(kt_ref[:, at], grad_scores)
            if b == 0:
                gqt_ref[m] = part
            else:
                gqt_ref[m] += part
        gv_ref[at, :] = grad_value.astype(bf16)
        gk_ref[at, :] = prep_tile_back(
            grad_key * 0.125, k_ref[at, :], ki_ref[at, :], cos_ref[at, :], sin_ref[at, :],
            scale, head_dim,
        )
    upper = row_iota((LANES, chunk)) < head_dim
    for m in range(slabs):
        own = slice(m * chunk, (m + 1) * chunk)
        both = gqt_ref[m]
        grad = jnp.where(upper, both[:, :chunk], both[:, chunk:]).T * 0.125
        there = at_rows(m * group + inner, chunk)
        gq_ref[own, :] = prep_tile_back(
            grad, q_ref[own, :], qi_ref[own, :], cos_ref[there, :], sin_ref[there, :],
            scale, head_dim,
        )


def run_attend_back(
    place, res, gm, go, mid, h_own, am, ao, rates, bo, wout, ah, start, q, k, v, o, inv,
    qi, ki, cos, sin, scale, slabs, group, head_dim,
):
    rows, model = h_own.shape
    chunk = rows // slabs
    width = q.shape[1]
    length = k.shape[0]
    rank = bo.shape[0]
    pairs = width // LANES
    full = whole_spec((rows, model))
    out = [
        ((rows, width), bf16, col_spec(rows)),
        ((length, width), bf16, col_spec(length)),
        ((length, width), bf16, col_spec(length)),
        ((rows, model), f32, full),
        ((rank, model), f32, whole_spec((rank, model))),
        ((rank, width), f32, col_spec(rank)),
    ]
    return pl.pallas_call(
        functools.partial(attend_back_kernel, (slabs, chunk, group, head_dim, rank, model)),
        grid_spec=pltpu.PrefetchScalarGridSpec(
            num_scalar_prefetch=1,
            grid=(pairs,),
            in_specs=[
                full,
                full,
                full,
                full,
                full,
                whole_spec((rows, model + LANES)),
                whole_spec((rows, model + LANES)),
                whole_spec((2, model)),
                whole_spec((rank, model)),
                pl.BlockSpec((LANES, model), lambda p, s: (p, 0)),
                col_spec(rank),
                whole_spec((slabs, chunk)),
                col_spec(rows),
                col_spec(length),
                col_spec(length),
                col_spec(rows),
                pl.BlockSpec((1, slabs, 2 * chunk), lambda p, s: (p, 0, 0)),
                col_spec(rows),
                col_spec(length),
                whole_spec((length, LANES)),
                whole_spec((length, LANES)),
                col_spec(1),
            ],
            out_specs=[o_[2] for o_ in out],
            scratch_shapes=[
                pltpu.VMEM((LANES, length), bf16),
                pltpu.VMEM((slabs, LANES, 2 * chunk), f32),
                pltpu.VMEM((rows, model), bf16),
                pltpu.VMEM((rows, rank), bf16),
                pltpu.VMEM((rank, rows), bf16),
                pltpu.VMEM((rows, rank), bf16),
            ],
        ),
        out_shape=[jax.ShapeDtypeStruct(o_[0], o_[1]) for o_ in out],
        compiler_params=params(),
        cost_estimate=cost(3e10, 4e7),
        name="attend_back",
    )(
        place, res, gm, go, mid, h_own, am, ao, rates, bo, wout, ah, start, q, k, v, o,
        inv, qi, ki, cos, sin, scale,
    )


def others_kernel(dims, place, gk_ref, gv_ref, w_ref, a_ref, b_ref, keep_ref, send_ref, acc_ref):
    slabs, chunk, rank, model = dims
    half = model // 2
    core = place[2]
    width = gk_ref.shape[-1]
    gk = gk_ref[...].reshape(slabs * chunk, width)
    gv = gv_ref[...].reshape(slabs * chunk, width)
    low_k = nt(gk, b_ref[1]).astype(bf16)
    low_v = nt(gv, b_ref[2]).astype(bf16)
    acc_ref[...] = (
        nt(gk, w_ref[1])
        + nt(gv, w_ref[2])
        + nn(low_k, a_ref[rank : 2 * rank, :])
        + nn(low_v, a_ref[2 * rank :, :])
    )
    keep_ref[0] = acc_ref[:, pl.ds(pl.multiple_of(core * half, half), half)]
    send_ref[0] = acc_ref[:, pl.ds(pl.multiple_of((1 - core) * half, half), half)].astype(bf16)


def run_others(place, gk, gv, w, a, b, slabs, group):
    length, width = gk.shape
    chunk = length // (slabs * group)
    rows = slabs * chunk
    model = w.shape[1]
    half = model // 2
    rank = b.shape[1]
    shaped = (slabs, group, chunk, width)
    peer = pl.BlockSpec(
        (slabs, 1, chunk, width), lambda g, s: (0, lax.rem(s[0] + 1 + g, group), 0, 0)
    )
    return pl.pallas_call(
        functools.partial(others_kernel, (slabs, chunk, rank, model)),
        grid_spec=pltpu.PrefetchScalarGridSpec(
            num_scalar_prefetch=1,
            grid=(group - 1,),
            in_specs=[
                peer,
                peer,
                whole_spec((3, model, width)),
                whole_spec((3 * rank, model)),
                whole_spec((3, rank, width)),
            ],
            out_specs=[pl.BlockSpec((1, rows, half), lambda g, s: (g, 0, 0))] * 2,
            scratch_shapes=[pltpu.VMEM((rows, model), f32)],
        ),
        out_shape=[
            jax.ShapeDtypeStruct((group - 1, rows, half), f32),
            jax.ShapeDtypeStruct((group - 1, rows, half), bf16),
        ],
        compiler_params=params(True),
        cost_estimate=cost(7e9, 1e7),
        name="others",
    )(place, gk.reshape(shaped), gv.reshape(shaped), w, a, b)


def own_kernel(
    dims, place, gq_ref, gk_ref, gv_ref, w_ref, a_ref, b_ref, res_ref, keep_ref, send_ref, acc_ref
):
    slabs, chunk, rank, model = dims
    half = model // 2
    rows = slabs * chunk
    core = place[2]
    width = gq_ref.shape[1]
    gq = gq_ref[...]
    gk = gk_ref[...].reshape(rows, width)
    gv = gv_ref[...].reshape(rows, width)
    acc_ref[...] = (
        nt(gq, w_ref[0])
        + nt(gk, w_ref[1])
        + nt(gv, w_ref[2])
        + nn(nt(gq, b_ref[0]).astype(bf16), a_ref[:rank, :])
        + nn(nt(gk, b_ref[1]).astype(bf16), a_ref[rank : 2 * rank, :])
        + nn(nt(gv, b_ref[2]).astype(bf16), a_ref[2 * rank :, :])
    )
    mine = pl.ds(pl.multiple_of(core * half, half), half)
    keep_ref[...] = acc_ref[:, mine] + res_ref[:, mine]
    send_ref[...] = acc_ref[:, pl.ds(pl.multiple_of((1 - core) * half, half), half)].astype(bf16)


def run_own(place, gq, gk, gv, w, a, b, res, slabs, group):
    length, width = gk.shape
    rows, model = res.shape
    chunk = rows // slabs
    half = model // 2
    rank = b.shape[1]
    shaped = (slabs, group, chunk, width)
    peer = pl.BlockSpec((slabs, 1, chunk, width), lambda g, s: (0, s[0], 0, 0))
    out = [((rows, half), f32), ((rows, half), bf16)]
    return pl.pallas_call(
        functools.partial(own_kernel, (slabs, chunk, rank, model)),
        grid_spec=pltpu.PrefetchScalarGridSpec(
            num_scalar_prefetch=1,
            grid=(1,),
            in_specs=[
                whole_spec((rows, width)),
                peer,
                peer,
                whole_spec((3, model, width)),
                whole_spec((3 * rank, model)),
                whole_spec((3, rank, width)),
                whole_spec((rows, model)),
            ],
            out_specs=[whole_spec(o[0]) for o in out],
            scratch_shapes=[pltpu.VMEM((rows, model), f32)],
        ),
        out_shape=[jax.ShapeDtypeStruct(o[0], o[1]) for o in out],
        compiler_params=params(True),
        cost_estimate=cost(7e9, 1e7),
        name="own",
    )(place, gq, gk.reshape(shaped), gv.reshape(shaped), w, a, b, res)


def grads_kernel(
    dims, place, gq_ref, gk_ref, gv_ref, b_ref, u_ref, h_ref, hown_ref, gbo_ref, gah_ref,
    table_ref, uq_ref,
):
    slabs, chunk, group, n_seq, rank, model, head_dim = dims
    inner = place[0]
    width = gq_ref.shape[1]
    heads = width // head_dim
    gq = gq_ref[...]
    low_q = nt(gq, b_ref[0]).astype(bf16)
    low_k = nt(gk_ref[...], b_ref[1]).astype(bf16)
    low_v = nt(gv_ref[...], b_ref[2]).astype(bf16)
    for m in range(slabs):
        uq_ref[m * chunk : (m + 1) * chunk, :] = u_ref[at_rows(m * group + inner, chunk), :]
    h = h_ref[...]
    model_rows = jnp.concatenate(
        [
            nn(low_q.T, hown_ref[...]),
            nn(low_k.T, h),
            nn(low_v.T, h),
            gbo_ref[...],
        ],
        axis=0,
    ).astype(bf16).astype(f32)
    ut = u_ref[...].T
    uqt = uq_ref[...].T
    head_rows = jnp.concatenate(
        [
            gah_ref[...],
            nn(uqt[:rank], gq),
            nn(ut[rank : 2 * rank], gk_ref[...]),
            nn(ut[2 * rank :], gv_ref[...]),
        ],
        axis=0,
    ).astype(bf16)
    owners = n_seq * slabs * group
    cols = model // owners
    each = head_dim // owners
    units = heads * each
    spots = lax.broadcasted_iota(i32, (width, 1), 0)
    owner = spots // units
    inside = spots % units
    source = inside // each * head_dim + owner * each + inside % each
    moved = jnp.where(lane_iota((width, width)) == source, 1.0, 0.0).astype(bf16)
    turned = nt(moved, head_rows)
    for y in range(group):
        for z in range(slabs):
            for x in range(n_seq):
                d = owner_index((y, z, x), group, slabs, n_seq)
                parts = [
                    pad_lanes(model_rows[:, d * cols : (d + 1) * cols]),
                    pad_lanes(turned[d * units : (d + 1) * units]),
                ]
                packed = jnp.concatenate(parts, axis=0)
                table_ref[y, z, x] = fold(packed, table_ref.shape[4] // LANES).astype(bf16)


def run_grads(place, gq, gk, gv, b, u, h, h_own, gbo, gah, slabs, group, n_seq, head_dim):
    length, width = gk.shape
    rows, model = h_own.shape
    chunk = rows // slabs
    rank = b.shape[1]
    heads = width // head_dim
    owners = n_seq * slabs * group
    units = heads * (head_dim // owners)
    half = model // 2
    shape = (group, slabs, n_seq, folded_rows(4 * rank + units, half // LANES), half)
    operands = (gq, gk, gv, b, u, h, h_own, gbo, gah)
    return pl.pallas_call(
        functools.partial(grads_kernel, (slabs, chunk, group, n_seq, rank, model, head_dim)),
        grid_spec=pltpu.PrefetchScalarGridSpec(
            num_scalar_prefetch=1,
            grid=(1,),
            in_specs=[whole_spec(operand.shape) for operand in operands],
            out_specs=whole_spec(shape),
            scratch_shapes=[pltpu.VMEM((rows, 3 * rank), bf16)],
        ),
        out_shape=jax.ShapeDtypeStruct(shape, bf16),
        compiler_params=params(True),
        cost_estimate=cost(1e10, 1e7),
        name="grads",
    )(place, *operands)


def join_kernel(slabs, place, *refs):
    out_ref = refs[-1]
    chunk, half = out_ref.shape[1], refs[0].shape[-1]
    core, slab = place[2], place[1]
    for shift in range(slabs):
        source = lax.rem(slab - shift + slabs, slabs)
        for which, ref in ((core, refs[shift]), (1 - core, refs[slabs + shift])):
            out_ref[source, :, pl.ds(pl.multiple_of(which * half, half), half)] = ref[
                :chunk, :
            ].astype(out_ref.dtype)


def run_join(place, mine, other, chunk, dtype):
    slabs = len(mine)
    half = mine[0].shape[1]
    return pl.pallas_call(
        functools.partial(join_kernel, slabs),
        grid_spec=pltpu.PrefetchScalarGridSpec(
            num_scalar_prefetch=1,
            grid=(1,),
            in_specs=[whole_spec(piece.shape) for piece in (*mine, *other)],
            out_specs=whole_spec((slabs, chunk, 2 * half)),
        ),
        out_shape=jax.ShapeDtypeStruct((slabs, chunk, 2 * half), dtype),
        compiler_params=params(True),
        cost_estimate=cost(1e6, 8e6),
        name="join",
    )(place, *mine, *other)


def tables_of(dims, place, index, refs):
    n_seq, slabs, chunk, size = dims
    home, home_other = refs[:slabs], refs[slabs : 2 * slabs]
    far, far_other = refs[2 * slabs : 2 * slabs + n_seq - 1], refs[2 * slabs + n_seq - 1 :]
    for r in range(slabs):
        at = pl.ds(pl.multiple_of(chunk + place[3] * size, 8), size)
        yield index[0, r], unfold(home[r][at, :]), unfold(home_other[r][at, :])
    for s in range(1, n_seq):
        for r in range(slabs):
            yield index[s, r], unfold(far[s - 1][r]), unfold(far_other[s - 1][r])


def unpack_early_kernel(dims, where, place, index, *refs):
    rank, cols, each, hidden_rows, tiles = dims
    am_ref, bm_ref, ad_ref, bd_ref = refs[-4:]
    core = place[2]
    for adapter, block, other in tables_of(where, place, index, refs[:-4]):
        both = block[: 2 * rank] + other[: 2 * rank]
        am = jnp.where(core == 0, both[:, : cols // 2], both[:, cols // 2 : cols])
        am_ref[adapter] = am.reshape(2, rank, cols // 2)
        bm_ref[adapter] = block[2 * rank : 3 * rank, :cols]
        base = 3 * rank
        wide = jnp.concatenate(
            [block[base + t * each : base + (t + 1) * each] for t in range(tiles)], axis=1
        )
        for k in range(rank):
            ad_ref[adapter, k] = wide[:, k * hidden_rows : (k + 1) * hidden_rows]
        for j in range(2):
            for k in range(rank):
                at = ((j + 1) * rank + k) * hidden_rows
                bd_ref[adapter, j, k] = wide[:, at : at + hidden_rows]


def unpack_late_kernel(dims, where, place, index, *refs):
    rank, cols, heads, each = dims
    am_gu_ref, bm_down_ref, am_ref, bm_ref, ah_ref, bh_ref = refs[-6:]
    core = place[2]
    for adapter, block, other in tables_of(where, place, index, refs[:-6]):
        both = block[: 3 * rank] + other[: 3 * rank]
        am = jnp.where(core == 0, both[:, : cols // 2], both[:, cols // 2 : cols])
        am_ref[adapter, 0:3] = am.reshape(3, rank, cols // 2)
        am_ref[adapter, 3:5] = am_gu_ref[adapter]
        bm_ref[adapter, 0] = block[3 * rank : 4 * rank, :cols]
        bm_ref[adapter, 1] = bm_down_ref[adapter]
        units = block[4 * rank : 4 * rank + heads * each]
        for n in range(heads):
            piece = units[n * each : (n + 1) * each]
            ah_ref[adapter, n] = piece[:, :rank]
            for j in range(3):
                bh_ref[adapter, j, n] = piece[:, (j + 1) * rank : (j + 2) * rank]


def run_unpack(kernel, dims, where, place, index, tables, extra, shapes, name):
    home, home_other, far, far_other = tables
    operands = [*home, *home_other, *far, *far_other, *extra]
    return pl.pallas_call(
        functools.partial(kernel, dims, where),
        grid_spec=pltpu.PrefetchScalarGridSpec(
            num_scalar_prefetch=2,
            grid=(1,),
            in_specs=[whole_spec(operand.shape) for operand in operands],
            out_specs=[whole_spec(shape) for shape in shapes],
        ),
        out_shape=[jax.ShapeDtypeStruct(shape, f32) for shape in shapes],
        compiler_params=params(True),
        cost_estimate=cost(1e6, 8e6),
        name=name,
    )(place, index, *operands)


def pick(array, index):
    return lax.dynamic_index_in_dim(array, index, 0, keepdims=False)


def body(
    tokens, segments, adapter_index, w_attn_in, w_attn_out, w_gate_up, w_down, qk_scale,
    mix_rates, mlp_scales, a_model, b_model, a_heads, b_heads, a_hidden, b_hidden, cotangent,
):
    slabs, chunk, model = tokens.shape
    n_seq = lax.axis_size("seq")
    n_ctx = lax.axis_size("ctx")
    group = n_ctx // slabs
    local_width = w_attn_out.shape[0]
    local_hidden = w_down.shape[0]
    head_dim = a_heads.shape[-1]
    local_heads = local_width // head_dim
    rank = a_model.shape[2]
    adapters = a_model.shape[0]
    row_width = a_hidden.shape[-1]
    half = model // 2
    ctx_place = lax.axis_index("ctx")
    slab = ctx_place // group
    inner = ctx_place % group
    core = lax.axis_index("wt")
    seq_place = lax.axis_index("seq")
    owners = n_seq * n_ctx
    rows = slabs * chunk
    length = rows * group
    place = jnp.stack([inner, slab, core, seq_place]).astype(i32)

    def to_slab(array, shift):
        pairs = [(c, (c + shift * group) % n_ctx) for c in range(n_ctx)]
        return lax.ppermute(array, "ctx", pairs)

    def within_slab(array, shift):
        pairs = [(c, c - c % group + (c % group + shift) % group) for c in range(n_ctx)]
        return lax.ppermute(array, "ctx", pairs)

    def to_seq(array, shift):
        return lax.ppermute(array, "seq", [(c, (c + shift) % n_seq) for c in range(n_seq)])

    def other_core(array):
        return lax.ppermute(array, "wt", [(0, 1), (1, 0)])

    def half_piece(array, index, which):
        return lax.dynamic_slice(array, (index, 0, which * half), (1, chunk, half))[0]

    def token_piece(index):
        seg = jnp.pad(pick(segments, index).astype(bf16), (0, half - chunk))
        return jnp.concatenate(
            [half_piece(tokens, index, core), jnp.broadcast_to(seg, (8, half))], axis=0
        )

    tie = lax.optimization_barrier

    adapter = pick(adapter_index, slab)
    am = pick(a_model, adapter)
    bm = pick(b_model, adapter)
    ah = pick(a_heads, adapter).reshape(rank, local_width)
    bh = pick(b_heads, adapter).reshape(3, rank, local_width)
    ad = pick(a_hidden, adapter).reshape(rank, local_hidden)
    bd = pick(b_hidden, adapter).reshape(2, rank, local_hidden)
    am_qkv = am[:3].reshape(3 * rank, model)
    am_gu = am[3:].reshape(2 * rank, model)
    ah_pad = jnp.pad(ah, ((0, LANES - rank), (0, 0)))
    ad_pad = jnp.pad(ad, ((0, LANES - rank), (0, 0)))

    spot = (jnp.arange(LANES, dtype=i32) % (head_dim // 2)).astype(f32)
    frequency = 10000.0 ** (-spot / (head_dim // 2))
    turn = jnp.arange(length, dtype=i32).astype(f32)[:, None] * frequency[None, :]
    cos = jnp.cos(turn)
    lower = jnp.arange(LANES) % head_dim < head_dim // 2
    sin = jnp.sin(turn) * jnp.where(lower, -1.0, 1.0)[None, :]
    scale = qk_scale[None, :]

    own_piece = token_piece(slab)
    got = [own_piece] + [
        to_slab(token_piece((slab + shift) % slabs), shift) for shift in range(1, slabs)
    ]
    index = [adapter_index]
    for shift in range(1, n_seq):
        index.append(to_seq(adapter_index, shift))
    received = {}
    for turn in range(1, group):
        for shift in range(slabs):
            received[turn, shift] = within_slab(got[shift], turn)
    got, g_send, cos, sin, am_qkv, am_gu, bh, ah_pad, ad_pad, ad, ah, bd, bm, index = tie(
        (
            got,
            [half_piece(cotangent, (slab + shift) % slabs, core) for shift in range(1, slabs)],
            cos, sin, am_qkv, am_gu, bh, ah_pad, ad_pad, ad, ah, bd, bm, index,
        )
    )
    g_mine = [to_slab(g_send[shift - 1], shift) for shift in range(1, slabs)]
    pieces = [own_piece]
    for shift in range(1, slabs):
        pieces += [got[shift], other_core(got[shift])]
    for turn in range(1, group):
        for shift in range(slabs):
            peer = received[turn, shift]
            pieces += [peer, other_core(peer)]

    h_full, h_own, u, q, k, v, qi, ki, o, inv, attn_msg, start = run_attend(
        place, tokens, pieces, w_attn_in, am_qkv, bh, cos, sin, scale, w_attn_out,
        ah_pad, group, head_dim,
    )
    g_mine, attn_msg = tie((g_mine, attn_msg))
    attn_other = other_core(attn_msg)
    g_mine = jnp.stack(g_mine)
    attn_other, g_other = tie((attn_other, other_core(g_mine)))
    mid, u_gu, gate, up, down_msg = run_feed(
        attn_msg, attn_other, h_own, bm[0], mix_rates, am_gu, w_gate_up, bd, w_down, ad_pad,
        mlp_scales, 512,
    )
    down_other = other_core(down_msg)
    out_half, mid_res, mid_msg, early = run_feed_back(
        place, down_msg, down_other, mid, cotangent, g_mine, g_other, bm[1], mix_rates, am_gu,
        u_gu, gate, up, w_gate_up, bd, w_down, ad, mlp_scales, 512, group, n_seq, row_width,
    )
    mid_other = other_core(mid_msg)

    order = (slab - jnp.arange(slabs, dtype=i32)) % slabs
    index = jnp.stack(index)[:, order]

    def sum_inner(table):
        return pick(table, inner), [
            within_slab(pick(table, (inner + turn) % group), turn) for turn in range(1, group)
        ]

    def add_inner(own, got):
        total = own.astype(f32)
        for piece in got:
            total = total + piece.astype(f32)
        return total.astype(bf16)

    def over_slabs(total):
        return [pick(total, slab)] + [
            to_slab(pick(total, (slab + shift) % slabs), shift) for shift in range(1, slabs)
        ]

    def pack(rows_part, table):
        return jnp.concatenate([rows_part, table.reshape(slabs, -1, half)], axis=1)

    def over_seqs(home):
        result = []
        for shift in range(1, n_seq):
            at = chunk + (seq_place + shift) % n_seq * size
            sent = [lax.dynamic_slice_in_dim(piece, at, size, 0) for piece in home]
            result.append(to_seq(jnp.stack(sent), shift))
        return result

    early_own, early_got = sum_inner(early)
    size = early.shape[3]
    gq, gk, gv, h_res, gbo, gah = run_attend_back(
        place, mid_res, mid_msg, mid_other, mid, h_own, attn_msg, attn_other, mix_rates, bm[0],
        w_attn_out, ah, start, q, k, v, o, inv, qi, ki, cos, sin, scale, slabs, group,
        head_dim,
    )
    early_got, gk, gv = tie((early_got, gk, gv))
    home = over_slabs(pack(out_half, add_inner(early_own, early_got)))
    keep, send = run_others(place, gk, gv, w_attn_in, am_qkv, bh, slabs, group)
    others = (keep + other_core(send).astype(f32)).astype(bf16)
    home, others, gq = tie((home, others, gq))
    others_got = [within_slab(others[turn - 1], turn) for turn in range(1, group)]
    home_other = [other_core(piece) for piece in home]
    far = over_seqs(home)
    late = run_grads(
        place, gq, gk, gv, bh, u, h_full, h_own, gbo, gah, slabs, group, n_seq, head_dim
    )
    far, late = tie((far, late))
    late_own, late_got = sum_inner(late)
    far_other = [other_core(piece) for piece in far]
    late_own, gq = tie((late_own, gq))
    own_keep, own_send = run_own(
        place, gq, gk, gv, w_attn_in, am_qkv, bh, h_res, slabs, group
    )
    late_got, own_send = tie((late_got, own_send))
    own_got = other_core(own_send)
    total = own_keep + own_got.astype(f32)
    for got_part in others_got:
        total = total + got_part.astype(f32)
    total = total.astype(bf16).reshape(slabs, chunk, half)
    total = pack(total, add_inner(late_own, late_got))
    total, home, far = tie((total, home, far))
    result = over_slabs(total)
    layer_out = run_join(place, home, home_other, chunk, bf16)
    cols = model // owners
    each = row_width // owners
    hidden_rows = local_hidden // row_width
    grad_am_gu, grad_bm_down, grad_ad, grad_bd = run_unpack(
        unpack_early_kernel,
        (rank, cols, each, hidden_rows, (3 * rank * hidden_rows + LANES - 1) // LANES),
        (n_seq, slabs, chunk, size),
        place, index, (home, home_other, far, far_other), [],
        [
            (adapters, 2, rank, cols // 2),
            (adapters, rank, cols),
            (adapters, rank, each, hidden_rows),
            (adapters, 2, rank, each, hidden_rows),
        ],
        "unpack_early",
    )
    size = late.shape[3]
    result, layer_out, grad_am_gu, grad_bm_down = tie(
        (result, layer_out, grad_am_gu, grad_bm_down)
    )
    result_other = [other_core(piece) for piece in result]
    far = over_seqs(result)
    input_grad = run_join(place, result, result_other, chunk, f32)
    far, input_grad = tie((far, input_grad))
    each = head_dim // owners
    grad_am, grad_bm, grad_ah, grad_bh = run_unpack(
        unpack_late_kernel,
        (rank, cols, local_heads, each),
        (n_seq, slabs, chunk, size),
        place, index, (result, result_other, far, [other_core(piece) for piece in far]),
        [grad_am_gu, grad_bm_down],
        [
            (adapters, 5, rank, cols // 2),
            (adapters, 2, rank, cols),
            (adapters, local_heads, each, rank),
            (adapters, 3, local_heads, each, rank),
        ],
        "unpack_late",
    )
    return (
        layer_out,
        input_grad,
        grad_am,
        grad_bm,
        jnp.transpose(grad_ah, (0, 3, 1, 2)),
        jnp.transpose(grad_bh, (0, 1, 4, 2, 3)),
        jnp.transpose(grad_ad, (0, 1, 3, 2)),
        jnp.transpose(grad_bd, (0, 1, 2, 4, 3)),
    )


def solution(mesh):
    return jax.shard_map(
        body,
        mesh=mesh,
        in_specs=(
            P("seq", "ctx", None),
            P("seq", "ctx"),
            P("seq"),
            P(None, None, "wt"),
            P("wt", None),
            P(None, None, "wt"),
            P("wt", None),
            P("wt"),
            P(),
            P(None, "wt"),
            P(),
            P(),
            P(None, None, "wt", None),
            P(None, None, None, "wt", None),
            P(None, None, "wt", None),
            P(None, None, None, "wt", None),
            P("seq", "ctx", None),
        ),
        out_specs=(
            P("seq", "ctx", None),
            P("seq", "ctx", None),
            P(None, None, None, ("seq", "ctx", "wt")),
            P(None, None, None, ("seq", "ctx")),
            P(None, None, "wt", ("seq", "ctx")),
            P(None, None, None, "wt", ("seq", "ctx")),
            P(None, None, "wt", ("seq", "ctx")),
            P(None, None, None, "wt", ("seq", "ctx")),
        ),
        check_vma=False,
    )
```

```python
import functools

import jax
import jax.numpy as jnp
from jax import lax
from jax.experimental import pallas as pl
from jax.experimental.pallas import tpu as pltpu
from jax.sharding import PartitionSpec as P

epsilon = 1e-06
f32 = jnp.float32
bf16 = jnp.bfloat16
i32 = jnp.int32
VMEM_LIMIT = 58 * 1024 * 1024
SMALL_LIMIT = 24 * 1024 * 1024
log2e = 1.4426950408889634
LANES = 128


def dot(left, right, contract):
    return lax.dot_general(left, right, (contract, ((), ())), preferred_element_type=f32)


def nn(left, right):
    return dot(left, right, ((1,), (0,)))


def nt(left, right):
    return dot(left, right, ((1,), (1,)))


def tn(left, right):
    return dot(left, right, ((0,), (0,)))


def lane_iota(shape):
    return lax.broadcasted_iota(i32, shape, len(shape) - 1)


def row_iota(shape):
    return lax.broadcasted_iota(i32, shape, 0)


def row_mean(values):
    return jnp.mean(values, axis=-1, keepdims=True)


def inverse_rms(values):
    return lax.rsqrt(row_mean(values * values) + epsilon)


def at_rows(index, size):
    return pl.ds(pl.multiple_of(index * size, size), size)


def by_rows(total, size, step):
    lax.fori_loop(0, total // size, lambda i, c: (step(at_rows(i, size)), c)[1], 0)


def swap_halves(tile, half):
    lower = lane_iota(tile.shape) % (2 * half) < half
    return jnp.where(lower, pltpu.roll(tile, LANES - half, 1), pltpu.roll(tile, half, 1))


def head_sums(tile, head_dim):
    same = row_iota((LANES, LANES)) // head_dim == lane_iota((LANES, LANES)) // head_dim
    ones = jnp.where(same, 1.0, 0.0).astype(bf16)
    return nn(tile.astype(bf16), ones)


def prep_tile(raw, cosine, sine, scale, head_dim):
    mean = head_sums(raw * raw, head_dim) * (1.0 / head_dim)
    inverse = lax.rsqrt(mean + epsilon)
    turned = raw * cosine + swap_halves(raw, head_dim // 2) * sine
    return (turned * inverse * scale).astype(bf16), inverse.astype(bf16)


def prep_tile_back(grad, low, inverse, cosine, sine, scale, head_dim):
    unit = low.astype(f32) / scale
    grad_unit = grad * scale
    mean = head_sums(grad_unit * unit, head_dim) * (1.0 / head_dim)
    grad_turned = inverse.astype(f32) * (grad_unit - unit * mean)
    return (grad_turned * cosine - swap_halves(grad_turned, head_dim // 2) * sine).astype(bf16)


def spread_pair(tile, head_dim):
    lower = lane_iota(tile.shape) < head_dim
    zero = jnp.zeros_like(tile)
    return jnp.concatenate([jnp.where(lower, tile, zero), jnp.where(lower, zero, tile)], axis=0)


def allowed_mask(first, last, key_start, rows, diagonal):
    keys = key_start + row_iota((rows, first.shape[1]))
    mask = keys >= first
    if diagonal:
        mask = mask & (keys <= last)
    return mask


def query_bounds(start_ref, m, place, group, chunk):
    first = start_ref[m : m + 1, :]
    last = (m * group + place) * chunk + lane_iota((1, chunk))
    return jnp.concatenate([first, first], axis=1), jnp.concatenate([last, last], axis=1)


def whole_spec(shape, buffers=1):
    return pl.BlockSpec(
        shape, lambda *a: (0,) * len(shape), pipeline_mode=pl.Buffered(buffers)
    )


def col_spec(size, width=LANES):
    return pl.BlockSpec((size, width), lambda p, s: (0, p))


def params(small=False):
    limit = SMALL_LIMIT if small else VMEM_LIMIT
    return pltpu.CompilerParams(vmem_limit_bytes=limit)


def cost(flops, moved, transcendentals=0):
    return pl.CostEstimate(
        flops=int(flops), bytes_accessed=int(moved), transcendentals=int(transcendentals)
    )


def attend_kernel(dims, place, *refs):
    slabs, chunk, group, head_dim, rank, half = dims
    count = 2 + (slabs - 1) * 2 + (group - 1) * slabs * 2
    pieces = refs[:count]
    (
        wq_ref, w_ref, a_ref, b_ref, bq_ref, cos_ref, sin_ref, scale_ref, wout_ref, ah_ref,
        hout_ref, ownout_ref, u_ref, q_ref, k_ref, v_ref, qi_ref, ki_ref, o_ref, inv_ref,
        msg_ref, start_ref, vt_ref, all_ref, seg_ref, h_ref, own_ref, raw_ref,
    ) = refs[count:]
    inner, slab, core = place[0], place[1], place[2]
    block = group * chunk
    length = slabs * block
    rows = slabs * chunk
    model = 2 * half
    step = pl.program_id(0)

    @pl.when(step == 0)
    def _():
        mine = pl.ds(pl.multiple_of(core * half, half), half)
        other = pl.ds(pl.multiple_of((1 - core) * half, half), half)
        h_ref[at_rows(slab * group + inner, chunk), :] = pieces[0][0]
        own_ref[at_rows(slab, chunk), :] = pieces[0][0]
        seg_ref[...] = jnp.zeros_like(seg_ref)

        def keep_segments(where, piece):
            tail = piece[chunk:, :chunk].astype(f32)
            seg_ref[pl.ds(where, 1), :] = tail[0:1]

        keep_segments(slab * group + inner, pieces[1])
        at = 2
        for shift in range(1, slabs):
            source = lax.rem(slab - shift + slabs, slabs)
            rows_at = at_rows(source * group + inner, chunk)
            h_ref[rows_at, mine] = pieces[at][:chunk, :]
            h_ref[rows_at, other] = pieces[at + 1][:chunk, :]
            own_ref[at_rows(source, chunk), mine] = pieces[at][:chunk, :]
            own_ref[at_rows(source, chunk), other] = pieces[at + 1][:chunk, :]
            keep_segments(source * group + inner, pieces[at])
            at += 2
        for turn in range(1, group):
            peer = lax.rem(inner - turn + group, group)
            for shift in range(slabs):
                source = lax.rem(slab - shift + slabs, slabs)
                rows_at = at_rows(source * group + peer, chunk)
                h_ref[rows_at, mine] = pieces[at][:chunk, :]
                h_ref[rows_at, other] = pieces[at + 1][:chunk, :]
                keep_segments(source * group + peer, pieces[at])
                at += 2
        columns = seg_ref[...].T
        for m in range(slabs):
            line = seg_ref[pl.ds(m * group + inner, 1), :]
            below = jnp.zeros((chunk, chunk), f32)
            for c in range(slabs * group):
                below = below + jnp.where(columns[:, c : c + 1] < line, 1.0, 0.0)
            start_ref[m : m + 1, :] = jnp.sum(below, axis=0, keepdims=True).astype(i32)

        def low_rows(sl):
            u_ref[sl, :] = nt(h_ref[sl, :], a_ref[...]).astype(bf16)

        by_rows(length, 512, low_rows)
        for m in range(slabs):
            low = u_ref[at_rows(m * group + inner, chunk), :rank]
            own = slice(m * chunk, (m + 1) * chunk)
            raw_ref[own, :] = nn(low, bq_ref[0])
        raw_ref[...] += nn(own_ref[...], wq_ref[0])

    last_block = lax.min(step, slabs - 1)
    hout_ref[...] = h_ref[at_rows(last_block, block), :]
    ownout_ref[...] = own_ref[at_rows(last_block, chunk), :]
    here = pl.ds(pl.multiple_of(step * LANES, LANES), LANES)
    scale = scale_ref[...]
    w_kv = jnp.concatenate([w_ref[0], w_ref[1]], axis=1)
    none = jnp.zeros((rank, LANES), bf16)
    b_kv = jnp.concatenate(
        [
            jnp.zeros((rank, 2 * LANES), bf16),
            jnp.concatenate([b_ref[0], none], axis=1),
            jnp.concatenate([none, b_ref[1]], axis=1),
        ],
        axis=0,
    )

    def keys_rows(sl):
        both = nn(h_ref[sl, :], w_kv) + nn(u_ref[sl, :], b_kv)
        k_ref[sl, :], ki_ref[sl, :] = prep_tile(
            both[:, :LANES], cos_ref[sl, :], sin_ref[sl, :], scale, head_dim
        )
        v_ref[sl, :] = both[:, LANES:].astype(bf16)

    by_rows(length, 512, keys_rows)
    for m in range(slabs):
        own = slice(m * chunk, (m + 1) * chunk)
        there = at_rows(m * group + inner, chunk)
        q_ref[own, :], qi_ref[own, :] = prep_tile(
            raw_ref[own, here], cos_ref[there, :], sin_ref[there, :], scale, head_dim
        )
    vt_ref[...] = v_ref[...].T
    for m in range(slabs):
        own = slice(m * chunk, (m + 1) * chunk)
        pair = spread_pair(q_ref[own, :], head_dim)
        first, last = query_bounds(start_ref, m, inner, group, chunk)
        total = jnp.zeros((1, 2 * chunk), f32)
        gathered = jnp.zeros((LANES, 2 * chunk), f32)
        for b in range(m + 1):
            at = slice(b * block, (b + 1) * block)
            scores = nt(k_ref[at, :], pair)
            mask = allowed_mask(first, last, b * block, block, b == m)
            weights = jnp.where(mask, jnp.exp2(scores * (0.125 * log2e)), 0.0)
            total = total + jnp.sum(weights, axis=0, keepdims=True)
            gathered = gathered + nn(vt_ref[:, at], weights.astype(bf16))
        inverse = 1.0 / total
        gathered = gathered * inverse
        upper = row_iota((LANES, chunk)) < head_dim
        final = jnp.where(upper, gathered[:, :chunk], gathered[:, chunk:])
        final = final.T.astype(bf16)
        o_ref[own, :] = final
        all_ref[own, here] = final
        inv_ref[0, m : m + 1, :] = inverse

    @pl.when(step == pl.num_programs(0) - 1)
    def _():
        low_o = all_ref[...]
        msg_ref[:, :model] = nn(low_o, wout_ref[...]).astype(bf16)
        msg_ref[:, model:] = nt(low_o, ah_ref[...]).astype(bf16)


def run_attend(place, tokens, pieces, w, a, b, cos, sin, scale, wout, ah, group, head_dim):
    slabs, chunk, model = tokens.shape
    width = w.shape[2]
    rank = b.shape[1]
    half = model // 2
    rows = slabs * chunk
    length = rows * group
    pairs = width // LANES
    in_specs = [pl.BlockSpec((1, chunk, model), lambda p, s: (s[1], 0, 0))]
    in_specs += [whole_spec(piece.shape) for piece in pieces]
    in_specs += [
        whole_spec((1, model, width)),
        pl.BlockSpec(
            (pl.Element(2), pl.Element(model), pl.Element(LANES)),
            lambda p, s: (1, 0, p * LANES),
        ),
        whole_spec((3 * rank, model)),
        pl.BlockSpec(
            (pl.Element(2), pl.Element(rank), pl.Element(LANES)),
            lambda p, s: (1, 0, p * LANES),
        ),
        whole_spec((1, rank, width)),
        whole_spec((length, LANES)),
        whole_spec((length, LANES)),
        col_spec(1),
        whole_spec((width, model)),
        whole_spec((LANES, width)),
    ]
    def step_rows(size):
        return pl.BlockSpec((size, model), lambda p, s: (lax.min(p, slabs - 1), 0))

    out = [
        ((length, model), bf16, step_rows(group * chunk)),
        ((rows, model), bf16, step_rows(chunk)),
        ((length, 3 * rank), bf16, whole_spec((length, 3 * rank))),
        ((rows, width), bf16, col_spec(rows)),
        ((length, width), bf16, col_spec(length)),
        ((length, width), bf16, col_spec(length)),
        ((rows, width), bf16, col_spec(rows)),
        ((length, width), bf16, col_spec(length)),
        ((rows, width), bf16, col_spec(rows)),
        (
            (pairs, slabs, 2 * chunk),
            f32,
            pl.BlockSpec((1, slabs, 2 * chunk), lambda p, s: (p, 0, 0)),
        ),
        ((rows, model + LANES), bf16, whole_spec((rows, model + LANES))),
        ((slabs, chunk), i32, whole_spec((slabs, chunk))),
    ]
    return pl.pallas_call(
        functools.partial(attend_kernel, (slabs, chunk, group, head_dim, rank, half)),
        grid_spec=pltpu.PrefetchScalarGridSpec(
            num_scalar_prefetch=1,
            grid=(pairs,),
            in_specs=in_specs,
            out_specs=[o[2] for o in out],
            scratch_shapes=[
                pltpu.VMEM((LANES, length), bf16),
                pltpu.VMEM((rows, width), bf16),
                pltpu.VMEM((chunk, chunk), f32),
                pltpu.VMEM((length, model), bf16),
                pltpu.VMEM((rows, model), bf16),
                pltpu.VMEM((rows, width), f32),
            ],
        ),
        out_shape=[jax.ShapeDtypeStruct(o[0], o[1]) for o in out],
        compiler_params=params(),
        cost_estimate=cost(3e10, 4e7),
        name="attend",
    )(place, tokens, *pieces, w, w, a, b, b, cos, sin, scale, wout, ah)


def feed_kernel(
    dims, mine_ref, other_ref, h_ref, bo_ref, rate_ref, a_ref, wgu_ref, bgu_ref, wd_ref, ad_ref,
    scales_ref, mid_ref, u_ref, gate_ref, up_ref, msg_ref, low_ref, acc_ref,
):
    rank, model = dims
    rows = h_ref.shape[0]
    step = pl.program_id(0)

    @pl.when(step == 0)
    def _():
        def mix(sl):
            both = mine_ref[sl, :].astype(f32) + other_ref[sl, :].astype(f32)
            low = both[:, model : model + rank].astype(bf16)
            raw = both[:, :model] + nn(low, bo_ref[...])
            unit = raw * inverse_rms(raw)
            state = h_ref[sl, :].astype(f32)
            mixed = state + rate_ref[0:1, :] * (unit - state)
            mixed = mixed * inverse_rms(mixed)
            mid_ref[sl, :] = mixed
            low_ref[sl, :] = mixed.astype(bf16)

        by_rows(rows, 128, mix)
        u_ref[...] = nt(low_ref[...], a_ref[...]).astype(bf16)
        acc_ref[...] = jnp.zeros_like(acc_ref)

    low = low_ref[...]
    u = u_ref[...]
    gate = nn(low, wgu_ref[0]) + nn(u[:, :rank], bgu_ref[0])
    up = nn(low, wgu_ref[1]) + nn(u[:, rank:], bgu_ref[1])
    gate_ref[...] = gate.astype(bf16)
    up_ref[...] = up.astype(bf16)
    turned = gate * scales_ref[1:2, :]
    hidden = (up * scales_ref[0:1, :] * (turned / (1.0 + jnp.exp(-turned)))).astype(bf16)
    acc_ref[:, :model] += nn(hidden, wd_ref[...])
    acc_ref[:, model:] += nt(hidden, ad_ref[...])

    @pl.when(step == pl.num_programs(0) - 1)
    def _():
        msg_ref[...] = acc_ref[...].astype(bf16)


def run_feed(mine, other, h_own, bo, rates, a, wgu, bgu, wd, ad, scales, block):
    rows, model = h_own.shape
    hidden = wd.shape[0]
    rank = bo.shape[0]
    out = [
        ((rows, model), f32, whole_spec((rows, model))),
        ((rows, 2 * rank), bf16, whole_spec((rows, 2 * rank))),
        ((rows, hidden), bf16, pl.BlockSpec((rows, block), lambda f: (0, f))),
        ((rows, hidden), bf16, pl.BlockSpec((rows, block), lambda f: (0, f))),
        ((rows, model + LANES), bf16, whole_spec((rows, model + LANES))),
    ]
    return pl.pallas_call(
        functools.partial(feed_kernel, (rank, model)),
        grid=(hidden // block,),
        in_specs=[
            whole_spec((rows, model + LANES)),
            whole_spec((rows, model + LANES)),
            whole_spec((rows, model)),
            whole_spec((rank, model)),
            whole_spec((2, model)),
            whole_spec((2 * rank, model)),
            pl.BlockSpec((2, model, block), lambda f: (0, 0, f)),
            pl.BlockSpec((2, rank, block), lambda f: (0, 0, f)),
            pl.BlockSpec((block, model), lambda f: (f, 0)),
            pl.BlockSpec((LANES, block), lambda f: (0, f)),
            pl.BlockSpec((2, block), lambda f: (0, f)),
        ],
        out_specs=[o[2] for o in out],
        out_shape=[jax.ShapeDtypeStruct(o[0], o[1]) for o in out],
        scratch_shapes=[
            pltpu.VMEM((rows, model), bf16),
            pltpu.VMEM((rows, model + LANES), f32),
        ],
        compiler_params=params(),
        cost_estimate=cost(2.4e10, 3e7),
        name="feed",
    )(mine, other, h_own, bo, rates, a, wgu, bgu, wd, ad, scales)


def owner_index(place, group, slabs, n_seq):
    inner, slab, seq = place
    return seq * slabs * group + slab * group + inner


def pad_to(tile, lanes):
    return jnp.pad(tile, ((0, 0), (0, lanes - tile.shape[1])))


def late_rows(rank, units):
    return max(4 * rank, 2 * units)


def folded_rows(rows, groups):
    return (rows + groups * 8 - 1) // (groups * 8) * 8


def fold(tile, groups):
    size = folded_rows(tile.shape[0], groups)
    tile = jnp.pad(tile, ((0, size * groups - tile.shape[0]), (0, 0)))
    return jnp.concatenate([tile[g * size : (g + 1) * size] for g in range(groups)], axis=1)


def unfold(block):
    groups = block.shape[1] // LANES
    return jnp.concatenate(
        [block[:, g * LANES : (g + 1) * LANES] for g in range(groups)], axis=0
    ).astype(f32)


def feed_back_kernel(
    dims, place, mine_ref, other_ref, mid_ref, g_own_ref, g_mine_ref, g_other_ref, bd_ref,
    rate_ref, a_ref, u_ref, gate_ref, up_ref, wgu_ref, bgu_ref, wd_ref, ad_ref, scales_ref,
    out_ref, res_ref, msg_ref, table_ref,
    gd_ref, gdt_ref, ut_ref, udt_ref, gud_ref, gudt_ref, low_ref, acc_ref, gu_ref, hid_ref,
    g_ref, lo_ref,
):
    slabs, chunk, group, n_seq, rank, model, row_width, hidden_rows = dims
    rows = slabs * chunk
    half = model // 2
    step = pl.program_id(0)
    slab, core = place[1], place[2]
    block = gate_ref.shape[1]

    @pl.when(step == 0)
    def _():
        mine = pl.ds(pl.multiple_of(core * half, half), half)
        other = pl.ds(pl.multiple_of((1 - core) * half, half), half)
        g_ref[at_rows(slab, chunk), :] = g_own_ref[0]
        for shift in range(1, slabs):
            source = at_rows(lax.rem(slab - shift + slabs, slabs), chunk)
            g_ref[source, mine] = g_mine_ref[shift - 1]
            g_ref[source, other] = g_other_ref[shift - 1]

        def mix(sl):
            both = mine_ref[sl, :].astype(f32) + other_ref[sl, :].astype(f32)
            low = both[:, model : model + rank].astype(bf16)
            hid_ref[sl, :] = low
            raw = both[:, :model] + nn(low, bd_ref[...])
            raw_inv = inverse_rms(raw)
            unit = raw * raw_inv
            state = mid_ref[sl, :]
            low_ref[sl, :] = state.astype(bf16)
            rate = rate_ref[1:2, :]
            mixed = state + rate * (unit - state)
            mixed_inv = inverse_rms(mixed)
            out = mixed * mixed_inv
            lo_ref[sl, :] = out.astype(bf16)
            grad = g_ref[sl, :].astype(f32)
            grad_mixed = mixed_inv * (grad - out * row_mean(grad * out))
            res_ref[sl, :] = (1.0 - rate) * grad_mixed
            grad_unit = rate * grad_mixed
            gd_ref[sl, :] = (raw_inv * (grad_unit - unit * row_mean(grad_unit * unit))).astype(bf16)

        by_rows(rows, 128, mix)
        out_ref[...] = lo_ref[:, mine].reshape(slabs, chunk, half)
        ut_ref[...] = u_ref[...].T
        udt_ref[...] = hid_ref[...].T
        low_gud = nt(gd_ref[...], bd_ref[...]).astype(bf16)
        gud_ref[...] = low_gud
        gudt_ref[...] = low_gud.T
        acc_ref[...] = jnp.zeros_like(acc_ref)
        gu_ref[...] = jnp.zeros_like(gu_ref)

    grad_hidden = nt(gd_ref[...], wd_ref[...]) + nn(gud_ref[...], ad_ref[...])
    gate = gate_ref[...].astype(f32)
    up = up_ref[...].astype(f32)
    up_scale = scales_ref[0:1, :]
    gate_scale = scales_ref[1:2, :]
    turned = gate * gate_scale
    sigmoid = 1.0 / (1.0 + jnp.exp(-turned))
    silu = turned * sigmoid
    up_scaled = up * up_scale
    hidden = (up_scaled * silu).astype(bf16)
    grad_up = (grad_hidden * up_scale * silu).astype(bf16)
    slope = sigmoid * (1.0 + turned * (1.0 - sigmoid)) * gate_scale
    grad_gate = (grad_hidden * up_scaled * slope).astype(bf16)
    acc_ref[...] += nt(grad_gate, wgu_ref[0]) + nt(grad_up, wgu_ref[1])
    gu_ref[:, :rank] += nt(grad_gate, bgu_ref[0])
    gu_ref[:, rank:] += nt(grad_up, bgu_ref[1])
    ut = ut_ref[...]
    parts = jnp.concatenate(
        [nn(gudt_ref[...], hidden), nn(ut[:rank], grad_gate), nn(ut[rank:], grad_up)], axis=0
    ).astype(bf16)
    tiles = block // row_width
    for tile in range(tiles):
        gdt_ref[step * tiles + tile] = parts[:, tile * row_width : (tile + 1) * row_width]

    @pl.when(step == pl.num_programs(0) - 1)
    def _():
        low_gu = gu_ref[...].astype(bf16)
        msg_ref[...] = (acc_ref[...] + nn(low_gu, a_ref[...])).astype(bf16)
        low = low_ref[...]
        model_rows = jnp.concatenate(
            [nn(low_gu.T, low), nn(udt_ref[...], gd_ref[...])], axis=0
        ).astype(bf16).astype(f32)
        ranks = 3 * rank
        units = ranks * hidden_rows
        padded = (units + LANES - 1) // LANES * LANES
        flat = gdt_ref[...].reshape(units, row_width)
        lanes = lane_iota((1, padded))
        target = lanes % hidden_rows * ranks + lanes // hidden_rows
        target = jnp.where(lanes < units, target, -1)
        moved = jnp.where(row_iota((units, padded)) == target, 1.0, 0.0).astype(bf16)
        turned_rows = tn(flat, moved)
        owners = n_seq * slabs * group
        cols = model // owners
        units_each = row_width // owners
        for y in range(group):
            for z in range(slabs):
                for x in range(n_seq):
                    d = owner_index((y, z, x), group, slabs, n_seq)
                    head = pad_to(model_rows[:, d * cols : (d + 1) * cols], LANES)
                    mine = turned_rows[d * units_each : (d + 1) * units_each]
                    tail = [
                        mine[:, t * LANES : (t + 1) * LANES] for t in range(padded // LANES)
                    ]
                    packed = jnp.concatenate([head] + tail, axis=0)
                    table_ref[z, y, x] = fold(packed, half // LANES).astype(bf16)


def run_feed_back(
    place, mine, other, mid, cotangent, g_mine, g_other, bd_model, rates, a, u, gate, up, wgu,
    bgu, wd, ad, scales, block, group, n_seq, row_width,
):
    slabs, chunk, model = cotangent.shape
    rows = slabs * chunk
    half = model // 2
    hidden = wd.shape[0]
    rank = bd_model.shape[0]
    hidden_rows = hidden // row_width
    owners = n_seq * slabs * group
    padded = (3 * rank * hidden_rows + LANES - 1) // LANES * LANES
    table_rows = 3 * rank + row_width // owners * (padded // LANES)
    out = [
        ((slabs, chunk, half), bf16),
        ((rows, model), f32),
        ((rows, model), bf16),
        ((slabs, group, n_seq, folded_rows(table_rows, half // LANES), half), bf16),
    ]
    return pl.pallas_call(
        functools.partial(
            feed_back_kernel,
            (slabs, chunk, group, n_seq, rank, model, row_width, hidden_rows),
        ),
        grid_spec=pltpu.PrefetchScalarGridSpec(
            num_scalar_prefetch=1,
            grid=(hidden // block,),
            in_specs=[
                whole_spec((rows, model + LANES)),
                whole_spec((rows, model + LANES)),
                whole_spec((rows, model)),
                pl.BlockSpec((1, chunk, model), lambda f, s: (s[1], 0, 0)),
                whole_spec((slabs - 1, chunk, half)),
                whole_spec((slabs - 1, chunk, half)),
                whole_spec((rank, model)),
                whole_spec((2, model)),
                whole_spec((2 * rank, model)),
                whole_spec((rows, 2 * rank)),
                col_spec(rows, block),
                col_spec(rows, block),
                pl.BlockSpec((2, model, block), lambda f, s: (0, 0, f)),
                pl.BlockSpec((2, rank, block), lambda f, s: (0, 0, f)),
                pl.BlockSpec((block, model), lambda f, s: (f, 0)),
                col_spec(rank, block),
                col_spec(2, block),
            ],
            out_specs=[whole_spec(o[0]) for o in out],
            scratch_shapes=[
                pltpu.VMEM((rows, model), bf16),
                pltpu.VMEM((hidden_rows, 3 * rank, row_width), bf16),
                pltpu.VMEM((2 * rank, rows), bf16),
                pltpu.VMEM((rank, rows), bf16),
                pltpu.VMEM((rows, rank), bf16),
                pltpu.VMEM((rank, rows), bf16),
                pltpu.VMEM((rows, model), bf16),
                pltpu.VMEM((rows, model), f32),
                pltpu.VMEM((rows, 2 * rank), f32),
                pltpu.VMEM((rows, rank), bf16),
                pltpu.VMEM((rows, model), bf16),
                pltpu.VMEM((rows, model), bf16),
            ],
        ),
        out_shape=[jax.ShapeDtypeStruct(o[0], o[1]) for o in out],
        compiler_params=params(),
        cost_estimate=cost(3e10, 4e7),
        name="feed_back",
    )(
        place, mine, other, mid, cotangent, g_mine, g_other, bd_model, rates, a, u, gate, up,
        wgu, bgu, wd, ad, scales,
    )


def attend_back_kernel(
    dims, place, res_ref, gm_ref, go_ref, mid_ref, h_ref, am_ref, ao_ref, rate_ref, bo_ref,
    wout_ref, ah_ref, start_ref, q_ref, k_ref, v_ref, o_ref, inv_ref, qi_ref, ki_ref,
    cos_ref, sin_ref, scale_ref,
    gq_ref, gk_ref, gv_ref, gres_ref, gbo_ref, gah_ref,
    kt_ref, gqt_ref, ga_ref, guo_ref, guot_ref, uo_ref,
):
    slabs, chunk, group, head_dim, rank, model = dims
    block = group * chunk
    rows = slabs * chunk
    inner = place[0]
    step = pl.program_id(0)

    @pl.when(step == 0)
    def _():
        def mix(sl):
            grad = res_ref[sl, :] + gm_ref[sl, :].astype(f32) + go_ref[sl, :].astype(f32)
            both = am_ref[sl, :].astype(f32) + ao_ref[sl, :].astype(f32)
            low = both[:, model : model + rank].astype(bf16)
            uo_ref[sl, :] = low
            raw = both[:, :model] + nn(low, bo_ref[...])
            raw_inv = inverse_rms(raw)
            unit = raw * raw_inv
            state = h_ref[sl, :].astype(f32)
            rate = rate_ref[0:1, :]
            mixed = state + rate * (unit - state)
            mixed_inv = inverse_rms(mixed)
            out = mid_ref[sl, :]
            grad_mixed = mixed_inv * (grad - out * row_mean(grad * out))
            gres_ref[sl, :] = (1.0 - rate) * grad_mixed
            grad_unit = rate * grad_mixed
            ga_ref[sl, :] = (raw_inv * (grad_unit - unit * row_mean(grad_unit * unit))).astype(bf16)

        by_rows(rows, 128, mix)
        gbo_ref[...] = nn(uo_ref[...].T, ga_ref[...])
        low_g = nt(ga_ref[...], bo_ref[...]).astype(bf16)
        guo_ref[...] = low_g
        guot_ref[...] = low_g.T

    kt_ref[...] = k_ref[...].T
    scale = scale_ref[...]
    grad_o = (nt(ga_ref[...], wout_ref[...]) + nn(guo_ref[...], ah_ref[...])).astype(bf16)
    gah_ref[...] = nn(guot_ref[...], o_ref[...])
    pairs_q, pairs_g, deltas, bounds = [], [], [], []
    for m in range(slabs):
        own = slice(m * chunk, (m + 1) * chunk)
        pairs_q.append(spread_pair(q_ref[own, :], head_dim))
        grad = grad_o[own]
        pairs_g.append(spread_pair(grad, head_dim))
        products = (grad.astype(f32) * o_ref[own, :].astype(f32)).T
        deltas.append(
            jnp.concatenate(
                [
                    jnp.sum(products[:head_dim], axis=0, keepdims=True),
                    jnp.sum(products[head_dim:], axis=0, keepdims=True),
                ],
                axis=1,
            )
        )
        bounds.append(query_bounds(start_ref, m, inner, group, chunk))
    for b in range(slabs):
        at = slice(b * block, (b + 1) * block)
        grad_key = jnp.zeros((block, LANES), f32)
        grad_value = jnp.zeros((block, LANES), f32)
        for m in range(b, slabs):
            first, last = bounds[m]
            scores = nt(k_ref[at, :], pairs_q[m])
            mask = allowed_mask(first, last, b * block, block, b == m)
            weights = jnp.exp2(scores * (0.125 * log2e)) * inv_ref[0, m : m + 1, :]
            weights = jnp.where(mask, weights, 0.0)
            grad_value = grad_value + nn(weights.astype(bf16), pairs_g[m])
            grad_weights = nt(v_ref[at, :], pairs_g[m])
            grad_scores = (weights * (grad_weights - deltas[m])).astype(bf16)
            grad_key = grad_key + nn(grad_scores, pairs_q[m])
            part = nn(kt_ref[:, at], grad_scores)
            if b == 0:
                gqt_ref[m] = part
            else:
                gqt_ref[m] += part
        gv_ref[at, :] = grad_value.astype(bf16)
        gk_ref[at, :] = prep_tile_back(
            grad_key * 0.125, k_ref[at, :], ki_ref[at, :], cos_ref[at, :], sin_ref[at, :],
            scale, head_dim,
        )
    upper = row_iota((LANES, chunk)) < head_dim
    for m in range(slabs):
        own = slice(m * chunk, (m + 1) * chunk)
        both = gqt_ref[m]
        grad = jnp.where(upper, both[:, :chunk], both[:, chunk:]).T * 0.125
        there = at_rows(m * group + inner, chunk)
        gq_ref[own, :] = prep_tile_back(
            grad, q_ref[own, :], qi_ref[own, :], cos_ref[there, :], sin_ref[there, :],
            scale, head_dim,
        )


def run_attend_back(
    place, res, gm, go, mid, h_own, am, ao, rates, bo, wout, ah, start, q, k, v, o, inv,
    qi, ki, cos, sin, scale, slabs, group, head_dim,
):
    rows, model = h_own.shape
    chunk = rows // slabs
    width = q.shape[1]
    length = k.shape[0]
    rank = bo.shape[0]
    pairs = width // LANES
    full = whole_spec((rows, model))
    out = [
        ((rows, width), bf16, col_spec(rows)),
        ((length, width), bf16, col_spec(length)),
        ((length, width), bf16, col_spec(length)),
        ((rows, model), f32, full),
        ((rank, model), f32, whole_spec((rank, model))),
        ((rank, width), f32, col_spec(rank)),
    ]
    return pl.pallas_call(
        functools.partial(attend_back_kernel, (slabs, chunk, group, head_dim, rank, model)),
        grid_spec=pltpu.PrefetchScalarGridSpec(
            num_scalar_prefetch=1,
            grid=(pairs,),
            in_specs=[
                full,
                full,
                full,
                full,
                full,
                whole_spec((rows, model + LANES)),
                whole_spec((rows, model + LANES)),
                whole_spec((2, model)),
                whole_spec((rank, model)),
                pl.BlockSpec((LANES, model), lambda p, s: (p, 0)),
                col_spec(rank),
                whole_spec((slabs, chunk)),
                col_spec(rows),
                col_spec(length),
                col_spec(length),
                col_spec(rows),
                pl.BlockSpec((1, slabs, 2 * chunk), lambda p, s: (p, 0, 0)),
                col_spec(rows),
                col_spec(length),
                whole_spec((length, LANES)),
                whole_spec((length, LANES)),
                col_spec(1),
            ],
            out_specs=[o_[2] for o_ in out],
            scratch_shapes=[
                pltpu.VMEM((LANES, length), bf16),
                pltpu.VMEM((slabs, LANES, 2 * chunk), f32),
                pltpu.VMEM((rows, model), bf16),
                pltpu.VMEM((rows, rank), bf16),
                pltpu.VMEM((rank, rows), bf16),
                pltpu.VMEM((rows, rank), bf16),
            ],
        ),
        out_shape=[jax.ShapeDtypeStruct(o_[0], o_[1]) for o_ in out],
        compiler_params=params(),
        cost_estimate=cost(3e10, 4e7),
        name="attend_back",
    )(
        place, res, gm, go, mid, h_own, am, ao, rates, bo, wout, ah, start, q, k, v, o,
        inv, qi, ki, cos, sin, scale,
    )


def others_kernel(dims, place, gk_ref, gv_ref, w_ref, a_ref, b_ref, keep_ref, send_ref, acc_ref):
    slabs, chunk, rank, model = dims
    half = model // 2
    core = place[2]
    width = gk_ref.shape[-1]
    gk = gk_ref[...].reshape(slabs * chunk, width)
    gv = gv_ref[...].reshape(slabs * chunk, width)
    low_k = nt(gk, b_ref[1]).astype(bf16)
    low_v = nt(gv, b_ref[2]).astype(bf16)
    acc_ref[...] = (
        nt(gk, w_ref[1])
        + nt(gv, w_ref[2])
        + nn(low_k, a_ref[rank : 2 * rank, :])
        + nn(low_v, a_ref[2 * rank :, :])
    )
    keep_ref[0] = acc_ref[:, pl.ds(pl.multiple_of(core * half, half), half)]
    send_ref[0] = acc_ref[:, pl.ds(pl.multiple_of((1 - core) * half, half), half)].astype(bf16)


def run_others(place, gk, gv, w, a, b, slabs, group):
    length, width = gk.shape
    chunk = length // (slabs * group)
    rows = slabs * chunk
    model = w.shape[1]
    half = model // 2
    rank = b.shape[1]
    shaped = (slabs, group, chunk, width)
    peer = pl.BlockSpec(
        (slabs, 1, chunk, width), lambda g, s: (0, lax.rem(s[0] + 1 + g, group), 0, 0)
    )
    return pl.pallas_call(
        functools.partial(others_kernel, (slabs, chunk, rank, model)),
        grid_spec=pltpu.PrefetchScalarGridSpec(
            num_scalar_prefetch=1,
            grid=(group - 1,),
            in_specs=[
                peer,
                peer,
                whole_spec((3, model, width)),
                whole_spec((3 * rank, model)),
                whole_spec((3, rank, width)),
            ],
            out_specs=[pl.BlockSpec((1, rows, half), lambda g, s: (g, 0, 0))] * 2,
            scratch_shapes=[pltpu.VMEM((rows, model), f32)],
        ),
        out_shape=[
            jax.ShapeDtypeStruct((group - 1, rows, half), f32),
            jax.ShapeDtypeStruct((group - 1, rows, half), bf16),
        ],
        compiler_params=params(True),
        cost_estimate=cost(7e9, 1e7),
        name="others",
    )(place, gk.reshape(shaped), gv.reshape(shaped), w, a, b)


def own_kernel(
    dims, place, gq_ref, gk_ref, gv_ref, w_ref, a_ref, b_ref, res_ref, keep_ref, send_ref, acc_ref
):
    slabs, chunk, rank, model = dims
    half = model // 2
    rows = slabs * chunk
    core = place[2]
    width = gq_ref.shape[1]
    gq = gq_ref[...]
    gk = gk_ref[...].reshape(rows, width)
    gv = gv_ref[...].reshape(rows, width)
    acc_ref[...] = (
        nt(gq, w_ref[0])
        + nt(gk, w_ref[1])
        + nt(gv, w_ref[2])
        + nn(nt(gq, b_ref[0]).astype(bf16), a_ref[:rank, :])
        + nn(nt(gk, b_ref[1]).astype(bf16), a_ref[rank : 2 * rank, :])
        + nn(nt(gv, b_ref[2]).astype(bf16), a_ref[2 * rank :, :])
    )
    mine = pl.ds(pl.multiple_of(core * half, half), half)
    keep_ref[...] = acc_ref[:, mine] + res_ref[:, mine]
    send_ref[...] = acc_ref[:, pl.ds(pl.multiple_of((1 - core) * half, half), half)].astype(bf16)


def run_own(place, gq, gk, gv, w, a, b, res, slabs, group):
    length, width = gk.shape
    rows, model = res.shape
    chunk = rows // slabs
    half = model // 2
    rank = b.shape[1]
    shaped = (slabs, group, chunk, width)
    peer = pl.BlockSpec((slabs, 1, chunk, width), lambda g, s: (0, s[0], 0, 0))
    out = [((rows, half), f32), ((rows, half), bf16)]
    return pl.pallas_call(
        functools.partial(own_kernel, (slabs, chunk, rank, model)),
        grid_spec=pltpu.PrefetchScalarGridSpec(
            num_scalar_prefetch=1,
            grid=(1,),
            in_specs=[
                whole_spec((rows, width)),
                peer,
                peer,
                whole_spec((3, model, width)),
                whole_spec((3 * rank, model)),
                whole_spec((3, rank, width)),
                whole_spec((rows, model)),
            ],
            out_specs=[whole_spec(o[0]) for o in out],
            scratch_shapes=[pltpu.VMEM((rows, model), f32)],
        ),
        out_shape=[jax.ShapeDtypeStruct(o[0], o[1]) for o in out],
        compiler_params=params(True),
        cost_estimate=cost(7e9, 1e7),
        name="own",
    )(place, gq, gk.reshape(shaped), gv.reshape(shaped), w, a, b, res)


def grads_kernel(
    dims, place, gq_ref, gk_ref, gv_ref, b_ref, u_ref, h_ref, hown_ref, gbo_ref, gah_ref,
    table_ref, uq_ref,
):
    slabs, chunk, group, n_seq, rank, model, head_dim = dims
    inner = place[0]
    width = gq_ref.shape[1]
    heads = width // head_dim
    gq = gq_ref[...]
    low_q = nt(gq, b_ref[0]).astype(bf16)
    low_k = nt(gk_ref[...], b_ref[1]).astype(bf16)
    low_v = nt(gv_ref[...], b_ref[2]).astype(bf16)
    for m in range(slabs):
        uq_ref[m * chunk : (m + 1) * chunk, :] = u_ref[at_rows(m * group + inner, chunk), :]
    h = h_ref[...]
    model_rows = jnp.concatenate(
        [
            nn(low_q.T, hown_ref[...]),
            nn(low_k.T, h),
            nn(low_v.T, h),
            gbo_ref[...],
        ],
        axis=0,
    ).astype(bf16).astype(f32)
    ut = u_ref[...].T
    uqt = uq_ref[...].T
    head_rows = jnp.concatenate(
        [
            gah_ref[...],
            nn(uqt[:rank], gq),
            nn(ut[rank : 2 * rank], gk_ref[...]),
            nn(ut[2 * rank :], gv_ref[...]),
        ],
        axis=0,
    ).astype(bf16)
    owners = n_seq * slabs * group
    cols = model // owners
    each = head_dim // owners
    units = heads * each
    spots = lax.broadcasted_iota(i32, (width, 1), 0)
    owner = spots // units
    inside = spots % units
    source = inside // each * head_dim + owner * each + inside % each
    moved = jnp.where(lane_iota((width, width)) == source, 1.0, 0.0).astype(bf16)
    turned = nt(moved, head_rows)
    for y in range(group):
        for z in range(slabs):
            for x in range(n_seq):
                d = owner_index((y, z, x), group, slabs, n_seq)
                left = model_rows[:, d * cols : (d + 1) * cols]
                heads_part = turned[d * units : (d + 1) * units]
                right = jnp.concatenate(
                    [heads_part[:, rank:], pad_to(heads_part[:, :rank], 3 * rank)], axis=0
                )
                tall = late_rows(rank, units)
                packed = jnp.concatenate(
                    [
                        jnp.pad(left, ((0, tall - left.shape[0]), (0, 0))),
                        jnp.pad(right, ((0, tall - right.shape[0]), (0, 0))),
                    ],
                    axis=1,
                )
                packed = pad_to(packed, LANES)
                table_ref[y, z, x] = fold(packed, table_ref.shape[4] // LANES).astype(bf16)


def run_grads(place, gq, gk, gv, b, u, h, h_own, gbo, gah, slabs, group, n_seq, head_dim):
    length, width = gk.shape
    rows, model = h_own.shape
    chunk = rows // slabs
    rank = b.shape[1]
    heads = width // head_dim
    owners = n_seq * slabs * group
    units = heads * (head_dim // owners)
    half = model // 2
    shape = (group, slabs, n_seq, folded_rows(late_rows(rank, units), half // LANES), half)
    operands = (gq, gk, gv, b, u, h, h_own, gbo, gah)
    return pl.pallas_call(
        functools.partial(grads_kernel, (slabs, chunk, group, n_seq, rank, model, head_dim)),
        grid_spec=pltpu.PrefetchScalarGridSpec(
            num_scalar_prefetch=1,
            grid=(1,),
            in_specs=[whole_spec(operand.shape) for operand in operands],
            out_specs=whole_spec(shape),
            scratch_shapes=[pltpu.VMEM((rows, 3 * rank), bf16)],
        ),
        out_shape=jax.ShapeDtypeStruct(shape, bf16),
        compiler_params=params(True),
        cost_estimate=cost(1e10, 1e7),
        name="grads",
    )(place, *operands)


def join_kernel(slabs, place, *refs):
    out_ref = refs[-1]
    chunk, half = out_ref.shape[1], refs[0].shape[-1]
    core, slab = place[2], place[1]
    for shift in range(slabs):
        source = lax.rem(slab - shift + slabs, slabs)
        for which, ref in ((core, refs[shift]), (1 - core, refs[slabs + shift])):
            out_ref[source, :, pl.ds(pl.multiple_of(which * half, half), half)] = ref[
                :chunk, :
            ].astype(out_ref.dtype)


def run_join(place, mine, other, chunk, dtype):
    slabs = len(mine)
    half = mine[0].shape[1]
    return pl.pallas_call(
        functools.partial(join_kernel, slabs),
        grid_spec=pltpu.PrefetchScalarGridSpec(
            num_scalar_prefetch=1,
            grid=(1,),
            in_specs=[whole_spec(piece.shape) for piece in (*mine, *other)],
            out_specs=whole_spec((slabs, chunk, 2 * half)),
        ),
        out_shape=jax.ShapeDtypeStruct((slabs, chunk, 2 * half), dtype),
        compiler_params=params(True),
        cost_estimate=cost(1e6, 8e6),
        name="join",
    )(place, *mine, *other)


def unpack_early_kernel(dims, where, place, index, *refs):
    rank, cols, each, hidden_rows, tiles = dims
    n_seq, slabs = where
    am_ref, bm_ref, ad_ref, bd_ref = refs[-4:]
    core = place[2]

    def put(s, r):
        adapter = index[s, r]
        block, other = unfold(refs[s][r]), unfold(refs[n_seq + s][r])
        both = block[: 2 * rank] + other[: 2 * rank]
        am = jnp.where(core == 0, both[:, : cols // 2], both[:, cols // 2 : cols])
        am_ref[adapter] = am.reshape(2, rank, cols // 2)
        bm_ref[adapter] = block[2 * rank : 3 * rank, :cols]
        base = 3 * rank
        wide = jnp.concatenate(
            [block[base + t * each : base + (t + 1) * each] for t in range(tiles)], axis=1
        )
        for k in range(rank):
            ad_ref[adapter, k] = wide[:, k * hidden_rows : (k + 1) * hidden_rows]
        for j in range(2):
            for k in range(rank):
                at = ((j + 1) * rank + k) * hidden_rows
                bd_ref[adapter, j, k] = wide[:, at : at + hidden_rows]

    for s in range(n_seq):
        lax.fori_loop(0, slabs, lambda r, c, s=s: (put(s, r), c)[1], 0)


def unpack_late_kernel(dims, where, place, index, *refs):
    rank, cols, heads, each = dims
    n_seq, slabs, chunk, size = where
    am_gu_ref, bm_down_ref, am_ref, bm_ref, ah_ref, bh_ref = refs[-6:]
    home, home_other = refs[:slabs], refs[slabs : 2 * slabs]
    far, far_other = refs[2 * slabs : 2 * slabs + n_seq - 1], refs[2 * slabs + n_seq - 1 : -6]
    core = place[2]

    def put(adapter, block, other):
        both = block[: 3 * rank] + other[: 3 * rank]
        am = jnp.where(core == 0, both[:, : cols // 2], both[:, cols // 2 : cols])
        am_ref[adapter, 0:3] = am.reshape(3, rank, cols // 2)
        am_ref[adapter, 3:5] = am_gu_ref[adapter]
        bm_ref[adapter, 0] = block[3 * rank : 4 * rank, :cols]
        bm_ref[adapter, 1] = bm_down_ref[adapter]
        units = heads * each
        for n in range(heads):
            at = n * each
            ah_ref[adapter, n] = block[units + at : units + at + each, cols : cols + rank]
            for j in range(3):
                lanes = slice(cols + j * rank, cols + (j + 1) * rank)
                bh_ref[adapter, j, n] = block[at : at + each, lanes]

    for r in range(slabs):
        at = pl.ds(pl.multiple_of(chunk + place[3] * size, 8), size)
        put(index[0, r], unfold(home[r][at, :]), unfold(home_other[r][at, :]))
    for s in range(1, n_seq):
        lax.fori_loop(
            0,
            slabs,
            lambda r, c, s=s: (
                put(index[s, r], unfold(far[s - 1][r]), unfold(far_other[s - 1][r])),
                c,
            )[1],
            0,
        )


def run_unpack(kernel, dims, where, place, index, tables, extra, shapes, name):
    operands = [*tables, *extra]
    return pl.pallas_call(
        functools.partial(kernel, dims, where),
        grid_spec=pltpu.PrefetchScalarGridSpec(
            num_scalar_prefetch=2,
            grid=(1,),
            in_specs=[whole_spec(operand.shape) for operand in operands],
            out_specs=[whole_spec(shape) for shape in shapes],
        ),
        out_shape=[jax.ShapeDtypeStruct(shape, f32) for shape in shapes],
        compiler_params=params(True),
        cost_estimate=cost(1e6, 8e6),
        name=name,
    )(place, index, *operands)


def pick(array, index):
    return lax.dynamic_index_in_dim(array, index, 0, keepdims=False)


def body(
    tokens, segments, adapter_index, w_attn_in, w_attn_out, w_gate_up, w_down, qk_scale,
    mix_rates, mlp_scales, a_model, b_model, a_heads, b_heads, a_hidden, b_hidden, cotangent,
):
    slabs, chunk, model = tokens.shape
    n_seq = lax.axis_size("seq")
    n_ctx = lax.axis_size("ctx")
    group = n_ctx // slabs
    local_width = w_attn_out.shape[0]
    local_hidden = w_down.shape[0]
    head_dim = a_heads.shape[-1]
    local_heads = local_width // head_dim
    rank = a_model.shape[2]
    adapters = a_model.shape[0]
    row_width = a_hidden.shape[-1]
    half = model // 2
    ctx_place = lax.axis_index("ctx")
    slab = ctx_place // group
    inner = ctx_place % group
    core = lax.axis_index("wt")
    seq_place = lax.axis_index("seq")
    owners = n_seq * n_ctx
    rows = slabs * chunk
    length = rows * group
    place = jnp.stack([inner, slab, core, seq_place]).astype(i32)

    def to_slab(array, shift):
        pairs = [(c, (c + shift * group) % n_ctx) for c in range(n_ctx)]
        return lax.ppermute(array, "ctx", pairs)

    def within_slab(array, shift):
        pairs = [(c, c - c % group + (c % group + shift) % group) for c in range(n_ctx)]
        return lax.ppermute(array, "ctx", pairs)

    def to_seq(array, shift):
        return lax.ppermute(array, "seq", [(c, (c + shift) % n_seq) for c in range(n_seq)])

    def other_core(array):
        return lax.ppermute(array, "wt", [(0, 1), (1, 0)])

    def half_piece(array, index, which):
        return lax.dynamic_slice(array, (index, 0, which * half), (1, chunk, half))[0]

    def token_piece(index):
        seg = jnp.pad(pick(segments, index).astype(bf16), (0, half - chunk))
        return jnp.concatenate(
            [half_piece(tokens, index, core), jnp.broadcast_to(seg, (8, half))], axis=0
        )

    tie = lax.optimization_barrier

    adapter = pick(adapter_index, slab)
    am = pick(a_model, adapter)
    bm = pick(b_model, adapter)
    ah = pick(a_heads, adapter).reshape(rank, local_width)
    bh = pick(b_heads, adapter).reshape(3, rank, local_width)
    ad = pick(a_hidden, adapter).reshape(rank, local_hidden)
    bd = pick(b_hidden, adapter).reshape(2, rank, local_hidden)
    am_qkv = am[:3].reshape(3 * rank, model)
    am_gu = am[3:].reshape(2 * rank, model)
    ah_pad = jnp.pad(ah, ((0, LANES - rank), (0, 0)))
    ad_pad = jnp.pad(ad, ((0, LANES - rank), (0, 0)))

    spot = (jnp.arange(LANES, dtype=i32) % (head_dim // 2)).astype(f32)
    frequency = 10000.0 ** (-spot / (head_dim // 2))
    turn = jnp.arange(length, dtype=i32).astype(f32)[:, None] * frequency[None, :]
    cos = jnp.cos(turn)
    lower = jnp.arange(LANES) % head_dim < head_dim // 2
    sin = jnp.sin(turn) * jnp.where(lower, -1.0, 1.0)[None, :]
    scale = qk_scale[None, :]

    own_piece = token_piece(slab)
    got = [own_piece] + [
        to_slab(token_piece((slab + shift) % slabs), shift) for shift in range(1, slabs)
    ]
    index = [adapter_index]
    for shift in range(1, n_seq):
        index.append(to_seq(adapter_index, shift))
    received = {}
    for turn in range(1, group):
        for shift in range(slabs):
            received[turn, shift] = within_slab(got[shift], turn)
    late_turns = {key: received[key] for key in received if key[1] == 2 % slabs}
    late_turns, g_send = tie(
        (
            late_turns,
            [half_piece(cotangent, (slab + shift) % slabs, core) for shift in range(1, slabs)],
        )
    )
    received.update(late_turns)
    g_mine = [to_slab(g_send[shift - 1], shift) for shift in range(1, slabs)]
    received, cos, sin, am_qkv, am_gu, bh, ah_pad, ad_pad, ad, ah, bd, bm, index = tie(
        (received, cos, sin, am_qkv, am_gu, bh, ah_pad, ad_pad, ad, ah, bd, bm, index)
    )
    pieces = [own_piece]
    for shift in range(1, slabs):
        pieces += [got[shift], other_core(got[shift])]
    for turn in range(1, group):
        for shift in range(slabs):
            peer = received[turn, shift]
            pieces += [peer, other_core(peer)]

    h_full, h_own, u, q, k, v, qi, ki, o, inv, attn_msg, start = run_attend(
        place, tokens, pieces, w_attn_in, am_qkv, bh, cos, sin, scale, w_attn_out,
        ah_pad, group, head_dim,
    )
    g_mine, attn_msg = tie((g_mine, attn_msg))
    attn_other = other_core(attn_msg)
    g_mine = jnp.stack(g_mine)
    g_mine, attn_other = tie((g_mine, attn_other))
    g_other = other_core(g_mine)
    mid, u_gu, gate, up, down_msg = run_feed(
        attn_msg, attn_other, h_own, bm[0], mix_rates, am_gu, w_gate_up, bd, w_down, ad_pad,
        mlp_scales, 512,
    )
    g_other, down_msg = tie((g_other, down_msg))
    down_other = other_core(down_msg)
    out_half, mid_res, mid_msg, early = run_feed_back(
        place, down_msg, down_other, mid, cotangent, g_mine, g_other, bm[1], mix_rates, am_gu,
        u_gu, gate, up, w_gate_up, bd, w_down, ad, mlp_scales, 512, group, n_seq, row_width,
    )
    mid_other = other_core(mid_msg)

    order = (slab - jnp.arange(slabs, dtype=i32)) % slabs
    index = jnp.stack(index)[:, order]

    def sum_inner(table):
        return pick(table, inner), [
            within_slab(pick(table, (inner + turn) % group), turn) for turn in range(1, group)
        ]

    def add_inner(own, got):
        total = own.astype(f32)
        for piece in got:
            total = total + piece.astype(f32)
        return total.astype(bf16)

    def over_slabs(total):
        return [pick(total, slab)] + [
            to_slab(pick(total, (slab + shift) % slabs), shift) for shift in range(1, slabs)
        ]

    def pack(rows_part, table):
        return jnp.concatenate([rows_part, table.reshape(slabs, -1, half)], axis=1)

    def over_seqs(table):
        return [
            to_seq(pick(table, (seq_place + shift) % n_seq), shift) for shift in range(1, n_seq)
        ]

    size = early.shape[3]
    home = over_slabs(pack(out_half, early))
    gq, gk, gv, h_res, gbo, gah = run_attend_back(
        place, mid_res, mid_msg, mid_other, mid, h_own, attn_msg, attn_other, mix_rates, bm[0],
        w_attn_out, ah, start, q, k, v, o, inv, qi, ki, cos, sin, scale, slabs, group,
        head_dim,
    )
    home, gk, gv = tie((home, gk, gv))
    keep, send = run_others(place, gk, gv, w_attn_in, am_qkv, bh, slabs, group)
    others = (keep + other_core(send).astype(f32)).astype(bf16)
    others, gq, gk, gv = tie((others, gq, gk, gv))
    waves = [[2, 1], [3, 0]] if slabs == 4 else [list(range(slabs))]
    others = others.reshape(group - 1, slabs, chunk, half)
    others_got = [
        [
            within_slab(
                jnp.stack([pick(others[turn - 1], (slab + shift) % slabs) for shift in wave]),
                turn,
            )
            for turn in range(1, group)
        ]
        for wave in waves
    ]
    tables = jnp.stack([piece[chunk:] for piece in home])
    tables = jnp.moveaxis(tables.reshape(slabs, group, n_seq, size, half), 0, 2)
    early_own, early_got = sum_inner(tables)
    late = run_grads(
        place, gq, gk, gv, bh, u, h_full, h_own, gbo, gah, slabs, group, n_seq, head_dim
    )
    early_got, late = tie((early_got, late))
    early = add_inner(early_own, early_got)
    late_own, late_got = sum_inner(late)
    early_far = over_seqs(early)
    early_mine = pick(early, seq_place)
    home_other = [other_core(piece[:chunk]) for piece in home]
    late_own, gq, others_got[0] = tie((late_own, gq, others_got[0]))
    own_keep, own_send = run_own(
        place, gq, gk, gv, w_attn_in, am_qkv, bh, h_res, slabs, group
    )
    late_got, early_far, own_send, others_got = tie(
        (late_got, early_far, own_send, others_got)
    )
    own_got = other_core(own_send)
    late_total = add_inner(late_own, late_got)
    own_sum = (own_keep + own_got.astype(f32)).reshape(slabs, chunk, half)
    size = late.shape[3]
    result = [None] * slabs
    for wave, got_wave in zip(waves, others_got):
        for n, shift in enumerate(wave):
            target = (slab + shift) % slabs
            total = pick(own_sum, target)
            for got_part in got_wave:
                total = total + got_part[n].astype(f32)
            total = jnp.concatenate(
                [total.astype(bf16), pick(late_total, target).reshape(n_seq * size, half)],
                axis=0,
            )
            result[shift] = to_slab(total, shift) if shift else total
    early_tables = [early_mine, *early_far]
    early_tables += [other_core(table) for table in early_tables]
    layer_out = run_join(place, home, home_other, chunk, bf16)
    cols = model // owners
    each = row_width // owners
    hidden_rows = local_hidden // row_width
    grad_am_gu, grad_bm_down, grad_ad, grad_bd = run_unpack(
        unpack_early_kernel,
        (rank, cols, each, hidden_rows, (3 * rank * hidden_rows + LANES - 1) // LANES),
        (n_seq, slabs),
        place, index, early_tables, [],
        [
            (adapters, 2, rank, cols // 2),
            (adapters, rank, cols),
            (adapters, rank, each, hidden_rows),
            (adapters, 2, rank, each, hidden_rows),
        ],
        "unpack_early",
    )
    result, layer_out, grad_am_gu, grad_bm_down = tie(
        (result, layer_out, grad_am_gu, grad_bm_down)
    )
    result_other = [other_core(piece) for piece in result]
    far = []
    for shift in range(1, n_seq):
        at = chunk + (seq_place + shift) % n_seq * size
        sent = [lax.dynamic_slice_in_dim(piece, at, size, 0) for piece in result]
        far.append(to_seq(jnp.stack(sent), shift))
    input_grad = run_join(place, result, result_other, chunk, f32)
    far, input_grad = tie((far, input_grad))
    each = head_dim // owners
    grad_am, grad_bm, grad_ah, grad_bh = run_unpack(
        unpack_late_kernel,
        (rank, cols, local_heads, each),
        (n_seq, slabs, chunk, size),
        place, index, [*result, *result_other, *far, *(other_core(piece) for piece in far)],
        [grad_am_gu, grad_bm_down],
        [
            (adapters, 5, rank, cols // 2),
            (adapters, 2, rank, cols),
            (adapters, local_heads, each, rank),
            (adapters, 3, local_heads, each, rank),
        ],
        "unpack_late",
    )
    return (
        layer_out,
        input_grad,
        grad_am,
        grad_bm,
        jnp.transpose(grad_ah, (0, 3, 1, 2)),
        jnp.transpose(grad_bh, (0, 1, 4, 2, 3)),
        jnp.transpose(grad_ad, (0, 1, 3, 2)),
        jnp.transpose(grad_bd, (0, 1, 2, 4, 3)),
    )


def solution(mesh):
    return jax.shard_map(
        body,
        mesh=mesh,
        in_specs=(
            P("seq", "ctx", None),
            P("seq", "ctx"),
            P("seq"),
            P(None, None, "wt"),
            P("wt", None),
            P(None, None, "wt"),
            P("wt", None),
            P("wt"),
            P(),
            P(None, "wt"),
            P(),
            P(),
            P(None, None, "wt", None),
            P(None, None, None, "wt", None),
            P(None, None, "wt", None),
            P(None, None, None, "wt", None),
            P("seq", "ctx", None),
        ),
        out_specs=(
            P("seq", "ctx", None),
            P("seq", "ctx", None),
            P(None, None, None, ("seq", "ctx", "wt")),
            P(None, None, None, ("seq", "ctx")),
            P(None, None, "wt", ("seq", "ctx")),
            P(None, None, None, "wt", ("seq", "ctx")),
            P(None, None, "wt", ("seq", "ctx")),
            P(None, None, None, "wt", ("seq", "ctx")),
        ),
        check_vma=False,
    )
```

```python
import functools

import jax
import jax.numpy as jnp
from jax import lax
from jax.experimental import pallas as pl
from jax.experimental.pallas import tpu as pltpu
from jax.sharding import PartitionSpec as P

epsilon = 1e-06
f32 = jnp.float32
bf16 = jnp.bfloat16
i32 = jnp.int32
VMEM_LIMIT = 58 * 1024 * 1024
SMALL_LIMIT = 24 * 1024 * 1024
log2e = 1.4426950408889634
LANES = 128


def dot(left, right, contract):
    return lax.dot_general(left, right, (contract, ((), ())), preferred_element_type=f32)


def nn(left, right):
    return dot(left, right, ((1,), (0,)))


def nt(left, right):
    return dot(left, right, ((1,), (1,)))


def tn(left, right):
    return dot(left, right, ((0,), (0,)))


def lane_iota(shape):
    return lax.broadcasted_iota(i32, shape, len(shape) - 1)


def row_iota(shape):
    return lax.broadcasted_iota(i32, shape, 0)


def row_mean(values):
    return jnp.mean(values, axis=-1, keepdims=True)


def inverse_rms(values):
    return lax.rsqrt(row_mean(values * values) + epsilon)


def at_rows(index, size):
    return pl.ds(pl.multiple_of(index * size, size), size)


def by_rows(total, size, step):
    lax.fori_loop(0, total // size, lambda i, c: (step(at_rows(i, size)), c)[1], 0)


def swap_halves(tile, half):
    lower = lane_iota(tile.shape) % (2 * half) < half
    return jnp.where(lower, pltpu.roll(tile, LANES - half, 1), pltpu.roll(tile, half, 1))


def head_sums(tile, head_dim):
    same = row_iota((LANES, LANES)) // head_dim == lane_iota((LANES, LANES)) // head_dim
    ones = jnp.where(same, 1.0, 0.0).astype(bf16)
    return nn(tile.astype(bf16), ones)


def prep_tile(raw, cosine, sine, scale, head_dim):
    mean = head_sums(raw * raw, head_dim) * (1.0 / head_dim)
    inverse = lax.rsqrt(mean + epsilon)
    turned = raw * cosine + swap_halves(raw, head_dim // 2) * sine
    return (turned * inverse * scale).astype(bf16), inverse.astype(bf16)


def prep_tile_back(grad, low, inverse, cosine, sine, scale, head_dim):
    unit = low.astype(f32) / scale
    grad_unit = grad * scale
    mean = head_sums(grad_unit * unit, head_dim) * (1.0 / head_dim)
    grad_turned = inverse.astype(f32) * (grad_unit - unit * mean)
    return (grad_turned * cosine - swap_halves(grad_turned, head_dim // 2) * sine).astype(bf16)


def spread_pair(tile, head_dim):
    lower = lane_iota(tile.shape) < head_dim
    zero = jnp.zeros_like(tile)
    return jnp.concatenate([jnp.where(lower, tile, zero), jnp.where(lower, zero, tile)], axis=0)


def allowed_mask(first, last, key_start, rows, diagonal):
    keys = key_start + row_iota((rows, first.shape[1]))
    mask = keys >= first
    if diagonal:
        mask = mask & (keys <= last)
    return mask


def query_bounds(start_ref, m, place, group, chunk):
    first = start_ref[m : m + 1, :]
    last = (m * group + place) * chunk + lane_iota((1, chunk))
    return jnp.concatenate([first, first], axis=1), jnp.concatenate([last, last], axis=1)


def whole_spec(shape, buffers=1):
    return pl.BlockSpec(
        shape, lambda *a: (0,) * len(shape), pipeline_mode=pl.Buffered(buffers)
    )


def col_spec(size, width=LANES, skip=0):
    return pl.BlockSpec((size, width), lambda p, s: (0, lax.max(p - skip, 0)))


def row_spec(size, width, last):
    return pl.BlockSpec((size, width), lambda p, s: (lax.min(p, last), 0))


def adapter_spec(shape):
    return pl.BlockSpec(
        (1,) + shape, lambda p, s: (s[4],) + (0,) * len(shape), pipeline_mode=pl.Buffered(1)
    )


def params(small=False, limit=None):
    limit = limit or (SMALL_LIMIT if small else VMEM_LIMIT)
    return pltpu.CompilerParams(vmem_limit_bytes=limit)


def cost(flops, moved, transcendentals=0):
    return pl.CostEstimate(
        flops=int(flops), bytes_accessed=int(moved), transcendentals=int(transcendentals)
    )


def attend_kernel(dims, place, *refs):
    slabs, chunk, group, head_dim, rank, half = dims
    count = 4 + (group - 1) * 4
    pieces = refs[:count]
    (
        wq_ref, w_ref, a_ref, b_table, a_table, cos_ref, sin_ref, scale_ref, wout_ref,
        hout_ref, ownout_ref, u_ref, q_ref, k_ref, v_ref, qi_ref, ki_ref, o_ref, inv_ref,
        msg_ref, start_ref, b_ref, ah_ref, vt_ref, all_ref, seg_ref, h_ref, own_ref, raw_ref,
    ) = refs[count:]
    inner, slab, core = place[0], place[1], place[2]
    block = group * chunk
    length = slabs * block
    rows = slabs * chunk
    model = 2 * half
    step = pl.program_id(0)

    @pl.when(step == 0)
    def _():
        mine = pl.ds(pl.multiple_of(core * half, half), half)
        other = pl.ds(pl.multiple_of((1 - core) * half, half), half)
        h_ref[at_rows(slab * group + inner, chunk), :] = pieces[0][0]
        seg_ref[...] = jnp.zeros_like(seg_ref)

        def keep_segments(where, piece):
            tail = piece[chunk:, :chunk].astype(f32)
            seg_ref[pl.ds(where, 1), :] = tail[0:1]

        keep_segments(slab * group + inner, pieces[1])

        def place_piece(shift, peer, ours, theirs):
            source = lax.rem(slab - shift + slabs, slabs)
            rows_at = at_rows(source * group + peer, chunk)
            h_ref[rows_at, mine] = ours[:chunk, :]
            h_ref[rows_at, other] = theirs[:chunk, :]
            keep_segments(source * group + peer, ours)

        for shift in range(1, slabs):
            place_piece(shift, inner, pieces[2].at[shift - 1], pieces[3].at[shift - 1])
        for turn in range(1, group):
            peer = lax.rem(inner - turn + group, group)
            near, near_other, rest, rest_other = pieces[4 * turn : 4 * turn + 4]
            place_piece(0, peer, near, near_other)
            for shift in range(1, slabs):
                place_piece(shift, peer, rest.at[shift - 1], rest_other.at[shift - 1])
        for m in range(slabs):
            own_ref[m * chunk : (m + 1) * chunk, :] = h_ref[
                at_rows(m * group + inner, chunk), :
            ]
        columns = seg_ref[...].T
        for m in range(slabs):
            line = seg_ref[pl.ds(m * group + inner, 1), :]
            below = jnp.zeros((chunk, chunk), f32)
            for c in range(slabs * group):
                below = below + jnp.where(columns[:, c : c + 1] < line, 1.0, 0.0)
            start_ref[m : m + 1, :] = jnp.sum(below, axis=0, keepdims=True).astype(i32)

        for n in range(b_ref.shape[2] // head_dim):
            cols = slice(n * head_dim, (n + 1) * head_dim)
            b_ref[:, :, cols] = b_table[0, :, n]
            ah_ref[:, cols] = a_table[0, n]
        down = a_ref[0, :3].reshape(3 * rank, model)

        def low_rows(sl):
            u_ref[sl, :] = nt(h_ref[sl, :], down).astype(bf16)

        by_rows(length, 512, low_rows)
        for m in range(slabs):
            low = u_ref[at_rows(m * group + inner, chunk), :rank]
            own = slice(m * chunk, (m + 1) * chunk)
            raw_ref[own, :] = nn(low, b_ref[0])
        raw_ref[...] += nn(own_ref[...], wq_ref[0])

    last_block = lax.min(step, slabs - 1)
    hout_ref[...] = h_ref[at_rows(last_block, block), :]
    ownout_ref[...] = own_ref[at_rows(last_block, chunk), :]
    here = pl.ds(pl.multiple_of(step * LANES, LANES), LANES)
    scale = scale_ref[...]
    w_kv = jnp.concatenate([w_ref[0], w_ref[1]], axis=1)
    none = jnp.zeros((rank, LANES), bf16)
    b_kv = jnp.concatenate(
        [
            jnp.zeros((rank, 2 * LANES), bf16),
            jnp.concatenate([b_ref[1, :, here], none], axis=1),
            jnp.concatenate([none, b_ref[2, :, here]], axis=1),
        ],
        axis=0,
    )

    def keys_rows(sl):
        both = nn(h_ref[sl, :], w_kv) + nn(u_ref[sl, :], b_kv)
        k_ref[sl, :], ki_ref[sl, :] = prep_tile(
            both[:, :LANES], cos_ref[sl, :], sin_ref[sl, :], scale, head_dim
        )
        v_ref[sl, :] = both[:, LANES:].astype(bf16)

    by_rows(length, 512, keys_rows)
    for m in range(slabs):
        own = slice(m * chunk, (m + 1) * chunk)
        there = at_rows(m * group + inner, chunk)
        q_ref[own, :], qi_ref[own, :] = prep_tile(
            raw_ref[own, here], cos_ref[there, :], sin_ref[there, :], scale, head_dim
        )
    vt_ref[...] = v_ref[...].T
    for m in range(slabs):
        own = slice(m * chunk, (m + 1) * chunk)
        pair = spread_pair(q_ref[own, :], head_dim)
        first, last = query_bounds(start_ref, m, inner, group, chunk)
        total = jnp.zeros((1, 2 * chunk), f32)
        gathered = jnp.zeros((LANES, 2 * chunk), f32)
        for b in range(m + 1):
            at = slice(b * block, (b + 1) * block)
            scores = nt(k_ref[at, :], pair)
            mask = allowed_mask(first, last, b * block, block, b == m)
            weights = jnp.where(mask, jnp.exp2(scores * (0.125 * log2e)), 0.0)
            total = total + jnp.sum(weights, axis=0, keepdims=True)
            gathered = gathered + nn(vt_ref[:, at], weights.astype(bf16))
        inverse = 1.0 / total
        gathered = gathered * inverse
        upper = row_iota((LANES, chunk)) < head_dim
        final = jnp.where(upper, gathered[:, :chunk], gathered[:, chunk:])
        final = final.T.astype(bf16)
        o_ref[own, :] = final
        all_ref[own, here] = final
        inv_ref[0, m : m + 1, :] = inverse

    @pl.when(step == pl.num_programs(0) - 1)
    def _():
        low_o = all_ref[...]
        msg_ref[:, :model] = nn(low_o, wout_ref[...]).astype(bf16)
        msg_ref[:, model:] = pad_to(nt(low_o, ah_ref[...]), LANES).astype(bf16)


def run_attend(place, tokens, pieces, w, a, b, ah, cos, sin, scale, wout, group, head_dim):
    slabs, chunk, model = tokens.shape
    width = w.shape[2]
    rank = a.shape[2]
    half = model // 2
    rows = slabs * chunk
    length = rows * group
    pairs = width // LANES
    in_specs = [pl.BlockSpec((1, chunk, model), lambda p, s: (s[1], 0, 0))]
    in_specs += [whole_spec(piece.shape) for piece in pieces]
    in_specs += [
        whole_spec((1, model, width)),
        pl.BlockSpec(
            (pl.Element(2), pl.Element(model), pl.Element(LANES)),
            lambda p, s: (1, 0, p * LANES),
        ),
        adapter_spec((5, rank, model)),
        adapter_spec(b.shape[1:]),
        adapter_spec(ah.shape[1:]),
        whole_spec((length, LANES)),
        whole_spec((length, LANES)),
        col_spec(1),
        whole_spec((width, model)),
    ]
    def step_rows(size):
        return pl.BlockSpec((size, model), lambda p, s: (lax.min(p, slabs - 1), 0))

    out = [
        ((length, model), bf16, step_rows(group * chunk)),
        ((rows, model), bf16, step_rows(chunk)),
        ((length, 3 * rank), bf16, whole_spec((length, 3 * rank))),
        ((rows, width), bf16, col_spec(rows)),
        ((length, width), bf16, col_spec(length)),
        ((length, width), bf16, col_spec(length)),
        ((rows, width), bf16, col_spec(rows)),
        ((length, width), bf16, col_spec(length)),
        ((rows, width), bf16, col_spec(rows)),
        (
            (pairs, slabs, 2 * chunk),
            f32,
            pl.BlockSpec((1, slabs, 2 * chunk), lambda p, s: (p, 0, 0)),
        ),
        ((rows, model + LANES), bf16, whole_spec((rows, model + LANES))),
        ((slabs, chunk), i32, whole_spec((slabs, chunk))),
        ((3, rank, width), bf16, whole_spec((3, rank, width))),
        ((rank, width), bf16, whole_spec((rank, width))),
    ]
    return pl.pallas_call(
        functools.partial(attend_kernel, (slabs, chunk, group, head_dim, rank, half)),
        grid_spec=pltpu.PrefetchScalarGridSpec(
            num_scalar_prefetch=1,
            grid=(pairs,),
            in_specs=in_specs,
            out_specs=[o[2] for o in out],
            scratch_shapes=[
                pltpu.VMEM((LANES, length), bf16),
                pltpu.VMEM((rows, width), bf16),
                pltpu.VMEM((chunk, chunk), f32),
                pltpu.VMEM((length, model), bf16),
                pltpu.VMEM((rows, model), bf16),
                pltpu.VMEM((rows, width), f32),
            ],
        ),
        out_shape=[jax.ShapeDtypeStruct(o[0], o[1]) for o in out],
        compiler_params=params(),
        cost_estimate=cost(1e8, 1e5),
        name="attend",
    )(place, tokens, *pieces, w, w, a, b, ah, cos, sin, scale, wout)


def join_tiles(ref, *at):
    block = ref[at]
    return jnp.concatenate([block[t] for t in range(block.shape[0])], axis=1)


def feed_kernel(
    dims, place, mine_ref, other_ref, h_ref, bo_ref, rate_ref, a_ref, wgu_ref, bgu_ref, wd_ref,
    ad_ref, scales_ref, mid_ref, u_ref, gate_ref, up_ref, msg_ref, low_ref, acc_ref,
):
    rank, model, slabs = dims
    chunk = h_ref.shape[0]
    step = pl.program_id(0)

    @pl.when(step < slabs)
    def _():
        both = mine_ref[...].astype(f32) + other_ref[...].astype(f32)
        low = both[:, model : model + rank].astype(bf16)
        raw = both[:, :model] + nn(low, bo_ref[0, 0])
        unit = raw * inverse_rms(raw)
        state = h_ref[...].astype(f32)
        mixed = state + rate_ref[0:1, :] * (unit - state)
        mixed = (mixed * inverse_rms(mixed)).astype(bf16)
        mid_ref[...] = mixed
        here = at_rows(step, chunk)
        low_ref[here, :] = mixed
        down = a_ref[0, 3:5].reshape(2 * rank, model)
        u_ref[here, :] = nt(mixed, down).astype(bf16)
        acc_ref[here, :] = jnp.zeros((chunk, model + LANES), f32)

    @pl.when(step >= slabs)
    def _():
        low = low_ref[...]
        u = u_ref[...]
        gate = nn(low, wgu_ref[0]) + nn(u[:, :rank], join_tiles(bgu_ref, 0, 0))
        up = nn(low, wgu_ref[1]) + nn(u[:, rank:], join_tiles(bgu_ref, 0, 1))
        gate_ref[...] = gate.astype(bf16)
        up_ref[...] = up.astype(bf16)
        turned = gate * scales_ref[1:2, :]
        hidden = (up * scales_ref[0:1, :] * (turned / (1.0 + jnp.exp(-turned)))).astype(bf16)
        acc_ref[:, :model] += nn(hidden, wd_ref[...])
        acc_ref[:, model : model + rank] += nt(hidden, join_tiles(ad_ref, 0))

    @pl.when(step == pl.num_programs(0) - 1)
    def _():
        msg_ref[...] = acc_ref[...].astype(bf16)


def hidden_specs(skip, model, rank, block, row_width):
    tiles = block // row_width
    at = lambda f: lax.max(f - skip, 0)
    return [
        pl.BlockSpec((2, model, block), lambda f, s: (0, 0, at(f))),
        pl.BlockSpec((1, 2, tiles, rank, row_width), lambda f, s: (s[4], 0, at(f), 0, 0)),
        pl.BlockSpec((block, model), lambda f, s: (at(f), 0)),
        pl.BlockSpec((1, tiles, rank, row_width), lambda f, s: (s[4], at(f), 0, 0)),
        pl.BlockSpec((2, block), lambda f, s: (0, at(f))),
    ]


def run_feed(place, mine, other, h_own, bm, rates, a, wgu, bgu, wd, ad, scales, block, slabs):
    rows, model = h_own.shape
    chunk = rows // slabs
    hidden = wd.shape[0]
    rank = a.shape[2]
    last = slabs - 1
    out = [
        ((rows, model), bf16, row_spec(chunk, model, last)),
        ((rows, 2 * rank), bf16, whole_spec((rows, 2 * rank))),
        ((rows, hidden), bf16, col_spec(rows, block, slabs)),
        ((rows, hidden), bf16, col_spec(rows, block, slabs)),
        ((rows, model + LANES), bf16, whole_spec((rows, model + LANES))),
    ]
    return pl.pallas_call(
        functools.partial(feed_kernel, (rank, model, slabs)),
        grid_spec=pltpu.PrefetchScalarGridSpec(
            num_scalar_prefetch=1,
            grid=(slabs + hidden // block,),
            in_specs=[
                row_spec(chunk, model + LANES, last),
                row_spec(chunk, model + LANES, last),
                row_spec(chunk, model, last),
                adapter_spec((2, rank, model)),
                whole_spec((2, model)),
                adapter_spec((5, rank, model)),
            ]
            + hidden_specs(slabs, model, rank, block, ad.shape[3]),
            out_specs=[o[2] for o in out],
            scratch_shapes=[
                pltpu.VMEM((rows, model), bf16),
                pltpu.VMEM((rows, model + LANES), f32),
            ],
        ),
        out_shape=[jax.ShapeDtypeStruct(o[0], o[1]) for o in out],
        compiler_params=params(),
        cost_estimate=cost(2.4e10, 3e7),
        name="feed",
    )(place, mine, other, h_own, bm, rates, a, wgu, bgu, wd, ad, scales)


def owner_index(place, group, slabs, n_seq):
    inner, slab, seq = place
    return seq * slabs * group + slab * group + inner


def pad_to(tile, lanes):
    return jnp.pad(tile, ((0, 0), (0, lanes - tile.shape[1])))


def late_rows(rank, units):
    return max(4 * rank, 2 * units)


def folded_rows(rows, groups):
    return (rows + groups * 8 - 1) // (groups * 8) * 8


def fold(tile, groups):
    size = folded_rows(tile.shape[0], groups)
    tile = jnp.pad(tile, ((0, size * groups - tile.shape[0]), (0, 0)))
    return jnp.concatenate([tile[g * size : (g + 1) * size] for g in range(groups)], axis=1)


def unfold(block):
    groups = block.shape[1] // LANES
    return jnp.concatenate(
        [block[:, g * LANES : (g + 1) * LANES] for g in range(groups)], axis=0
    ).astype(f32)


def feed_back_kernel(
    dims, place, mine_ref, other_ref, mid_ref, g_own_ref, g_mine_ref, g_other_ref, bd_ref,
    rate_ref, a_ref, u_ref, gate_ref, up_ref, wgu_ref, bgu_ref, wd_ref, ad_ref, scales_ref,
    out_ref, res_ref, msg_ref, table_ref,
    gd_ref, gdt_ref, ut_ref, udt_ref, gud_ref, gudt_ref, low_ref, acc_ref, gu_ref, hid_ref,
    g_ref, lo_ref,
):
    slabs, chunk, group, n_seq, rank, model, row_width, hidden_rows = dims
    half = model // 2
    step = pl.program_id(0)
    slab, core = place[1], place[2]
    block = gate_ref.shape[1]

    @pl.when(step < slabs)
    def _():
        mine = pl.ds(pl.multiple_of(core * half, half), half)
        other = pl.ds(pl.multiple_of((1 - core) * half, half), half)
        shift = lax.rem(slab - step + slabs, slabs)

        @pl.when(shift == 0)
        def _():
            g_ref[...] = g_own_ref[0]

        @pl.when(shift > 0)
        def _():
            g_ref[:, mine] = g_mine_ref[shift - 1]
            g_ref[:, other] = g_other_ref[shift - 1]

        here = at_rows(step, chunk)
        both = mine_ref[...].astype(f32) + other_ref[...].astype(f32)
        low = both[:, model : model + rank].astype(bf16)
        hid_ref[here, :] = low
        raw = both[:, :model] + nn(low, bd_ref[0, 1])
        raw_inv = inverse_rms(raw)
        unit = raw * raw_inv
        state = mid_ref[...]
        low_ref[here, :] = state
        state = state.astype(f32)
        rate = rate_ref[1:2, :]
        mixed = state + rate * (unit - state)
        mixed_inv = inverse_rms(mixed)
        out = mixed * mixed_inv
        lo_ref[...] = out.astype(bf16)
        grad = g_ref[...].astype(f32)
        grad_mixed = mixed_inv * (grad - out * row_mean(grad * out))
        res_ref[...] = (1.0 - rate) * grad_mixed
        grad_unit = rate * grad_mixed
        gd_ref[here, :] = (raw_inv * (grad_unit - unit * row_mean(grad_unit * unit))).astype(bf16)
        out_ref[0] = lo_ref[:, mine]
        acc_ref[here, :] = jnp.zeros((chunk, model), f32)
        gu_ref[here, :] = jnp.zeros((chunk, 2 * rank), f32)

    @pl.when(step == slabs)
    def _():
        ut_ref[...] = u_ref[...].T
        udt_ref[...] = hid_ref[...].T
        low_gud = nt(gd_ref[...], bd_ref[0, 1]).astype(bf16)
        gud_ref[...] = low_gud
        gudt_ref[...] = low_gud.T

    @pl.when(step >= slabs)
    def _():
        grad_hidden = nt(gd_ref[...], wd_ref[...]) + nn(gud_ref[...], join_tiles(ad_ref, 0))
        gate = gate_ref[...].astype(f32)
        up = up_ref[...].astype(f32)
        up_scale = scales_ref[0:1, :]
        gate_scale = scales_ref[1:2, :]
        turned = gate * gate_scale
        sigmoid = 1.0 / (1.0 + jnp.exp(-turned))
        silu = turned * sigmoid
        up_scaled = up * up_scale
        hidden = (up_scaled * silu).astype(bf16)
        grad_up = (grad_hidden * up_scale * silu).astype(bf16)
        slope = sigmoid * (1.0 + turned * (1.0 - sigmoid)) * gate_scale
        grad_gate = (grad_hidden * up_scaled * slope).astype(bf16)
        acc_ref[...] += nt(grad_gate, wgu_ref[0]) + nt(grad_up, wgu_ref[1])
        gu_ref[:, :rank] += nt(grad_gate, join_tiles(bgu_ref, 0, 0))
        gu_ref[:, rank:] += nt(grad_up, join_tiles(bgu_ref, 0, 1))
        ut = ut_ref[...]
        parts = jnp.concatenate(
            [nn(gudt_ref[...], hidden), nn(ut[:rank], grad_gate), nn(ut[rank:], grad_up)], axis=0
        ).astype(bf16)
        tiles = block // row_width
        for tile in range(tiles):
            gdt_ref[(step - slabs) * tiles + tile] = parts[
                :, tile * row_width : (tile + 1) * row_width
            ]

    @pl.when(step == pl.num_programs(0) - 1)
    def _():
        low_gu = gu_ref[...].astype(bf16)
        down = a_ref[0, 3:5].reshape(2 * rank, model)
        msg_ref[...] = (acc_ref[...] + nn(low_gu, down)).astype(bf16)
        low = low_ref[...]
        model_rows = jnp.concatenate(
            [nn(low_gu.T, low), nn(udt_ref[...], gd_ref[...])], axis=0
        ).astype(bf16).astype(f32)
        ranks = 3 * rank
        units = ranks * hidden_rows
        padded = (units + LANES - 1) // LANES * LANES
        flat = gdt_ref[...].reshape(units, row_width)
        lanes = lane_iota((1, padded))
        target = lanes % hidden_rows * ranks + lanes // hidden_rows
        target = jnp.where(lanes < units, target, -1)
        moved = jnp.where(row_iota((units, padded)) == target, 1.0, 0.0).astype(bf16)
        turned_rows = tn(flat, moved)
        owners = n_seq * slabs * group
        cols = model // owners
        units_each = row_width // owners
        for y in range(group):
            for z in range(slabs):
                for x in range(n_seq):
                    d = owner_index((y, z, x), group, slabs, n_seq)
                    head = pad_to(model_rows[:, d * cols : (d + 1) * cols], LANES)
                    mine = turned_rows[d * units_each : (d + 1) * units_each]
                    tail = [
                        mine[:, t * LANES : (t + 1) * LANES] for t in range(padded // LANES)
                    ]
                    packed = jnp.concatenate([head] + tail, axis=0)
                    table_ref[y, z, x] = fold(packed, half // LANES).astype(bf16)


def run_feed_back(
    place, mine, other, mid, cotangent, g_mine, g_other, bm, rates, a, u, gate, up, wgu, bgu,
    wd, ad, scales, block, group, n_seq,
):
    slabs, chunk, model = cotangent.shape
    rows = slabs * chunk
    half = model // 2
    hidden = wd.shape[0]
    rank = a.shape[2]
    row_width = ad.shape[3]
    last = slabs - 1
    hidden_rows = hidden // row_width
    owners = n_seq * slabs * group
    padded = (3 * rank * hidden_rows + LANES - 1) // LANES * LANES
    table_rows = 3 * rank + row_width // owners * (padded // LANES)
    table = (group, slabs, n_seq, folded_rows(table_rows, half // LANES), half)
    out = [
        (
            (slabs, chunk, half),
            bf16,
            pl.BlockSpec((1, chunk, half), lambda f, s: (lax.min(f, last), 0, 0)),
        ),
        ((rows, model), f32, row_spec(chunk, model, last)),
        ((rows, model), bf16, whole_spec((rows, model))),
        (table, bf16, whole_spec(table)),
    ]
    return pl.pallas_call(
        functools.partial(
            feed_back_kernel,
            (slabs, chunk, group, n_seq, rank, model, row_width, hidden_rows),
        ),
        grid_spec=pltpu.PrefetchScalarGridSpec(
            num_scalar_prefetch=1,
            grid=(slabs + hidden // block,),
            in_specs=[
                row_spec(chunk, model + LANES, last),
                row_spec(chunk, model + LANES, last),
                row_spec(chunk, model, last),
                pl.BlockSpec(
                    (1, chunk, model), lambda f, s: (s[1], 0, 0), pipeline_mode=pl.Buffered(1)
                ),
                whole_spec((slabs - 1, chunk, half)),
                whole_spec((slabs - 1, chunk, half)),
                adapter_spec((2, rank, model)),
                whole_spec((2, model)),
                adapter_spec((5, rank, model)),
                whole_spec((rows, 2 * rank)),
                col_spec(rows, block, slabs),
                col_spec(rows, block, slabs),
            ]
            + hidden_specs(slabs, model, rank, block, row_width),
            out_specs=[o[2] for o in out],
            scratch_shapes=[
                pltpu.VMEM((rows, model), bf16),
                pltpu.VMEM((hidden_rows, 3 * rank, row_width), bf16),
                pltpu.VMEM((2 * rank, rows), bf16),
                pltpu.VMEM((rank, rows), bf16),
                pltpu.VMEM((rows, rank), bf16),
                pltpu.VMEM((rank, rows), bf16),
                pltpu.VMEM((rows, model), bf16),
                pltpu.VMEM((rows, model), f32),
                pltpu.VMEM((rows, 2 * rank), f32),
                pltpu.VMEM((rows, rank), bf16),
                pltpu.VMEM((chunk, model), bf16),
                pltpu.VMEM((chunk, model), bf16),
            ],
        ),
        out_shape=[jax.ShapeDtypeStruct(o[0], o[1]) for o in out],
        compiler_params=params(),
        cost_estimate=cost(3e10, 4e7),
        name="feed_back",
    )(
        place, mine, other, mid, cotangent, g_mine, g_other, bm, rates, a, u, gate, up, wgu,
        bgu, wd, ad, scales,
    )


def attend_back_kernel(
    dims, place, res_ref, gm_ref, go_ref, h_ref, am_ref, ao_ref, rate_ref, bo_ref, wout_ref,
    ah_ref, start_ref, q_ref, k_ref, v_ref, o_ref, inv_ref, qi_ref, ki_ref, cos_ref, sin_ref,
    scale_ref,
    gq_ref, gk_ref, gv_ref, gres_ref, gbo_ref, gah_ref,
    kt_ref, gqt_ref, ga_ref, guo_ref, guot_ref, uo_ref,
):
    slabs, chunk, group, head_dim, rank, model = dims
    inner = place[0]
    step = pl.program_id(0)

    @pl.when(step < slabs)
    def _():
        here = at_rows(step, chunk)
        grad = res_ref[...] + gm_ref[...].astype(f32) + go_ref[...].astype(f32)
        both = am_ref[...].astype(f32) + ao_ref[...].astype(f32)
        low = both[:, model : model + rank].astype(bf16)
        uo_ref[here, :] = low
        raw = both[:, :model] + nn(low, bo_ref[0, 0])
        raw_inv = inverse_rms(raw)
        unit = raw * raw_inv
        state = h_ref[...].astype(f32)
        rate = rate_ref[0:1, :]
        mixed = state + rate * (unit - state)
        mixed_inv = inverse_rms(mixed)
        out = mixed * mixed_inv
        grad_mixed = mixed_inv * (grad - out * row_mean(grad * out))
        gres_ref[...] = (1.0 - rate) * grad_mixed
        grad_unit = rate * grad_mixed
        ga_ref[here, :] = (raw_inv * (grad_unit - unit * row_mean(grad_unit * unit))).astype(bf16)

    @pl.when(step == slabs)
    def _():
        gbo_ref[...] = nn(uo_ref[...].T, ga_ref[...])
        low_g = nt(ga_ref[...], bo_ref[0, 0]).astype(bf16)
        guo_ref[...] = low_g
        guot_ref[...] = low_g.T

    @pl.when(step >= slabs)
    def _():
        attend_back_pair(
            dims, inner, wout_ref, ah_ref, start_ref, q_ref, k_ref, v_ref, o_ref, inv_ref,
            qi_ref, ki_ref, cos_ref, sin_ref, scale_ref, gq_ref, gk_ref, gv_ref, gah_ref,
            kt_ref, gqt_ref, ga_ref, guo_ref, guot_ref,
        )


def attend_back_pair(
    dims, inner, wout_ref, ah_ref, start_ref, q_ref, k_ref, v_ref, o_ref, inv_ref, qi_ref,
    ki_ref, cos_ref, sin_ref, scale_ref, gq_ref, gk_ref, gv_ref, gah_ref, kt_ref, gqt_ref,
    ga_ref, guo_ref, guot_ref,
):
    slabs, chunk, group, head_dim, rank, model = dims
    block = group * chunk
    kt_ref[...] = k_ref[...].T
    scale = scale_ref[...]
    grad_o = (nt(ga_ref[...], wout_ref[...]) + nn(guo_ref[...], ah_ref[...])).astype(bf16)
    gah_ref[...] = nn(guot_ref[...], o_ref[...])
    pairs_q, pairs_g, deltas, bounds = [], [], [], []
    for m in range(slabs):
        own = slice(m * chunk, (m + 1) * chunk)
        pairs_q.append(spread_pair(q_ref[own, :], head_dim))
        grad = grad_o[own]
        pairs_g.append(spread_pair(grad, head_dim))
        products = (grad.astype(f32) * o_ref[own, :].astype(f32)).T
        deltas.append(
            jnp.concatenate(
                [
                    jnp.sum(products[:head_dim], axis=0, keepdims=True),
                    jnp.sum(products[head_dim:], axis=0, keepdims=True),
                ],
                axis=1,
            )
        )
        bounds.append(query_bounds(start_ref, m, inner, group, chunk))
    for b in range(slabs):
        at = slice(b * block, (b + 1) * block)
        grad_key = jnp.zeros((block, LANES), f32)
        grad_value = jnp.zeros((block, LANES), f32)
        for m in range(b, slabs):
            first, last = bounds[m]
            scores = nt(k_ref[at, :], pairs_q[m])
            mask = allowed_mask(first, last, b * block, block, b == m)
            weights = jnp.exp2(scores * (0.125 * log2e)) * inv_ref[0, m : m + 1, :]
            weights = jnp.where(mask, weights, 0.0)
            grad_value = grad_value + nn(weights.astype(bf16), pairs_g[m])
            grad_weights = nt(v_ref[at, :], pairs_g[m])
            grad_scores = (weights * (grad_weights - deltas[m])).astype(bf16)
            grad_key = grad_key + nn(grad_scores, pairs_q[m])
            part = nn(kt_ref[:, at], grad_scores)
            if b == 0:
                gqt_ref[m] = part
            else:
                gqt_ref[m] += part
        gv_ref[at, :] = grad_value.astype(bf16)
        gk_ref[at, :] = prep_tile_back(
            grad_key * 0.125, k_ref[at, :], ki_ref[at, :], cos_ref[at, :], sin_ref[at, :],
            scale, head_dim,
        )
    upper = row_iota((LANES, chunk)) < head_dim
    for m in range(slabs):
        own = slice(m * chunk, (m + 1) * chunk)
        both = gqt_ref[m]
        grad = jnp.where(upper, both[:, :chunk], both[:, chunk:]).T * 0.125
        there = at_rows(m * group + inner, chunk)
        gq_ref[own, :] = prep_tile_back(
            grad, q_ref[own, :], qi_ref[own, :], cos_ref[there, :], sin_ref[there, :],
            scale, head_dim,
        )


def run_attend_back(
    place, res, gm, go, h_own, am, ao, rates, bm, wout, ah, start, q, k, v, o, inv, qi, ki, cos, sin, scale, slabs, group, head_dim,
):
    rows, model = h_own.shape
    chunk = rows // slabs
    width = q.shape[1]
    length = k.shape[0]
    rank = bm.shape[2]
    pairs = width // LANES
    last = slabs - 1
    wide = row_spec(chunk, model + LANES, last)
    narrow = row_spec(chunk, model, last)
    cols = lambda size: col_spec(size, LANES, slabs)
    out = [
        ((rows, width), bf16, cols(rows)),
        ((length, width), bf16, cols(length)),
        ((length, width), bf16, cols(length)),
        ((rows, model), f32, narrow),
        ((rank, model), f32, whole_spec((rank, model))),
        ((rank, width), f32, cols(rank)),
    ]
    return pl.pallas_call(
        functools.partial(attend_back_kernel, (slabs, chunk, group, head_dim, rank, model)),
        grid_spec=pltpu.PrefetchScalarGridSpec(
            num_scalar_prefetch=1,
            grid=(slabs + pairs,),
            in_specs=[
                narrow,
                narrow,
                narrow,
                narrow,
                wide,
                wide,
                whole_spec((2, model)),
                adapter_spec((2, rank, model)),
                pl.BlockSpec((LANES, model), lambda p, s: (lax.max(p - slabs, 0), 0)),
                cols(rank),
                whole_spec((slabs, chunk)),
                cols(rows),
                cols(length),
                cols(length),
                cols(rows),
                pl.BlockSpec(
                    (1, slabs, 2 * chunk), lambda p, s: (lax.max(p - slabs, 0), 0, 0)
                ),
                cols(rows),
                cols(length),
                whole_spec((length, LANES)),
                whole_spec((length, LANES)),
                cols(1),
            ],
            out_specs=[o_[2] for o_ in out],
            scratch_shapes=[
                pltpu.VMEM((LANES, length), bf16),
                pltpu.VMEM((slabs, LANES, 2 * chunk), f32),
                pltpu.VMEM((rows, model), bf16),
                pltpu.VMEM((rows, rank), bf16),
                pltpu.VMEM((rank, rows), bf16),
                pltpu.VMEM((rows, rank), bf16),
            ],
        ),
        out_shape=[jax.ShapeDtypeStruct(o_[0], o_[1]) for o_ in out],
        compiler_params=params(),
        cost_estimate=cost(3e10, 4e7),
        name="attend_back",
    )(
        place, res, gm, go, h_own, am, ao, rates, bm, wout, ah, start, q, k, v, o, inv, qi, ki,
        cos, sin, scale,
    )


def apart(blocks):
    none = jnp.zeros_like(blocks[0])
    return jnp.concatenate(
        [
            jnp.concatenate([b if n == m else none for n in range(len(blocks))], axis=1)
            for m, b in enumerate(blocks)
        ],
        axis=0,
    )


def others_kernel(
    place, gk_ref, gv_ref, wk_ref, wv_ref, a_ref, b_ref, keep_ref, send_ref, low_ref
):
    rows, width = keep_ref.shape[1], gk_ref.shape[-1]
    half = keep_ref.shape[2]
    rank = b_ref.shape[1]
    both = jnp.concatenate(
        [gk_ref[...].reshape(rows, width), gv_ref[...].reshape(rows, width)], axis=1
    )
    turn = pl.program_id(1)

    @pl.when(turn == 0)
    def _():
        low_ref[...] = nt(both, apart([b_ref[1], b_ref[2]])).astype(bf16)

    weights = jnp.concatenate([wk_ref[0], wv_ref[0]], axis=1)
    part = nt(both, weights) + nn(low_ref[...], a_ref[0, 1:3].reshape(2 * rank, half))

    @pl.when(turn == 0)
    def _():
        send_ref[0] = part.astype(bf16)

    @pl.when(turn == 1)
    def _():
        keep_ref[0] = part


def half_weight(half, width, member):
    return pl.BlockSpec(
        (1, half, width), lambda *a: (member, lax.rem(a[-1][2] + 1 + a[-2], 2), 0)
    )


def half_factors(rank, half):
    return pl.BlockSpec(
        (1, 5, rank, half), lambda *a: (a[-1][4], 0, 0, lax.rem(a[-1][2] + 1 + a[-2], 2))
    )


def run_others(place, gk, gv, w, a, b, slabs, group):
    length, width = gk.shape
    chunk = length // (slabs * group)
    rows = slabs * chunk
    half = w.shape[1] // 2
    rank = b.shape[1]
    shaped = (slabs, group, chunk, width)
    peer = pl.BlockSpec(
        (slabs, 1, chunk, width), lambda g, t, s: (0, lax.rem(s[0] + 1 + g, group), 0, 0)
    )
    return pl.pallas_call(
        others_kernel,
        grid_spec=pltpu.PrefetchScalarGridSpec(
            num_scalar_prefetch=1,
            grid=(group - 1, 2),
            in_specs=[
                peer,
                peer,
                half_weight(half, width, 1),
                half_weight(half, width, 2),
                half_factors(rank, half),
                whole_spec((3, rank, width)),
            ],
            out_specs=[pl.BlockSpec((1, rows, half), lambda g, t, s: (g, 0, 0))] * 2,
            scratch_shapes=[pltpu.VMEM((rows, 2 * rank), bf16)],
        ),
        out_shape=[
            jax.ShapeDtypeStruct((group - 1, rows, half), f32),
            jax.ShapeDtypeStruct((group - 1, rows, half), bf16),
        ],
        compiler_params=params(True),
        cost_estimate=cost(7e9, 1e7),
        name="others",
    )(place, gk.reshape(shaped), gv.reshape(shaped), w, w, a, b)


def own_kernel(
    place, gq_ref, gk_ref, gv_ref, wq_ref, wk_ref, wv_ref, a_ref, b_ref, res_ref, keep_ref,
    send_ref, low_ref,
):
    rows, width = gq_ref.shape
    half = keep_ref.shape[1]
    rank = b_ref.shape[1]
    grads = jnp.concatenate(
        [gq_ref[...], gk_ref[...].reshape(rows, width), gv_ref[...].reshape(rows, width)], axis=1
    )
    turn = pl.program_id(0)

    @pl.when(turn == 0)
    def _():
        low_ref[...] = nt(grads, apart([b_ref[0], b_ref[1], b_ref[2]])).astype(bf16)

    weights = jnp.concatenate([wq_ref[0], wk_ref[0], wv_ref[0]], axis=1)
    part = nt(grads, weights) + nn(low_ref[...], a_ref[0, 0:3].reshape(3 * rank, half))

    @pl.when(turn == 0)
    def _():
        send_ref[...] = part.astype(bf16)

    @pl.when(turn == 1)
    def _():
        keep_ref[...] = part + res_ref[...]


def run_own(place, gq, gk, gv, w, a, b, res, slabs, group):
    length, width = gk.shape
    rows, model = res.shape
    chunk = rows // slabs
    half = model // 2
    rank = b.shape[1]
    shaped = (slabs, group, chunk, width)
    peer = pl.BlockSpec((slabs, 1, chunk, width), lambda t, s: (0, s[0], 0, 0))
    out = [((rows, half), f32), ((rows, half), bf16)]
    return pl.pallas_call(
        own_kernel,
        grid_spec=pltpu.PrefetchScalarGridSpec(
            num_scalar_prefetch=1,
            grid=(2,),
            in_specs=[
                whole_spec((rows, width)),
                peer,
                peer,
                half_weight(half, width, 0),
                half_weight(half, width, 1),
                half_weight(half, width, 2),
                half_factors(rank, half),
                whole_spec((3, rank, width)),
                pl.BlockSpec((rows, half), lambda t, s: (0, s[2])),
            ],
            out_specs=[whole_spec(o[0]) for o in out],
            scratch_shapes=[pltpu.VMEM((rows, 3 * rank), bf16)],
        ),
        out_shape=[jax.ShapeDtypeStruct(o[0], o[1]) for o in out],
        compiler_params=params(True),
        cost_estimate=cost(7e9, 1e7),
        name="own",
    )(place, gq, gk.reshape(shaped), gv.reshape(shaped), w, w, w, a, b, res)


def grads_kernel(
    dims, place, gq_ref, gk_ref, gv_ref, b_ref, u_ref, h_ref, gbo_ref, gah_ref, table_ref,
    uq_ref, low_ref,
):
    slabs, chunk, group, n_seq, rank, model, head_dim = dims
    inner = place[0]
    width = gq_ref.shape[1]
    heads = width // head_dim
    gq = gq_ref[...]
    both = jnp.concatenate([gk_ref[...], gv_ref[...]], axis=1)
    low_q = nt(gq, b_ref[0]).astype(bf16)
    low_ref[:, : 2 * rank] = nt(both, apart([b_ref[1], b_ref[2]])).astype(bf16)
    low_ref[:, 2 * rank :] = jnp.zeros((low_ref.shape[0], rank), bf16)
    for m in range(slabs):
        there = at_rows(m * group + inner, chunk)
        uq_ref[m * chunk : (m + 1) * chunk, :] = u_ref[there, :]
        low_ref[there, 2 * rank :] = low_q[m * chunk : (m + 1) * chunk]
    products = nn(low_ref[...].T, h_ref[...])
    model_rows = jnp.concatenate(
        [products[2 * rank :], products[: 2 * rank], gbo_ref[...]], axis=0
    ).astype(bf16).astype(f32)
    uqt = uq_ref[...].T
    pair = nn(u_ref[...].T[rank:], both)
    head_rows = jnp.concatenate(
        [gah_ref[...], nn(uqt[:rank], gq), pair[:rank, :width], pair[rank:, width:]], axis=0
    ).astype(bf16)
    owners = n_seq * slabs * group
    cols = model // owners
    each = head_dim // owners
    units = heads * each
    spots = lax.broadcasted_iota(i32, (width, 1), 0)
    owner = spots // units
    inside = spots % units
    source = inside // each * head_dim + owner * each + inside % each
    moved = jnp.where(lane_iota((width, width)) == source, 1.0, 0.0).astype(bf16)
    turned = nt(moved, head_rows)
    for y in range(group):
        for z in range(slabs):
            for x in range(n_seq):
                d = owner_index((y, z, x), group, slabs, n_seq)
                left = model_rows[:, d * cols : (d + 1) * cols]
                heads_part = turned[d * units : (d + 1) * units]
                right = jnp.concatenate(
                    [heads_part[:, rank:], pad_to(heads_part[:, :rank], 3 * rank)], axis=0
                )
                tall = late_rows(rank, units)
                packed = jnp.concatenate(
                    [
                        jnp.pad(left, ((0, tall - left.shape[0]), (0, 0))),
                        jnp.pad(right, ((0, tall - right.shape[0]), (0, 0))),
                    ],
                    axis=1,
                )
                packed = pad_to(packed, LANES)
                table_ref[y, z, x] = fold(packed, table_ref.shape[4] // LANES).astype(bf16)


def run_grads(place, gq, gk, gv, b, u, h, gbo, gah, slabs, group, n_seq, head_dim):
    length, width = gk.shape
    rows, model = gq.shape[0], h.shape[1]
    chunk = rows // slabs
    rank = b.shape[1]
    heads = width // head_dim
    owners = n_seq * slabs * group
    units = heads * (head_dim // owners)
    half = model // 2
    shape = (group, slabs, n_seq, folded_rows(late_rows(rank, units), half // LANES), half)
    operands = (gq, gk, gv, b, u, h, gbo, gah)
    return pl.pallas_call(
        functools.partial(grads_kernel, (slabs, chunk, group, n_seq, rank, model, head_dim)),
        grid_spec=pltpu.PrefetchScalarGridSpec(
            num_scalar_prefetch=1,
            grid=(1,),
            in_specs=[whole_spec(operand.shape) for operand in operands],
            out_specs=whole_spec(shape),
            scratch_shapes=[
                pltpu.VMEM((rows, 3 * rank), bf16),
                pltpu.VMEM((length, 3 * rank), bf16),
            ],
        ),
        out_shape=jax.ShapeDtypeStruct(shape, bf16),
        compiler_params=params(True),
        cost_estimate=cost(1e10, 1e7),
        name="grads",
    )(place, *operands)


def join_kernel(slabs, place, *refs):
    out_ref = refs[-1]
    chunk, half = out_ref.shape[1], refs[0].shape[-1]
    core, slab = place[2], place[1]
    for shift in range(slabs):
        source = lax.rem(slab - shift + slabs, slabs)
        for which, ref in ((core, refs[shift]), (1 - core, refs[slabs + shift])):
            out_ref[source, :, pl.ds(pl.multiple_of(which * half, half), half)] = ref[
                :chunk, :
            ].astype(out_ref.dtype)


def run_join(place, mine, other, chunk, dtype):
    slabs = len(mine)
    half = mine[0].shape[1]
    return pl.pallas_call(
        functools.partial(join_kernel, slabs),
        grid_spec=pltpu.PrefetchScalarGridSpec(
            num_scalar_prefetch=1,
            grid=(1,),
            in_specs=[whole_spec(piece.shape) for piece in (*mine, *other)],
            out_specs=whole_spec((slabs, chunk, 2 * half)),
        ),
        out_shape=jax.ShapeDtypeStruct((slabs, chunk, 2 * half), dtype),
        compiler_params=params(True),
        cost_estimate=cost(1e6, 8e6),
        name="join",
    )(place, *mine, *other)


def for_tables(where, place, index, refs, put):
    n_seq, slabs, chunk, size = where
    home, home_other = refs[:slabs], refs[slabs : 2 * slabs]
    far, far_other = refs[2 * slabs : 2 * slabs + n_seq - 1], refs[2 * slabs + n_seq - 1 :]
    for r in range(slabs):
        at = pl.ds(pl.multiple_of(chunk + place[3] * size, 8), size)
        put(index[0, r], unfold(home[r][at, :]), unfold(home_other[r][at, :]))
    for s in range(1, n_seq):

        def one(r, carry, s=s):
            put(index[s, r], unfold(far[s - 1][r]), unfold(far_other[s - 1][r]))
            return carry

        lax.fori_loop(0, slabs, one, 0)


def unpack_early_kernel(dims, where, place, index, *refs):
    rank, cols, each, hidden_rows, tiles = dims
    am_ref, bm_ref, ad_ref, bd_ref = refs[-4:]
    core = place[2]

    def put(adapter, block, other):
        both = block[: 2 * rank] + other[: 2 * rank]
        am = jnp.where(core == 0, both[:, : cols // 2], both[:, cols // 2 : cols])
        am_ref[adapter] = am.reshape(2, rank, cols // 2)
        bm_ref[adapter] = block[2 * rank : 3 * rank, :cols]
        base = 3 * rank
        wide = jnp.concatenate(
            [block[base + t * each : base + (t + 1) * each] for t in range(tiles)], axis=1
        )
        for k in range(rank):
            ad_ref[adapter, k] = wide[:, k * hidden_rows : (k + 1) * hidden_rows]
        for j in range(2):
            for k in range(rank):
                at = ((j + 1) * rank + k) * hidden_rows
                bd_ref[adapter, j, k] = wide[:, at : at + hidden_rows]

    for_tables(where, place, index, refs[:-4], put)


def unpack_late_kernel(dims, where, place, index, *refs):
    rank, cols, heads, each = dims
    am_gu_ref, bm_down_ref, am_ref, bm_ref, ah_ref, bh_ref = refs[-6:]
    core = place[2]

    def put(adapter, block, other):
        both = block[: 3 * rank] + other[: 3 * rank]
        am = jnp.where(core == 0, both[:, : cols // 2], both[:, cols // 2 : cols])
        am_ref[adapter, 0:3] = am.reshape(3, rank, cols // 2)
        am_ref[adapter, 3:5] = am_gu_ref[adapter]
        bm_ref[adapter, 0] = block[3 * rank : 4 * rank, :cols]
        bm_ref[adapter, 1] = bm_down_ref[adapter]
        units = heads * each
        for n in range(heads):
            at = n * each
            ah_ref[adapter, n] = block[units + at : units + at + each, cols : cols + rank]
            for j in range(3):
                lanes = slice(cols + j * rank, cols + (j + 1) * rank)
                bh_ref[adapter, j, n] = block[at : at + each, lanes]

    for_tables(where, place, index, refs[:-6], put)


def run_unpack(kernel, dims, where, place, index, tables, extra, shapes, name):
    operands = [*tables, *extra]
    return pl.pallas_call(
        functools.partial(kernel, dims, where),
        grid_spec=pltpu.PrefetchScalarGridSpec(
            num_scalar_prefetch=2,
            grid=(1,),
            in_specs=[whole_spec(operand.shape) for operand in operands],
            out_specs=[whole_spec(shape) for shape in shapes],
        ),
        out_shape=[jax.ShapeDtypeStruct(shape, f32) for shape in shapes],
        compiler_params=params(True),
        cost_estimate=cost(1e6, 8e6),
        name=name,
    )(place, index, *operands)


def pick(array, index):
    return lax.dynamic_index_in_dim(array, index, 0, keepdims=False)


def body(
    tokens, segments, adapter_index, w_attn_in, w_attn_out, w_gate_up, w_down, qk_scale,
    mix_rates, mlp_scales, a_model, b_model, a_heads, b_heads, a_hidden, b_hidden, cotangent,
):
    slabs, chunk, model = tokens.shape
    n_seq = lax.axis_size("seq")
    n_ctx = lax.axis_size("ctx")
    group = n_ctx // slabs
    local_width = w_attn_out.shape[0]
    head_dim = a_heads.shape[-1]
    row_width = a_hidden.shape[-1]
    local_hidden = w_down.shape[0]
    local_heads = local_width // head_dim
    rank = a_model.shape[2]
    adapters = a_model.shape[0]
    half = model // 2
    ctx_place = lax.axis_index("ctx")
    slab = ctx_place // group
    inner = ctx_place % group
    core = lax.axis_index("wt")
    seq_place = lax.axis_index("seq")
    owners = n_seq * n_ctx
    rows = slabs * chunk
    length = rows * group
    place = jnp.stack([inner, slab, core, seq_place, pick(adapter_index, slab)]).astype(i32)
    a_heads = jnp.transpose(a_heads, (0, 2, 1, 3))
    b_heads = jnp.transpose(b_heads, (0, 1, 3, 2, 4))
    a_hidden = jnp.transpose(a_hidden, (0, 2, 1, 3))
    b_hidden = jnp.transpose(b_hidden, (0, 1, 3, 2, 4))

    def to_slab(array, shift):
        pairs = [(c, (c + shift * group) % n_ctx) for c in range(n_ctx)]
        return lax.ppermute(array, "ctx", pairs)

    def within_slab(array, shift):
        pairs = [(c, c - c % group + (c % group + shift) % group) for c in range(n_ctx)]
        return lax.ppermute(array, "ctx", pairs)

    def to_seq(array, shift):
        return lax.ppermute(array, "seq", [(c, (c + shift) % n_seq) for c in range(n_seq)])

    def other_core(array):
        return lax.ppermute(array, "wt", [(0, 1), (1, 0)])

    def half_piece(array, index, which):
        return lax.dynamic_slice(array, (index, 0, which * half), (1, chunk, half))[0]

    def token_piece(index):
        seg = jnp.pad(pick(segments, index).astype(bf16), (0, half - chunk))
        return jnp.concatenate(
            [half_piece(tokens, index, core), jnp.broadcast_to(seg, (8, half))], axis=0
        )

    tie = lax.optimization_barrier

    spot = (jnp.arange(LANES, dtype=i32) % (head_dim // 2)).astype(f32)
    frequency = 10000.0 ** (-spot / (head_dim // 2))
    turn = jnp.arange(length, dtype=i32).astype(f32)[:, None] * frequency[None, :]
    cos = jnp.cos(turn)
    lower = jnp.arange(LANES) % head_dim < head_dim // 2
    sin = jnp.sin(turn) * jnp.where(lower, -1.0, 1.0)[None, :]
    scale = qk_scale[None, :]

    own_piece = token_piece(slab)
    got = [own_piece] + [
        to_slab(token_piece((slab + shift) % slabs), shift) for shift in range(1, slabs)
    ]
    index = [adapter_index]
    for shift in range(1, n_seq):
        index.append(to_seq(adapter_index, shift))
    got, cos, sin, place, index = tie((got, cos, sin, place, index))
    near = [within_slab(own_piece, turn) for turn in range(1, group)]
    g_send = [half_piece(cotangent, (slab + shift) % slabs, core) for shift in range(1, slabs)]
    rest, near, g_send = tie((jnp.stack(got[1:]), near, g_send))
    rest_other = other_core(rest)
    peers = [within_slab(rest, turn) for turn in range(1, group)]
    g_mine = [to_slab(g_send[shift - 1], shift) for shift in range(1, slabs)]
    pieces = [own_piece, rest, rest_other]
    for turn in range(1, group):
        pieces += [
            near[turn - 1], other_core(near[turn - 1]),
            peers[turn - 1], other_core(peers[turn - 1]),
        ]
    h_full, h_own, u, q, k, v, qi, ki, o, inv, attn_msg, start, bh, ah = run_attend(
        place, tokens, pieces, w_attn_in, a_model, b_heads, a_heads, cos, sin, scale,
        w_attn_out, group, head_dim,
    )
    g_mine, attn_msg = tie((g_mine, attn_msg))
    attn_other = other_core(attn_msg)
    g_mine, attn_msg = tie((jnp.stack(g_mine), attn_msg))
    g_mine, attn_other = tie((g_mine, attn_other))
    g_other = other_core(g_mine)
    mid, u_gu, gate, up, down_msg = run_feed(
        place, attn_msg, attn_other, h_own, b_model, mix_rates, a_model, w_gate_up, b_hidden,
        w_down, a_hidden, mlp_scales, 512, slabs,
    )
    g_other, down_msg = tie((g_other, down_msg))
    down_other = other_core(down_msg)
    out_half, mid_res, mid_msg, early = run_feed_back(
        place, down_msg, down_other, mid, cotangent, g_mine, g_other, b_model, mix_rates,
        a_model, u_gu, gate, up, w_gate_up, b_hidden, w_down, a_hidden, mlp_scales, 512, group,
        n_seq,
    )
    mid_other = other_core(mid_msg)

    order = (slab - jnp.arange(slabs, dtype=i32)) % slabs
    index = jnp.stack(index)[:, order]

    def sum_inner(table):
        return pick(table, inner), [
            within_slab(pick(table, (inner + turn) % group), turn) for turn in range(1, group)
        ]

    def add_inner(own, got):
        total = own.astype(f32)
        for piece in got:
            total = total + piece.astype(f32)
        return total.astype(bf16)

    def over_slabs(total):
        return [pick(total, slab)] + [
            to_slab(pick(total, (slab + shift) % slabs), shift) for shift in range(1, slabs)
        ]

    def pack(rows_part, table):
        return jnp.concatenate([rows_part, table.reshape(slabs, -1, half)], axis=1)

    early_size = early.shape[3]
    early_own, early_got = sum_inner(early)
    gq, gk, gv, h_res, gbo, gah = run_attend_back(
        place, mid_res, mid_msg, mid_other, h_own, attn_msg, attn_other, mix_rates, b_model,
        w_attn_out, ah, start, q, k, v, o, inv, qi, ki, cos, sin, scale, slabs, group,
        head_dim,
    )
    early_got, gk, gv = tie((early_got, gk, gv))
    keep, send = run_others(place, gk, gv, w_attn_in, a_model, bh, slabs, group)
    others = (keep + other_core(send).astype(f32)).astype(bf16)
    others, gq, gk, gv = tie((others, gq, gk, gv))
    waves = [[2, 1], [3, 0]] if slabs == 4 else [list(range(slabs))]
    others = others.reshape(group - 1, slabs, chunk, half)
    others_got = []
    for wave in waves:
        if others_got:
            others_got[-1], others = tie((others_got[-1], others))
        others_got.append(
            [
                within_slab(
                    jnp.stack(
                        [pick(others[turn - 1], (slab + shift) % slabs) for shift in wave]
                    ),
                    turn,
                )
                for turn in range(1, group)
            ]
        )
    home = over_slabs(pack(out_half, add_inner(early_own, early_got)))
    late = run_grads(
        place, gq, gk, gv, bh, u, h_full, gbo, gah, slabs, group, n_seq, head_dim
    )
    late_own, late_got = sum_inner(late)
    late_own, gq, home, others_got[0] = tie((late_own, gq, home, others_got[0]))
    home_other = [other_core(piece) for piece in home]
    early_far = []
    for shift in range(1, n_seq):
        at = chunk + (seq_place + shift) % n_seq * early_size
        sent = [lax.dynamic_slice_in_dim(piece, at, early_size, 0) for piece in home]
        early_far.append(to_seq(jnp.stack(sent), shift))
    own_keep, own_send = run_own(
        place, gq, gk, gv, w_attn_in, a_model, bh, h_res, slabs, group
    )
    late_got, early_far, own_send, others_got = tie(
        (late_got, early_far, own_send, others_got)
    )
    own_got = other_core(own_send)
    late_total = add_inner(late_own, late_got)
    own_sum = (own_keep + own_got.astype(f32)).reshape(slabs, chunk, half)
    size = late.shape[3]
    result = [None] * slabs
    for wave, got_wave in zip(waves, others_got):
        for n, shift in enumerate(wave):
            target = (slab + shift) % slabs
            total = pick(own_sum, target)
            for got_part in got_wave:
                total = total + got_part[n].astype(f32)
            result[shift] = jnp.concatenate(
                [total.astype(bf16), pick(late_total, target).reshape(n_seq * size, half)],
                axis=0,
            )
    result, home, home_other, early_far = tie((result, home, home_other, early_far))
    result = result[:1] + [to_slab(result[shift], shift) for shift in range(1, slabs)]
    early_tables = [*home, *home_other, *early_far, *(other_core(t) for t in early_far)]
    layer_out = run_join(place, home, home_other, chunk, bf16)
    cols = model // owners
    each = row_width // owners
    hidden_rows = local_hidden // row_width
    grad_am_gu, grad_bm_down, grad_ad, grad_bd = run_unpack(
        unpack_early_kernel,
        (rank, cols, each, hidden_rows, (3 * rank * hidden_rows + LANES - 1) // LANES),
        (n_seq, slabs, chunk, early_size),
        place, index, early_tables, [],
        [
            (adapters, 2, rank, cols // 2),
            (adapters, rank, cols),
            (adapters, rank, each, hidden_rows),
            (adapters, 2, rank, each, hidden_rows),
        ],
        "unpack_early",
    )
    result, layer_out, grad_am_gu, grad_bm_down = tie(
        (result, layer_out, grad_am_gu, grad_bm_down)
    )
    result_other = [other_core(piece) for piece in result]
    far = []
    for shift in range(1, n_seq):
        at = chunk + (seq_place + shift) % n_seq * size
        sent = [lax.dynamic_slice_in_dim(piece, at, size, 0) for piece in result]
        far.append(to_seq(jnp.stack(sent), shift))
    input_grad = run_join(place, result, result_other, chunk, f32)
    far, input_grad = tie((far, input_grad))
    each = head_dim // owners
    grad_am, grad_bm, grad_ah, grad_bh = run_unpack(
        unpack_late_kernel,
        (rank, cols, local_heads, each),
        (n_seq, slabs, chunk, size),
        place, index, [*result, *result_other, *far, *(other_core(piece) for piece in far)],
        [grad_am_gu, grad_bm_down],
        [
            (adapters, 5, rank, cols // 2),
            (adapters, 2, rank, cols),
            (adapters, local_heads, each, rank),
            (adapters, 3, local_heads, each, rank),
        ],
        "unpack_late",
    )
    return (
        layer_out,
        input_grad,
        grad_am,
        grad_bm,
        jnp.transpose(grad_ah, (0, 3, 1, 2)),
        jnp.transpose(grad_bh, (0, 1, 4, 2, 3)),
        jnp.transpose(grad_ad, (0, 1, 3, 2)),
        jnp.transpose(grad_bd, (0, 1, 2, 4, 3)),
    )


def solution(mesh):
    return jax.shard_map(
        body,
        mesh=mesh,
        in_specs=(
            P("seq", "ctx", None),
            P("seq", "ctx"),
            P("seq"),
            P(None, None, "wt"),
            P("wt", None),
            P(None, None, "wt"),
            P("wt", None),
            P("wt"),
            P(),
            P(None, "wt"),
            P(),
            P(),
            P(None, None, "wt", None),
            P(None, None, None, "wt", None),
            P(None, None, "wt", None),
            P(None, None, None, "wt", None),
            P("seq", "ctx", None),
        ),
        out_specs=(
            P("seq", "ctx", None),
            P("seq", "ctx", None),
            P(None, None, None, ("seq", "ctx", "wt")),
            P(None, None, None, ("seq", "ctx")),
            P(None, None, "wt", ("seq", "ctx")),
            P(None, None, None, "wt", ("seq", "ctx")),
            P(None, None, "wt", ("seq", "ctx")),
            P(None, None, None, "wt", ("seq", "ctx")),
        ),
        check_vma=False,
    )
```

```python
import functools

import jax
import jax.numpy as jnp
from jax import lax
from jax.experimental import pallas as pl
from jax.experimental.pallas import tpu as pltpu
from jax.sharding import PartitionSpec as P

epsilon = 1e-06
f32 = jnp.float32
bf16 = jnp.bfloat16
i32 = jnp.int32
VMEM_LIMIT = 58 * 1024 * 1024
SMALL_LIMIT = 24 * 1024 * 1024
log2e = 1.4426950408889634
LANES = 128


def dot(left, right, contract):
    return lax.dot_general(left, right, (contract, ((), ())), preferred_element_type=f32)


def nn(left, right):
    return dot(left, right, ((1,), (0,)))


def nt(left, right):
    return dot(left, right, ((1,), (1,)))


def tn(left, right):
    return dot(left, right, ((0,), (0,)))


def lane_iota(shape):
    return lax.broadcasted_iota(i32, shape, len(shape) - 1)


def row_iota(shape):
    return lax.broadcasted_iota(i32, shape, 0)


def row_mean(values):
    return jnp.mean(values, axis=-1, keepdims=True)


def inverse_rms(values):
    return lax.rsqrt(row_mean(values * values) + epsilon)


def at_rows(index, size):
    return pl.ds(pl.multiple_of(index * size, size), size)


def by_rows(total, size, step):
    lax.fori_loop(0, total // size, lambda i, c: (step(at_rows(i, size)), c)[1], 0)


def swap_halves(tile, half):
    lower = lane_iota(tile.shape) % (2 * half) < half
    return jnp.where(lower, pltpu.roll(tile, LANES - half, 1), pltpu.roll(tile, half, 1))


def head_sums(tile, head_dim):
    same = row_iota((LANES, LANES)) // head_dim == lane_iota((LANES, LANES)) // head_dim
    ones = jnp.where(same, 1.0, 0.0).astype(bf16)
    return nn(tile.astype(bf16), ones)


def prep_tile(raw, cosine, sine, scale, head_dim):
    mean = head_sums(raw * raw, head_dim) * (1.0 / head_dim)
    inverse = lax.rsqrt(mean + epsilon)
    turned = raw * cosine + swap_halves(raw, head_dim // 2) * sine
    return (turned * inverse * scale).astype(bf16), inverse.astype(bf16)


def prep_tile_back(grad, low, inverse, cosine, sine, scale, head_dim):
    unit = low.astype(f32) / scale
    grad_unit = grad * scale
    mean = head_sums(grad_unit * unit, head_dim) * (1.0 / head_dim)
    grad_turned = inverse.astype(f32) * (grad_unit - unit * mean)
    return (grad_turned * cosine - swap_halves(grad_turned, head_dim // 2) * sine).astype(bf16)


def spread_pair(tile, head_dim):
    lower = lane_iota(tile.shape) < head_dim
    zero = jnp.zeros_like(tile)
    return jnp.concatenate([jnp.where(lower, tile, zero), jnp.where(lower, zero, tile)], axis=0)


def allowed_mask(first, last, key_start, rows, diagonal):
    keys = key_start + row_iota((rows, first.shape[1]))
    mask = keys >= first
    if diagonal:
        mask = mask & (keys <= last)
    return mask


def query_bounds(start_ref, m, place, group, chunk):
    first = start_ref[m : m + 1, :]
    last = (m * group + place) * chunk + lane_iota((1, chunk))
    return jnp.concatenate([first, first], axis=1), jnp.concatenate([last, last], axis=1)


def whole_spec(shape, buffers=1):
    return pl.BlockSpec(
        shape, lambda *a: (0,) * len(shape), pipeline_mode=pl.Buffered(buffers)
    )


def col_spec(size, width=LANES, skip=0):
    return pl.BlockSpec((size, width), lambda p, s: (0, lax.max(p - skip, 0)))


def row_spec(size, width, last):
    return pl.BlockSpec((size, width), lambda p, s: (lax.min(p, last), 0))


def adapter_spec(shape):
    return pl.BlockSpec(
        (1,) + shape, lambda p, s: (s[4],) + (0,) * len(shape), pipeline_mode=pl.Buffered(1)
    )


def params(small=False, limit=None):
    limit = limit or (SMALL_LIMIT if small else VMEM_LIMIT)
    return pltpu.CompilerParams(vmem_limit_bytes=limit)


def cost(flops, moved, transcendentals=0):
    return pl.CostEstimate(
        flops=int(flops), bytes_accessed=int(moved), transcendentals=int(transcendentals)
    )


def attend_kernel(dims, place, *refs):
    slabs, chunk, group, head_dim, rank, half = dims
    count = 4 + (group - 1) * 4
    pieces = refs[:count]
    (
        wq_ref, w_ref, a_ref, b_table, a_table, cos_ref, sin_ref, scale_ref, wout_ref,
        hout_ref, ownout_ref, u_ref, q_ref, k_ref, v_ref, qi_ref, ki_ref, o_ref, inv_ref,
        msg_ref, start_ref, b_ref, ah_ref, first_ref, all_ref, seg_ref, h_ref, own_ref, raw_ref,
    ) = refs[count:]
    inner, slab, core = place[0], place[1], place[2]
    block = group * chunk
    length = slabs * block
    rows = slabs * chunk
    model = 2 * half
    step = pl.program_id(0)

    @pl.when(step == 0)
    def _():
        mine = pl.ds(pl.multiple_of(core * half, half), half)
        other = pl.ds(pl.multiple_of((1 - core) * half, half), half)
        h_ref[at_rows(slab * group + inner, chunk), :] = pieces[0][0]
        seg_ref[...] = jnp.zeros_like(seg_ref)

        def keep_segments(where, piece):
            tail = piece[chunk:, :chunk].astype(f32)
            seg_ref[pl.ds(where, 1), :] = tail[0:1]

        keep_segments(slab * group + inner, pieces[1])

        def place_piece(shift, peer, ours, theirs):
            source = lax.rem(slab - shift + slabs, slabs)
            rows_at = at_rows(source * group + peer, chunk)
            h_ref[rows_at, mine] = ours[:chunk, :]
            h_ref[rows_at, other] = theirs[:chunk, :]
            keep_segments(source * group + peer, ours)

        for shift in range(1, slabs):
            place_piece(shift, inner, pieces[2].at[shift - 1], pieces[3].at[shift - 1])
        for turn in range(1, group):
            peer = lax.rem(inner - turn + group, group)
            near, near_other, rest, rest_other = pieces[4 * turn : 4 * turn + 4]
            place_piece(0, peer, near, near_other)
            for shift in range(1, slabs):
                place_piece(shift, peer, rest.at[shift - 1], rest_other.at[shift - 1])
        for m in range(slabs):
            own_ref[m * chunk : (m + 1) * chunk, :] = h_ref[
                at_rows(m * group + inner, chunk), :
            ]
        columns = seg_ref[...].T
        for m in range(slabs):
            line = seg_ref[pl.ds(m * group + inner, 1), :]
            below = jnp.zeros((chunk, chunk), f32)
            for c in range(slabs * group):
                below = below + jnp.where(columns[:, c : c + 1] < line, 1.0, 0.0)
            count = jnp.sum(below, axis=0, keepdims=True)
            start_ref[m : m + 1, :] = count.astype(i32)
            first_ref[m * chunk : (m + 1) * chunk, :] = (
                jnp.broadcast_to(count, (LANES, chunk)).T.astype(i32)
            )

        for n in range(b_ref.shape[2] // head_dim):
            cols = slice(n * head_dim, (n + 1) * head_dim)
            b_ref[:, :, cols] = b_table[0, :, n]
            ah_ref[:, cols] = a_table[0, n]
        down = a_ref[0, :3].reshape(3 * rank, model)

        def low_rows(sl):
            u_ref[sl, :] = nt(h_ref[sl, :], down).astype(bf16)

        by_rows(length, 512, low_rows)
        for m in range(slabs):
            low = u_ref[at_rows(m * group + inner, chunk), :rank]
            own = slice(m * chunk, (m + 1) * chunk)
            raw_ref[own, :] = nn(low, b_ref[0])
        raw_ref[...] += nn(own_ref[...], wq_ref[0])

    last_block = lax.min(step, slabs - 1)
    hout_ref[...] = h_ref[at_rows(last_block, block), :]
    ownout_ref[...] = own_ref[at_rows(last_block, chunk), :]
    here = pl.ds(pl.multiple_of(step * LANES, LANES), LANES)
    scale = scale_ref[...]
    w_kv = jnp.concatenate([w_ref[0], w_ref[1]], axis=1)
    none = jnp.zeros((rank, LANES), bf16)
    b_kv = jnp.concatenate(
        [
            jnp.zeros((rank, 2 * LANES), bf16),
            jnp.concatenate([b_ref[1, :, here], none], axis=1),
            jnp.concatenate([none, b_ref[2, :, here]], axis=1),
        ],
        axis=0,
    )

    def keys_rows(sl):
        both = nn(h_ref[sl, :], w_kv) + nn(u_ref[sl, :], b_kv)
        k_ref[sl, :], ki_ref[sl, :] = prep_tile(
            both[:, :LANES], cos_ref[sl, :], sin_ref[sl, :], scale, head_dim
        )
        v_ref[sl, :] = both[:, LANES:].astype(bf16)

    by_rows(length, 512, keys_rows)
    for m in range(slabs):
        own = slice(m * chunk, (m + 1) * chunk)
        there = at_rows(m * group + inner, chunk)
        q_ref[own, :], qi_ref[own, :] = prep_tile(
            raw_ref[own, here], cos_ref[there, :], sin_ref[there, :], scale, head_dim
        )
    ones = jnp.ones((block, LANES), bf16)
    left = lane_iota((chunk, LANES)) < head_dim
    for m in range(slabs):
        own = slice(m * chunk, (m + 1) * chunk)
        pair = spread_pair(q_ref[own, :], head_dim)
        first = first_ref[own, :]
        first = jnp.concatenate([first] * (block // LANES), axis=1)
        first = jnp.concatenate([first, first], axis=0)
        gathered = jnp.zeros((2 * chunk, 2 * LANES), f32)
        for b in range(m + 1):
            at = slice(b * block, (b + 1) * block)
            scores = nt(pair, k_ref[at, :])
            keys = b * block + lane_iota(scores.shape)
            mask = keys >= first
            if b == m:
                queries = lax.rem(row_iota(scores.shape), chunk)
                mask = mask & (keys <= queries + (m * group + inner) * chunk)
            weights = jnp.where(mask, jnp.exp2(scores * (0.125 * log2e)), 0.0).astype(bf16)
            gathered = gathered + nn(weights, jnp.concatenate([v_ref[at, :], ones], axis=1))
        inverse = 1.0 / gathered[:, LANES:]
        final = gathered[:, :LANES] * inverse
        final = jnp.where(left, final[:chunk], final[chunk:]).astype(bf16)
        o_ref[own, :] = final
        all_ref[own, here] = final
        inv_ref[0, m : m + 1, :] = inverse.T[0:1, :]

    @pl.when(step == pl.num_programs(0) - 1)
    def _():
        low_o = all_ref[...]
        msg_ref[:, :model] = nn(low_o, wout_ref[...]).astype(bf16)
        msg_ref[:, model:] = pad_to(nt(low_o, ah_ref[...]), LANES).astype(bf16)


def run_attend(place, tokens, pieces, w, a, b, ah, cos, sin, scale, wout, group, head_dim):
    slabs, chunk, model = tokens.shape
    width = w.shape[2]
    rank = a.shape[2]
    half = model // 2
    rows = slabs * chunk
    length = rows * group
    pairs = width // LANES
    in_specs = [pl.BlockSpec((1, chunk, model), lambda p, s: (s[1], 0, 0))]
    in_specs += [whole_spec(piece.shape) for piece in pieces]
    in_specs += [
        whole_spec((1, model, width)),
        pl.BlockSpec(
            (pl.Element(2), pl.Element(model), pl.Element(LANES)),
            lambda p, s: (1, 0, p * LANES),
        ),
        adapter_spec((5, rank, model)),
        adapter_spec(b.shape[1:]),
        adapter_spec(ah.shape[1:]),
        whole_spec((length, LANES)),
        whole_spec((length, LANES)),
        col_spec(1),
        whole_spec((width, model)),
    ]
    def step_rows(size):
        return pl.BlockSpec((size, model), lambda p, s: (lax.min(p, slabs - 1), 0))

    out = [
        ((length, model), bf16, step_rows(group * chunk)),
        ((rows, model), bf16, step_rows(chunk)),
        ((length, 3 * rank), bf16, whole_spec((length, 3 * rank))),
        ((rows, width), bf16, col_spec(rows)),
        ((length, width), bf16, col_spec(length)),
        ((length, width), bf16, col_spec(length)),
        ((rows, width), bf16, col_spec(rows)),
        ((length, width), bf16, col_spec(length)),
        ((rows, width), bf16, col_spec(rows)),
        (
            (pairs, slabs, 2 * chunk),
            f32,
            pl.BlockSpec((1, slabs, 2 * chunk), lambda p, s: (p, 0, 0)),
        ),
        ((rows, model + LANES), bf16, whole_spec((rows, model + LANES))),
        ((slabs, chunk), i32, whole_spec((slabs, chunk))),
        ((3, rank, width), bf16, whole_spec((3, rank, width))),
        ((rank, width), bf16, whole_spec((rank, width))),
    ]
    return pl.pallas_call(
        functools.partial(attend_kernel, (slabs, chunk, group, head_dim, rank, half)),
        grid_spec=pltpu.PrefetchScalarGridSpec(
            num_scalar_prefetch=1,
            grid=(pairs,),
            in_specs=in_specs,
            out_specs=[o[2] for o in out],
            scratch_shapes=[
                pltpu.VMEM((rows, LANES), i32),
                pltpu.VMEM((rows, width), bf16),
                pltpu.VMEM((chunk, chunk), f32),
                pltpu.VMEM((length, model), bf16),
                pltpu.VMEM((rows, model), bf16),
                pltpu.VMEM((rows, width), f32),
            ],
        ),
        out_shape=[jax.ShapeDtypeStruct(o[0], o[1]) for o in out],
        compiler_params=params(),
        cost_estimate=cost(1e8, 1e5),
        name="attend",
    )(place, tokens, *pieces, w, w, a, b, ah, cos, sin, scale, wout)


def join_tiles(ref, *at):
    block = ref[at]
    return jnp.concatenate([block[t] for t in range(block.shape[0])], axis=1)


def feed_kernel(
    dims, place, mine_ref, other_ref, h_ref, bo_ref, rate_ref, a_ref, wgu_ref, bgu_ref, wd_ref,
    ad_ref, scales_ref, mid_ref, u_ref, gate_ref, up_ref, msg_ref, low_ref, acc_ref,
):
    rank, model, slabs = dims
    chunk = h_ref.shape[0]
    step = pl.program_id(0)

    @pl.when(step < slabs)
    def _():
        both = mine_ref[...].astype(f32) + other_ref[...].astype(f32)
        low = both[:, model : model + rank].astype(bf16)
        raw = both[:, :model] + nn(low, bo_ref[0, 0])
        unit = raw * inverse_rms(raw)
        state = h_ref[...].astype(f32)
        mixed = state + rate_ref[0:1, :] * (unit - state)
        mixed = (mixed * inverse_rms(mixed)).astype(bf16)
        mid_ref[...] = mixed
        here = at_rows(step, chunk)
        low_ref[here, :] = mixed
        down = a_ref[0, 3:5].reshape(2 * rank, model)
        u_ref[here, :] = nt(mixed, down).astype(bf16)
        acc_ref[here, :] = jnp.zeros((chunk, model + LANES), f32)

    @pl.when(step >= slabs)
    def _():
        low = low_ref[...]
        u = u_ref[...]
        gate = nn(low, wgu_ref[0]) + nn(u[:, :rank], join_tiles(bgu_ref, 0, 0))
        up = nn(low, wgu_ref[1]) + nn(u[:, rank:], join_tiles(bgu_ref, 0, 1))
        gate_ref[...] = gate.astype(bf16)
        up_ref[...] = up.astype(bf16)
        turned = gate * scales_ref[1:2, :]
        hidden = (up * scales_ref[0:1, :] * (turned / (1.0 + jnp.exp(-turned)))).astype(bf16)
        acc_ref[:, :model] += nn(hidden, wd_ref[...])
        acc_ref[:, model : model + rank] += nt(hidden, join_tiles(ad_ref, 0))

    @pl.when(step == pl.num_programs(0) - 1)
    def _():
        msg_ref[...] = acc_ref[...].astype(bf16)


def hidden_specs(skip, model, rank, block, row_width):
    tiles = block // row_width
    at = lambda f: lax.max(f - skip, 0)
    return [
        pl.BlockSpec((2, model, block), lambda f, s: (0, 0, at(f))),
        pl.BlockSpec((1, 2, tiles, rank, row_width), lambda f, s: (s[4], 0, at(f), 0, 0)),
        pl.BlockSpec((block, model), lambda f, s: (at(f), 0)),
        pl.BlockSpec((1, tiles, rank, row_width), lambda f, s: (s[4], at(f), 0, 0)),
        pl.BlockSpec((2, block), lambda f, s: (0, at(f))),
    ]


def run_feed(place, mine, other, h_own, bm, rates, a, wgu, bgu, wd, ad, scales, block, slabs):
    rows, model = h_own.shape
    chunk = rows // slabs
    hidden = wd.shape[0]
    rank = a.shape[2]
    last = slabs - 1
    out = [
        ((rows, model), bf16, row_spec(chunk, model, last)),
        ((rows, 2 * rank), bf16, whole_spec((rows, 2 * rank))),
        ((rows, hidden), bf16, col_spec(rows, block, slabs)),
        ((rows, hidden), bf16, col_spec(rows, block, slabs)),
        ((rows, model + LANES), bf16, whole_spec((rows, model + LANES))),
    ]
    return pl.pallas_call(
        functools.partial(feed_kernel, (rank, model, slabs)),
        grid_spec=pltpu.PrefetchScalarGridSpec(
            num_scalar_prefetch=1,
            grid=(slabs + hidden // block,),
            in_specs=[
                row_spec(chunk, model + LANES, last),
                row_spec(chunk, model + LANES, last),
                row_spec(chunk, model, last),
                adapter_spec((2, rank, model)),
                whole_spec((2, model)),
                adapter_spec((5, rank, model)),
            ]
            + hidden_specs(slabs, model, rank, block, ad.shape[3]),
            out_specs=[o[2] for o in out],
            scratch_shapes=[
                pltpu.VMEM((rows, model), bf16),
                pltpu.VMEM((rows, model + LANES), f32),
            ],
        ),
        out_shape=[jax.ShapeDtypeStruct(o[0], o[1]) for o in out],
        compiler_params=params(),
        cost_estimate=cost(2.4e10, 3e7),
        name="feed",
    )(place, mine, other, h_own, bm, rates, a, wgu, bgu, wd, ad, scales)


def owner_index(place, group, slabs, n_seq):
    inner, slab, seq = place
    return seq * slabs * group + slab * group + inner


def pad_to(tile, lanes):
    return jnp.pad(tile, ((0, 0), (0, lanes - tile.shape[1])))


def late_rows(rank, units):
    return max(4 * rank, 2 * units)


def folded_rows(rows, groups):
    return (rows + groups * 8 - 1) // (groups * 8) * 8


def fold(tile, groups):
    size = folded_rows(tile.shape[0], groups)
    tile = jnp.pad(tile, ((0, size * groups - tile.shape[0]), (0, 0)))
    return jnp.concatenate([tile[g * size : (g + 1) * size] for g in range(groups)], axis=1)


def unfold(block):
    groups = block.shape[1] // LANES
    return jnp.concatenate(
        [block[:, g * LANES : (g + 1) * LANES] for g in range(groups)], axis=0
    ).astype(f32)


def feed_back_kernel(
    dims, place, mine_ref, other_ref, mid_ref, g_own_ref, g_mine_ref, g_other_ref, bd_ref,
    rate_ref, a_ref, u_ref, gate_ref, up_ref, wgu_ref, bgu_ref, wd_ref, ad_ref, scales_ref,
    out_ref, res_ref, msg_ref, table_ref,
    gd_ref, gdt_ref, ut_ref, udt_ref, gud_ref, gudt_ref, low_ref, acc_ref, gu_ref, hid_ref,
    g_ref, lo_ref,
):
    slabs, chunk, group, n_seq, rank, model, row_width, hidden_rows = dims
    half = model // 2
    step = pl.program_id(0)
    slab, core = place[1], place[2]
    block = gate_ref.shape[1]

    @pl.when(step < slabs)
    def _():
        mine = pl.ds(pl.multiple_of(core * half, half), half)
        other = pl.ds(pl.multiple_of((1 - core) * half, half), half)
        shift = lax.rem(slab - step + slabs, slabs)

        @pl.when(shift == 0)
        def _():
            g_ref[...] = g_own_ref[0]

        @pl.when(shift > 0)
        def _():
            g_ref[:, mine] = g_mine_ref[shift - 1]
            g_ref[:, other] = g_other_ref[shift - 1]

        here = at_rows(step, chunk)
        both = mine_ref[...].astype(f32) + other_ref[...].astype(f32)
        low = both[:, model : model + rank].astype(bf16)
        hid_ref[here, :] = low
        raw = both[:, :model] + nn(low, bd_ref[0, 1])
        raw_inv = inverse_rms(raw)
        unit = raw * raw_inv
        state = mid_ref[...]
        low_ref[here, :] = state
        state = state.astype(f32)
        rate = rate_ref[1:2, :]
        mixed = state + rate * (unit - state)
        mixed_inv = inverse_rms(mixed)
        out = mixed * mixed_inv
        lo_ref[...] = out.astype(bf16)
        grad = g_ref[...].astype(f32)
        grad_mixed = mixed_inv * (grad - out * row_mean(grad * out))
        res_ref[...] = (1.0 - rate) * grad_mixed
        grad_unit = rate * grad_mixed
        gd_ref[here, :] = (raw_inv * (grad_unit - unit * row_mean(grad_unit * unit))).astype(bf16)
        out_ref[0] = lo_ref[:, mine]
        acc_ref[here, :] = jnp.zeros((chunk, model), f32)
        gu_ref[here, :] = jnp.zeros((chunk, 2 * rank), f32)

    @pl.when(step == slabs)
    def _():
        ut_ref[...] = u_ref[...].T
        udt_ref[...] = hid_ref[...].T
        low_gud = nt(gd_ref[...], bd_ref[0, 1]).astype(bf16)
        gud_ref[...] = low_gud
        gudt_ref[...] = low_gud.T

    @pl.when(step >= slabs)
    def _():
        grad_hidden = nt(gd_ref[...], wd_ref[...]) + nn(gud_ref[...], join_tiles(ad_ref, 0))
        gate = gate_ref[...].astype(f32)
        up = up_ref[...].astype(f32)
        up_scale = scales_ref[0:1, :]
        gate_scale = scales_ref[1:2, :]
        turned = gate * gate_scale
        sigmoid = 1.0 / (1.0 + jnp.exp(-turned))
        silu = turned * sigmoid
        up_scaled = up * up_scale
        hidden = (up_scaled * silu).astype(bf16)
        grad_up = (grad_hidden * up_scale * silu).astype(bf16)
        slope = sigmoid * (1.0 + turned * (1.0 - sigmoid)) * gate_scale
        grad_gate = (grad_hidden * up_scaled * slope).astype(bf16)
        acc_ref[...] += nt(grad_gate, wgu_ref[0]) + nt(grad_up, wgu_ref[1])
        gu_ref[:, :rank] += nt(grad_gate, join_tiles(bgu_ref, 0, 0))
        gu_ref[:, rank:] += nt(grad_up, join_tiles(bgu_ref, 0, 1))
        ut = ut_ref[...]
        parts = jnp.concatenate(
            [nn(gudt_ref[...], hidden), nn(ut[:rank], grad_gate), nn(ut[rank:], grad_up)], axis=0
        ).astype(bf16)
        tiles = block // row_width
        for tile in range(tiles):
            gdt_ref[(step - slabs) * tiles + tile] = parts[
                :, tile * row_width : (tile + 1) * row_width
            ]

    @pl.when(step == pl.num_programs(0) - 1)
    def _():
        low_gu = gu_ref[...].astype(bf16)
        down = a_ref[0, 3:5].reshape(2 * rank, model)
        msg_ref[...] = (acc_ref[...] + nn(low_gu, down)).astype(bf16)
        low = low_ref[...]
        model_rows = jnp.concatenate(
            [nn(low_gu.T, low), nn(udt_ref[...], gd_ref[...])], axis=0
        ).astype(bf16).astype(f32)
        ranks = 3 * rank
        units = ranks * hidden_rows
        padded = (units + LANES - 1) // LANES * LANES
        flat = gdt_ref[...].reshape(units, row_width)
        lanes = lane_iota((1, padded))
        target = lanes % hidden_rows * ranks + lanes // hidden_rows
        target = jnp.where(lanes < units, target, -1)
        moved = jnp.where(row_iota((units, padded)) == target, 1.0, 0.0).astype(bf16)
        turned_rows = tn(flat, moved)
        owners = n_seq * slabs * group
        cols = model // owners
        units_each = row_width // owners
        for y in range(group):
            for z in range(slabs):
                for x in range(n_seq):
                    d = owner_index((y, z, x), group, slabs, n_seq)
                    head = pad_to(model_rows[:, d * cols : (d + 1) * cols], LANES)
                    mine = turned_rows[d * units_each : (d + 1) * units_each]
                    tail = [
                        mine[:, t * LANES : (t + 1) * LANES] for t in range(padded // LANES)
                    ]
                    packed = jnp.concatenate([head] + tail, axis=0)
                    table_ref[y, z, x] = fold(packed, half // LANES).astype(bf16)


def run_feed_back(
    place, mine, other, mid, cotangent, g_mine, g_other, bm, rates, a, u, gate, up, wgu, bgu,
    wd, ad, scales, block, group, n_seq,
):
    slabs, chunk, model = cotangent.shape
    rows = slabs * chunk
    half = model // 2
    hidden = wd.shape[0]
    rank = a.shape[2]
    row_width = ad.shape[3]
    last = slabs - 1
    hidden_rows = hidden // row_width
    owners = n_seq * slabs * group
    padded = (3 * rank * hidden_rows + LANES - 1) // LANES * LANES
    table_rows = 3 * rank + row_width // owners * (padded // LANES)
    table = (group, slabs, n_seq, folded_rows(table_rows, half // LANES), half)
    out = [
        (
            (slabs, chunk, half),
            bf16,
            pl.BlockSpec((1, chunk, half), lambda f, s: (lax.min(f, last), 0, 0)),
        ),
        ((rows, model), f32, row_spec(chunk, model, last)),
        ((rows, model), bf16, whole_spec((rows, model))),
        (table, bf16, whole_spec(table)),
    ]
    return pl.pallas_call(
        functools.partial(
            feed_back_kernel,
            (slabs, chunk, group, n_seq, rank, model, row_width, hidden_rows),
        ),
        grid_spec=pltpu.PrefetchScalarGridSpec(
            num_scalar_prefetch=1,
            grid=(slabs + hidden // block,),
            in_specs=[
                row_spec(chunk, model + LANES, last),
                row_spec(chunk, model + LANES, last),
                row_spec(chunk, model, last),
                pl.BlockSpec(
                    (1, chunk, model), lambda f, s: (s[1], 0, 0), pipeline_mode=pl.Buffered(1)
                ),
                whole_spec((slabs - 1, chunk, half)),
                whole_spec((slabs - 1, chunk, half)),
                adapter_spec((2, rank, model)),
                whole_spec((2, model)),
                adapter_spec((5, rank, model)),
                whole_spec((rows, 2 * rank)),
                col_spec(rows, block, slabs),
                col_spec(rows, block, slabs),
            ]
            + hidden_specs(slabs, model, rank, block, row_width),
            out_specs=[o[2] for o in out],
            scratch_shapes=[
                pltpu.VMEM((rows, model), bf16),
                pltpu.VMEM((hidden_rows, 3 * rank, row_width), bf16),
                pltpu.VMEM((2 * rank, rows), bf16),
                pltpu.VMEM((rank, rows), bf16),
                pltpu.VMEM((rows, rank), bf16),
                pltpu.VMEM((rank, rows), bf16),
                pltpu.VMEM((rows, model), bf16),
                pltpu.VMEM((rows, model), f32),
                pltpu.VMEM((rows, 2 * rank), f32),
                pltpu.VMEM((rows, rank), bf16),
                pltpu.VMEM((chunk, model), bf16),
                pltpu.VMEM((chunk, model), bf16),
            ],
        ),
        out_shape=[jax.ShapeDtypeStruct(o[0], o[1]) for o in out],
        compiler_params=params(),
        cost_estimate=cost(3e10, 4e7),
        name="feed_back",
    )(
        place, mine, other, mid, cotangent, g_mine, g_other, bm, rates, a, u, gate, up, wgu,
        bgu, wd, ad, scales,
    )


def attend_back_kernel(
    dims, place, res_ref, gm_ref, go_ref, h_ref, am_ref, ao_ref, rate_ref, bo_ref, wout_ref,
    ah_ref, start_ref, q_ref, k_ref, v_ref, o_ref, inv_ref, qi_ref, ki_ref, cos_ref, sin_ref,
    scale_ref,
    gq_ref, gk_ref, gv_ref, gres_ref, gbo_ref, gah_ref,
    kt_ref, gqt_ref, ga_ref, go_all_ref, guot_ref, uo_ref,
):
    slabs, chunk, group, head_dim, rank, model = dims
    inner = place[0]
    step = pl.program_id(0)

    @pl.when(step < slabs)
    def _():
        here = at_rows(step, chunk)
        grad = res_ref[...] + gm_ref[...].astype(f32) + go_ref[...].astype(f32)
        both = am_ref[...].astype(f32) + ao_ref[...].astype(f32)
        low = both[:, model : model + rank].astype(bf16)
        uo_ref[here, :] = low
        raw = both[:, :model] + nn(low, bo_ref[0, 0])
        raw_inv = inverse_rms(raw)
        unit = raw * raw_inv
        state = h_ref[...].astype(f32)
        rate = rate_ref[0:1, :]
        mixed = state + rate * (unit - state)
        mixed_inv = inverse_rms(mixed)
        out = mixed * mixed_inv
        grad_mixed = mixed_inv * (grad - out * row_mean(grad * out))
        gres_ref[...] = (1.0 - rate) * grad_mixed
        grad_unit = rate * grad_mixed
        ga_ref[here, :] = (raw_inv * (grad_unit - unit * row_mean(grad_unit * unit))).astype(bf16)

    @pl.when(step == slabs)
    def _():
        gbo_ref[...] = nn(uo_ref[...].T, ga_ref[...])
        low_g = nt(ga_ref[...], bo_ref[0, 0]).astype(bf16)
        guot_ref[...] = low_g.T
        go_all_ref[...] = (nt(ga_ref[...], wout_ref[...]) + nn(low_g, ah_ref[...])).astype(bf16)

    @pl.when(step >= slabs)
    def _():
        attend_back_pair(
            dims, inner, step - slabs, start_ref, q_ref, k_ref, v_ref, o_ref, inv_ref,
            qi_ref, ki_ref, cos_ref, sin_ref, scale_ref, gq_ref, gk_ref, gv_ref, gah_ref,
            kt_ref, gqt_ref, go_all_ref, guot_ref,
        )


def attend_back_pair(
    dims, inner, turn, start_ref, q_ref, k_ref, v_ref, o_ref, inv_ref, qi_ref, ki_ref,
    cos_ref, sin_ref, scale_ref, gq_ref, gk_ref, gv_ref, gah_ref, kt_ref, gqt_ref,
    go_all_ref, guot_ref,
):
    slabs, chunk, group, head_dim, rank, model = dims
    block = group * chunk
    kt_ref[...] = k_ref[...].T
    scale = scale_ref[...]
    grad_o = go_all_ref[:, pl.ds(pl.multiple_of(turn * LANES, LANES), LANES)]
    gah_ref[...] = nn(guot_ref[...], o_ref[...])
    pairs_q, pairs_g, deltas, bounds = [], [], [], []
    for m in range(slabs):
        own = slice(m * chunk, (m + 1) * chunk)
        pairs_q.append(spread_pair(q_ref[own, :], head_dim))
        grad = grad_o[own]
        pairs_g.append(spread_pair(grad, head_dim))
        products = (grad.astype(f32) * o_ref[own, :].astype(f32)).T
        deltas.append(
            jnp.concatenate(
                [
                    jnp.sum(products[:head_dim], axis=0, keepdims=True),
                    jnp.sum(products[head_dim:], axis=0, keepdims=True),
                ],
                axis=1,
            )
        )
        bounds.append(query_bounds(start_ref, m, inner, group, chunk))
    for b in range(slabs):
        at = slice(b * block, (b + 1) * block)
        grad_key = jnp.zeros((block, LANES), f32)
        grad_value = jnp.zeros((block, LANES), f32)
        for m in range(b, slabs):
            first, last = bounds[m]
            scores = nt(k_ref[at, :], pairs_q[m])
            mask = allowed_mask(first, last, b * block, block, b == m)
            weights = jnp.exp2(scores * (0.125 * log2e)) * inv_ref[0, m : m + 1, :]
            weights = jnp.where(mask, weights, 0.0)
            grad_value = grad_value + nn(weights.astype(bf16), pairs_g[m])
            grad_weights = nt(v_ref[at, :], pairs_g[m])
            grad_scores = (weights * (grad_weights - deltas[m])).astype(bf16)
            grad_key = grad_key + nn(grad_scores, pairs_q[m])
            part = nn(kt_ref[:, at], grad_scores)
            if b == 0:
                gqt_ref[m] = part
            else:
                gqt_ref[m] += part
        gv_ref[at, :] = grad_value.astype(bf16)
        gk_ref[at, :] = prep_tile_back(
            grad_key * 0.125, k_ref[at, :], ki_ref[at, :], cos_ref[at, :], sin_ref[at, :],
            scale, head_dim,
        )
    upper = row_iota((LANES, chunk)) < head_dim
    for m in range(slabs):
        own = slice(m * chunk, (m + 1) * chunk)
        both = gqt_ref[m]
        grad = jnp.where(upper, both[:, :chunk], both[:, chunk:]).T * 0.125
        there = at_rows(m * group + inner, chunk)
        gq_ref[own, :] = prep_tile_back(
            grad, q_ref[own, :], qi_ref[own, :], cos_ref[there, :], sin_ref[there, :],
            scale, head_dim,
        )


def run_attend_back(
    place, res, gm, go, h_own, am, ao, rates, bm, wout, ah, start, q, k, v, o, inv, qi, ki, cos, sin, scale, slabs, group, head_dim,
):
    rows, model = h_own.shape
    chunk = rows // slabs
    width = q.shape[1]
    length = k.shape[0]
    rank = bm.shape[2]
    pairs = width // LANES
    last = slabs - 1
    wide = row_spec(chunk, model + LANES, last)
    narrow = row_spec(chunk, model, last)
    cols = lambda size: col_spec(size, LANES, slabs)
    out = [
        ((rows, width), bf16, cols(rows)),
        ((length, width), bf16, cols(length)),
        ((length, width), bf16, cols(length)),
        ((rows, model), f32, narrow),
        ((rank, model), f32, whole_spec((rank, model))),
        ((rank, width), f32, cols(rank)),
    ]
    return pl.pallas_call(
        functools.partial(attend_back_kernel, (slabs, chunk, group, head_dim, rank, model)),
        grid_spec=pltpu.PrefetchScalarGridSpec(
            num_scalar_prefetch=1,
            grid=(slabs + pairs,),
            in_specs=[
                narrow,
                narrow,
                narrow,
                narrow,
                wide,
                wide,
                whole_spec((2, model)),
                adapter_spec((2, rank, model)),
                whole_spec((width, model)),
                whole_spec((rank, width)),
                whole_spec((slabs, chunk)),
                cols(rows),
                cols(length),
                cols(length),
                cols(rows),
                pl.BlockSpec(
                    (1, slabs, 2 * chunk), lambda p, s: (lax.max(p - slabs, 0), 0, 0)
                ),
                cols(rows),
                cols(length),
                whole_spec((length, LANES)),
                whole_spec((length, LANES)),
                cols(1),
            ],
            out_specs=[o_[2] for o_ in out],
            scratch_shapes=[
                pltpu.VMEM((LANES, length), bf16),
                pltpu.VMEM((slabs, LANES, 2 * chunk), f32),
                pltpu.VMEM((rows, model), bf16),
                pltpu.VMEM((rows, width), bf16),
                pltpu.VMEM((rank, rows), bf16),
                pltpu.VMEM((rows, rank), bf16),
            ],
        ),
        out_shape=[jax.ShapeDtypeStruct(o_[0], o_[1]) for o_ in out],
        compiler_params=params(),
        cost_estimate=cost(3e10, 4e7),
        name="attend_back",
    )(
        place, res, gm, go, h_own, am, ao, rates, bm, wout, ah, start, q, k, v, o, inv, qi, ki,
        cos, sin, scale,
    )


def apart(blocks):
    none = jnp.zeros_like(blocks[0])
    return jnp.concatenate(
        [
            jnp.concatenate([b if n == m else none for n in range(len(blocks))], axis=1)
            for m, b in enumerate(blocks)
        ],
        axis=0,
    )


def others_kernel(
    place, gk_ref, gv_ref, wk_ref, wv_ref, a_ref, b_ref, keep_ref, send_ref, low_ref
):
    rows, width = keep_ref.shape[1], gk_ref.shape[-1]
    half = keep_ref.shape[2]
    rank = b_ref.shape[1]
    both = jnp.concatenate(
        [gk_ref[...].reshape(rows, width), gv_ref[...].reshape(rows, width)], axis=1
    )
    turn = pl.program_id(1)

    @pl.when(turn == 0)
    def _():
        low_ref[...] = nt(both, apart([b_ref[1], b_ref[2]])).astype(bf16)

    weights = jnp.concatenate([wk_ref[0], wv_ref[0]], axis=1)
    part = nt(both, weights) + nn(low_ref[...], a_ref[0, 1:3].reshape(2 * rank, half))

    @pl.when(turn == 0)
    def _():
        send_ref[0] = part.astype(bf16)

    @pl.when(turn == 1)
    def _():
        keep_ref[0] = part


def half_weight(half, width, member):
    return pl.BlockSpec(
        (1, half, width), lambda *a: (member, lax.rem(a[-1][2] + 1 + a[-2], 2), 0)
    )


def half_factors(rank, half):
    return pl.BlockSpec(
        (1, 5, rank, half), lambda *a: (a[-1][4], 0, 0, lax.rem(a[-1][2] + 1 + a[-2], 2))
    )


def run_others(place, gk, gv, w, a, b, slabs, group):
    length, width = gk.shape
    chunk = length // (slabs * group)
    rows = slabs * chunk
    half = w.shape[1] // 2
    rank = b.shape[1]
    shaped = (slabs, group, chunk, width)
    peer = pl.BlockSpec(
        (slabs, 1, chunk, width), lambda g, t, s: (0, lax.rem(s[0] + 1 + g, group), 0, 0)
    )
    return pl.pallas_call(
        others_kernel,
        grid_spec=pltpu.PrefetchScalarGridSpec(
            num_scalar_prefetch=1,
            grid=(group - 1, 2),
            in_specs=[
                peer,
                peer,
                half_weight(half, width, 1),
                half_weight(half, width, 2),
                half_factors(rank, half),
                whole_spec((3, rank, width)),
            ],
            out_specs=[pl.BlockSpec((1, rows, half), lambda g, t, s: (g, 0, 0))] * 2,
            scratch_shapes=[pltpu.VMEM((rows, 2 * rank), bf16)],
        ),
        out_shape=[
            jax.ShapeDtypeStruct((group - 1, rows, half), f32),
            jax.ShapeDtypeStruct((group - 1, rows, half), bf16),
        ],
        compiler_params=params(),
        cost_estimate=cost(7e9, 1e7),
        name="others",
    )(place, gk.reshape(shaped), gv.reshape(shaped), w, w, a, b)


def own_kernel(
    place, gq_ref, gk_ref, gv_ref, wq_ref, wk_ref, wv_ref, a_ref, b_ref, res_ref, keep_ref,
    send_ref, low_ref,
):
    rows, width = gq_ref.shape
    half = keep_ref.shape[1]
    rank = b_ref.shape[1]
    grads = jnp.concatenate(
        [gq_ref[...], gk_ref[...].reshape(rows, width), gv_ref[...].reshape(rows, width)], axis=1
    )
    turn = pl.program_id(0)

    @pl.when(turn == 0)
    def _():
        low_ref[...] = nt(grads, apart([b_ref[0], b_ref[1], b_ref[2]])).astype(bf16)

    weights = jnp.concatenate([wq_ref[0], wk_ref[0], wv_ref[0]], axis=1)
    part = nt(grads, weights) + nn(low_ref[...], a_ref[0, 0:3].reshape(3 * rank, half))

    @pl.when(turn == 0)
    def _():
        send_ref[...] = part.astype(bf16)

    @pl.when(turn == 1)
    def _():
        keep_ref[...] = part + res_ref[...]


def run_own(place, gq, gk, gv, w, a, b, res, slabs, group):
    length, width = gk.shape
    rows, model = res.shape
    chunk = rows // slabs
    half = model // 2
    rank = b.shape[1]
    shaped = (slabs, group, chunk, width)
    peer = pl.BlockSpec((slabs, 1, chunk, width), lambda t, s: (0, s[0], 0, 0))
    out = [((rows, half), f32), ((rows, half), bf16)]
    return pl.pallas_call(
        own_kernel,
        grid_spec=pltpu.PrefetchScalarGridSpec(
            num_scalar_prefetch=1,
            grid=(2,),
            in_specs=[
                whole_spec((rows, width)),
                peer,
                peer,
                half_weight(half, width, 0),
                half_weight(half, width, 1),
                half_weight(half, width, 2),
                half_factors(rank, half),
                whole_spec((3, rank, width)),
                pl.BlockSpec((rows, half), lambda t, s: (0, s[2])),
            ],
            out_specs=[whole_spec(o[0]) for o in out],
            scratch_shapes=[pltpu.VMEM((rows, 3 * rank), bf16)],
        ),
        out_shape=[jax.ShapeDtypeStruct(o[0], o[1]) for o in out],
        compiler_params=params(True),
        cost_estimate=cost(7e9, 1e7),
        name="own",
    )(place, gq, gk.reshape(shaped), gv.reshape(shaped), w, w, w, a, b, res)


def grads_kernel(
    dims, place, gq_ref, gk_ref, gv_ref, b_ref, u_ref, h_ref, gbo_ref, gah_ref, table_ref,
    uq_ref, low_ref,
):
    slabs, chunk, group, n_seq, rank, model, head_dim = dims
    inner = place[0]
    width = gq_ref.shape[1]
    heads = width // head_dim
    gq = gq_ref[...]
    both = jnp.concatenate([gk_ref[...], gv_ref[...]], axis=1)
    low_q = nt(gq, b_ref[0]).astype(bf16)
    low_ref[:, : 2 * rank] = nt(both, apart([b_ref[1], b_ref[2]])).astype(bf16)
    low_ref[:, 2 * rank :] = jnp.zeros((low_ref.shape[0], rank), bf16)
    for m in range(slabs):
        there = at_rows(m * group + inner, chunk)
        uq_ref[m * chunk : (m + 1) * chunk, :] = u_ref[there, :]
        low_ref[there, 2 * rank :] = low_q[m * chunk : (m + 1) * chunk]
    products = nn(low_ref[...].T, h_ref[...])
    model_rows = jnp.concatenate(
        [products[2 * rank :], products[: 2 * rank], gbo_ref[...]], axis=0
    ).astype(bf16).astype(f32)
    uqt = uq_ref[...].T
    pair = nn(u_ref[...].T[rank:], both)
    head_rows = jnp.concatenate(
        [gah_ref[...], nn(uqt[:rank], gq), pair[:rank, :width], pair[rank:, width:]], axis=0
    ).astype(bf16)
    owners = n_seq * slabs * group
    cols = model // owners
    each = head_dim // owners
    units = heads * each
    spots = lax.broadcasted_iota(i32, (width, 1), 0)
    owner = spots // units
    inside = spots % units
    source = inside // each * head_dim + owner * each + inside % each
    moved = jnp.where(lane_iota((width, width)) == source, 1.0, 0.0).astype(bf16)
    turned = nt(moved, head_rows)
    for y in range(group):
        for z in range(slabs):
            for x in range(n_seq):
                d = owner_index((y, z, x), group, slabs, n_seq)
                left = model_rows[:, d * cols : (d + 1) * cols]
                heads_part = turned[d * units : (d + 1) * units]
                right = jnp.concatenate(
                    [heads_part[:, rank:], pad_to(heads_part[:, :rank], 3 * rank)], axis=0
                )
                tall = late_rows(rank, units)
                packed = jnp.concatenate(
                    [
                        jnp.pad(left, ((0, tall - left.shape[0]), (0, 0))),
                        jnp.pad(right, ((0, tall - right.shape[0]), (0, 0))),
                    ],
                    axis=1,
                )
                packed = pad_to(packed, LANES)
                table_ref[y, z, x] = fold(packed, table_ref.shape[4] // LANES).astype(bf16)


def run_grads(place, gq, gk, gv, b, u, h, gbo, gah, slabs, group, n_seq, head_dim):
    length, width = gk.shape
    rows, model = gq.shape[0], h.shape[1]
    chunk = rows // slabs
    rank = b.shape[1]
    heads = width // head_dim
    owners = n_seq * slabs * group
    units = heads * (head_dim // owners)
    half = model // 2
    shape = (group, slabs, n_seq, folded_rows(late_rows(rank, units), half // LANES), half)
    operands = (gq, gk, gv, b, u, h, gbo, gah)
    return pl.pallas_call(
        functools.partial(grads_kernel, (slabs, chunk, group, n_seq, rank, model, head_dim)),
        grid_spec=pltpu.PrefetchScalarGridSpec(
            num_scalar_prefetch=1,
            grid=(1,),
            in_specs=[whole_spec(operand.shape) for operand in operands],
            out_specs=whole_spec(shape),
            scratch_shapes=[
                pltpu.VMEM((rows, 3 * rank), bf16),
                pltpu.VMEM((length, 3 * rank), bf16),
            ],
        ),
        out_shape=jax.ShapeDtypeStruct(shape, bf16),
        compiler_params=params(True),
        cost_estimate=cost(1e10, 1e7),
        name="grads",
    )(place, *operands)


def join_kernel(slabs, place, *refs):
    out_ref = refs[-1]
    chunk, half = out_ref.shape[1], refs[0].shape[-1]
    core, slab = place[2], place[1]
    for shift in range(slabs):
        source = lax.rem(slab - shift + slabs, slabs)
        for which, ref in ((core, refs[shift]), (1 - core, refs[slabs + shift])):
            out_ref[source, :, pl.ds(pl.multiple_of(which * half, half), half)] = ref[
                :chunk, :
            ].astype(out_ref.dtype)


def run_join(place, mine, other, chunk, dtype):
    slabs = len(mine)
    half = mine[0].shape[1]
    return pl.pallas_call(
        functools.partial(join_kernel, slabs),
        grid_spec=pltpu.PrefetchScalarGridSpec(
            num_scalar_prefetch=1,
            grid=(1,),
            in_specs=[whole_spec(piece.shape) for piece in (*mine, *other)],
            out_specs=whole_spec((slabs, chunk, 2 * half)),
        ),
        out_shape=jax.ShapeDtypeStruct((slabs, chunk, 2 * half), dtype),
        compiler_params=params(True),
        cost_estimate=cost(1e6, 8e6),
        name="join",
    )(place, *mine, *other)


def for_tables(where, place, index, refs, put):
    n_seq, slabs, chunk, size = where
    home, home_other = refs[:slabs], refs[slabs : 2 * slabs]
    far, far_other = refs[2 * slabs : 2 * slabs + n_seq - 1], refs[2 * slabs + n_seq - 1 :]
    for r in range(slabs):
        at = pl.ds(pl.multiple_of(chunk + place[3] * size, 8), size)
        put(index[0, r], unfold(home[r][at, :]), unfold(home_other[r][at, :]))
    for s in range(1, n_seq):

        def one(r, carry, s=s):
            put(index[s, r], unfold(far[s - 1][r]), unfold(far_other[s - 1][r]))
            return carry

        lax.fori_loop(0, slabs, one, 0)


def unpack_early_kernel(dims, where, place, index, *refs):
    rank, cols, each, hidden_rows, tiles = dims
    am_ref, bm_ref, ad_ref, bd_ref = refs[-4:]
    core = place[2]

    def put(adapter, block, other):
        both = block[: 2 * rank] + other[: 2 * rank]
        am = jnp.where(core == 0, both[:, : cols // 2], both[:, cols // 2 : cols])
        am_ref[adapter] = am.reshape(2, rank, cols // 2)
        bm_ref[adapter] = block[2 * rank : 3 * rank, :cols]
        base = 3 * rank
        wide = jnp.concatenate(
            [block[base + t * each : base + (t + 1) * each] for t in range(tiles)], axis=1
        )
        for k in range(rank):
            ad_ref[adapter, k] = wide[:, k * hidden_rows : (k + 1) * hidden_rows]
        for j in range(2):
            for k in range(rank):
                at = ((j + 1) * rank + k) * hidden_rows
                bd_ref[adapter, j, k] = wide[:, at : at + hidden_rows]

    for_tables(where, place, index, refs[:-4], put)


def unpack_late_kernel(dims, where, place, index, *refs):
    rank, cols, heads, each = dims
    am_gu_ref, bm_down_ref, am_ref, bm_ref, ah_ref, bh_ref = refs[-6:]
    core = place[2]

    def put(adapter, block, other):
        both = block[: 3 * rank] + other[: 3 * rank]
        am = jnp.where(core == 0, both[:, : cols // 2], both[:, cols // 2 : cols])
        am_ref[adapter, 0:3] = am.reshape(3, rank, cols // 2)
        am_ref[adapter, 3:5] = am_gu_ref[adapter]
        bm_ref[adapter, 0] = block[3 * rank : 4 * rank, :cols]
        bm_ref[adapter, 1] = bm_down_ref[adapter]
        units = heads * each
        for n in range(heads):
            at = n * each
            ah_ref[adapter, n] = block[units + at : units + at + each, cols : cols + rank]
            for j in range(3):
                lanes = slice(cols + j * rank, cols + (j + 1) * rank)
                bh_ref[adapter, j, n] = block[at : at + each, lanes]

    for_tables(where, place, index, refs[:-6], put)


def run_unpack(kernel, dims, where, place, index, tables, extra, shapes, name):
    operands = [*tables, *extra]
    return pl.pallas_call(
        functools.partial(kernel, dims, where),
        grid_spec=pltpu.PrefetchScalarGridSpec(
            num_scalar_prefetch=2,
            grid=(1,),
            in_specs=[whole_spec(operand.shape) for operand in operands],
            out_specs=[whole_spec(shape) for shape in shapes],
        ),
        out_shape=[jax.ShapeDtypeStruct(shape, f32) for shape in shapes],
        compiler_params=params(True),
        cost_estimate=cost(1e6, 8e6),
        name=name,
    )(place, index, *operands)


def pick(array, index):
    return lax.dynamic_index_in_dim(array, index, 0, keepdims=False)


def body(
    tokens, segments, adapter_index, w_attn_in, w_attn_out, w_gate_up, w_down, qk_scale,
    mix_rates, mlp_scales, a_model, b_model, a_heads, b_heads, a_hidden, b_hidden, cotangent,
):
    slabs, chunk, model = tokens.shape
    n_seq = lax.axis_size("seq")
    n_ctx = lax.axis_size("ctx")
    group = n_ctx // slabs
    local_width = w_attn_out.shape[0]
    head_dim = a_heads.shape[-1]
    row_width = a_hidden.shape[-1]
    local_hidden = w_down.shape[0]
    local_heads = local_width // head_dim
    rank = a_model.shape[2]
    adapters = a_model.shape[0]
    half = model // 2
    ctx_place = lax.axis_index("ctx")
    slab = ctx_place // group
    inner = ctx_place % group
    core = lax.axis_index("wt")
    seq_place = lax.axis_index("seq")
    owners = n_seq * n_ctx
    rows = slabs * chunk
    length = rows * group
    place = jnp.stack([inner, slab, core, seq_place, pick(adapter_index, slab)]).astype(i32)
    a_heads = jnp.transpose(a_heads, (0, 2, 1, 3))
    b_heads = jnp.transpose(b_heads, (0, 1, 3, 2, 4))
    a_hidden = jnp.transpose(a_hidden, (0, 2, 1, 3))
    b_hidden = jnp.transpose(b_hidden, (0, 1, 3, 2, 4))

    def to_slab(array, shift):
        pairs = [(c, (c + shift * group) % n_ctx) for c in range(n_ctx)]
        return lax.ppermute(array, "ctx", pairs)

    def within_slab(array, shift):
        pairs = [(c, c - c % group + (c % group + shift) % group) for c in range(n_ctx)]
        return lax.ppermute(array, "ctx", pairs)

    def to_seq(array, shift):
        return lax.ppermute(array, "seq", [(c, (c + shift) % n_seq) for c in range(n_seq)])

    def other_core(array):
        return lax.ppermute(array, "wt", [(0, 1), (1, 0)])

    def half_piece(array, index, which):
        return lax.dynamic_slice(array, (index, 0, which * half), (1, chunk, half))[0]

    def token_piece(index):
        seg = jnp.pad(pick(segments, index).astype(bf16), (0, half - chunk))
        return jnp.concatenate(
            [half_piece(tokens, index, core), jnp.broadcast_to(seg, (8, half))], axis=0
        )

    tie = lax.optimization_barrier

    spot = (jnp.arange(LANES, dtype=i32) % (head_dim // 2)).astype(f32)
    frequency = 10000.0 ** (-spot / (head_dim // 2))
    turn = jnp.arange(length, dtype=i32).astype(f32)[:, None] * frequency[None, :]
    cos = jnp.cos(turn)
    lower = jnp.arange(LANES) % head_dim < head_dim // 2
    sin = jnp.sin(turn) * jnp.where(lower, -1.0, 1.0)[None, :]
    scale = qk_scale[None, :]

    own_piece = token_piece(slab)
    got = [own_piece] + [
        to_slab(token_piece((slab + shift) % slabs), shift) for shift in range(1, slabs)
    ]
    index = [adapter_index]
    for shift in range(1, n_seq):
        index.append(to_seq(adapter_index, shift))
    got, cos, sin, place, index = tie((got, cos, sin, place, index))
    near = [within_slab(own_piece, turn) for turn in range(1, group)]
    g_send = [half_piece(cotangent, (slab + shift) % slabs, core) for shift in range(1, slabs)]
    rest, near, g_send = tie((jnp.stack(got[1:]), near, g_send))
    rest_other = other_core(rest)
    peers = [within_slab(rest, turn) for turn in range(1, group)]
    g_mine = [to_slab(g_send[shift - 1], shift) for shift in range(1, slabs)]
    peers, g_mine = tie((peers, g_mine))
    pieces = [own_piece, rest, rest_other]
    for turn in range(1, group):
        pieces += [
            near[turn - 1], other_core(near[turn - 1]),
            peers[turn - 1], other_core(peers[turn - 1]),
        ]
    h_full, h_own, u, q, k, v, qi, ki, o, inv, attn_msg, start, bh, ah = run_attend(
        place, tokens, pieces, w_attn_in, a_model, b_heads, a_heads, cos, sin, scale,
        w_attn_out, group, head_dim,
    )
    g_mine, attn_msg = tie((g_mine, attn_msg))
    attn_other = other_core(attn_msg)
    g_mine, attn_msg = tie((jnp.stack(g_mine), attn_msg))
    g_mine, attn_other = tie((g_mine, attn_other))
    g_other = other_core(g_mine)
    mid, u_gu, gate, up, down_msg = run_feed(
        place, attn_msg, attn_other, h_own, b_model, mix_rates, a_model, w_gate_up, b_hidden,
        w_down, a_hidden, mlp_scales, 512, slabs,
    )
    g_other, down_msg = tie((g_other, down_msg))
    down_other = other_core(down_msg)
    out_half, mid_res, mid_msg, early = run_feed_back(
        place, down_msg, down_other, mid, cotangent, g_mine, g_other, b_model, mix_rates,
        a_model, u_gu, gate, up, w_gate_up, b_hidden, w_down, a_hidden, mlp_scales, 512, group,
        n_seq,
    )
    mid_other = other_core(mid_msg)

    order = (slab - jnp.arange(slabs, dtype=i32)) % slabs
    index = jnp.stack(index)[:, order]

    def sum_inner(table):
        return pick(table, inner), [
            within_slab(pick(table, (inner + turn) % group), turn) for turn in range(1, group)
        ]

    def add_inner(own, got):
        total = own.astype(f32)
        for piece in got:
            total = total + piece.astype(f32)
        return total.astype(bf16)

    def over_slabs(total):
        return [pick(total, slab)] + [
            to_slab(pick(total, (slab + shift) % slabs), shift) for shift in range(1, slabs)
        ]

    def pack(rows_part, table):
        return jnp.concatenate([rows_part, table.reshape(slabs, -1, half)], axis=1)

    early_size = early.shape[3]
    early_own, early_got = sum_inner(early)
    gq, gk, gv, h_res, gbo, gah = run_attend_back(
        place, mid_res, mid_msg, mid_other, h_own, attn_msg, attn_other, mix_rates, b_model,
        w_attn_out, ah, start, q, k, v, o, inv, qi, ki, cos, sin, scale, slabs, group,
        head_dim,
    )
    early_got, gk, gv = tie((early_got, gk, gv))
    keep, send = run_others(place, gk, gv, w_attn_in, a_model, bh, slabs, group)
    others = (keep + other_core(send).astype(f32)).astype(bf16)
    others, gq, gk, gv = tie((others, gq, gk, gv))
    waves = [[2, 1], [3, 0]] if slabs == 4 else [list(range(slabs))]
    others = others.reshape(group - 1, slabs, chunk, half)
    others_got = []
    for wave in waves:
        if others_got:
            others_got[-1], others = tie((others_got[-1], others))
        others_got.append(
            [
                within_slab(
                    jnp.stack(
                        [pick(others[turn - 1], (slab + shift) % slabs) for shift in wave]
                    ),
                    turn,
                )
                for turn in range(1, group)
            ]
        )
    home = over_slabs(pack(out_half, add_inner(early_own, early_got)))
    late = run_grads(
        place, gq, gk, gv, bh, u, h_full, gbo, gah, slabs, group, n_seq, head_dim
    )
    late_own, late_got = sum_inner(late)
    late_own, gq, home, others_got[0] = tie((late_own, gq, home, others_got[0]))
    home_other = [other_core(piece) for piece in home]
    early_far = []
    for shift in range(1, n_seq):
        at = chunk + (seq_place + shift) % n_seq * early_size
        sent = [lax.dynamic_slice_in_dim(piece, at, early_size, 0) for piece in home]
        early_far.append(to_seq(jnp.stack(sent), shift))
    own_keep, own_send = run_own(
        place, gq, gk, gv, w_attn_in, a_model, bh, h_res, slabs, group
    )
    late_got, early_far, own_send, others_got = tie(
        (late_got, early_far, own_send, others_got)
    )
    own_got = other_core(own_send)
    late_total = add_inner(late_own, late_got)
    own_sum = (own_keep + own_got.astype(f32)).reshape(slabs, chunk, half)
    size = late.shape[3]
    result = [None] * slabs
    for wave, got_wave in zip(waves, others_got):
        for n, shift in enumerate(wave):
            target = (slab + shift) % slabs
            total = pick(own_sum, target)
            for got_part in got_wave:
                total = total + got_part[n].astype(f32)
            result[shift] = jnp.concatenate(
                [total.astype(bf16), pick(late_total, target).reshape(n_seq * size, half)],
                axis=0,
            )
    result, home, home_other, early_far = tie((result, home, home_other, early_far))
    result = result[:1] + [to_slab(result[shift], shift) for shift in range(1, slabs)]
    early_tables = [*home, *home_other, *early_far, *(other_core(t) for t in early_far)]
    layer_out = run_join(place, home, home_other, chunk, bf16)
    cols = model // owners
    each = row_width // owners
    hidden_rows = local_hidden // row_width
    grad_am_gu, grad_bm_down, grad_ad, grad_bd = run_unpack(
        unpack_early_kernel,
        (rank, cols, each, hidden_rows, (3 * rank * hidden_rows + LANES - 1) // LANES),
        (n_seq, slabs, chunk, early_size),
        place, index, early_tables, [],
        [
            (adapters, 2, rank, cols // 2),
            (adapters, rank, cols),
            (adapters, rank, each, hidden_rows),
            (adapters, 2, rank, each, hidden_rows),
        ],
        "unpack_early",
    )
    result, layer_out, grad_am_gu, grad_bm_down = tie(
        (result, layer_out, grad_am_gu, grad_bm_down)
    )
    result_other = [other_core(piece) for piece in result]
    far = []
    for shift in range(1, n_seq):
        at = chunk + (seq_place + shift) % n_seq * size
        sent = [lax.dynamic_slice_in_dim(piece, at, size, 0) for piece in result]
        far.append(to_seq(jnp.stack(sent), shift))
    input_grad = run_join(place, result, result_other, chunk, f32)
    far, input_grad = tie((far, input_grad))
    each = head_dim // owners
    grad_am, grad_bm, grad_ah, grad_bh = run_unpack(
        unpack_late_kernel,
        (rank, cols, local_heads, each),
        (n_seq, slabs, chunk, size),
        place, index, [*result, *result_other, *far, *(other_core(piece) for piece in far)],
        [grad_am_gu, grad_bm_down],
        [
            (adapters, 5, rank, cols // 2),
            (adapters, 2, rank, cols),
            (adapters, local_heads, each, rank),
            (adapters, 3, local_heads, each, rank),
        ],
        "unpack_late",
    )
    return (
        layer_out,
        input_grad,
        grad_am,
        grad_bm,
        jnp.transpose(grad_ah, (0, 3, 1, 2)),
        jnp.transpose(grad_bh, (0, 1, 4, 2, 3)),
        jnp.transpose(grad_ad, (0, 1, 3, 2)),
        jnp.transpose(grad_bd, (0, 1, 2, 4, 3)),
    )


def solution(mesh):
    return jax.shard_map(
        body,
        mesh=mesh,
        in_specs=(
            P("seq", "ctx", None),
            P("seq", "ctx"),
            P("seq"),
            P(None, None, "wt"),
            P("wt", None),
            P(None, None, "wt"),
            P("wt", None),
            P("wt"),
            P(),
            P(None, "wt"),
            P(),
            P(),
            P(None, None, "wt", None),
            P(None, None, None, "wt", None),
            P(None, None, "wt", None),
            P(None, None, None, "wt", None),
            P("seq", "ctx", None),
        ),
        out_specs=(
            P("seq", "ctx", None),
            P("seq", "ctx", None),
            P(None, None, None, ("seq", "ctx", "wt")),
            P(None, None, None, ("seq", "ctx")),
            P(None, None, "wt", ("seq", "ctx")),
            P(None, None, None, "wt", ("seq", "ctx")),
            P(None, None, "wt", ("seq", "ctx")),
            P(None, None, None, "wt", ("seq", "ctx")),
        ),
        check_vma=False,
    )
```

```python
import functools

import jax
import jax.numpy as jnp
from jax import lax
from jax.experimental import pallas as pl
from jax.experimental.pallas import tpu as pltpu
from jax.sharding import PartitionSpec as P

epsilon = 1e-06
f32 = jnp.float32
bf16 = jnp.bfloat16
i32 = jnp.int32
VMEM_LIMIT = 58 * 1024 * 1024
SMALL_LIMIT = 24 * 1024 * 1024
log2e = 1.4426950408889634
LANES = 128


def dot(left, right, contract):
    return lax.dot_general(left, right, (contract, ((), ())), preferred_element_type=f32)


def nn(left, right):
    return dot(left, right, ((1,), (0,)))


def nt(left, right):
    return dot(left, right, ((1,), (1,)))


def tn(left, right):
    return dot(left, right, ((0,), (0,)))


def lane_iota(shape):
    return lax.broadcasted_iota(i32, shape, len(shape) - 1)


def row_iota(shape):
    return lax.broadcasted_iota(i32, shape, 0)


def row_mean(values):
    return jnp.mean(values, axis=-1, keepdims=True)


def inverse_rms(values):
    return lax.rsqrt(row_mean(values * values) + epsilon)


def at_rows(index, size):
    return pl.ds(pl.multiple_of(index * size, size), size)


def by_rows(total, size, step):
    lax.fori_loop(0, total // size, lambda i, c: (step(at_rows(i, size)), c)[1], 0)


def swap_halves(tile, half):
    lower = lane_iota(tile.shape) % (2 * half) < half
    return jnp.where(lower, pltpu.roll(tile, LANES - half, 1), pltpu.roll(tile, half, 1))


def head_sums(tile, head_dim):
    same = row_iota((LANES, LANES)) // head_dim == lane_iota((LANES, LANES)) // head_dim
    ones = jnp.where(same, 1.0, 0.0).astype(bf16)
    return nn(tile.astype(bf16), ones)


def prep_tile(raw, cosine, sine, scale, head_dim):
    mean = head_sums(raw * raw, head_dim) * (1.0 / head_dim)
    inverse = lax.rsqrt(mean + epsilon)
    turned = raw * cosine + swap_halves(raw, head_dim // 2) * sine
    return (turned * inverse * scale).astype(bf16), inverse.astype(bf16)


def prep_tile_back(grad, low, inverse, cosine, sine, scale, head_dim):
    unit = low.astype(f32) / scale
    grad_unit = grad * scale
    mean = head_sums(grad_unit * unit, head_dim) * (1.0 / head_dim)
    grad_turned = inverse.astype(f32) * (grad_unit - unit * mean)
    return (grad_turned * cosine - swap_halves(grad_turned, head_dim // 2) * sine).astype(bf16)


def spread_pair(tile, head_dim):
    lower = lane_iota(tile.shape) < head_dim
    zero = jnp.zeros_like(tile)
    return jnp.concatenate([jnp.where(lower, tile, zero), jnp.where(lower, zero, tile)], axis=0)


def allowed_mask(first, last, key_start, rows, diagonal):
    keys = key_start + row_iota((rows, first.shape[1]))
    mask = keys >= first
    if diagonal:
        mask = mask & (keys <= last)
    return mask


def query_bounds(start_ref, m, place, group, chunk):
    first = start_ref[m : m + 1, :]
    last = (m * group + place) * chunk + lane_iota((1, chunk))
    return jnp.concatenate([first, first], axis=1), jnp.concatenate([last, last], axis=1)


def whole_spec(shape, buffers=1):
    return pl.BlockSpec(
        shape, lambda *a: (0,) * len(shape), pipeline_mode=pl.Buffered(buffers)
    )


def col_spec(size, width=LANES, skip=0):
    return pl.BlockSpec((size, width), lambda p, s: (0, lax.max(p - skip, 0)))


def row_spec(size, width, last):
    return pl.BlockSpec((size, width), lambda p, s: (lax.min(p, last), 0))


def adapter_spec(shape):
    return pl.BlockSpec(
        (1,) + shape, lambda p, s: (s[4],) + (0,) * len(shape), pipeline_mode=pl.Buffered(1)
    )


def params(small=False, limit=None):
    limit = limit or (SMALL_LIMIT if small else VMEM_LIMIT)
    return pltpu.CompilerParams(vmem_limit_bytes=limit)


def cost(flops, moved, transcendentals=0):
    return pl.CostEstimate(
        flops=int(flops), bytes_accessed=int(moved), transcendentals=int(transcendentals)
    )


def attend_kernel(dims, place, *refs):
    slabs, chunk, group, head_dim, rank, half = dims
    count = 4 + (group - 1) * 4
    pieces = refs[:count]
    (
        wq_ref, w_ref, a_ref, b_table, a_table, cos_ref, sin_ref, scale_ref, wout_ref,
        hout_ref, ownout_ref, u_ref, q_ref, k_ref, v_ref, qi_ref, ki_ref, o_ref, inv_ref,
        msg_ref, start_ref, b_ref, ah_ref, first_ref, all_ref, seg_ref, h_ref, own_ref, raw_ref,
    ) = refs[count:]
    inner, slab, core = place[0], place[1], place[2]
    block = group * chunk
    length = slabs * block
    rows = slabs * chunk
    model = 2 * half
    step = pl.program_id(0)

    @pl.when(step == 0)
    def _():
        mine = pl.ds(pl.multiple_of(core * half, half), half)
        other = pl.ds(pl.multiple_of((1 - core) * half, half), half)
        h_ref[at_rows(slab * group + inner, chunk), :] = pieces[0][0]
        seg_ref[...] = jnp.zeros_like(seg_ref)

        def keep_segments(where, piece):
            tail = piece[chunk:, :chunk].astype(f32)
            seg_ref[pl.ds(where, 1), :] = tail[0:1]

        keep_segments(slab * group + inner, pieces[1])

        def place_piece(shift, peer, ours, theirs):
            source = lax.rem(slab - shift + slabs, slabs)
            rows_at = at_rows(source * group + peer, chunk)
            h_ref[rows_at, mine] = ours[:chunk, :]
            h_ref[rows_at, other] = theirs[:chunk, :]
            keep_segments(source * group + peer, ours)

        for shift in range(1, slabs):
            place_piece(shift, inner, pieces[2].at[shift - 1], pieces[3].at[shift - 1])
        for turn in range(1, group):
            peer = lax.rem(inner - turn + group, group)
            near, near_other, rest, rest_other = pieces[4 * turn : 4 * turn + 4]
            place_piece(0, peer, near, near_other)
            for shift in range(1, slabs):
                place_piece(shift, peer, rest.at[shift - 1], rest_other.at[shift - 1])
        for m in range(slabs):
            own_ref[m * chunk : (m + 1) * chunk, :] = h_ref[
                at_rows(m * group + inner, chunk), :
            ]
        columns = seg_ref[...].T
        for m in range(slabs):
            line = seg_ref[pl.ds(m * group + inner, 1), :]
            below = jnp.zeros((chunk, chunk), f32)
            for c in range(slabs * group):
                below = below + jnp.where(columns[:, c : c + 1] < line, 1.0, 0.0)
            count = jnp.sum(below, axis=0, keepdims=True)
            start_ref[m : m + 1, :] = count.astype(i32)
            first_ref[m * chunk : (m + 1) * chunk, :] = (
                jnp.broadcast_to(count, (LANES, chunk)).T.astype(i32)
            )

        for n in range(b_ref.shape[2] // head_dim):
            cols = slice(n * head_dim, (n + 1) * head_dim)
            b_ref[:, :, cols] = b_table[0, :, n]
            ah_ref[:, cols] = a_table[0, n]
        down = a_ref[0, :3].reshape(3 * rank, model)

        def low_rows(sl):
            u_ref[sl, :] = nt(h_ref[sl, :], down).astype(bf16)

        by_rows(length, 512, low_rows)
        for m in range(slabs):
            low = u_ref[at_rows(m * group + inner, chunk), :rank]
            own = slice(m * chunk, (m + 1) * chunk)
            raw_ref[own, :] = nn(low, b_ref[0])
        raw_ref[...] += nn(own_ref[...], wq_ref[0])

    last_block = lax.min(step, slabs - 1)
    hout_ref[...] = h_ref[at_rows(last_block, block), :]
    ownout_ref[...] = own_ref[at_rows(last_block, chunk), :]
    here = pl.ds(pl.multiple_of(step * LANES, LANES), LANES)
    scale = scale_ref[...]
    w_kv = jnp.concatenate([w_ref[0], w_ref[1]], axis=1)
    none = jnp.zeros((rank, LANES), bf16)
    b_kv = jnp.concatenate(
        [
            jnp.zeros((rank, 2 * LANES), bf16),
            jnp.concatenate([b_ref[1, :, here], none], axis=1),
            jnp.concatenate([none, b_ref[2, :, here]], axis=1),
        ],
        axis=0,
    )

    def keys_rows(sl):
        both = nn(h_ref[sl, :], w_kv) + nn(u_ref[sl, :], b_kv)
        k_ref[sl, :], ki_ref[sl, :] = prep_tile(
            both[:, :LANES], cos_ref[sl, :], sin_ref[sl, :], scale, head_dim
        )
        v_ref[sl, :] = both[:, LANES:].astype(bf16)

    by_rows(length, 512, keys_rows)
    for m in range(slabs):
        own = slice(m * chunk, (m + 1) * chunk)
        there = at_rows(m * group + inner, chunk)
        q_ref[own, :], qi_ref[own, :] = prep_tile(
            raw_ref[own, here], cos_ref[there, :], sin_ref[there, :], scale, head_dim
        )
    ones = jnp.ones((block, LANES), bf16)
    left = lane_iota((chunk, LANES)) < head_dim
    for m in range(slabs):
        own = slice(m * chunk, (m + 1) * chunk)
        pair = spread_pair(q_ref[own, :], head_dim)
        first = first_ref[own, :]
        first = jnp.concatenate([first] * (block // LANES), axis=1)
        first = jnp.concatenate([first, first], axis=0)
        gathered = jnp.zeros((2 * chunk, 2 * LANES), f32)
        for b in range(m + 1):
            at = slice(b * block, (b + 1) * block)
            scores = nt(pair, k_ref[at, :])
            keys = b * block + lane_iota(scores.shape)
            mask = keys >= first
            if b == m:
                queries = lax.rem(row_iota(scores.shape), chunk)
                mask = mask & (keys <= queries + (m * group + inner) * chunk)
            weights = jnp.where(mask, jnp.exp2(scores * (0.125 * log2e)), 0.0).astype(bf16)
            gathered = gathered + nn(weights, jnp.concatenate([v_ref[at, :], ones], axis=1))
        inverse = 1.0 / gathered[:, LANES:]
        final = gathered[:, :LANES] * inverse
        final = jnp.where(left, final[:chunk], final[chunk:]).astype(bf16)
        o_ref[own, :] = final
        all_ref[own, here] = final
        inv_ref[0, m : m + 1, :] = inverse.T[0:1, :]

    @pl.when(step == pl.num_programs(0) - 1)
    def _():
        low_o = all_ref[...]
        msg_ref[:, :model] = nn(low_o, wout_ref[...]).astype(bf16)
        msg_ref[:, model:] = pad_to(nt(low_o, ah_ref[...]), LANES).astype(bf16)


def run_attend(place, tokens, pieces, w, a, b, ah, cos, sin, scale, wout, group, head_dim):
    slabs, chunk, model = tokens.shape
    width = w.shape[2]
    rank = a.shape[2]
    half = model // 2
    rows = slabs * chunk
    length = rows * group
    pairs = width // LANES
    in_specs = [pl.BlockSpec((1, chunk, model), lambda p, s: (s[1], 0, 0))]
    in_specs += [whole_spec(piece.shape) for piece in pieces]
    in_specs += [
        whole_spec((1, model, width)),
        pl.BlockSpec(
            (pl.Element(2), pl.Element(model), pl.Element(LANES)),
            lambda p, s: (1, 0, p * LANES),
        ),
        adapter_spec((5, rank, model)),
        adapter_spec(b.shape[1:]),
        adapter_spec(ah.shape[1:]),
        whole_spec((length, LANES)),
        whole_spec((length, LANES)),
        col_spec(1),
        whole_spec((width, model)),
    ]
    def step_rows(size):
        return pl.BlockSpec((size, model), lambda p, s: (lax.min(p, slabs - 1), 0))

    out = [
        ((length, model), bf16, step_rows(group * chunk)),
        ((rows, model), bf16, step_rows(chunk)),
        ((length, 3 * rank), bf16, whole_spec((length, 3 * rank))),
        ((rows, width), bf16, col_spec(rows)),
        ((length, width), bf16, col_spec(length)),
        ((length, width), bf16, col_spec(length)),
        ((rows, width), bf16, col_spec(rows)),
        ((length, width), bf16, col_spec(length)),
        ((rows, width), bf16, col_spec(rows)),
        (
            (pairs, slabs, 2 * chunk),
            f32,
            pl.BlockSpec((1, slabs, 2 * chunk), lambda p, s: (p, 0, 0)),
        ),
        ((rows, model + LANES), bf16, whole_spec((rows, model + LANES))),
        ((slabs, chunk), i32, whole_spec((slabs, chunk))),
        ((3, rank, width), bf16, whole_spec((3, rank, width))),
        ((rank, width), bf16, whole_spec((rank, width))),
    ]
    return pl.pallas_call(
        functools.partial(attend_kernel, (slabs, chunk, group, head_dim, rank, half)),
        grid_spec=pltpu.PrefetchScalarGridSpec(
            num_scalar_prefetch=1,
            grid=(pairs,),
            in_specs=in_specs,
            out_specs=[o[2] for o in out],
            scratch_shapes=[
                pltpu.VMEM((rows, LANES), i32),
                pltpu.VMEM((rows, width), bf16),
                pltpu.VMEM((chunk, chunk), f32),
                pltpu.VMEM((length, model), bf16),
                pltpu.VMEM((rows, model), bf16),
                pltpu.VMEM((rows, width), f32),
            ],
        ),
        out_shape=[jax.ShapeDtypeStruct(o[0], o[1]) for o in out],
        compiler_params=params(),
        cost_estimate=cost(1e8, 1e5),
        name="attend",
    )(place, tokens, *pieces, w, w, a, b, ah, cos, sin, scale, wout)


def join_tiles(ref, *at):
    block = ref[at]
    return jnp.concatenate([block[t] for t in range(block.shape[0])], axis=1)


def feed_kernel(
    dims, place, mine_ref, other_ref, h_ref, bo_ref, rate_ref, a_ref, wgu_ref, bgu_ref, wd_ref,
    ad_ref, scales_ref, mid_ref, u_ref, gate_ref, up_ref, msg_ref, low_ref, acc_ref,
):
    rank, model, slabs = dims
    chunk = h_ref.shape[0]
    step = pl.program_id(0)

    @pl.when(step < slabs)
    def _():
        both = mine_ref[...].astype(f32) + other_ref[...].astype(f32)
        low = both[:, model : model + rank].astype(bf16)
        raw = both[:, :model] + nn(low, bo_ref[0, 0])
        unit = raw * inverse_rms(raw)
        state = h_ref[...].astype(f32)
        mixed = state + rate_ref[0:1, :] * (unit - state)
        mixed = (mixed * inverse_rms(mixed)).astype(bf16)
        mid_ref[...] = mixed
        here = at_rows(step, chunk)
        low_ref[here, :] = mixed
        down = a_ref[0, 3:5].reshape(2 * rank, model)
        u_ref[here, :] = nt(mixed, down).astype(bf16)
        acc_ref[here, :] = jnp.zeros((chunk, model + LANES), f32)

    @pl.when(step >= slabs)
    def _():
        low = low_ref[...]
        u = u_ref[...]
        gate = nn(low, wgu_ref[0]) + nn(u[:, :rank], join_tiles(bgu_ref, 0, 0))
        up = nn(low, wgu_ref[1]) + nn(u[:, rank:], join_tiles(bgu_ref, 0, 1))
        gate_ref[...] = gate.astype(bf16)
        up_ref[...] = up.astype(bf16)
        turned = gate * scales_ref[1:2, :]
        hidden = (up * scales_ref[0:1, :] * (turned / (1.0 + jnp.exp(-turned)))).astype(bf16)
        acc_ref[:, :model] += nn(hidden, wd_ref[...])
        acc_ref[:, model : model + rank] += nt(hidden, join_tiles(ad_ref, 0))

    @pl.when(step == pl.num_programs(0) - 1)
    def _():
        msg_ref[...] = acc_ref[...].astype(bf16)


def hidden_specs(skip, model, rank, block, row_width):
    tiles = block // row_width
    at = lambda f: lax.max(f - skip, 0)
    return [
        pl.BlockSpec((2, model, block), lambda f, s: (0, 0, at(f))),
        pl.BlockSpec((1, 2, tiles, rank, row_width), lambda f, s: (s[4], 0, at(f), 0, 0)),
        pl.BlockSpec((block, model), lambda f, s: (at(f), 0)),
        pl.BlockSpec((1, tiles, rank, row_width), lambda f, s: (s[4], at(f), 0, 0)),
        pl.BlockSpec((2, block), lambda f, s: (0, at(f))),
    ]


def run_feed(place, mine, other, h_own, bm, rates, a, wgu, bgu, wd, ad, scales, block, slabs):
    rows, model = h_own.shape
    chunk = rows // slabs
    hidden = wd.shape[0]
    rank = a.shape[2]
    last = slabs - 1
    out = [
        ((rows, model), bf16, row_spec(chunk, model, last)),
        ((rows, 2 * rank), bf16, whole_spec((rows, 2 * rank))),
        ((rows, hidden), bf16, col_spec(rows, block, slabs)),
        ((rows, hidden), bf16, col_spec(rows, block, slabs)),
        ((rows, model + LANES), bf16, whole_spec((rows, model + LANES))),
    ]
    return pl.pallas_call(
        functools.partial(feed_kernel, (rank, model, slabs)),
        grid_spec=pltpu.PrefetchScalarGridSpec(
            num_scalar_prefetch=1,
            grid=(slabs + hidden // block,),
            in_specs=[
                row_spec(chunk, model + LANES, last),
                row_spec(chunk, model + LANES, last),
                row_spec(chunk, model, last),
                adapter_spec((2, rank, model)),
                whole_spec((2, model)),
                adapter_spec((5, rank, model)),
            ]
            + hidden_specs(slabs, model, rank, block, ad.shape[3]),
            out_specs=[o[2] for o in out],
            scratch_shapes=[
                pltpu.VMEM((rows, model), bf16),
                pltpu.VMEM((rows, model + LANES), f32),
            ],
        ),
        out_shape=[jax.ShapeDtypeStruct(o[0], o[1]) for o in out],
        compiler_params=params(),
        cost_estimate=cost(2.4e10, 3e7),
        name="feed",
    )(place, mine, other, h_own, bm, rates, a, wgu, bgu, wd, ad, scales)


def owner_index(place, group, slabs, n_seq):
    inner, slab, seq = place
    return seq * slabs * group + slab * group + inner


def pad_to(tile, lanes):
    return jnp.pad(tile, ((0, 0), (0, lanes - tile.shape[1])))


def late_rows(rank, units):
    return max(4 * rank, 2 * units)


def folded_rows(rows, groups):
    return (rows + groups * 8 - 1) // (groups * 8) * 8


def fold(tile, groups):
    size = folded_rows(tile.shape[0], groups)
    tile = jnp.pad(tile, ((0, size * groups - tile.shape[0]), (0, 0)))
    return jnp.concatenate([tile[g * size : (g + 1) * size] for g in range(groups)], axis=1)


def unfold(block):
    groups = block.shape[1] // LANES
    return jnp.concatenate(
        [block[:, g * LANES : (g + 1) * LANES] for g in range(groups)], axis=0
    ).astype(f32)


def feed_back_kernel(
    dims, place, mine_ref, other_ref, mid_ref, g_own_ref, g_mine_ref, g_other_ref, bd_ref,
    rate_ref, a_ref, u_ref, gate_ref, up_ref, wgu_ref, bgu_ref, wd_ref, ad_ref, scales_ref,
    out_ref, res_ref, msg_ref, table_ref,
    gd_ref, gdt_ref, ut_ref, udt_ref, gud_ref, gudt_ref, low_ref, acc_ref, gu_ref, hid_ref,
    g_ref, lo_ref,
):
    slabs, chunk, group, n_seq, rank, model, row_width, hidden_rows = dims
    half = model // 2
    step = pl.program_id(0)
    slab, core = place[1], place[2]
    block = gate_ref.shape[1]

    @pl.when(step < slabs)
    def _():
        mine = pl.ds(pl.multiple_of(core * half, half), half)
        other = pl.ds(pl.multiple_of((1 - core) * half, half), half)
        shift = lax.rem(slab - step + slabs, slabs)

        @pl.when(shift == 0)
        def _():
            g_ref[...] = g_own_ref[0]

        @pl.when(shift > 0)
        def _():
            g_ref[:, mine] = g_mine_ref[shift - 1]
            g_ref[:, other] = g_other_ref[shift - 1]

        here = at_rows(step, chunk)
        both = mine_ref[...].astype(f32) + other_ref[...].astype(f32)
        low = both[:, model : model + rank].astype(bf16)
        hid_ref[here, :] = low
        raw = both[:, :model] + nn(low, bd_ref[0, 1])
        raw_inv = inverse_rms(raw)
        unit = raw * raw_inv
        state = mid_ref[...]
        low_ref[here, :] = state
        state = state.astype(f32)
        rate = rate_ref[1:2, :]
        mixed = state + rate * (unit - state)
        mixed_inv = inverse_rms(mixed)
        out = mixed * mixed_inv
        lo_ref[...] = out.astype(bf16)
        grad = g_ref[...].astype(f32)
        grad_mixed = mixed_inv * (grad - out * row_mean(grad * out))
        res_ref[...] = (1.0 - rate) * grad_mixed
        grad_unit = rate * grad_mixed
        gd_ref[here, :] = (raw_inv * (grad_unit - unit * row_mean(grad_unit * unit))).astype(bf16)
        out_ref[0] = lo_ref[:, mine]
        acc_ref[here, :] = jnp.zeros((chunk, model), f32)
        gu_ref[here, :] = jnp.zeros((chunk, 2 * rank), f32)

    @pl.when(step == slabs)
    def _():
        ut_ref[...] = u_ref[...].T
        udt_ref[...] = hid_ref[...].T
        low_gud = nt(gd_ref[...], bd_ref[0, 1]).astype(bf16)
        gud_ref[...] = low_gud
        gudt_ref[...] = low_gud.T

    @pl.when(step >= slabs)
    def _():
        grad_hidden = nt(gd_ref[...], wd_ref[...]) + nn(gud_ref[...], join_tiles(ad_ref, 0))
        gate = gate_ref[...].astype(f32)
        up = up_ref[...].astype(f32)
        up_scale = scales_ref[0:1, :]
        gate_scale = scales_ref[1:2, :]
        turned = gate * gate_scale
        sigmoid = 1.0 / (1.0 + jnp.exp(-turned))
        silu = turned * sigmoid
        up_scaled = up * up_scale
        hidden = (up_scaled * silu).astype(bf16)
        grad_up = (grad_hidden * up_scale * silu).astype(bf16)
        slope = sigmoid * (1.0 + turned * (1.0 - sigmoid)) * gate_scale
        grad_gate = (grad_hidden * up_scaled * slope).astype(bf16)
        acc_ref[...] += nt(grad_gate, wgu_ref[0]) + nt(grad_up, wgu_ref[1])
        gu_ref[:, :rank] += nt(grad_gate, join_tiles(bgu_ref, 0, 0))
        gu_ref[:, rank:] += nt(grad_up, join_tiles(bgu_ref, 0, 1))
        ut = ut_ref[...]
        parts = jnp.concatenate(
            [nn(gudt_ref[...], hidden), nn(ut[:rank], grad_gate), nn(ut[rank:], grad_up)], axis=0
        ).astype(bf16)
        tiles = block // row_width
        for tile in range(tiles):
            gdt_ref[(step - slabs) * tiles + tile] = parts[
                :, tile * row_width : (tile + 1) * row_width
            ]

    @pl.when(step == pl.num_programs(0) - 1)
    def _():
        low_gu = gu_ref[...].astype(bf16)
        down = a_ref[0, 3:5].reshape(2 * rank, model)
        msg_ref[...] = (acc_ref[...] + nn(low_gu, down)).astype(bf16)
        low = low_ref[...]
        model_rows = jnp.concatenate(
            [nn(low_gu.T, low), nn(udt_ref[...], gd_ref[...])], axis=0
        ).astype(bf16).astype(f32)
        ranks = 3 * rank
        units = ranks * hidden_rows
        padded = (units + LANES - 1) // LANES * LANES
        flat = gdt_ref[...].reshape(units, row_width)
        lanes = lane_iota((1, padded))
        target = lanes % hidden_rows * ranks + lanes // hidden_rows
        target = jnp.where(lanes < units, target, -1)
        moved = jnp.where(row_iota((units, padded)) == target, 1.0, 0.0).astype(bf16)
        turned_rows = tn(flat, moved)
        owners = n_seq * slabs * group
        cols = model // owners
        units_each = row_width // owners
        for y in range(group):
            for z in range(slabs):
                for x in range(n_seq):
                    d = owner_index((y, z, x), group, slabs, n_seq)
                    head = pad_to(model_rows[:, d * cols : (d + 1) * cols], LANES)
                    mine = turned_rows[d * units_each : (d + 1) * units_each]
                    tail = [
                        mine[:, t * LANES : (t + 1) * LANES] for t in range(padded // LANES)
                    ]
                    packed = jnp.concatenate([head] + tail, axis=0)
                    table_ref[y, z, x] = fold(packed, half // LANES).astype(bf16)


def run_feed_back(
    place, mine, other, mid, cotangent, g_mine, g_other, bm, rates, a, u, gate, up, wgu, bgu,
    wd, ad, scales, block, group, n_seq,
):
    slabs, chunk, model = cotangent.shape
    rows = slabs * chunk
    half = model // 2
    hidden = wd.shape[0]
    rank = a.shape[2]
    row_width = ad.shape[3]
    last = slabs - 1
    hidden_rows = hidden // row_width
    owners = n_seq * slabs * group
    padded = (3 * rank * hidden_rows + LANES - 1) // LANES * LANES
    table_rows = 3 * rank + row_width // owners * (padded // LANES)
    table = (group, slabs, n_seq, folded_rows(table_rows, half // LANES), half)
    out = [
        (
            (slabs, chunk, half),
            bf16,
            pl.BlockSpec((1, chunk, half), lambda f, s: (lax.min(f, last), 0, 0)),
        ),
        ((rows, model), f32, row_spec(chunk, model, last)),
        ((rows, model), bf16, whole_spec((rows, model))),
        (table, bf16, whole_spec(table)),
    ]
    return pl.pallas_call(
        functools.partial(
            feed_back_kernel,
            (slabs, chunk, group, n_seq, rank, model, row_width, hidden_rows),
        ),
        grid_spec=pltpu.PrefetchScalarGridSpec(
            num_scalar_prefetch=1,
            grid=(slabs + hidden // block,),
            in_specs=[
                row_spec(chunk, model + LANES, last),
                row_spec(chunk, model + LANES, last),
                row_spec(chunk, model, last),
                pl.BlockSpec(
                    (1, chunk, model), lambda f, s: (s[1], 0, 0), pipeline_mode=pl.Buffered(1)
                ),
                whole_spec((slabs - 1, chunk, half)),
                whole_spec((slabs - 1, chunk, half)),
                adapter_spec((2, rank, model)),
                whole_spec((2, model)),
                adapter_spec((5, rank, model)),
                whole_spec((rows, 2 * rank)),
                col_spec(rows, block, slabs),
                col_spec(rows, block, slabs),
            ]
            + hidden_specs(slabs, model, rank, block, row_width),
            out_specs=[o[2] for o in out],
            scratch_shapes=[
                pltpu.VMEM((rows, model), bf16),
                pltpu.VMEM((hidden_rows, 3 * rank, row_width), bf16),
                pltpu.VMEM((2 * rank, rows), bf16),
                pltpu.VMEM((rank, rows), bf16),
                pltpu.VMEM((rows, rank), bf16),
                pltpu.VMEM((rank, rows), bf16),
                pltpu.VMEM((rows, model), bf16),
                pltpu.VMEM((rows, model), f32),
                pltpu.VMEM((rows, 2 * rank), f32),
                pltpu.VMEM((rows, rank), bf16),
                pltpu.VMEM((chunk, model), bf16),
                pltpu.VMEM((chunk, model), bf16),
            ],
        ),
        out_shape=[jax.ShapeDtypeStruct(o[0], o[1]) for o in out],
        compiler_params=params(),
        cost_estimate=cost(3e10, 4e7),
        name="feed_back",
    )(
        place, mine, other, mid, cotangent, g_mine, g_other, bm, rates, a, u, gate, up, wgu,
        bgu, wd, ad, scales,
    )


def attend_back_kernel(
    dims, place, res_ref, gm_ref, go_ref, h_ref, am_ref, ao_ref, rate_ref, bo_ref, wout_ref,
    ah_ref, start_ref, q_ref, k_ref, v_ref, o_ref, inv_ref, qi_ref, ki_ref, cos_ref, sin_ref,
    scale_ref,
    gq_ref, gk_ref, gv_ref, gres_ref, gbo_ref, gah_ref,
    kt_ref, gqt_ref, ga_ref, go_all_ref, guot_ref, uo_ref,
):
    slabs, chunk, group, head_dim, rank, model = dims
    inner = place[0]
    step = pl.program_id(0)

    @pl.when(step < slabs)
    def _():
        here = at_rows(step, chunk)
        grad = res_ref[...] + gm_ref[...].astype(f32) + go_ref[...].astype(f32)
        both = am_ref[...].astype(f32) + ao_ref[...].astype(f32)
        low = both[:, model : model + rank].astype(bf16)
        uo_ref[here, :] = low
        raw = both[:, :model] + nn(low, bo_ref[0, 0])
        raw_inv = inverse_rms(raw)
        unit = raw * raw_inv
        state = h_ref[...].astype(f32)
        rate = rate_ref[0:1, :]
        mixed = state + rate * (unit - state)
        mixed_inv = inverse_rms(mixed)
        out = mixed * mixed_inv
        grad_mixed = mixed_inv * (grad - out * row_mean(grad * out))
        gres_ref[...] = (1.0 - rate) * grad_mixed
        grad_unit = rate * grad_mixed
        ga_ref[here, :] = (raw_inv * (grad_unit - unit * row_mean(grad_unit * unit))).astype(bf16)

    @pl.when(step == slabs)
    def _():
        gbo_ref[...] = nn(uo_ref[...].T, ga_ref[...])
        low_g = nt(ga_ref[...], bo_ref[0, 0]).astype(bf16)
        guot_ref[...] = low_g.T
        go_all_ref[...] = (nt(ga_ref[...], wout_ref[...]) + nn(low_g, ah_ref[...])).astype(bf16)

    @pl.when(step >= slabs)
    def _():
        attend_back_pair(
            dims, inner, step - slabs, start_ref, q_ref, k_ref, v_ref, o_ref, inv_ref,
            qi_ref, ki_ref, cos_ref, sin_ref, scale_ref, gq_ref, gk_ref, gv_ref, gah_ref,
            kt_ref, gqt_ref, go_all_ref, guot_ref,
        )


def attend_back_pair(
    dims, inner, turn, start_ref, q_ref, k_ref, v_ref, o_ref, inv_ref, qi_ref, ki_ref,
    cos_ref, sin_ref, scale_ref, gq_ref, gk_ref, gv_ref, gah_ref, kt_ref, gqt_ref,
    go_all_ref, guot_ref,
):
    slabs, chunk, group, head_dim, rank, model = dims
    block = group * chunk
    kt_ref[...] = k_ref[...].T
    scale = scale_ref[...]
    grad_o = go_all_ref[:, pl.ds(pl.multiple_of(turn * LANES, LANES), LANES)]
    gah_ref[...] = nn(guot_ref[...], o_ref[...])
    pairs_q, pairs_g, deltas, bounds = [], [], [], []
    for m in range(slabs):
        own = slice(m * chunk, (m + 1) * chunk)
        pairs_q.append(spread_pair(q_ref[own, :], head_dim))
        grad = grad_o[own]
        pairs_g.append(spread_pair(grad, head_dim))
        products = (grad.astype(f32) * o_ref[own, :].astype(f32)).T
        deltas.append(
            jnp.concatenate(
                [
                    jnp.sum(products[:head_dim], axis=0, keepdims=True),
                    jnp.sum(products[head_dim:], axis=0, keepdims=True),
                ],
                axis=1,
            )
        )
        bounds.append(query_bounds(start_ref, m, inner, group, chunk))
    for b in range(slabs):
        at = slice(b * block, (b + 1) * block)
        grad_key = jnp.zeros((block, LANES), f32)
        grad_value = jnp.zeros((block, LANES), f32)
        for m in range(b, slabs):
            first, last = bounds[m]
            scores = nt(k_ref[at, :], pairs_q[m])
            mask = allowed_mask(first, last, b * block, block, b == m)
            weights = jnp.exp2(scores * (0.125 * log2e)) * inv_ref[0, m : m + 1, :]
            weights = jnp.where(mask, weights, 0.0)
            grad_value = grad_value + nn(weights.astype(bf16), pairs_g[m])
            grad_weights = nt(v_ref[at, :], pairs_g[m])
            grad_scores = (weights * (grad_weights - deltas[m])).astype(bf16)
            grad_key = grad_key + nn(grad_scores, pairs_q[m])
            part = nn(kt_ref[:, at], grad_scores)
            if b == 0:
                gqt_ref[m] = part
            else:
                gqt_ref[m] += part
        gv_ref[at, :] = grad_value.astype(bf16)
        gk_ref[at, :] = prep_tile_back(
            grad_key * 0.125, k_ref[at, :], ki_ref[at, :], cos_ref[at, :], sin_ref[at, :],
            scale, head_dim,
        )
    upper = row_iota((LANES, chunk)) < head_dim
    for m in range(slabs):
        own = slice(m * chunk, (m + 1) * chunk)
        both = gqt_ref[m]
        grad = jnp.where(upper, both[:, :chunk], both[:, chunk:]).T * 0.125
        there = at_rows(m * group + inner, chunk)
        gq_ref[own, :] = prep_tile_back(
            grad, q_ref[own, :], qi_ref[own, :], cos_ref[there, :], sin_ref[there, :],
            scale, head_dim,
        )


def run_attend_back(
    place, res, gm, go, h_own, am, ao, rates, bm, wout, ah, start, q, k, v, o, inv, qi, ki, cos, sin, scale, slabs, group, head_dim,
):
    rows, model = h_own.shape
    chunk = rows // slabs
    width = q.shape[1]
    length = k.shape[0]
    rank = bm.shape[2]
    pairs = width // LANES
    last = slabs - 1
    wide = row_spec(chunk, model + LANES, last)
    narrow = row_spec(chunk, model, last)
    cols = lambda size: col_spec(size, LANES, slabs)
    out = [
        ((rows, width), bf16, cols(rows)),
        ((length, width), bf16, cols(length)),
        ((length, width), bf16, cols(length)),
        ((rows, model), f32, narrow),
        ((rank, model), f32, whole_spec((rank, model))),
        ((rank, width), f32, cols(rank)),
    ]
    return pl.pallas_call(
        functools.partial(attend_back_kernel, (slabs, chunk, group, head_dim, rank, model)),
        grid_spec=pltpu.PrefetchScalarGridSpec(
            num_scalar_prefetch=1,
            grid=(slabs + pairs,),
            in_specs=[
                narrow,
                narrow,
                narrow,
                narrow,
                wide,
                wide,
                whole_spec((2, model)),
                adapter_spec((2, rank, model)),
                whole_spec((width, model)),
                whole_spec((rank, width)),
                whole_spec((slabs, chunk)),
                cols(rows),
                cols(length),
                cols(length),
                cols(rows),
                pl.BlockSpec(
                    (1, slabs, 2 * chunk), lambda p, s: (lax.max(p - slabs, 0), 0, 0)
                ),
                cols(rows),
                cols(length),
                whole_spec((length, LANES)),
                whole_spec((length, LANES)),
                cols(1),
            ],
            out_specs=[o_[2] for o_ in out],
            scratch_shapes=[
                pltpu.VMEM((LANES, length), bf16),
                pltpu.VMEM((slabs, LANES, 2 * chunk), f32),
                pltpu.VMEM((rows, model), bf16),
                pltpu.VMEM((rows, width), bf16),
                pltpu.VMEM((rank, rows), bf16),
                pltpu.VMEM((rows, rank), bf16),
            ],
        ),
        out_shape=[jax.ShapeDtypeStruct(o_[0], o_[1]) for o_ in out],
        compiler_params=params(),
        cost_estimate=cost(3e10, 4e7),
        name="attend_back",
    )(
        place, res, gm, go, h_own, am, ao, rates, bm, wout, ah, start, q, k, v, o, inv, qi, ki,
        cos, sin, scale,
    )


def apart(blocks):
    none = jnp.zeros_like(blocks[0])
    return jnp.concatenate(
        [
            jnp.concatenate([b if n == m else none for n in range(len(blocks))], axis=1)
            for m, b in enumerate(blocks)
        ],
        axis=0,
    )


def others_kernel(
    place, gk_ref, gv_ref, wk_ref, wv_ref, a_ref, b_ref, keep_ref, send_ref, low_ref
):
    rows, width = keep_ref.shape[1], gk_ref.shape[-1]
    half = keep_ref.shape[2]
    rank = b_ref.shape[1]
    both = jnp.concatenate(
        [gk_ref[...].reshape(rows, width), gv_ref[...].reshape(rows, width)], axis=1
    )
    turn = pl.program_id(1)

    @pl.when(turn == 0)
    def _():
        low_ref[...] = nt(both, apart([b_ref[1], b_ref[2]])).astype(bf16)

    weights = jnp.concatenate([wk_ref[0], wv_ref[0]], axis=1)
    part = nt(both, weights) + nn(low_ref[...], a_ref[0, 1:3].reshape(2 * rank, half))

    @pl.when(turn == 0)
    def _():
        send_ref[0] = part.astype(bf16)

    @pl.when(turn == 1)
    def _():
        keep_ref[0] = part.astype(bf16)


def half_weight(half, width, member):
    return pl.BlockSpec(
        (1, half, width), lambda *a: (member, lax.rem(a[-1][2] + 1 + a[-2], 2), 0)
    )


def half_factors(rank, half):
    return pl.BlockSpec(
        (1, 5, rank, half), lambda *a: (a[-1][4], 0, 0, lax.rem(a[-1][2] + 1 + a[-2], 2))
    )


def run_others(place, gk, gv, w, a, b, slabs, group):
    length, width = gk.shape
    chunk = length // (slabs * group)
    rows = slabs * chunk
    half = w.shape[1] // 2
    rank = b.shape[1]
    shaped = (slabs, group, chunk, width)
    peer = pl.BlockSpec(
        (slabs, 1, chunk, width), lambda g, t, s: (0, lax.rem(s[0] + 1 + g, group), 0, 0)
    )
    return pl.pallas_call(
        others_kernel,
        grid_spec=pltpu.PrefetchScalarGridSpec(
            num_scalar_prefetch=1,
            grid=(group - 1, 2),
            in_specs=[
                peer,
                peer,
                half_weight(half, width, 1),
                half_weight(half, width, 2),
                half_factors(rank, half),
                whole_spec((3, rank, width)),
            ],
            out_specs=[pl.BlockSpec((1, rows, half), lambda g, t, s: (g, 0, 0))] * 2,
            scratch_shapes=[pltpu.VMEM((rows, 2 * rank), bf16)],
        ),
        out_shape=[
            jax.ShapeDtypeStruct((group - 1, rows, half), bf16),
            jax.ShapeDtypeStruct((group - 1, rows, half), bf16),
        ],
        compiler_params=params(),
        cost_estimate=cost(7e9, 1e7),
        name="others",
    )(place, gk.reshape(shaped), gv.reshape(shaped), w, w, a, b)


def own_kernel(
    place, gq_ref, gk_ref, gv_ref, wq_ref, wk_ref, wv_ref, a_ref, b_ref, res_ref, keep_ref,
    send_ref, low_ref,
):
    rows, width = gq_ref.shape
    half = keep_ref.shape[1]
    rank = b_ref.shape[1]
    grads = jnp.concatenate(
        [gq_ref[...], gk_ref[...].reshape(rows, width), gv_ref[...].reshape(rows, width)], axis=1
    )
    turn = pl.program_id(0)

    @pl.when(turn == 0)
    def _():
        low_ref[...] = nt(grads, apart([b_ref[0], b_ref[1], b_ref[2]])).astype(bf16)

    weights = jnp.concatenate([wq_ref[0], wk_ref[0], wv_ref[0]], axis=1)
    part = nt(grads, weights) + nn(low_ref[...], a_ref[0, 0:3].reshape(3 * rank, half))

    @pl.when(turn == 0)
    def _():
        send_ref[...] = part.astype(bf16)

    @pl.when(turn == 1)
    def _():
        keep_ref[...] = (part + res_ref[...]).astype(bf16)


def run_own(place, gq, gk, gv, w, a, b, res, slabs, group):
    length, width = gk.shape
    rows, model = res.shape
    chunk = rows // slabs
    half = model // 2
    rank = b.shape[1]
    shaped = (slabs, group, chunk, width)
    peer = pl.BlockSpec((slabs, 1, chunk, width), lambda t, s: (0, s[0], 0, 0))
    out = [((rows, half), bf16), ((rows, half), bf16)]
    return pl.pallas_call(
        own_kernel,
        grid_spec=pltpu.PrefetchScalarGridSpec(
            num_scalar_prefetch=1,
            grid=(2,),
            in_specs=[
                whole_spec((rows, width)),
                peer,
                peer,
                half_weight(half, width, 0),
                half_weight(half, width, 1),
                half_weight(half, width, 2),
                half_factors(rank, half),
                whole_spec((3, rank, width)),
                pl.BlockSpec((rows, half), lambda t, s: (0, s[2])),
            ],
            out_specs=[whole_spec(o[0]) for o in out],
            scratch_shapes=[pltpu.VMEM((rows, 3 * rank), bf16)],
        ),
        out_shape=[jax.ShapeDtypeStruct(o[0], o[1]) for o in out],
        compiler_params=params(True),
        cost_estimate=cost(7e9, 1e7),
        name="own",
    )(place, gq, gk.reshape(shaped), gv.reshape(shaped), w, w, w, a, b, res)


def grads_kernel(
    dims, place, gq_ref, gk_ref, gv_ref, b_ref, u_ref, h_ref, gbo_ref, gah_ref, table_ref,
    uq_ref, low_ref,
):
    slabs, chunk, group, n_seq, rank, model, head_dim = dims
    inner = place[0]
    width = gq_ref.shape[1]
    heads = width // head_dim
    gq = gq_ref[...]
    both = jnp.concatenate([gk_ref[...], gv_ref[...]], axis=1)
    low_q = nt(gq, b_ref[0]).astype(bf16)
    low_ref[:, : 2 * rank] = nt(both, apart([b_ref[1], b_ref[2]])).astype(bf16)
    low_ref[:, 2 * rank :] = jnp.zeros((low_ref.shape[0], rank), bf16)
    for m in range(slabs):
        there = at_rows(m * group + inner, chunk)
        uq_ref[m * chunk : (m + 1) * chunk, :] = u_ref[there, :]
        low_ref[there, 2 * rank :] = low_q[m * chunk : (m + 1) * chunk]
    products = nn(low_ref[...].T, h_ref[...])
    model_rows = jnp.concatenate(
        [products[2 * rank :], products[: 2 * rank], gbo_ref[...]], axis=0
    ).astype(bf16).astype(f32)
    uqt = uq_ref[...].T
    pair = nn(u_ref[...].T[rank:], both)
    head_rows = jnp.concatenate(
        [gah_ref[...], nn(uqt[:rank], gq), pair[:rank, :width], pair[rank:, width:]], axis=0
    ).astype(bf16)
    owners = n_seq * slabs * group
    cols = model // owners
    each = head_dim // owners
    units = heads * each
    spots = lax.broadcasted_iota(i32, (width, 1), 0)
    owner = spots // units
    inside = spots % units
    source = inside // each * head_dim + owner * each + inside % each
    moved = jnp.where(lane_iota((width, width)) == source, 1.0, 0.0).astype(bf16)
    turned = nt(moved, head_rows)
    for y in range(group):
        for z in range(slabs):
            for x in range(n_seq):
                d = owner_index((y, z, x), group, slabs, n_seq)
                left = model_rows[:, d * cols : (d + 1) * cols]
                heads_part = turned[d * units : (d + 1) * units]
                right = jnp.concatenate(
                    [heads_part[:, rank:], pad_to(heads_part[:, :rank], 3 * rank)], axis=0
                )
                tall = late_rows(rank, units)
                packed = jnp.concatenate(
                    [
                        jnp.pad(left, ((0, tall - left.shape[0]), (0, 0))),
                        jnp.pad(right, ((0, tall - right.shape[0]), (0, 0))),
                    ],
                    axis=1,
                )
                packed = pad_to(packed, LANES)
                table_ref[y, z, x] = fold(packed, table_ref.shape[4] // LANES).astype(bf16)


def run_grads(place, gq, gk, gv, b, u, h, gbo, gah, slabs, group, n_seq, head_dim):
    length, width = gk.shape
    rows, model = gq.shape[0], h.shape[1]
    chunk = rows // slabs
    rank = b.shape[1]
    heads = width // head_dim
    owners = n_seq * slabs * group
    units = heads * (head_dim // owners)
    half = model // 2
    shape = (group, slabs, n_seq, folded_rows(late_rows(rank, units), half // LANES), half)
    operands = (gq, gk, gv, b, u, h, gbo, gah)
    return pl.pallas_call(
        functools.partial(grads_kernel, (slabs, chunk, group, n_seq, rank, model, head_dim)),
        grid_spec=pltpu.PrefetchScalarGridSpec(
            num_scalar_prefetch=1,
            grid=(1,),
            in_specs=[whole_spec(operand.shape) for operand in operands],
            out_specs=whole_spec(shape),
            scratch_shapes=[
                pltpu.VMEM((rows, 3 * rank), bf16),
                pltpu.VMEM((length, 3 * rank), bf16),
            ],
        ),
        out_shape=jax.ShapeDtypeStruct(shape, bf16),
        compiler_params=params(True),
        cost_estimate=cost(1e10, 1e7),
        name="grads",
    )(place, *operands)


def join_kernel(slabs, place, *refs):
    out_ref = refs[-1]
    chunk, half = out_ref.shape[1], refs[0].shape[-1]
    core, slab = place[2], place[1]
    for shift in range(slabs):
        source = lax.rem(slab - shift + slabs, slabs)
        for which, ref in ((core, refs[shift]), (1 - core, refs[slabs + shift])):
            out_ref[source, :, pl.ds(pl.multiple_of(which * half, half), half)] = ref[
                :chunk, :
            ].astype(out_ref.dtype)


def run_join(place, mine, other, chunk, dtype):
    slabs = len(mine)
    half = mine[0].shape[1]
    return pl.pallas_call(
        functools.partial(join_kernel, slabs),
        grid_spec=pltpu.PrefetchScalarGridSpec(
            num_scalar_prefetch=1,
            grid=(1,),
            in_specs=[whole_spec(piece.shape) for piece in (*mine, *other)],
            out_specs=whole_spec((slabs, chunk, 2 * half)),
        ),
        out_shape=jax.ShapeDtypeStruct((slabs, chunk, 2 * half), dtype),
        compiler_params=params(True),
        cost_estimate=cost(1e6, 8e6),
        name="join",
    )(place, *mine, *other)


def for_tables(where, place, index, refs, put):
    n_seq, slabs, chunk, size = where
    home, home_other = refs[:slabs], refs[slabs : 2 * slabs]
    far, far_other = refs[2 * slabs : 2 * slabs + n_seq - 1], refs[2 * slabs + n_seq - 1 :]
    for r in range(slabs):
        at = pl.ds(pl.multiple_of(chunk + place[3] * size, 8), size)
        put(index[0, r], unfold(home[r][at, :]), unfold(home_other[r][at, :]))
    for s in range(1, n_seq):

        def one(r, carry, s=s):
            put(index[s, r], unfold(far[s - 1][r]), unfold(far_other[s - 1][r]))
            return carry

        lax.fori_loop(0, slabs, one, 0)


def unpack_early_kernel(dims, where, place, index, *refs):
    rank, cols, each, hidden_rows, tiles = dims
    am_ref, bm_ref, ad_ref, bd_ref = refs[-4:]
    core = place[2]

    def put(adapter, block, other):
        both = block[: 2 * rank] + other[: 2 * rank]
        am = jnp.where(core == 0, both[:, : cols // 2], both[:, cols // 2 : cols])
        am_ref[adapter] = am.reshape(2, rank, cols // 2)
        bm_ref[adapter] = block[2 * rank : 3 * rank, :cols]
        base = 3 * rank
        wide = jnp.concatenate(
            [block[base + t * each : base + (t + 1) * each] for t in range(tiles)], axis=1
        )
        for k in range(rank):
            ad_ref[adapter, k] = wide[:, k * hidden_rows : (k + 1) * hidden_rows]
        for j in range(2):
            for k in range(rank):
                at = ((j + 1) * rank + k) * hidden_rows
                bd_ref[adapter, j, k] = wide[:, at : at + hidden_rows]

    for_tables(where, place, index, refs[:-4], put)


def unpack_late_kernel(dims, where, place, index, *refs):
    rank, cols, heads, each = dims
    am_gu_ref, bm_down_ref, am_ref, bm_ref, ah_ref, bh_ref = refs[-6:]
    core = place[2]

    def put(adapter, block, other):
        both = block[: 3 * rank] + other[: 3 * rank]
        am = jnp.where(core == 0, both[:, : cols // 2], both[:, cols // 2 : cols])
        am_ref[adapter, 0:3] = am.reshape(3, rank, cols // 2)
        am_ref[adapter, 3:5] = am_gu_ref[adapter]
        bm_ref[adapter, 0] = block[3 * rank : 4 * rank, :cols]
        bm_ref[adapter, 1] = bm_down_ref[adapter]
        units = heads * each
        for n in range(heads):
            at = n * each
            ah_ref[adapter, n] = block[units + at : units + at + each, cols : cols + rank]
            for j in range(3):
                lanes = slice(cols + j * rank, cols + (j + 1) * rank)
                bh_ref[adapter, j, n] = block[at : at + each, lanes]

    for_tables(where, place, index, refs[:-6], put)


def run_unpack(kernel, dims, where, place, index, tables, extra, shapes, name):
    operands = [*tables, *extra]
    return pl.pallas_call(
        functools.partial(kernel, dims, where),
        grid_spec=pltpu.PrefetchScalarGridSpec(
            num_scalar_prefetch=2,
            grid=(1,),
            in_specs=[whole_spec(operand.shape) for operand in operands],
            out_specs=[whole_spec(shape) for shape in shapes],
        ),
        out_shape=[jax.ShapeDtypeStruct(shape, f32) for shape in shapes],
        compiler_params=params(True),
        cost_estimate=cost(1e6, 8e6),
        name=name,
    )(place, index, *operands)


def pick(array, index):
    return lax.dynamic_index_in_dim(array, index, 0, keepdims=False)


def body(
    tokens, segments, adapter_index, w_attn_in, w_attn_out, w_gate_up, w_down, qk_scale,
    mix_rates, mlp_scales, a_model, b_model, a_heads, b_heads, a_hidden, b_hidden, cotangent,
):
    slabs, chunk, model = tokens.shape
    n_seq = lax.axis_size("seq")
    n_ctx = lax.axis_size("ctx")
    group = n_ctx // slabs
    local_width = w_attn_out.shape[0]
    head_dim = a_heads.shape[-1]
    row_width = a_hidden.shape[-1]
    local_hidden = w_down.shape[0]
    local_heads = local_width // head_dim
    rank = a_model.shape[2]
    adapters = a_model.shape[0]
    half = model // 2
    ctx_place = lax.axis_index("ctx")
    slab = ctx_place // group
    inner = ctx_place % group
    core = lax.axis_index("wt")
    seq_place = lax.axis_index("seq")
    owners = n_seq * n_ctx
    rows = slabs * chunk
    length = rows * group
    place = jnp.stack([inner, slab, core, seq_place, pick(adapter_index, slab)]).astype(i32)
    a_heads = jnp.transpose(a_heads, (0, 2, 1, 3))
    b_heads = jnp.transpose(b_heads, (0, 1, 3, 2, 4))
    a_hidden = jnp.transpose(a_hidden, (0, 2, 1, 3))
    b_hidden = jnp.transpose(b_hidden, (0, 1, 3, 2, 4))

    def to_slab(array, shift):
        pairs = [(c, (c + shift * group) % n_ctx) for c in range(n_ctx)]
        return lax.ppermute(array, "ctx", pairs)

    def within_slab(array, shift):
        pairs = [(c, c - c % group + (c % group + shift) % group) for c in range(n_ctx)]
        return lax.ppermute(array, "ctx", pairs)

    def to_seq(array, shift):
        return lax.ppermute(array, "seq", [(c, (c + shift) % n_seq) for c in range(n_seq)])

    def other_core(array):
        return lax.ppermute(array, "wt", [(0, 1), (1, 0)])

    def half_piece(array, index, which):
        return lax.dynamic_slice(array, (index, 0, which * half), (1, chunk, half))[0]

    def token_piece(index):
        seg = jnp.pad(pick(segments, index).astype(bf16), (0, half - chunk))
        return jnp.concatenate(
            [half_piece(tokens, index, core), jnp.broadcast_to(seg, (8, half))], axis=0
        )

    tie = lax.optimization_barrier

    spot = (jnp.arange(LANES, dtype=i32) % (head_dim // 2)).astype(f32)
    frequency = 10000.0 ** (-spot / (head_dim // 2))
    turn = jnp.arange(length, dtype=i32).astype(f32)[:, None] * frequency[None, :]
    cos = jnp.cos(turn)
    lower = jnp.arange(LANES) % head_dim < head_dim // 2
    sin = jnp.sin(turn) * jnp.where(lower, -1.0, 1.0)[None, :]
    scale = qk_scale[None, :]

    own_piece = token_piece(slab)
    got = [own_piece] + [
        to_slab(token_piece((slab + shift) % slabs), shift) for shift in range(1, slabs)
    ]
    index = [adapter_index]
    for shift in range(1, n_seq):
        index.append(to_seq(adapter_index, shift))
    got, cos, sin, place, index = tie((got, cos, sin, place, index))
    near = [within_slab(own_piece, turn) for turn in range(1, group)]
    g_send = [half_piece(cotangent, (slab + shift) % slabs, core) for shift in range(1, slabs)]
    rest, near, g_send = tie((jnp.stack(got[1:]), near, g_send))
    rest_other = other_core(rest)
    peers = [within_slab(rest, turn) for turn in range(1, group)]
    g_mine = [to_slab(g_send[shift - 1], shift) for shift in range(1, slabs)]
    peers, g_mine[0], g_mine[-1] = tie((peers, g_mine[0], g_mine[-1]))
    pieces = [own_piece, rest, rest_other]
    for turn in range(1, group):
        pieces += [
            near[turn - 1], other_core(near[turn - 1]),
            peers[turn - 1], other_core(peers[turn - 1]),
        ]
    h_full, h_own, u, q, k, v, qi, ki, o, inv, attn_msg, start, bh, ah = run_attend(
        place, tokens, pieces, w_attn_in, a_model, b_heads, a_heads, cos, sin, scale,
        w_attn_out, group, head_dim,
    )
    g_mine, attn_msg = tie((g_mine, attn_msg))
    attn_other = other_core(attn_msg)
    g_mine, attn_msg = tie((jnp.stack(g_mine), attn_msg))
    g_mine, attn_other = tie((g_mine, attn_other))
    g_other = other_core(g_mine)
    mid, u_gu, gate, up, down_msg = run_feed(
        place, attn_msg, attn_other, h_own, b_model, mix_rates, a_model, w_gate_up, b_hidden,
        w_down, a_hidden, mlp_scales, 512, slabs,
    )
    g_other, down_msg = tie((g_other, down_msg))
    down_other = other_core(down_msg)
    out_half, mid_res, mid_msg, early = run_feed_back(
        place, down_msg, down_other, mid, cotangent, g_mine, g_other, b_model, mix_rates,
        a_model, u_gu, gate, up, w_gate_up, b_hidden, w_down, a_hidden, mlp_scales, 512, group,
        n_seq,
    )
    mid_other = other_core(mid_msg)

    order = (slab - jnp.arange(slabs, dtype=i32)) % slabs
    index = jnp.stack(index)[:, order]

    def sum_inner(table):
        return pick(table, inner), [
            within_slab(pick(table, (inner + turn) % group), turn) for turn in range(1, group)
        ]

    def add_inner(own, got):
        total = own.astype(f32)
        for piece in got:
            total = total + piece.astype(f32)
        return total.astype(bf16)

    def over_slabs(total):
        return [pick(total, slab)] + [
            to_slab(pick(total, (slab + shift) % slabs), shift) for shift in range(1, slabs)
        ]

    def pack(rows_part, table):
        return jnp.concatenate([rows_part, table.reshape(slabs, -1, half)], axis=1)

    early_size = early.shape[3]
    early_own, early_got = sum_inner(early)
    gq, gk, gv, h_res, gbo, gah = run_attend_back(
        place, mid_res, mid_msg, mid_other, h_own, attn_msg, attn_other, mix_rates, b_model,
        w_attn_out, ah, start, q, k, v, o, inv, qi, ki, cos, sin, scale, slabs, group,
        head_dim,
    )
    early_got, gk, gv = tie((early_got, gk, gv))
    keep, send = run_others(place, gk, gv, w_attn_in, a_model, bh, slabs, group)
    others = (keep.astype(f32) + other_core(send).astype(f32)).astype(bf16)
    others, gq, gk, gv = tie((others, gq, gk, gv))
    waves = [[2, 1], [3, 0]] if slabs == 4 else [list(range(slabs))]
    others = others.reshape(group - 1, slabs, chunk, half)
    others_got = []
    for wave in waves:
        if others_got:
            others_got[-1], others = tie((others_got[-1], others))
        others_got.append(
            [
                within_slab(
                    jnp.stack(
                        [pick(others[turn - 1], (slab + shift) % slabs) for shift in wave]
                    ),
                    turn,
                )
                for turn in range(1, group)
            ]
        )
    home = over_slabs(pack(out_half, add_inner(early_own, early_got)))
    late = run_grads(
        place, gq, gk, gv, bh, u, h_full, gbo, gah, slabs, group, n_seq, head_dim
    )
    late_own, late_got = sum_inner(late)
    late_own, gq, home, others_got[0] = tie((late_own, gq, home, others_got[0]))
    home_other = [other_core(piece) for piece in home]
    early_far = []
    for shift in range(1, n_seq):
        at = chunk + (seq_place + shift) % n_seq * early_size
        sent = [lax.dynamic_slice_in_dim(piece, at, early_size, 0) for piece in home]
        early_far.append(to_seq(jnp.stack(sent), shift))
    own_keep, own_send = run_own(
        place, gq, gk, gv, w_attn_in, a_model, bh, h_res, slabs, group
    )
    late_got, early_far, own_send, others_got = tie(
        (late_got, early_far, own_send, others_got)
    )
    own_got = other_core(own_send)
    late_total = add_inner(late_own, late_got)
    own_sum = (own_keep.astype(f32) + own_got.astype(f32)).reshape(slabs, chunk, half)
    size = late.shape[3]
    result = [None] * slabs
    for wave, got_wave in zip(waves, others_got):
        for n, shift in enumerate(wave):
            target = (slab + shift) % slabs
            total = pick(own_sum, target)
            for got_part in got_wave:
                total = total + got_part[n].astype(f32)
            result[shift] = jnp.concatenate(
                [total.astype(bf16), pick(late_total, target).reshape(n_seq * size, half)],
                axis=0,
            )
    result, home, home_other, early_far = tie((result, home, home_other, early_far))
    result = result[:1] + [to_slab(result[shift], shift) for shift in range(1, slabs)]
    early_tables = [*home, *home_other, *early_far, *(other_core(t) for t in early_far)]
    layer_out = run_join(place, home, home_other, chunk, bf16)
    cols = model // owners
    each = row_width // owners
    hidden_rows = local_hidden // row_width
    grad_am_gu, grad_bm_down, grad_ad, grad_bd = run_unpack(
        unpack_early_kernel,
        (rank, cols, each, hidden_rows, (3 * rank * hidden_rows + LANES - 1) // LANES),
        (n_seq, slabs, chunk, early_size),
        place, index, early_tables, [],
        [
            (adapters, 2, rank, cols // 2),
            (adapters, rank, cols),
            (adapters, rank, each, hidden_rows),
            (adapters, 2, rank, each, hidden_rows),
        ],
        "unpack_early",
    )
    result, layer_out, grad_am_gu, grad_bm_down = tie(
        (result, layer_out, grad_am_gu, grad_bm_down)
    )
    result_other = [other_core(piece) for piece in result]
    far = []
    for shift in range(1, n_seq):
        at = chunk + (seq_place + shift) % n_seq * size
        sent = [lax.dynamic_slice_in_dim(piece, at, size, 0) for piece in result]
        far.append(to_seq(jnp.stack(sent), shift))
    input_grad = run_join(place, result, result_other, chunk, f32)
    far, input_grad = tie((far, input_grad))
    each = head_dim // owners
    grad_am, grad_bm, grad_ah, grad_bh = run_unpack(
        unpack_late_kernel,
        (rank, cols, local_heads, each),
        (n_seq, slabs, chunk, size),
        place, index, [*result, *result_other, *far, *(other_core(piece) for piece in far)],
        [grad_am_gu, grad_bm_down],
        [
            (adapters, 5, rank, cols // 2),
            (adapters, 2, rank, cols),
            (adapters, local_heads, each, rank),
            (adapters, 3, local_heads, each, rank),
        ],
        "unpack_late",
    )
    return (
        layer_out,
        input_grad,
        grad_am,
        grad_bm,
        jnp.transpose(grad_ah, (0, 3, 1, 2)),
        jnp.transpose(grad_bh, (0, 1, 4, 2, 3)),
        jnp.transpose(grad_ad, (0, 1, 3, 2)),
        jnp.transpose(grad_bd, (0, 1, 2, 4, 3)),
    )


def solution(mesh):
    return jax.shard_map(
        body,
        mesh=mesh,
        in_specs=(
            P("seq", "ctx", None),
            P("seq", "ctx"),
            P("seq"),
            P(None, None, "wt"),
            P("wt", None),
            P(None, None, "wt"),
            P("wt", None),
            P("wt"),
            P(),
            P(None, "wt"),
            P(),
            P(),
            P(None, None, "wt", None),
            P(None, None, None, "wt", None),
            P(None, None, "wt", None),
            P(None, None, None, "wt", None),
            P("seq", "ctx", None),
        ),
        out_specs=(
            P("seq", "ctx", None),
            P("seq", "ctx", None),
            P(None, None, None, ("seq", "ctx", "wt")),
            P(None, None, None, ("seq", "ctx")),
            P(None, None, "wt", ("seq", "ctx")),
            P(None, None, None, "wt", ("seq", "ctx")),
            P(None, None, "wt", ("seq", "ctx")),
            P(None, None, None, "wt", ("seq", "ctx")),
        ),
        check_vma=False,
    )
```

```python
import functools

import jax
import jax.numpy as jnp
from jax import lax
from jax.experimental import pallas as pl
from jax.experimental.pallas import tpu as pltpu
from jax.sharding import PartitionSpec as P

epsilon = 1e-06
f32 = jnp.float32
bf16 = jnp.bfloat16
i32 = jnp.int32
VMEM_LIMIT = 58 * 1024 * 1024
SMALL_LIMIT = 24 * 1024 * 1024
log2e = 1.4426950408889634
LANES = 128


def dot(left, right, contract):
    return lax.dot_general(left, right, (contract, ((), ())), preferred_element_type=f32)


def nn(left, right):
    return dot(left, right, ((1,), (0,)))


def nt(left, right):
    return dot(left, right, ((1,), (1,)))


def tn(left, right):
    return dot(left, right, ((0,), (0,)))


def lane_iota(shape):
    return lax.broadcasted_iota(i32, shape, len(shape) - 1)


def row_iota(shape):
    return lax.broadcasted_iota(i32, shape, 0)


def row_mean(values):
    return jnp.mean(values, axis=-1, keepdims=True)


def inverse_rms(values):
    return lax.rsqrt(row_mean(values * values) + epsilon)


def at_rows(index, size):
    return pl.ds(pl.multiple_of(index * size, size), size)


def by_rows(total, size, step):
    lax.fori_loop(0, total // size, lambda i, c: (step(at_rows(i, size)), c)[1], 0)


def swap_halves(tile, half):
    lower = lane_iota(tile.shape) % (2 * half) < half
    return jnp.where(lower, pltpu.roll(tile, LANES - half, 1), pltpu.roll(tile, half, 1))


def head_sums(tile, head_dim):
    same = row_iota((LANES, LANES)) // head_dim == lane_iota((LANES, LANES)) // head_dim
    ones = jnp.where(same, 1.0, 0.0).astype(bf16)
    return nn(tile.astype(bf16), ones)


def prep_tile(raw, cosine, sine, scale, head_dim):
    mean = head_sums(raw * raw, head_dim) * (1.0 / head_dim)
    inverse = lax.rsqrt(mean + epsilon)
    turned = raw * cosine + swap_halves(raw, head_dim // 2) * sine
    return (turned * inverse * scale).astype(bf16), inverse.astype(bf16)


def prep_tile_back(grad, low, inverse, cosine, sine, scale, head_dim):
    unit = low.astype(f32) / scale
    grad_unit = grad * scale
    mean = head_sums(grad_unit * unit, head_dim) * (1.0 / head_dim)
    grad_turned = inverse.astype(f32) * (grad_unit - unit * mean)
    return (grad_turned * cosine - swap_halves(grad_turned, head_dim // 2) * sine).astype(bf16)


def spread_pair(tile, head_dim):
    lower = lane_iota(tile.shape) < head_dim
    zero = jnp.zeros_like(tile)
    return jnp.concatenate([jnp.where(lower, tile, zero), jnp.where(lower, zero, tile)], axis=0)


def allowed_mask(first, last, key_start, rows, diagonal):
    keys = key_start + row_iota((rows, first.shape[1]))
    mask = keys >= first
    if diagonal:
        mask = mask & (keys <= last)
    return mask


def query_bounds(start_ref, m, place, group, chunk):
    first = start_ref[m : m + 1, :]
    last = (m * group + place) * chunk + lane_iota((1, chunk))
    return jnp.concatenate([first, first], axis=1), jnp.concatenate([last, last], axis=1)


def whole_spec(shape, buffers=1):
    return pl.BlockSpec(
        shape, lambda *a: (0,) * len(shape), pipeline_mode=pl.Buffered(buffers)
    )


def col_spec(size, width=LANES, skip=0):
    return pl.BlockSpec((size, width), lambda p, s: (0, lax.max(p - skip, 0)))


def row_spec(size, width, last):
    return pl.BlockSpec((size, width), lambda p, s: (lax.min(p, last), 0))


def adapter_spec(shape):
    return pl.BlockSpec(
        (1,) + shape, lambda p, s: (s[4],) + (0,) * len(shape), pipeline_mode=pl.Buffered(1)
    )


def params(small=False, limit=None):
    limit = limit or (SMALL_LIMIT if small else VMEM_LIMIT)
    return pltpu.CompilerParams(vmem_limit_bytes=limit)


def near_last(out, place):
    return [
        pltpu.VMEM(o[0], o[1]) if n == place else jax.ShapeDtypeStruct(o[0], o[1])
        for n, o in enumerate(out)
    ]


def cost(flops, moved, transcendentals=0):
    return pl.CostEstimate(
        flops=int(flops), bytes_accessed=int(moved), transcendentals=int(transcendentals)
    )


def attend_kernel(dims, place, *refs):
    slabs, chunk, group, head_dim, rank, half = dims
    count = 4 + (group - 1) * 4
    pieces = refs[:count]
    (
        wq_ref, w_ref, a_ref, b_table, a_table, cos_ref, sin_ref, scale_ref, wout_ref,
        hout_ref, ownout_ref, u_ref, q_ref, k_ref, v_ref, qi_ref, ki_ref, o_ref, inv_ref,
        msg_ref, start_ref, b_ref, ah_ref, first_ref, all_ref, seg_ref, h_ref, own_ref, raw_ref,
    ) = refs[count:]
    inner, slab, core = place[0], place[1], place[2]
    block = group * chunk
    length = slabs * block
    rows = slabs * chunk
    model = 2 * half
    step = pl.program_id(0)

    @pl.when(step == 0)
    def _():
        mine = pl.ds(pl.multiple_of(core * half, half), half)
        other = pl.ds(pl.multiple_of((1 - core) * half, half), half)
        h_ref[at_rows(slab * group + inner, chunk), :] = pieces[0][0]
        seg_ref[...] = jnp.zeros_like(seg_ref)

        def keep_segments(where, piece):
            tail = piece[chunk:, :chunk].astype(f32)
            seg_ref[pl.ds(where, 1), :] = tail[0:1]

        keep_segments(slab * group + inner, pieces[1])

        def place_piece(shift, peer, ours, theirs):
            source = lax.rem(slab - shift + slabs, slabs)
            rows_at = at_rows(source * group + peer, chunk)
            h_ref[rows_at, mine] = ours[:chunk, :]
            h_ref[rows_at, other] = theirs[:chunk, :]
            keep_segments(source * group + peer, ours)

        for shift in range(1, slabs):
            place_piece(shift, inner, pieces[2].at[shift - 1], pieces[3].at[shift - 1])
        for turn in range(1, group):
            peer = lax.rem(inner - turn + group, group)
            near, near_other, rest, rest_other = pieces[4 * turn : 4 * turn + 4]
            place_piece(0, peer, near, near_other)
            for shift in range(1, slabs):
                place_piece(shift, peer, rest.at[shift - 1], rest_other.at[shift - 1])
        for m in range(slabs):
            own_ref[m * chunk : (m + 1) * chunk, :] = h_ref[
                at_rows(m * group + inner, chunk), :
            ]
        columns = seg_ref[...].T
        for m in range(slabs):
            line = seg_ref[pl.ds(m * group + inner, 1), :]
            below = jnp.zeros((chunk, chunk), f32)
            for c in range(slabs * group):
                below = below + jnp.where(columns[:, c : c + 1] < line, 1.0, 0.0)
            count = jnp.sum(below, axis=0, keepdims=True)
            start_ref[m : m + 1, :] = count.astype(i32)
            first_ref[m * chunk : (m + 1) * chunk, :] = (
                jnp.broadcast_to(count, (LANES, chunk)).T.astype(i32)
            )

        for n in range(b_ref.shape[2] // head_dim):
            cols = slice(n * head_dim, (n + 1) * head_dim)
            b_ref[:, :, cols] = b_table[0, :, n]
            ah_ref[:, cols] = a_table[0, n]
        down = a_ref[0, :3].reshape(3 * rank, model)

        def low_rows(sl):
            u_ref[sl, :] = nt(h_ref[sl, :], down).astype(bf16)

        by_rows(length, 512, low_rows)
        for m in range(slabs):
            low = u_ref[at_rows(m * group + inner, chunk), :rank]
            own = slice(m * chunk, (m + 1) * chunk)
            raw_ref[own, :] = nn(low, b_ref[0])
        raw_ref[...] += nn(own_ref[...], wq_ref[0])

    last_block = lax.min(step, slabs - 1)
    hout_ref[...] = h_ref[at_rows(last_block, block), :]
    ownout_ref[...] = own_ref[at_rows(last_block, chunk), :]
    here = pl.ds(pl.multiple_of(step * LANES, LANES), LANES)
    scale = scale_ref[...]
    w_kv = jnp.concatenate([w_ref[0], w_ref[1]], axis=1)
    none = jnp.zeros((rank, LANES), bf16)
    b_kv = jnp.concatenate(
        [
            jnp.zeros((rank, 2 * LANES), bf16),
            jnp.concatenate([b_ref[1, :, here], none], axis=1),
            jnp.concatenate([none, b_ref[2, :, here]], axis=1),
        ],
        axis=0,
    )

    def keys_rows(sl):
        both = nn(h_ref[sl, :], w_kv) + nn(u_ref[sl, :], b_kv)
        k_ref[sl, :], ki_ref[sl, :] = prep_tile(
            both[:, :LANES], cos_ref[sl, :], sin_ref[sl, :], scale, head_dim
        )
        v_ref[sl, :] = both[:, LANES:].astype(bf16)

    by_rows(length, 512, keys_rows)
    for m in range(slabs):
        own = slice(m * chunk, (m + 1) * chunk)
        there = at_rows(m * group + inner, chunk)
        q_ref[own, :], qi_ref[own, :] = prep_tile(
            raw_ref[own, here], cos_ref[there, :], sin_ref[there, :], scale, head_dim
        )
    ones = jnp.ones((block, LANES), bf16)
    left = lane_iota((chunk, LANES)) < head_dim
    for m in range(slabs):
        own = slice(m * chunk, (m + 1) * chunk)
        pair = spread_pair(q_ref[own, :], head_dim)
        first = first_ref[own, :]
        first = jnp.concatenate([first] * (block // LANES), axis=1)
        first = jnp.concatenate([first, first], axis=0)
        gathered = jnp.zeros((2 * chunk, 2 * LANES), f32)
        for b in range(m + 1):
            at = slice(b * block, (b + 1) * block)
            scores = nt(pair, k_ref[at, :])
            keys = b * block + lane_iota(scores.shape)
            mask = keys >= first
            if b == m:
                queries = lax.rem(row_iota(scores.shape), chunk)
                mask = mask & (keys <= queries + (m * group + inner) * chunk)
            weights = jnp.where(mask, jnp.exp2(scores * (0.125 * log2e)), 0.0).astype(bf16)
            gathered = gathered + nn(weights, jnp.concatenate([v_ref[at, :], ones], axis=1))
        inverse = 1.0 / gathered[:, LANES:]
        final = gathered[:, :LANES] * inverse
        final = jnp.where(left, final[:chunk], final[chunk:]).astype(bf16)
        o_ref[own, :] = final
        all_ref[own, here] = final
        inv_ref[0, m : m + 1, :] = inverse.T[0:1, :]

    @pl.when(step == pl.num_programs(0) - 1)
    def _():
        low_o = all_ref[...]
        msg_ref[:, :model] = nn(low_o, wout_ref[...]).astype(bf16)
        msg_ref[:, model:] = pad_to(nt(low_o, ah_ref[...]), LANES).astype(bf16)


def run_attend(place, tokens, pieces, w, a, b, ah, cos, sin, scale, wout, group, head_dim):
    slabs, chunk, model = tokens.shape
    width = w.shape[2]
    rank = a.shape[2]
    half = model // 2
    rows = slabs * chunk
    length = rows * group
    pairs = width // LANES
    in_specs = [pl.BlockSpec((1, chunk, model), lambda p, s: (s[1], 0, 0))]
    in_specs += [whole_spec(piece.shape) for piece in pieces]
    in_specs += [
        whole_spec((1, model, width)),
        pl.BlockSpec(
            (pl.Element(2), pl.Element(model), pl.Element(LANES)),
            lambda p, s: (1, 0, p * LANES),
        ),
        adapter_spec((5, rank, model)),
        adapter_spec(b.shape[1:]),
        adapter_spec(ah.shape[1:]),
        whole_spec((length, LANES)),
        whole_spec((length, LANES)),
        col_spec(1),
        whole_spec((width, model)),
    ]
    def step_rows(size):
        return pl.BlockSpec((size, model), lambda p, s: (lax.min(p, slabs - 1), 0))

    out = [
        ((length, model), bf16, step_rows(group * chunk)),
        ((rows, model), bf16, step_rows(chunk)),
        ((length, 3 * rank), bf16, whole_spec((length, 3 * rank))),
        ((rows, width), bf16, col_spec(rows)),
        ((length, width), bf16, col_spec(length)),
        ((length, width), bf16, col_spec(length)),
        ((rows, width), bf16, col_spec(rows)),
        ((length, width), bf16, col_spec(length)),
        ((rows, width), bf16, col_spec(rows)),
        (
            (pairs, slabs, 2 * chunk),
            f32,
            pl.BlockSpec((1, slabs, 2 * chunk), lambda p, s: (p, 0, 0)),
        ),
        ((rows, model + LANES), bf16, whole_spec((rows, model + LANES))),
        ((slabs, chunk), i32, whole_spec((slabs, chunk))),
        ((3, rank, width), bf16, whole_spec((3, rank, width))),
        ((rank, width), bf16, whole_spec((rank, width))),
    ]
    return pl.pallas_call(
        functools.partial(attend_kernel, (slabs, chunk, group, head_dim, rank, half)),
        grid_spec=pltpu.PrefetchScalarGridSpec(
            num_scalar_prefetch=1,
            grid=(pairs,),
            in_specs=in_specs,
            out_specs=[o[2] for o in out],
            scratch_shapes=[
                pltpu.VMEM((rows, LANES), i32),
                pltpu.VMEM((rows, width), bf16),
                pltpu.VMEM((chunk, chunk), f32),
                pltpu.VMEM((length, model), bf16),
                pltpu.VMEM((rows, model), bf16),
                pltpu.VMEM((rows, width), f32),
            ],
        ),
        out_shape=[jax.ShapeDtypeStruct(o[0], o[1]) for o in out],
        compiler_params=params(),
        cost_estimate=cost(1e8, 1e5),
        name="attend",
    )(place, tokens, *pieces, w, w, a, b, ah, cos, sin, scale, wout)


def join_tiles(ref, *at):
    block = ref[at]
    return jnp.concatenate([block[t] for t in range(block.shape[0])], axis=1)


def feed_kernel(
    dims, place, mine_ref, other_ref, h_ref, bo_ref, rate_ref, a_ref, wgu_ref, bgu_ref, wd_ref,
    ad_ref, scales_ref, mid_ref, u_ref, gate_ref, up_ref, msg_ref, low_ref, acc_ref,
):
    rank, model, slabs = dims
    chunk = h_ref.shape[0]
    step = pl.program_id(0)

    @pl.when(step < slabs)
    def _():
        both = mine_ref[...].astype(f32) + other_ref[...].astype(f32)
        low = both[:, model : model + rank].astype(bf16)
        raw = both[:, :model] + nn(low, bo_ref[0, 0])
        unit = raw * inverse_rms(raw)
        state = h_ref[...].astype(f32)
        mixed = state + rate_ref[0:1, :] * (unit - state)
        mixed = (mixed * inverse_rms(mixed)).astype(bf16)
        mid_ref[...] = mixed
        here = at_rows(step, chunk)
        low_ref[here, :] = mixed
        down = a_ref[0, 3:5].reshape(2 * rank, model)
        u_ref[here, :] = nt(mixed, down).astype(bf16)
        acc_ref[here, :] = jnp.zeros((chunk, model + LANES), f32)

    @pl.when(step >= slabs)
    def _():
        low = low_ref[...]
        u = u_ref[...]
        gate = nn(low, wgu_ref[0]) + nn(u[:, :rank], join_tiles(bgu_ref, 0, 0))
        up = nn(low, wgu_ref[1]) + nn(u[:, rank:], join_tiles(bgu_ref, 0, 1))
        gate_ref[...] = gate.astype(bf16)
        up_ref[...] = up.astype(bf16)
        turned = gate * scales_ref[1:2, :]
        hidden = (up * scales_ref[0:1, :] * (turned / (1.0 + jnp.exp(-turned)))).astype(bf16)
        acc_ref[:, :model] += nn(hidden, wd_ref[...])
        acc_ref[:, model : model + rank] += nt(hidden, join_tiles(ad_ref, 0))

    @pl.when(step == pl.num_programs(0) - 1)
    def _():
        msg_ref[...] = acc_ref[...].astype(bf16)


def hidden_specs(skip, model, rank, block, row_width):
    tiles = block // row_width
    at = lambda f: lax.max(f - skip, 0)
    return [
        pl.BlockSpec((2, model, block), lambda f, s: (0, 0, at(f))),
        pl.BlockSpec((1, 2, tiles, rank, row_width), lambda f, s: (s[4], 0, at(f), 0, 0)),
        pl.BlockSpec((block, model), lambda f, s: (at(f), 0)),
        pl.BlockSpec((1, tiles, rank, row_width), lambda f, s: (s[4], at(f), 0, 0)),
        pl.BlockSpec((2, block), lambda f, s: (0, at(f))),
    ]


def run_feed(place, mine, other, h_own, bm, rates, a, wgu, bgu, wd, ad, scales, block, slabs):
    rows, model = h_own.shape
    chunk = rows // slabs
    hidden = wd.shape[0]
    rank = a.shape[2]
    last = slabs - 1
    out = [
        ((rows, model), bf16, row_spec(chunk, model, last)),
        ((rows, 2 * rank), bf16, whole_spec((rows, 2 * rank))),
        ((rows, hidden), bf16, col_spec(rows, block, slabs)),
        ((rows, hidden), bf16, col_spec(rows, block, slabs)),
        ((rows, model + LANES), bf16, whole_spec((rows, model + LANES))),
    ]
    return pl.pallas_call(
        functools.partial(feed_kernel, (rank, model, slabs)),
        grid_spec=pltpu.PrefetchScalarGridSpec(
            num_scalar_prefetch=1,
            grid=(slabs + hidden // block,),
            in_specs=[
                row_spec(chunk, model + LANES, last),
                row_spec(chunk, model + LANES, last),
                row_spec(chunk, model, last),
                adapter_spec((2, rank, model)),
                whole_spec((2, model)),
                adapter_spec((5, rank, model)),
            ]
            + hidden_specs(slabs, model, rank, block, ad.shape[3]),
            out_specs=[o[2] for o in out],
            scratch_shapes=[
                pltpu.VMEM((rows, model), bf16),
                pltpu.VMEM((rows, model + LANES), f32),
            ],
        ),
        out_shape=near_last(out, 4),
        compiler_params=params(),
        cost_estimate=cost(2.4e10, 3e7),
        name="feed",
    )(place, mine, other, h_own, bm, rates, a, wgu, bgu, wd, ad, scales)


def owner_index(place, group, slabs, n_seq):
    inner, slab, seq = place
    return seq * slabs * group + slab * group + inner


def pad_to(tile, lanes):
    return jnp.pad(tile, ((0, 0), (0, lanes - tile.shape[1])))


def late_rows(rank, units):
    return max(4 * rank, 2 * units)


def folded_rows(rows, groups):
    return (rows + groups * 8 - 1) // (groups * 8) * 8


def fold(tile, groups):
    size = folded_rows(tile.shape[0], groups)
    tile = jnp.pad(tile, ((0, size * groups - tile.shape[0]), (0, 0)))
    return jnp.concatenate([tile[g * size : (g + 1) * size] for g in range(groups)], axis=1)


def unfold(block):
    groups = block.shape[1] // LANES
    return jnp.concatenate(
        [block[:, g * LANES : (g + 1) * LANES] for g in range(groups)], axis=0
    ).astype(f32)


def feed_back_kernel(
    dims, place, mine_ref, other_ref, mid_ref, g_own_ref, g_mine_ref, g_other_ref, bd_ref,
    rate_ref, a_ref, u_ref, gate_ref, up_ref, wgu_ref, bgu_ref, wd_ref, ad_ref, scales_ref,
    out_ref, res_ref, msg_ref, table_ref,
    gd_ref, gdt_ref, ut_ref, udt_ref, gud_ref, gudt_ref, low_ref, acc_ref, gu_ref, hid_ref,
    g_ref, lo_ref,
):
    slabs, chunk, group, n_seq, rank, model, row_width, hidden_rows = dims
    half = model // 2
    step = pl.program_id(0)
    slab, core = place[1], place[2]
    block = gate_ref.shape[1]

    @pl.when(step < slabs)
    def _():
        mine = pl.ds(pl.multiple_of(core * half, half), half)
        other = pl.ds(pl.multiple_of((1 - core) * half, half), half)
        shift = lax.rem(slab - step + slabs, slabs)

        @pl.when(shift == 0)
        def _():
            g_ref[...] = g_own_ref[0]

        @pl.when(shift > 0)
        def _():
            g_ref[:, mine] = g_mine_ref[shift - 1]
            g_ref[:, other] = g_other_ref[shift - 1]

        here = at_rows(step, chunk)
        both = mine_ref[...].astype(f32) + other_ref[...].astype(f32)
        low = both[:, model : model + rank].astype(bf16)
        hid_ref[here, :] = low
        raw = both[:, :model] + nn(low, bd_ref[0, 1])
        raw_inv = inverse_rms(raw)
        unit = raw * raw_inv
        state = mid_ref[...]
        low_ref[here, :] = state
        state = state.astype(f32)
        rate = rate_ref[1:2, :]
        mixed = state + rate * (unit - state)
        mixed_inv = inverse_rms(mixed)
        out = mixed * mixed_inv
        lo_ref[...] = out.astype(bf16)
        grad = g_ref[...].astype(f32)
        grad_mixed = mixed_inv * (grad - out * row_mean(grad * out))
        res_ref[...] = (1.0 - rate) * grad_mixed
        grad_unit = rate * grad_mixed
        gd_ref[here, :] = (raw_inv * (grad_unit - unit * row_mean(grad_unit * unit))).astype(bf16)
        out_ref[0] = lo_ref[:, mine]
        acc_ref[here, :] = jnp.zeros((chunk, model), f32)
        gu_ref[here, :] = jnp.zeros((chunk, 2 * rank), f32)

    @pl.when(step == slabs)
    def _():
        ut_ref[...] = u_ref[...].T
        udt_ref[...] = hid_ref[...].T
        low_gud = nt(gd_ref[...], bd_ref[0, 1]).astype(bf16)
        gud_ref[...] = low_gud
        gudt_ref[...] = low_gud.T

    @pl.when(step >= slabs)
    def _():
        grad_hidden = nt(gd_ref[...], wd_ref[...]) + nn(gud_ref[...], join_tiles(ad_ref, 0))
        gate = gate_ref[...].astype(f32)
        up = up_ref[...].astype(f32)
        up_scale = scales_ref[0:1, :]
        gate_scale = scales_ref[1:2, :]
        turned = gate * gate_scale
        sigmoid = 1.0 / (1.0 + jnp.exp(-turned))
        silu = turned * sigmoid
        up_scaled = up * up_scale
        hidden = (up_scaled * silu).astype(bf16)
        grad_up = (grad_hidden * up_scale * silu).astype(bf16)
        slope = sigmoid * (1.0 + turned * (1.0 - sigmoid)) * gate_scale
        grad_gate = (grad_hidden * up_scaled * slope).astype(bf16)
        acc_ref[...] += nt(grad_gate, wgu_ref[0]) + nt(grad_up, wgu_ref[1])
        gu_ref[:, :rank] += nt(grad_gate, join_tiles(bgu_ref, 0, 0))
        gu_ref[:, rank:] += nt(grad_up, join_tiles(bgu_ref, 0, 1))
        ut = ut_ref[...]
        parts = jnp.concatenate(
            [nn(gudt_ref[...], hidden), nn(ut[:rank], grad_gate), nn(ut[rank:], grad_up)], axis=0
        ).astype(bf16)
        tiles = block // row_width
        for tile in range(tiles):
            gdt_ref[(step - slabs) * tiles + tile] = parts[
                :, tile * row_width : (tile + 1) * row_width
            ]

    @pl.when(step == pl.num_programs(0) - 1)
    def _():
        low_gu = gu_ref[...].astype(bf16)
        down = a_ref[0, 3:5].reshape(2 * rank, model)
        msg_ref[...] = (acc_ref[...] + nn(low_gu, down)).astype(bf16)
        low = low_ref[...]
        model_rows = jnp.concatenate(
            [nn(low_gu.T, low), nn(udt_ref[...], gd_ref[...])], axis=0
        ).astype(bf16).astype(f32)
        ranks = 3 * rank
        units = ranks * hidden_rows
        padded = (units + LANES - 1) // LANES * LANES
        flat = gdt_ref[...].reshape(units, row_width)
        lanes = lane_iota((1, padded))
        target = lanes % hidden_rows * ranks + lanes // hidden_rows
        target = jnp.where(lanes < units, target, -1)
        moved = jnp.where(row_iota((units, padded)) == target, 1.0, 0.0).astype(bf16)
        turned_rows = tn(flat, moved)
        owners = n_seq * slabs * group
        cols = model // owners
        units_each = row_width // owners
        for y in range(group):
            for z in range(slabs):
                for x in range(n_seq):
                    d = owner_index((y, z, x), group, slabs, n_seq)
                    head = pad_to(model_rows[:, d * cols : (d + 1) * cols], LANES)
                    mine = turned_rows[d * units_each : (d + 1) * units_each]
                    tail = [
                        mine[:, t * LANES : (t + 1) * LANES] for t in range(padded // LANES)
                    ]
                    packed = jnp.concatenate([head] + tail, axis=0)
                    table_ref[y, z, x] = fold(packed, half // LANES).astype(bf16)


def run_feed_back(
    place, mine, other, mid, cotangent, g_mine, g_other, bm, rates, a, u, gate, up, wgu, bgu,
    wd, ad, scales, block, group, n_seq,
):
    slabs, chunk, model = cotangent.shape
    rows = slabs * chunk
    half = model // 2
    hidden = wd.shape[0]
    rank = a.shape[2]
    row_width = ad.shape[3]
    last = slabs - 1
    hidden_rows = hidden // row_width
    owners = n_seq * slabs * group
    padded = (3 * rank * hidden_rows + LANES - 1) // LANES * LANES
    table_rows = 3 * rank + row_width // owners * (padded // LANES)
    table = (group, slabs, n_seq, folded_rows(table_rows, half // LANES), half)
    out = [
        (
            (slabs, chunk, half),
            bf16,
            pl.BlockSpec((1, chunk, half), lambda f, s: (lax.min(f, last), 0, 0)),
        ),
        ((rows, model), f32, row_spec(chunk, model, last)),
        ((rows, model), bf16, whole_spec((rows, model))),
        (table, bf16, whole_spec(table)),
    ]
    return pl.pallas_call(
        functools.partial(
            feed_back_kernel,
            (slabs, chunk, group, n_seq, rank, model, row_width, hidden_rows),
        ),
        grid_spec=pltpu.PrefetchScalarGridSpec(
            num_scalar_prefetch=1,
            grid=(slabs + hidden // block,),
            in_specs=[
                row_spec(chunk, model + LANES, last),
                row_spec(chunk, model + LANES, last),
                row_spec(chunk, model, last),
                pl.BlockSpec(
                    (1, chunk, model), lambda f, s: (s[1], 0, 0), pipeline_mode=pl.Buffered(1)
                ),
                whole_spec((slabs - 1, chunk, half)),
                whole_spec((slabs - 1, chunk, half)),
                adapter_spec((2, rank, model)),
                whole_spec((2, model)),
                adapter_spec((5, rank, model)),
                whole_spec((rows, 2 * rank)),
                col_spec(rows, block, slabs),
                col_spec(rows, block, slabs),
            ]
            + hidden_specs(slabs, model, rank, block, row_width),
            out_specs=[o[2] for o in out],
            scratch_shapes=[
                pltpu.VMEM((rows, model), bf16),
                pltpu.VMEM((hidden_rows, 3 * rank, row_width), bf16),
                pltpu.VMEM((2 * rank, rows), bf16),
                pltpu.VMEM((rank, rows), bf16),
                pltpu.VMEM((rows, rank), bf16),
                pltpu.VMEM((rank, rows), bf16),
                pltpu.VMEM((rows, model), bf16),
                pltpu.VMEM((rows, model), f32),
                pltpu.VMEM((rows, 2 * rank), f32),
                pltpu.VMEM((rows, rank), bf16),
                pltpu.VMEM((chunk, model), bf16),
                pltpu.VMEM((chunk, model), bf16),
            ],
        ),
        out_shape=near_last(out, 2),
        compiler_params=params(),
        cost_estimate=cost(3e10, 4e7),
        name="feed_back",
    )(
        place, mine, other, mid, cotangent, g_mine, g_other, bm, rates, a, u, gate, up, wgu,
        bgu, wd, ad, scales,
    )


def attend_back_kernel(
    dims, place, res_ref, gm_ref, go_ref, h_ref, am_ref, ao_ref, rate_ref, bo_ref, wout_ref,
    ah_ref, start_ref, q_ref, k_ref, v_ref, o_ref, inv_ref, qi_ref, ki_ref, cos_ref, sin_ref,
    scale_ref,
    gq_ref, gk_ref, gv_ref, gres_ref, gbo_ref, gah_ref,
    kt_ref, gqt_ref, ga_ref, go_all_ref, guot_ref, uo_ref,
):
    slabs, chunk, group, head_dim, rank, model = dims
    inner = place[0]
    step = pl.program_id(0)

    @pl.when(step < slabs)
    def _():
        here = at_rows(step, chunk)
        grad = res_ref[...] + gm_ref[...].astype(f32) + go_ref[...].astype(f32)
        both = am_ref[...].astype(f32) + ao_ref[...].astype(f32)
        low = both[:, model : model + rank].astype(bf16)
        uo_ref[here, :] = low
        raw = both[:, :model] + nn(low, bo_ref[0, 0])
        raw_inv = inverse_rms(raw)
        unit = raw * raw_inv
        state = h_ref[...].astype(f32)
        rate = rate_ref[0:1, :]
        mixed = state + rate * (unit - state)
        mixed_inv = inverse_rms(mixed)
        out = mixed * mixed_inv
        grad_mixed = mixed_inv * (grad - out * row_mean(grad * out))
        gres_ref[...] = (1.0 - rate) * grad_mixed
        grad_unit = rate * grad_mixed
        ga_ref[here, :] = (raw_inv * (grad_unit - unit * row_mean(grad_unit * unit))).astype(bf16)

    @pl.when(step == slabs)
    def _():
        gbo_ref[...] = nn(uo_ref[...].T, ga_ref[...])
        low_g = nt(ga_ref[...], bo_ref[0, 0]).astype(bf16)
        guot_ref[...] = low_g.T
        go_all_ref[...] = (nt(ga_ref[...], wout_ref[...]) + nn(low_g, ah_ref[...])).astype(bf16)

    @pl.when(step >= slabs)
    def _():
        attend_back_pair(
            dims, inner, step - slabs, start_ref, q_ref, k_ref, v_ref, o_ref, inv_ref,
            qi_ref, ki_ref, cos_ref, sin_ref, scale_ref, gq_ref, gk_ref, gv_ref, gah_ref,
            kt_ref, gqt_ref, go_all_ref, guot_ref,
        )


def attend_back_pair(
    dims, inner, turn, start_ref, q_ref, k_ref, v_ref, o_ref, inv_ref, qi_ref, ki_ref,
    cos_ref, sin_ref, scale_ref, gq_ref, gk_ref, gv_ref, gah_ref, kt_ref, gqt_ref,
    go_all_ref, guot_ref,
):
    slabs, chunk, group, head_dim, rank, model = dims
    block = group * chunk
    kt_ref[...] = k_ref[...].T
    scale = scale_ref[...]
    grad_o = go_all_ref[:, pl.ds(pl.multiple_of(turn * LANES, LANES), LANES)]
    gah_ref[...] = nn(guot_ref[...], o_ref[...])
    pairs_q, pairs_g, deltas, bounds = [], [], [], []
    for m in range(slabs):
        own = slice(m * chunk, (m + 1) * chunk)
        pairs_q.append(spread_pair(q_ref[own, :], head_dim))
        grad = grad_o[own]
        pairs_g.append(spread_pair(grad, head_dim))
        products = (grad.astype(f32) * o_ref[own, :].astype(f32)).T
        deltas.append(
            jnp.concatenate(
                [
                    jnp.sum(products[:head_dim], axis=0, keepdims=True),
                    jnp.sum(products[head_dim:], axis=0, keepdims=True),
                ],
                axis=1,
            )
        )
        bounds.append(query_bounds(start_ref, m, inner, group, chunk))
    for b in range(slabs):
        at = slice(b * block, (b + 1) * block)
        grad_key = jnp.zeros((block, LANES), f32)
        grad_value = jnp.zeros((block, LANES), f32)
        for m in range(b, slabs):
            first, last = bounds[m]
            scores = nt(k_ref[at, :], pairs_q[m])
            mask = allowed_mask(first, last, b * block, block, b == m)
            weights = jnp.exp2(scores * (0.125 * log2e)) * inv_ref[0, m : m + 1, :]
            weights = jnp.where(mask, weights, 0.0)
            grad_value = grad_value + nn(weights.astype(bf16), pairs_g[m])
            grad_weights = nt(v_ref[at, :], pairs_g[m])
            grad_scores = (weights * (grad_weights - deltas[m])).astype(bf16)
            grad_key = grad_key + nn(grad_scores, pairs_q[m])
            part = nn(kt_ref[:, at], grad_scores)
            if b == 0:
                gqt_ref[m] = part
            else:
                gqt_ref[m] += part
        gv_ref[at, :] = grad_value.astype(bf16)
        gk_ref[at, :] = prep_tile_back(
            grad_key * 0.125, k_ref[at, :], ki_ref[at, :], cos_ref[at, :], sin_ref[at, :],
            scale, head_dim,
        )
    upper = row_iota((LANES, chunk)) < head_dim
    for m in range(slabs):
        own = slice(m * chunk, (m + 1) * chunk)
        both = gqt_ref[m]
        grad = jnp.where(upper, both[:, :chunk], both[:, chunk:]).T * 0.125
        there = at_rows(m * group + inner, chunk)
        gq_ref[own, :] = prep_tile_back(
            grad, q_ref[own, :], qi_ref[own, :], cos_ref[there, :], sin_ref[there, :],
            scale, head_dim,
        )


def run_attend_back(
    place, res, gm, go, h_own, am, ao, rates, bm, wout, ah, start, q, k, v, o, inv, qi, ki, cos, sin, scale, slabs, group, head_dim,
):
    rows, model = h_own.shape
    chunk = rows // slabs
    width = q.shape[1]
    length = k.shape[0]
    rank = bm.shape[2]
    pairs = width // LANES
    last = slabs - 1
    wide = row_spec(chunk, model + LANES, last)
    narrow = row_spec(chunk, model, last)
    cols = lambda size: col_spec(size, LANES, slabs)
    out = [
        ((rows, width), bf16, cols(rows)),
        ((length, width), bf16, cols(length)),
        ((length, width), bf16, cols(length)),
        ((rows, model), f32, narrow),
        ((rank, model), f32, whole_spec((rank, model))),
        ((rank, width), f32, cols(rank)),
    ]
    return pl.pallas_call(
        functools.partial(attend_back_kernel, (slabs, chunk, group, head_dim, rank, model)),
        grid_spec=pltpu.PrefetchScalarGridSpec(
            num_scalar_prefetch=1,
            grid=(slabs + pairs,),
            in_specs=[
                narrow,
                narrow,
                narrow,
                narrow,
                wide,
                wide,
                whole_spec((2, model)),
                adapter_spec((2, rank, model)),
                whole_spec((width, model)),
                whole_spec((rank, width)),
                whole_spec((slabs, chunk)),
                cols(rows),
                cols(length),
                cols(length),
                cols(rows),
                pl.BlockSpec(
                    (1, slabs, 2 * chunk), lambda p, s: (lax.max(p - slabs, 0), 0, 0)
                ),
                cols(rows),
                cols(length),
                whole_spec((length, LANES)),
                whole_spec((length, LANES)),
                cols(1),
            ],
            out_specs=[o_[2] for o_ in out],
            scratch_shapes=[
                pltpu.VMEM((LANES, length), bf16),
                pltpu.VMEM((slabs, LANES, 2 * chunk), f32),
                pltpu.VMEM((rows, model), bf16),
                pltpu.VMEM((rows, width), bf16),
                pltpu.VMEM((rank, rows), bf16),
                pltpu.VMEM((rows, rank), bf16),
            ],
        ),
        out_shape=[jax.ShapeDtypeStruct(o_[0], o_[1]) for o_ in out],
        compiler_params=params(),
        cost_estimate=cost(3e10, 4e7),
        name="attend_back",
    )(
        place, res, gm, go, h_own, am, ao, rates, bm, wout, ah, start, q, k, v, o, inv, qi, ki,
        cos, sin, scale,
    )


def apart(blocks):
    none = jnp.zeros_like(blocks[0])
    return jnp.concatenate(
        [
            jnp.concatenate([b if n == m else none for n in range(len(blocks))], axis=1)
            for m, b in enumerate(blocks)
        ],
        axis=0,
    )


def others_kernel(
    place, gk_ref, gv_ref, wk_ref, wv_ref, a_ref, b_ref, keep_ref, send_ref, low_ref
):
    rows, width = keep_ref.shape[1], gk_ref.shape[-1]
    half = keep_ref.shape[2]
    rank = b_ref.shape[1]
    both = jnp.concatenate(
        [gk_ref[...].reshape(rows, width), gv_ref[...].reshape(rows, width)], axis=1
    )
    turn = pl.program_id(1)

    @pl.when(turn == 0)
    def _():
        low_ref[...] = nt(both, apart([b_ref[1], b_ref[2]])).astype(bf16)

    weights = jnp.concatenate([wk_ref[0], wv_ref[0]], axis=1)
    part = nt(both, weights) + nn(low_ref[...], a_ref[0, 1:3].reshape(2 * rank, half))

    @pl.when(turn == 0)
    def _():
        send_ref[0] = part.astype(bf16)

    @pl.when(turn == 1)
    def _():
        keep_ref[0] = part.astype(bf16)


def half_weight(half, width, member):
    return pl.BlockSpec(
        (1, half, width), lambda *a: (member, lax.rem(a[-1][2] + 1 + a[-2], 2), 0)
    )


def half_factors(rank, half):
    return pl.BlockSpec(
        (1, 5, rank, half), lambda *a: (a[-1][4], 0, 0, lax.rem(a[-1][2] + 1 + a[-2], 2))
    )


def run_others(place, gk, gv, w, a, b, slabs, group):
    length, width = gk.shape
    chunk = length // (slabs * group)
    rows = slabs * chunk
    half = w.shape[1] // 2
    rank = b.shape[1]
    shaped = (slabs, group, chunk, width)
    peer = pl.BlockSpec(
        (slabs, 1, chunk, width), lambda g, t, s: (0, lax.rem(s[0] + 1 + g, group), 0, 0)
    )
    return pl.pallas_call(
        others_kernel,
        grid_spec=pltpu.PrefetchScalarGridSpec(
            num_scalar_prefetch=1,
            grid=(group - 1, 2),
            in_specs=[
                peer,
                peer,
                half_weight(half, width, 1),
                half_weight(half, width, 2),
                half_factors(rank, half),
                whole_spec((3, rank, width)),
            ],
            out_specs=[pl.BlockSpec((1, rows, half), lambda g, t, s: (g, 0, 0))] * 2,
            scratch_shapes=[pltpu.VMEM((rows, 2 * rank), bf16)],
        ),
        out_shape=[
            jax.ShapeDtypeStruct((group - 1, rows, half), bf16),
            jax.ShapeDtypeStruct((group - 1, rows, half), bf16),
        ],
        compiler_params=params(),
        cost_estimate=cost(7e9, 1e7),
        name="others",
    )(place, gk.reshape(shaped), gv.reshape(shaped), w, w, a, b)


def own_kernel(
    place, gq_ref, gk_ref, gv_ref, wq_ref, wk_ref, wv_ref, a_ref, b_ref, res_ref, keep_ref,
    send_ref, low_ref,
):
    rows, width = gq_ref.shape
    half = keep_ref.shape[1]
    rank = b_ref.shape[1]
    grads = jnp.concatenate(
        [gq_ref[...], gk_ref[...].reshape(rows, width), gv_ref[...].reshape(rows, width)], axis=1
    )
    turn = pl.program_id(0)

    @pl.when(turn == 0)
    def _():
        low_ref[...] = nt(grads, apart([b_ref[0], b_ref[1], b_ref[2]])).astype(bf16)

    weights = jnp.concatenate([wq_ref[0], wk_ref[0], wv_ref[0]], axis=1)
    part = nt(grads, weights) + nn(low_ref[...], a_ref[0, 0:3].reshape(3 * rank, half))

    @pl.when(turn == 0)
    def _():
        send_ref[...] = part.astype(bf16)

    @pl.when(turn == 1)
    def _():
        keep_ref[...] = (part + res_ref[...]).astype(bf16)


def run_own(place, gq, gk, gv, w, a, b, res, slabs, group):
    length, width = gk.shape
    rows, model = res.shape
    chunk = rows // slabs
    half = model // 2
    rank = b.shape[1]
    shaped = (slabs, group, chunk, width)
    peer = pl.BlockSpec((slabs, 1, chunk, width), lambda t, s: (0, s[0], 0, 0))
    out = [((rows, half), bf16), ((rows, half), bf16)]
    return pl.pallas_call(
        own_kernel,
        grid_spec=pltpu.PrefetchScalarGridSpec(
            num_scalar_prefetch=1,
            grid=(2,),
            in_specs=[
                whole_spec((rows, width)),
                peer,
                peer,
                half_weight(half, width, 0),
                half_weight(half, width, 1),
                half_weight(half, width, 2),
                half_factors(rank, half),
                whole_spec((3, rank, width)),
                pl.BlockSpec((rows, half), lambda t, s: (0, s[2])),
            ],
            out_specs=[whole_spec(o[0]) for o in out],
            scratch_shapes=[pltpu.VMEM((rows, 3 * rank), bf16)],
        ),
        out_shape=[jax.ShapeDtypeStruct(o[0], o[1]) for o in out],
        compiler_params=params(True),
        cost_estimate=cost(7e9, 1e7),
        name="own",
    )(place, gq, gk.reshape(shaped), gv.reshape(shaped), w, w, w, a, b, res)


def grads_kernel(
    dims, place, gq_ref, gk_ref, gv_ref, b_ref, u_ref, h_ref, gbo_ref, gah_ref, table_ref,
    uq_ref, low_ref,
):
    slabs, chunk, group, n_seq, rank, model, head_dim = dims
    inner = place[0]
    width = gq_ref.shape[1]
    heads = width // head_dim
    gq = gq_ref[...]
    both = jnp.concatenate([gk_ref[...], gv_ref[...]], axis=1)
    low_q = nt(gq, b_ref[0]).astype(bf16)
    low_ref[:, : 2 * rank] = nt(both, apart([b_ref[1], b_ref[2]])).astype(bf16)
    low_ref[:, 2 * rank :] = jnp.zeros((low_ref.shape[0], rank), bf16)
    for m in range(slabs):
        there = at_rows(m * group + inner, chunk)
        uq_ref[m * chunk : (m + 1) * chunk, :] = u_ref[there, :]
        low_ref[there, 2 * rank :] = low_q[m * chunk : (m + 1) * chunk]
    products = nn(low_ref[...].T, h_ref[...])
    model_rows = jnp.concatenate(
        [products[2 * rank :], products[: 2 * rank], gbo_ref[...]], axis=0
    ).astype(bf16).astype(f32)
    uqt = uq_ref[...].T
    pair = nn(u_ref[...].T[rank:], both)
    head_rows = jnp.concatenate(
        [gah_ref[...], nn(uqt[:rank], gq), pair[:rank, :width], pair[rank:, width:]], axis=0
    ).astype(bf16)
    owners = n_seq * slabs * group
    cols = model // owners
    each = head_dim // owners
    units = heads * each
    spots = lax.broadcasted_iota(i32, (width, 1), 0)
    owner = spots // units
    inside = spots % units
    source = inside // each * head_dim + owner * each + inside % each
    moved = jnp.where(lane_iota((width, width)) == source, 1.0, 0.0).astype(bf16)
    turned = nt(moved, head_rows)
    for y in range(group):
        for z in range(slabs):
            for x in range(n_seq):
                d = owner_index((y, z, x), group, slabs, n_seq)
                left = model_rows[:, d * cols : (d + 1) * cols]
                heads_part = turned[d * units : (d + 1) * units]
                right = jnp.concatenate(
                    [heads_part[:, rank:], pad_to(heads_part[:, :rank], 3 * rank)], axis=0
                )
                tall = late_rows(rank, units)
                packed = jnp.concatenate(
                    [
                        jnp.pad(left, ((0, tall - left.shape[0]), (0, 0))),
                        jnp.pad(right, ((0, tall - right.shape[0]), (0, 0))),
                    ],
                    axis=1,
                )
                packed = pad_to(packed, LANES)
                table_ref[y, z, x] = fold(packed, table_ref.shape[4] // LANES).astype(bf16)


def run_grads(place, gq, gk, gv, b, u, h, gbo, gah, slabs, group, n_seq, head_dim):
    length, width = gk.shape
    rows, model = gq.shape[0], h.shape[1]
    chunk = rows // slabs
    rank = b.shape[1]
    heads = width // head_dim
    owners = n_seq * slabs * group
    units = heads * (head_dim // owners)
    half = model // 2
    shape = (group, slabs, n_seq, folded_rows(late_rows(rank, units), half // LANES), half)
    operands = (gq, gk, gv, b, u, h, gbo, gah)
    return pl.pallas_call(
        functools.partial(grads_kernel, (slabs, chunk, group, n_seq, rank, model, head_dim)),
        grid_spec=pltpu.PrefetchScalarGridSpec(
            num_scalar_prefetch=1,
            grid=(1,),
            in_specs=[whole_spec(operand.shape) for operand in operands],
            out_specs=whole_spec(shape),
            scratch_shapes=[
                pltpu.VMEM((rows, 3 * rank), bf16),
                pltpu.VMEM((length, 3 * rank), bf16),
            ],
        ),
        out_shape=jax.ShapeDtypeStruct(shape, bf16),
        compiler_params=params(True),
        cost_estimate=cost(1e10, 1e7),
        name="grads",
    )(place, *operands)


def join_kernel(slabs, place, *refs):
    out_ref = refs[-1]
    chunk, half = out_ref.shape[1], refs[0].shape[-1]
    core, slab = place[2], place[1]
    for shift in range(slabs):
        source = lax.rem(slab - shift + slabs, slabs)
        for which, ref in ((core, refs[shift]), (1 - core, refs[slabs + shift])):
            out_ref[source, :, pl.ds(pl.multiple_of(which * half, half), half)] = ref[
                :chunk, :
            ].astype(out_ref.dtype)


def run_join(place, mine, other, chunk, dtype):
    slabs = len(mine)
    half = mine[0].shape[1]
    return pl.pallas_call(
        functools.partial(join_kernel, slabs),
        grid_spec=pltpu.PrefetchScalarGridSpec(
            num_scalar_prefetch=1,
            grid=(1,),
            in_specs=[whole_spec(piece.shape) for piece in (*mine, *other)],
            out_specs=whole_spec((slabs, chunk, 2 * half)),
        ),
        out_shape=jax.ShapeDtypeStruct((slabs, chunk, 2 * half), dtype),
        compiler_params=params(True),
        cost_estimate=cost(1e6, 8e6),
        name="join",
    )(place, *mine, *other)


def for_tables(where, place, index, refs, put):
    n_seq, slabs, chunk, size = where
    home, home_other = refs[:slabs], refs[slabs : 2 * slabs]
    far, far_other = refs[2 * slabs : 2 * slabs + n_seq - 1], refs[2 * slabs + n_seq - 1 :]
    for r in range(slabs):
        at = pl.ds(pl.multiple_of(chunk + place[3] * size, 8), size)
        put(index[0, r], unfold(home[r][at, :]), unfold(home_other[r][at, :]))
    for s in range(1, n_seq):

        def one(r, carry, s=s):
            put(index[s, r], unfold(far[s - 1][r]), unfold(far_other[s - 1][r]))
            return carry

        lax.fori_loop(0, slabs, one, 0)


def unpack_early_kernel(dims, where, place, index, *refs):
    rank, cols, each, hidden_rows, tiles = dims
    am_ref, bm_ref, ad_ref, bd_ref = refs[-4:]
    core = place[2]

    def put(adapter, block, other):
        both = block[: 2 * rank] + other[: 2 * rank]
        am = jnp.where(core == 0, both[:, : cols // 2], both[:, cols // 2 : cols])
        am_ref[adapter] = am.reshape(2, rank, cols // 2)
        bm_ref[adapter] = block[2 * rank : 3 * rank, :cols]
        base = 3 * rank
        wide = jnp.concatenate(
            [block[base + t * each : base + (t + 1) * each] for t in range(tiles)], axis=1
        )
        for k in range(rank):
            ad_ref[adapter, k] = wide[:, k * hidden_rows : (k + 1) * hidden_rows]
        for j in range(2):
            for k in range(rank):
                at = ((j + 1) * rank + k) * hidden_rows
                bd_ref[adapter, j, k] = wide[:, at : at + hidden_rows]

    for_tables(where, place, index, refs[:-4], put)


def unpack_late_kernel(dims, where, place, index, *refs):
    rank, cols, heads, each = dims
    am_gu_ref, bm_down_ref, am_ref, bm_ref, ah_ref, bh_ref = refs[-6:]
    core = place[2]

    def put(adapter, block, other):
        both = block[: 3 * rank] + other[: 3 * rank]
        am = jnp.where(core == 0, both[:, : cols // 2], both[:, cols // 2 : cols])
        am_ref[adapter, 0:3] = am.reshape(3, rank, cols // 2)
        am_ref[adapter, 3:5] = am_gu_ref[adapter]
        bm_ref[adapter, 0] = block[3 * rank : 4 * rank, :cols]
        bm_ref[adapter, 1] = bm_down_ref[adapter]
        units = heads * each
        for n in range(heads):
            at = n * each
            ah_ref[adapter, n] = block[units + at : units + at + each, cols : cols + rank]
            for j in range(3):
                lanes = slice(cols + j * rank, cols + (j + 1) * rank)
                bh_ref[adapter, j, n] = block[at : at + each, lanes]

    for_tables(where, place, index, refs[:-6], put)


def run_unpack(kernel, dims, where, place, index, tables, extra, shapes, name):
    operands = [*tables, *extra]
    return pl.pallas_call(
        functools.partial(kernel, dims, where),
        grid_spec=pltpu.PrefetchScalarGridSpec(
            num_scalar_prefetch=2,
            grid=(1,),
            in_specs=[whole_spec(operand.shape) for operand in operands],
            out_specs=[whole_spec(shape) for shape in shapes],
        ),
        out_shape=[jax.ShapeDtypeStruct(shape, f32) for shape in shapes],
        compiler_params=params(True),
        cost_estimate=cost(1e6, 8e6),
        name=name,
    )(place, index, *operands)


def pick(array, index):
    return lax.dynamic_index_in_dim(array, index, 0, keepdims=False)


def body(
    tokens, segments, adapter_index, w_attn_in, w_attn_out, w_gate_up, w_down, qk_scale,
    mix_rates, mlp_scales, a_model, b_model, a_heads, b_heads, a_hidden, b_hidden, cotangent,
):
    slabs, chunk, model = tokens.shape
    n_seq = lax.axis_size("seq")
    n_ctx = lax.axis_size("ctx")
    group = n_ctx // slabs
    local_width = w_attn_out.shape[0]
    head_dim = a_heads.shape[-1]
    row_width = a_hidden.shape[-1]
    local_hidden = w_down.shape[0]
    local_heads = local_width // head_dim
    rank = a_model.shape[2]
    adapters = a_model.shape[0]
    half = model // 2
    ctx_place = lax.axis_index("ctx")
    slab = ctx_place // group
    inner = ctx_place % group
    core = lax.axis_index("wt")
    seq_place = lax.axis_index("seq")
    owners = n_seq * n_ctx
    rows = slabs * chunk
    length = rows * group
    place = jnp.stack([inner, slab, core, seq_place, pick(adapter_index, slab)]).astype(i32)
    a_heads = jnp.transpose(a_heads, (0, 2, 1, 3))
    b_heads = jnp.transpose(b_heads, (0, 1, 3, 2, 4))
    a_hidden = jnp.transpose(a_hidden, (0, 2, 1, 3))
    b_hidden = jnp.transpose(b_hidden, (0, 1, 3, 2, 4))

    def to_slab(array, shift):
        pairs = [(c, (c + shift * group) % n_ctx) for c in range(n_ctx)]
        return lax.ppermute(array, "ctx", pairs)

    def within_slab(array, shift):
        pairs = [(c, c - c % group + (c % group + shift) % group) for c in range(n_ctx)]
        return lax.ppermute(array, "ctx", pairs)

    def to_seq(array, shift):
        return lax.ppermute(array, "seq", [(c, (c + shift) % n_seq) for c in range(n_seq)])

    def other_core(array):
        return lax.ppermute(array, "wt", [(0, 1), (1, 0)])

    def half_piece(array, index, which):
        return lax.dynamic_slice(array, (index, 0, which * half), (1, chunk, half))[0]

    def token_piece(index):
        seg = jnp.pad(pick(segments, index).astype(bf16), (0, half - chunk))
        return jnp.concatenate(
            [half_piece(tokens, index, core), jnp.broadcast_to(seg, (8, half))], axis=0
        )

    tie = lax.optimization_barrier

    spot = (jnp.arange(LANES, dtype=i32) % (head_dim // 2)).astype(f32)
    frequency = 10000.0 ** (-spot / (head_dim // 2))
    turn = jnp.arange(length, dtype=i32).astype(f32)[:, None] * frequency[None, :]
    cos = jnp.cos(turn)
    lower = jnp.arange(LANES) % head_dim < head_dim // 2
    sin = jnp.sin(turn) * jnp.where(lower, -1.0, 1.0)[None, :]
    scale = qk_scale[None, :]

    own_piece = token_piece(slab)
    got = [own_piece] + [
        to_slab(token_piece((slab + shift) % slabs), shift) for shift in range(1, slabs)
    ]
    index = [adapter_index]
    for shift in range(1, n_seq):
        index.append(to_seq(adapter_index, shift))
    got, cos, sin, place, index = tie((got, cos, sin, place, index))
    near = [within_slab(own_piece, turn) for turn in range(1, group)]
    g_send = [half_piece(cotangent, (slab + shift) % slabs, core) for shift in range(1, slabs)]
    rest, near, g_send = tie((jnp.stack(got[1:]), near, g_send))
    rest_other = other_core(rest)
    peers = [within_slab(rest, turn) for turn in range(1, group)]
    g_mine = [to_slab(g_send[shift - 1], shift) for shift in range(1, slabs)]
    peers, g_mine[0], g_mine[-1] = tie((peers, g_mine[0], g_mine[-1]))
    pieces = [own_piece, rest, rest_other]
    for turn in range(1, group):
        pieces += [
            near[turn - 1], other_core(near[turn - 1]),
            peers[turn - 1], other_core(peers[turn - 1]),
        ]
    h_full, h_own, u, q, k, v, qi, ki, o, inv, attn_msg, start, bh, ah = run_attend(
        place, tokens, pieces, w_attn_in, a_model, b_heads, a_heads, cos, sin, scale,
        w_attn_out, group, head_dim,
    )
    g_mine, attn_msg = tie((g_mine, attn_msg))
    attn_other = other_core(attn_msg)
    g_mine, attn_msg = tie((jnp.stack(g_mine), attn_msg))
    g_mine, attn_other = tie((g_mine, attn_other))
    g_other = other_core(g_mine)
    mid, u_gu, gate, up, down_msg = run_feed(
        place, attn_msg, pltpu.with_memory_space_constraint(attn_other, pltpu.VMEM), h_own,
        b_model, mix_rates, a_model, w_gate_up, b_hidden,
        w_down, a_hidden, mlp_scales, 512, slabs,
    )
    g_other, down_msg = tie((g_other, down_msg))
    down_other = pltpu.with_memory_space_constraint(other_core(down_msg), pltpu.VMEM)
    out_half, mid_res, mid_msg, early = run_feed_back(
        place, down_msg, down_other, mid, cotangent, g_mine, g_other, b_model, mix_rates,
        a_model, u_gu, gate, up, w_gate_up, b_hidden, w_down, a_hidden, mlp_scales, 512, group,
        n_seq,
    )
    mid_other = pltpu.with_memory_space_constraint(other_core(mid_msg), pltpu.VMEM)

    order = (slab - jnp.arange(slabs, dtype=i32)) % slabs
    index = jnp.stack(index)[:, order]

    def sum_inner(table):
        return pick(table, inner), [
            within_slab(pick(table, (inner + turn) % group), turn) for turn in range(1, group)
        ]

    def add_inner(own, got):
        total = own.astype(f32)
        for piece in got:
            total = total + piece.astype(f32)
        return total.astype(bf16)

    def over_slabs(total):
        return [pick(total, slab)] + [
            to_slab(pick(total, (slab + shift) % slabs), shift) for shift in range(1, slabs)
        ]

    def pack(rows_part, table):
        return jnp.concatenate([rows_part, table.reshape(slabs, -1, half)], axis=1)

    early_size = early.shape[3]
    early_own, early_got = sum_inner(early)
    gq, gk, gv, h_res, gbo, gah = run_attend_back(
        place, mid_res, mid_msg, mid_other, h_own, attn_msg, attn_other, mix_rates, b_model,
        w_attn_out, ah, start, q, k, v, o, inv, qi, ki, cos, sin, scale, slabs, group,
        head_dim,
    )
    early_got, gk, gv = tie((early_got, gk, gv))
    keep, send = run_others(place, gk, gv, w_attn_in, a_model, bh, slabs, group)
    others = (keep.astype(f32) + other_core(send).astype(f32)).astype(bf16)
    others, gq, gk, gv = tie((others, gq, gk, gv))
    waves = [[2, 1], [3, 0]] if slabs == 4 else [list(range(slabs))]
    others = others.reshape(group - 1, slabs, chunk, half)
    others_got = []
    for wave in waves:
        if others_got:
            others_got[-1], others = tie((others_got[-1], others))
        others_got.append(
            [
                within_slab(
                    jnp.stack(
                        [pick(others[turn - 1], (slab + shift) % slabs) for shift in wave]
                    ),
                    turn,
                )
                for turn in range(1, group)
            ]
        )
    home = over_slabs(pack(out_half, add_inner(early_own, early_got)))
    late = run_grads(
        place, gq, gk, gv, bh, u, h_full, gbo, gah, slabs, group, n_seq, head_dim
    )
    late_own, late_got = sum_inner(late)
    late_own, gq, home, others_got[0] = tie((late_own, gq, home, others_got[0]))
    home_other = [other_core(piece) for piece in home]
    early_far = []
    for shift in range(1, n_seq):
        at = chunk + (seq_place + shift) % n_seq * early_size
        sent = [lax.dynamic_slice_in_dim(piece, at, early_size, 0) for piece in home]
        early_far.append(to_seq(jnp.stack(sent), shift))
    own_keep, own_send = run_own(
        place, gq, gk, gv, w_attn_in, a_model, bh, h_res, slabs, group
    )
    late_got, early_far, own_send, others_got = tie(
        (late_got, early_far, own_send, others_got)
    )
    own_got = other_core(own_send)
    late_total = add_inner(late_own, late_got)
    own_sum = (own_keep.astype(f32) + own_got.astype(f32)).reshape(slabs, chunk, half)
    size = late.shape[3]
    result = [None] * slabs
    for wave, got_wave in zip(waves, others_got):
        for n, shift in enumerate(wave):
            target = (slab + shift) % slabs
            total = pick(own_sum, target)
            for got_part in got_wave:
                total = total + got_part[n].astype(f32)
            result[shift] = jnp.concatenate(
                [total.astype(bf16), pick(late_total, target).reshape(n_seq * size, half)],
                axis=0,
            )
    result, home, home_other, early_far = tie((result, home, home_other, early_far))
    result = result[:1] + [to_slab(result[shift], shift) for shift in range(1, slabs)]
    early_tables = [*home, *home_other, *early_far, *(other_core(t) for t in early_far)]
    layer_out = run_join(place, home, home_other, chunk, bf16)
    cols = model // owners
    each = row_width // owners
    hidden_rows = local_hidden // row_width
    grad_am_gu, grad_bm_down, grad_ad, grad_bd = run_unpack(
        unpack_early_kernel,
        (rank, cols, each, hidden_rows, (3 * rank * hidden_rows + LANES - 1) // LANES),
        (n_seq, slabs, chunk, early_size),
        place, index, early_tables, [],
        [
            (adapters, 2, rank, cols // 2),
            (adapters, rank, cols),
            (adapters, rank, each, hidden_rows),
            (adapters, 2, rank, each, hidden_rows),
        ],
        "unpack_early",
    )
    result, layer_out, grad_am_gu, grad_bm_down = tie(
        (result, layer_out, grad_am_gu, grad_bm_down)
    )
    result_other = [other_core(piece) for piece in result]
    far = []
    for shift in range(1, n_seq):
        at = chunk + (seq_place + shift) % n_seq * size
        sent = [lax.dynamic_slice_in_dim(piece, at, size, 0) for piece in result]
        far.append(to_seq(jnp.stack(sent), shift))
    input_grad = run_join(place, result, result_other, chunk, f32)
    far, input_grad = tie((far, input_grad))
    each = head_dim // owners
    grad_am, grad_bm, grad_ah, grad_bh = run_unpack(
        unpack_late_kernel,
        (rank, cols, local_heads, each),
        (n_seq, slabs, chunk, size),
        place, index, [*result, *result_other, *far, *(other_core(piece) for piece in far)],
        [grad_am_gu, grad_bm_down],
        [
            (adapters, 5, rank, cols // 2),
            (adapters, 2, rank, cols),
            (adapters, local_heads, each, rank),
            (adapters, 3, local_heads, each, rank),
        ],
        "unpack_late",
    )
    return (
        layer_out,
        input_grad,
        grad_am,
        grad_bm,
        jnp.transpose(grad_ah, (0, 3, 1, 2)),
        jnp.transpose(grad_bh, (0, 1, 4, 2, 3)),
        jnp.transpose(grad_ad, (0, 1, 3, 2)),
        jnp.transpose(grad_bd, (0, 1, 2, 4, 3)),
    )


def solution(mesh):
    return jax.shard_map(
        body,
        mesh=mesh,
        in_specs=(
            P("seq", "ctx", None),
            P("seq", "ctx"),
            P("seq"),
            P(None, None, "wt"),
            P("wt", None),
            P(None, None, "wt"),
            P("wt", None),
            P("wt"),
            P(),
            P(None, "wt"),
            P(),
            P(),
            P(None, None, "wt", None),
            P(None, None, None, "wt", None),
            P(None, None, "wt", None),
            P(None, None, None, "wt", None),
            P("seq", "ctx", None),
        ),
        out_specs=(
            P("seq", "ctx", None),
            P("seq", "ctx", None),
            P(None, None, None, ("seq", "ctx", "wt")),
            P(None, None, None, ("seq", "ctx")),
            P(None, None, "wt", ("seq", "ctx")),
            P(None, None, None, "wt", ("seq", "ctx")),
            P(None, None, "wt", ("seq", "ctx")),
            P(None, None, None, "wt", ("seq", "ctx")),
        ),
        check_vma=False,
    )
```

```python
import functools

import jax
import jax.numpy as jnp
from jax import lax
from jax.experimental import pallas as pl
from jax.experimental.pallas import tpu as pltpu
from jax.sharding import PartitionSpec as P

epsilon = 1e-06
f32 = jnp.float32
bf16 = jnp.bfloat16
i32 = jnp.int32
VMEM_LIMIT = 58 * 1024 * 1024
SMALL_LIMIT = 24 * 1024 * 1024
log2e = 1.4426950408889634
LANES = 128


def dot(left, right, contract):
    return lax.dot_general(left, right, (contract, ((), ())), preferred_element_type=f32)


def nn(left, right):
    return dot(left, right, ((1,), (0,)))


def nt(left, right):
    return dot(left, right, ((1,), (1,)))


def tn(left, right):
    return dot(left, right, ((0,), (0,)))


def lane_iota(shape):
    return lax.broadcasted_iota(i32, shape, len(shape) - 1)


def row_iota(shape):
    return lax.broadcasted_iota(i32, shape, 0)


def row_mean(values):
    return jnp.mean(values, axis=-1, keepdims=True)


def inverse_rms(values):
    return lax.rsqrt(row_mean(values * values) + epsilon)


def at_rows(index, size):
    return pl.ds(pl.multiple_of(index * size, size), size)


def by_rows(total, size, step):
    lax.fori_loop(0, total // size, lambda i, c: (step(at_rows(i, size)), c)[1], 0)


def swap_halves(tile, half):
    lower = lane_iota(tile.shape) % (2 * half) < half
    return jnp.where(lower, pltpu.roll(tile, LANES - half, 1), pltpu.roll(tile, half, 1))


def head_sums(tile, head_dim):
    same = row_iota((LANES, LANES)) // head_dim == lane_iota((LANES, LANES)) // head_dim
    ones = jnp.where(same, 1.0, 0.0).astype(bf16)
    return nn(tile.astype(bf16), ones)


def prep_tile(raw, cosine, sine, scale, head_dim):
    mean = head_sums(raw * raw, head_dim) * (1.0 / head_dim)
    inverse = lax.rsqrt(mean + epsilon)
    turned = raw * cosine + swap_halves(raw, head_dim // 2) * sine
    return (turned * inverse * scale).astype(bf16), inverse.astype(bf16)


def prep_tile_back(grad, low, inverse, cosine, sine, scale, head_dim):
    unit = low.astype(f32) / scale
    grad_unit = grad * scale
    mean = head_sums(grad_unit * unit, head_dim) * (1.0 / head_dim)
    grad_turned = inverse.astype(f32) * (grad_unit - unit * mean)
    return (grad_turned * cosine - swap_halves(grad_turned, head_dim // 2) * sine).astype(bf16)


def spread_pair(tile, head_dim):
    lower = lane_iota(tile.shape) < head_dim
    zero = jnp.zeros_like(tile)
    return jnp.concatenate([jnp.where(lower, tile, zero), jnp.where(lower, zero, tile)], axis=0)


def allowed_mask(first, last, key_start, rows, diagonal):
    keys = key_start + row_iota((rows, first.shape[1]))
    mask = keys >= first
    if diagonal:
        mask = mask & (keys <= last)
    return mask


def query_bounds(start_ref, m, place, group, chunk):
    first = start_ref[m : m + 1, :]
    last = (m * group + place) * chunk + lane_iota((1, chunk))
    return jnp.concatenate([first, first], axis=1), jnp.concatenate([last, last], axis=1)


def whole_spec(shape, buffers=1):
    return pl.BlockSpec(
        shape, lambda *a: (0,) * len(shape), pipeline_mode=pl.Buffered(buffers)
    )


def col_spec(size, width=LANES, skip=0):
    return pl.BlockSpec((size, width), lambda p, s: (0, lax.max(p - skip, 0)))


def row_spec(size, width, last):
    return pl.BlockSpec((size, width), lambda p, s: (lax.min(p, last), 0))


def adapter_spec(shape):
    return pl.BlockSpec(
        (1,) + shape, lambda p, s: (s[4],) + (0,) * len(shape), pipeline_mode=pl.Buffered(1)
    )


def params(small=False, limit=None):
    limit = limit or (SMALL_LIMIT if small else VMEM_LIMIT)
    return pltpu.CompilerParams(vmem_limit_bytes=limit)


def near_last(out, place):
    return [
        pltpu.VMEM(o[0], o[1]) if n == place else jax.ShapeDtypeStruct(o[0], o[1])
        for n, o in enumerate(out)
    ]


def cost(flops, moved, transcendentals=0):
    return pl.CostEstimate(
        flops=int(flops), bytes_accessed=int(moved), transcendentals=int(transcendentals)
    )


def attend_kernel(dims, place, *refs):
    slabs, chunk, group, head_dim, rank, half = dims
    count = 4 + (group - 1) * 4
    pieces = refs[:count]
    (
        wq_ref, w_ref, a_ref, b_table, a_table, cos_ref, sin_ref, scale_ref, wout_ref,
        hout_ref, ownout_ref, u_ref, q_ref, k_ref, v_ref, qi_ref, ki_ref, o_ref, inv_ref,
        msg_ref, start_ref, b_ref, ah_ref, first_ref, all_ref, seg_ref, h_ref, own_ref, raw_ref,
    ) = refs[count:]
    inner, slab, core = place[0], place[1], place[2]
    block = group * chunk
    length = slabs * block
    rows = slabs * chunk
    model = 2 * half
    step = pl.program_id(0)

    @pl.when(step == 0)
    def _():
        mine = pl.ds(pl.multiple_of(core * half, half), half)
        other = pl.ds(pl.multiple_of((1 - core) * half, half), half)
        h_ref[at_rows(slab * group + inner, chunk), :] = pieces[0][0]
        seg_ref[...] = jnp.zeros_like(seg_ref)

        def keep_segments(where, piece):
            tail = piece[chunk:, :chunk].astype(f32)
            seg_ref[pl.ds(where, 1), :] = tail[0:1]

        keep_segments(slab * group + inner, pieces[1])

        def place_piece(shift, peer, ours, theirs):
            source = lax.rem(slab - shift + slabs, slabs)
            rows_at = at_rows(source * group + peer, chunk)
            h_ref[rows_at, mine] = ours[:chunk, :]
            h_ref[rows_at, other] = theirs[:chunk, :]
            keep_segments(source * group + peer, ours)

        for shift in range(1, slabs):
            place_piece(shift, inner, pieces[2].at[shift - 1], pieces[3].at[shift - 1])
        for turn in range(1, group):
            peer = lax.rem(inner - turn + group, group)
            near, near_other, rest, rest_other = pieces[4 * turn : 4 * turn + 4]
            place_piece(0, peer, near, near_other)
            for shift in range(1, slabs):
                place_piece(shift, peer, rest.at[shift - 1], rest_other.at[shift - 1])
        for m in range(slabs):
            own_ref[m * chunk : (m + 1) * chunk, :] = h_ref[
                at_rows(m * group + inner, chunk), :
            ]
        columns = seg_ref[...].T
        for m in range(slabs):
            line = seg_ref[pl.ds(m * group + inner, 1), :]
            below = jnp.zeros((chunk, chunk), f32)
            for c in range(slabs * group):
                below = below + jnp.where(columns[:, c : c + 1] < line, 1.0, 0.0)
            count = jnp.sum(below, axis=0, keepdims=True)
            start_ref[m : m + 1, :] = count.astype(i32)
            first_ref[m * chunk : (m + 1) * chunk, :] = (
                jnp.broadcast_to(count, (LANES, chunk)).T.astype(i32)
            )

        for n in range(b_ref.shape[2] // head_dim):
            cols = slice(n * head_dim, (n + 1) * head_dim)
            b_ref[:, :, cols] = b_table[0, :, n]
            ah_ref[:, cols] = a_table[0, n]
        down = a_ref[0, :3].reshape(3 * rank, model)

        def low_rows(sl):
            u_ref[sl, :] = nt(h_ref[sl, :], down).astype(bf16)

        by_rows(length, 512, low_rows)
        for m in range(slabs):
            low = u_ref[at_rows(m * group + inner, chunk), :rank]
            own = slice(m * chunk, (m + 1) * chunk)
            raw_ref[own, :] = nn(low, b_ref[0])
        raw_ref[...] += nn(own_ref[...], wq_ref[0])

    last_block = lax.min(step, slabs - 1)
    hout_ref[...] = h_ref[at_rows(last_block, block), :]
    ownout_ref[...] = own_ref[at_rows(last_block, chunk), :]
    here = pl.ds(pl.multiple_of(step * LANES, LANES), LANES)
    scale = scale_ref[...]
    w_kv = jnp.concatenate([w_ref[0], w_ref[1]], axis=1)
    none = jnp.zeros((rank, LANES), bf16)
    b_kv = jnp.concatenate(
        [
            jnp.zeros((rank, 2 * LANES), bf16),
            jnp.concatenate([b_ref[1, :, here], none], axis=1),
            jnp.concatenate([none, b_ref[2, :, here]], axis=1),
        ],
        axis=0,
    )

    def keys_rows(sl):
        both = nn(h_ref[sl, :], w_kv) + nn(u_ref[sl, :], b_kv)
        k_ref[sl, :], ki_ref[sl, :] = prep_tile(
            both[:, :LANES], cos_ref[sl, :], sin_ref[sl, :], scale, head_dim
        )
        v_ref[sl, :] = both[:, LANES:].astype(bf16)

    by_rows(length, 512, keys_rows)
    for m in range(slabs):
        own = slice(m * chunk, (m + 1) * chunk)
        there = at_rows(m * group + inner, chunk)
        q_ref[own, :], qi_ref[own, :] = prep_tile(
            raw_ref[own, here], cos_ref[there, :], sin_ref[there, :], scale, head_dim
        )
    ones = jnp.ones((block, LANES), bf16)
    left = lane_iota((chunk, LANES)) < head_dim
    for m in range(slabs):
        own = slice(m * chunk, (m + 1) * chunk)
        pair = spread_pair(q_ref[own, :], head_dim)
        first = first_ref[own, :]
        first = jnp.concatenate([first] * (block // LANES), axis=1)
        first = jnp.concatenate([first, first], axis=0)
        gathered = jnp.zeros((2 * chunk, 2 * LANES), f32)
        for b in range(m + 1):
            at = slice(b * block, (b + 1) * block)
            scores = nt(pair, k_ref[at, :])
            keys = b * block + lane_iota(scores.shape)
            mask = keys >= first
            if b == m:
                queries = lax.rem(row_iota(scores.shape), chunk)
                mask = mask & (keys <= queries + (m * group + inner) * chunk)
            weights = jnp.where(mask, jnp.exp2(scores * (0.125 * log2e)), 0.0).astype(bf16)
            gathered = gathered + nn(weights, jnp.concatenate([v_ref[at, :], ones], axis=1))
        inverse = 1.0 / gathered[:, LANES:]
        final = gathered[:, :LANES] * inverse
        final = jnp.where(left, final[:chunk], final[chunk:]).astype(bf16)
        o_ref[own, :] = final
        all_ref[own, here] = final
        inv_ref[0, m : m + 1, :] = inverse.T[0:1, :]

    @pl.when(step == pl.num_programs(0) - 1)
    def _():
        low_o = all_ref[...]
        msg_ref[:, :model] = nn(low_o, wout_ref[...]).astype(bf16)
        msg_ref[:, model:] = pad_to(nt(low_o, ah_ref[...]), LANES).astype(bf16)


def run_attend(place, tokens, pieces, w, a, b, ah, cos, sin, scale, wout, group, head_dim):
    slabs, chunk, model = tokens.shape
    width = w.shape[2]
    rank = a.shape[2]
    half = model // 2
    rows = slabs * chunk
    length = rows * group
    pairs = width // LANES
    in_specs = [pl.BlockSpec((1, chunk, model), lambda p, s: (s[1], 0, 0))]
    in_specs += [whole_spec(piece.shape) for piece in pieces]
    in_specs += [
        whole_spec((1, model, width)),
        pl.BlockSpec(
            (pl.Element(2), pl.Element(model), pl.Element(LANES)),
            lambda p, s: (1, 0, p * LANES),
        ),
        adapter_spec((5, rank, model)),
        adapter_spec(b.shape[1:]),
        adapter_spec(ah.shape[1:]),
        whole_spec((length, LANES)),
        whole_spec((length, LANES)),
        col_spec(1),
        whole_spec((width, model)),
    ]
    def step_rows(size):
        return pl.BlockSpec((size, model), lambda p, s: (lax.min(p, slabs - 1), 0))

    out = [
        ((length, model), bf16, step_rows(group * chunk)),
        ((rows, model), bf16, step_rows(chunk)),
        ((length, 3 * rank), bf16, whole_spec((length, 3 * rank))),
        ((rows, width), bf16, col_spec(rows)),
        ((length, width), bf16, col_spec(length)),
        ((length, width), bf16, col_spec(length)),
        ((rows, width), bf16, col_spec(rows)),
        ((length, width), bf16, col_spec(length)),
        ((rows, width), bf16, col_spec(rows)),
        (
            (pairs, slabs, 2 * chunk),
            f32,
            pl.BlockSpec((1, slabs, 2 * chunk), lambda p, s: (p, 0, 0)),
        ),
        ((rows, model + LANES), bf16, whole_spec((rows, model + LANES))),
        ((slabs, chunk), i32, whole_spec((slabs, chunk))),
        ((3, rank, width), bf16, whole_spec((3, rank, width))),
        ((rank, width), bf16, whole_spec((rank, width))),
    ]
    return pl.pallas_call(
        functools.partial(attend_kernel, (slabs, chunk, group, head_dim, rank, half)),
        grid_spec=pltpu.PrefetchScalarGridSpec(
            num_scalar_prefetch=1,
            grid=(pairs,),
            in_specs=in_specs,
            out_specs=[o[2] for o in out],
            scratch_shapes=[
                pltpu.VMEM((rows, LANES), i32),
                pltpu.VMEM((rows, width), bf16),
                pltpu.VMEM((chunk, chunk), f32),
                pltpu.VMEM((length, model), bf16),
                pltpu.VMEM((rows, model), bf16),
                pltpu.VMEM((rows, width), f32),
            ],
        ),
        out_shape=[jax.ShapeDtypeStruct(o[0], o[1]) for o in out],
        compiler_params=params(),
        cost_estimate=cost(1e8, 1e5),
        name="attend",
    )(place, tokens, *pieces, w, w, a, b, ah, cos, sin, scale, wout)


def join_tiles(ref, *at):
    block = ref[at]
    return jnp.concatenate([block[t] for t in range(block.shape[0])], axis=1)


def feed_kernel(
    dims, place, mine_ref, other_ref, h_ref, bo_ref, rate_ref, a_ref, wgu_ref, bgu_ref, wd_ref,
    ad_ref, scales_ref, mid_ref, u_ref, gate_ref, up_ref, msg_ref, low_ref, acc_ref,
):
    rank, model, slabs = dims
    chunk = h_ref.shape[0]
    step = pl.program_id(0)

    @pl.when(step < slabs)
    def _():
        both = mine_ref[...].astype(f32) + other_ref[...].astype(f32)
        low = both[:, model : model + rank].astype(bf16)
        raw = both[:, :model] + nn(low, bo_ref[0, 0])
        unit = raw * inverse_rms(raw)
        state = h_ref[...].astype(f32)
        mixed = state + rate_ref[0:1, :] * (unit - state)
        mixed = (mixed * inverse_rms(mixed)).astype(bf16)
        mid_ref[...] = mixed
        here = at_rows(step, chunk)
        low_ref[here, :] = mixed
        down = a_ref[0, 3:5].reshape(2 * rank, model)
        u_ref[here, :] = nt(mixed, down).astype(bf16)
        acc_ref[here, :] = jnp.zeros((chunk, model + LANES), f32)

    @pl.when(step >= slabs)
    def _():
        low = low_ref[...]
        u = u_ref[...]
        gate = nn(low, wgu_ref[0]) + nn(u[:, :rank], join_tiles(bgu_ref, 0, 0))
        up = nn(low, wgu_ref[1]) + nn(u[:, rank:], join_tiles(bgu_ref, 0, 1))
        gate_ref[...] = gate.astype(bf16)
        up_ref[...] = up.astype(bf16)
        turned = gate * scales_ref[1:2, :]
        hidden = (up * scales_ref[0:1, :] * (turned / (1.0 + jnp.exp(-turned)))).astype(bf16)
        acc_ref[:, :model] += nn(hidden, wd_ref[...])
        acc_ref[:, model : model + rank] += nt(hidden, join_tiles(ad_ref, 0))

    @pl.when(step == pl.num_programs(0) - 1)
    def _():
        msg_ref[...] = acc_ref[...].astype(bf16)


def hidden_specs(skip, model, rank, block, row_width):
    tiles = block // row_width
    at = lambda f: lax.max(f - skip, 0)
    return [
        pl.BlockSpec((2, model, block), lambda f, s: (0, 0, at(f))),
        pl.BlockSpec((1, 2, tiles, rank, row_width), lambda f, s: (s[4], 0, at(f), 0, 0)),
        pl.BlockSpec((block, model), lambda f, s: (at(f), 0)),
        pl.BlockSpec((1, tiles, rank, row_width), lambda f, s: (s[4], at(f), 0, 0)),
        pl.BlockSpec((2, block), lambda f, s: (0, at(f))),
    ]


def run_feed(place, mine, other, h_own, bm, rates, a, wgu, bgu, wd, ad, scales, block, slabs):
    rows, model = h_own.shape
    chunk = rows // slabs
    hidden = wd.shape[0]
    rank = a.shape[2]
    last = slabs - 1
    out = [
        ((rows, model), bf16, row_spec(chunk, model, last)),
        ((rows, 2 * rank), bf16, whole_spec((rows, 2 * rank))),
        ((rows, hidden), bf16, col_spec(rows, block, slabs)),
        ((rows, hidden), bf16, col_spec(rows, block, slabs)),
        ((rows, model + LANES), bf16, whole_spec((rows, model + LANES))),
    ]
    return pl.pallas_call(
        functools.partial(feed_kernel, (rank, model, slabs)),
        grid_spec=pltpu.PrefetchScalarGridSpec(
            num_scalar_prefetch=1,
            grid=(slabs + hidden // block,),
            in_specs=[
                row_spec(chunk, model + LANES, last),
                row_spec(chunk, model + LANES, last),
                row_spec(chunk, model, last),
                adapter_spec((2, rank, model)),
                whole_spec((2, model)),
                adapter_spec((5, rank, model)),
            ]
            + hidden_specs(slabs, model, rank, block, ad.shape[3]),
            out_specs=[o[2] for o in out],
            scratch_shapes=[
                pltpu.VMEM((rows, model), bf16),
                pltpu.VMEM((rows, model + LANES), f32),
            ],
        ),
        out_shape=near_last(out, 4),
        compiler_params=params(),
        cost_estimate=cost(2.4e10, 3e7),
        name="feed",
    )(place, mine, other, h_own, bm, rates, a, wgu, bgu, wd, ad, scales)


def owner_index(place, group, slabs, n_seq):
    inner, slab, seq = place
    return seq * slabs * group + slab * group + inner


def pad_to(tile, lanes):
    return jnp.pad(tile, ((0, 0), (0, lanes - tile.shape[1])))


def late_rows(rank, units):
    return max(4 * rank, 2 * units)


def folded_rows(rows, groups):
    return (rows + groups * 8 - 1) // (groups * 8) * 8


def fold(tile, groups):
    size = folded_rows(tile.shape[0], groups)
    tile = jnp.pad(tile, ((0, size * groups - tile.shape[0]), (0, 0)))
    return jnp.concatenate([tile[g * size : (g + 1) * size] for g in range(groups)], axis=1)


def unfold(block):
    groups = block.shape[1] // LANES
    return jnp.concatenate(
        [block[:, g * LANES : (g + 1) * LANES] for g in range(groups)], axis=0
    ).astype(f32)


def feed_back_kernel(
    dims, place, mine_ref, other_ref, mid_ref, g_own_ref, g_mine_ref, g_other_ref, bd_ref,
    rate_ref, a_ref, u_ref, gate_ref, up_ref, wgu_ref, bgu_ref, wd_ref, ad_ref, scales_ref,
    out_ref, res_ref, msg_ref, table_ref,
    gd_ref, gdt_ref, ut_ref, udt_ref, gud_ref, gudt_ref, low_ref, acc_ref, gu_ref, hid_ref,
    g_ref, lo_ref,
):
    slabs, chunk, group, n_seq, rank, model, row_width, hidden_rows = dims
    half = model // 2
    step = pl.program_id(0)
    slab, core = place[1], place[2]
    block = gate_ref.shape[1]

    @pl.when(step < slabs)
    def _():
        mine = pl.ds(pl.multiple_of(core * half, half), half)
        other = pl.ds(pl.multiple_of((1 - core) * half, half), half)
        shift = lax.rem(slab - step + slabs, slabs)

        @pl.when(shift == 0)
        def _():
            g_ref[...] = g_own_ref[0]

        @pl.when(shift > 0)
        def _():
            g_ref[:, mine] = g_mine_ref[shift - 1]
            g_ref[:, other] = g_other_ref[shift - 1]

        here = at_rows(step, chunk)
        both = mine_ref[...].astype(f32) + other_ref[...].astype(f32)
        low = both[:, model : model + rank].astype(bf16)
        hid_ref[here, :] = low
        raw = both[:, :model] + nn(low, bd_ref[0, 1])
        raw_inv = inverse_rms(raw)
        unit = raw * raw_inv
        state = mid_ref[...]
        low_ref[here, :] = state
        state = state.astype(f32)
        rate = rate_ref[1:2, :]
        mixed = state + rate * (unit - state)
        mixed_inv = inverse_rms(mixed)
        out = mixed * mixed_inv
        lo_ref[...] = out.astype(bf16)
        grad = g_ref[...].astype(f32)
        grad_mixed = mixed_inv * (grad - out * row_mean(grad * out))
        res_ref[...] = (1.0 - rate) * grad_mixed
        grad_unit = rate * grad_mixed
        gd_ref[here, :] = (raw_inv * (grad_unit - unit * row_mean(grad_unit * unit))).astype(bf16)
        out_ref[0] = lo_ref[:, mine]
        acc_ref[here, :] = jnp.zeros((chunk, model), f32)
        gu_ref[here, :] = jnp.zeros((chunk, 2 * rank), f32)

    @pl.when(step == slabs)
    def _():
        ut_ref[...] = u_ref[...].T
        udt_ref[...] = hid_ref[...].T
        low_gud = nt(gd_ref[...], bd_ref[0, 1]).astype(bf16)
        gud_ref[...] = low_gud
        gudt_ref[...] = low_gud.T

    @pl.when(step >= slabs)
    def _():
        grad_hidden = nt(gd_ref[...], wd_ref[...]) + nn(gud_ref[...], join_tiles(ad_ref, 0))
        gate = gate_ref[...].astype(f32)
        up = up_ref[...].astype(f32)
        up_scale = scales_ref[0:1, :]
        gate_scale = scales_ref[1:2, :]
        turned = gate * gate_scale
        sigmoid = 1.0 / (1.0 + jnp.exp(-turned))
        silu = turned * sigmoid
        up_scaled = up * up_scale
        hidden = (up_scaled * silu).astype(bf16)
        grad_up = (grad_hidden * up_scale * silu).astype(bf16)
        slope = sigmoid * (1.0 + turned * (1.0 - sigmoid)) * gate_scale
        grad_gate = (grad_hidden * up_scaled * slope).astype(bf16)
        acc_ref[...] += nt(grad_gate, wgu_ref[0]) + nt(grad_up, wgu_ref[1])
        gu_ref[:, :rank] += nt(grad_gate, join_tiles(bgu_ref, 0, 0))
        gu_ref[:, rank:] += nt(grad_up, join_tiles(bgu_ref, 0, 1))
        ut = ut_ref[...]
        parts = jnp.concatenate(
            [nn(gudt_ref[...], hidden), nn(ut[:rank], grad_gate), nn(ut[rank:], grad_up)], axis=0
        ).astype(bf16)
        tiles = block // row_width
        for tile in range(tiles):
            gdt_ref[(step - slabs) * tiles + tile] = parts[
                :, tile * row_width : (tile + 1) * row_width
            ]

    @pl.when(step == pl.num_programs(0) - 1)
    def _():
        low_gu = gu_ref[...].astype(bf16)
        down = a_ref[0, 3:5].reshape(2 * rank, model)
        msg_ref[...] = (acc_ref[...] + nn(low_gu, down)).astype(bf16)
        low = low_ref[...]
        model_rows = jnp.concatenate(
            [nn(low_gu.T, low), nn(udt_ref[...], gd_ref[...])], axis=0
        ).astype(bf16).astype(f32)
        ranks = 3 * rank
        units = ranks * hidden_rows
        padded = (units + LANES - 1) // LANES * LANES
        flat = gdt_ref[...].reshape(units, row_width)
        lanes = lane_iota((1, padded))
        target = lanes % hidden_rows * ranks + lanes // hidden_rows
        target = jnp.where(lanes < units, target, -1)
        moved = jnp.where(row_iota((units, padded)) == target, 1.0, 0.0).astype(bf16)
        turned_rows = tn(flat, moved)
        owners = n_seq * slabs * group
        cols = model // owners
        units_each = row_width // owners
        for y in range(group):
            for z in range(slabs):
                for x in range(n_seq):
                    d = owner_index((y, z, x), group, slabs, n_seq)
                    head = pad_to(model_rows[:, d * cols : (d + 1) * cols], LANES)
                    mine = turned_rows[d * units_each : (d + 1) * units_each]
                    tail = [
                        mine[:, t * LANES : (t + 1) * LANES] for t in range(padded // LANES)
                    ]
                    packed = jnp.concatenate([head] + tail, axis=0)
                    table_ref[y, z, x] = fold(packed, half // LANES).astype(bf16)


def run_feed_back(
    place, mine, other, mid, cotangent, g_mine, g_other, bm, rates, a, u, gate, up, wgu, bgu,
    wd, ad, scales, block, group, n_seq,
):
    slabs, chunk, model = cotangent.shape
    rows = slabs * chunk
    half = model // 2
    hidden = wd.shape[0]
    rank = a.shape[2]
    row_width = ad.shape[3]
    last = slabs - 1
    hidden_rows = hidden // row_width
    owners = n_seq * slabs * group
    padded = (3 * rank * hidden_rows + LANES - 1) // LANES * LANES
    table_rows = 3 * rank + row_width // owners * (padded // LANES)
    table = (group, slabs, n_seq, folded_rows(table_rows, half // LANES), half)
    out = [
        (
            (slabs, chunk, half),
            bf16,
            pl.BlockSpec((1, chunk, half), lambda f, s: (lax.min(f, last), 0, 0)),
        ),
        ((rows, model), f32, row_spec(chunk, model, last)),
        ((rows, model), bf16, whole_spec((rows, model))),
        (table, bf16, whole_spec(table)),
    ]
    return pl.pallas_call(
        functools.partial(
            feed_back_kernel,
            (slabs, chunk, group, n_seq, rank, model, row_width, hidden_rows),
        ),
        grid_spec=pltpu.PrefetchScalarGridSpec(
            num_scalar_prefetch=1,
            grid=(slabs + hidden // block,),
            in_specs=[
                row_spec(chunk, model + LANES, last),
                row_spec(chunk, model + LANES, last),
                row_spec(chunk, model, last),
                pl.BlockSpec(
                    (1, chunk, model), lambda f, s: (s[1], 0, 0), pipeline_mode=pl.Buffered(1)
                ),
                whole_spec((slabs - 1, chunk, half)),
                whole_spec((slabs - 1, chunk, half)),
                adapter_spec((2, rank, model)),
                whole_spec((2, model)),
                adapter_spec((5, rank, model)),
                whole_spec((rows, 2 * rank)),
                col_spec(rows, block, slabs),
                col_spec(rows, block, slabs),
            ]
            + hidden_specs(slabs, model, rank, block, row_width),
            out_specs=[o[2] for o in out],
            scratch_shapes=[
                pltpu.VMEM((rows, model), bf16),
                pltpu.VMEM((hidden_rows, 3 * rank, row_width), bf16),
                pltpu.VMEM((2 * rank, rows), bf16),
                pltpu.VMEM((rank, rows), bf16),
                pltpu.VMEM((rows, rank), bf16),
                pltpu.VMEM((rank, rows), bf16),
                pltpu.VMEM((rows, model), bf16),
                pltpu.VMEM((rows, model), f32),
                pltpu.VMEM((rows, 2 * rank), f32),
                pltpu.VMEM((rows, rank), bf16),
                pltpu.VMEM((chunk, model), bf16),
                pltpu.VMEM((chunk, model), bf16),
            ],
        ),
        out_shape=near_last(out, 2),
        compiler_params=params(),
        cost_estimate=cost(3e10, 4e7),
        name="feed_back",
    )(
        place, mine, other, mid, cotangent, g_mine, g_other, bm, rates, a, u, gate, up, wgu,
        bgu, wd, ad, scales,
    )


def attend_back_kernel(
    dims, place, res_ref, gm_ref, go_ref, h_ref, am_ref, ao_ref, rate_ref, bo_ref, wout_ref,
    ah_ref, start_ref, q_ref, k_ref, v_ref, o_ref, inv_ref, qi_ref, ki_ref, cos_ref, sin_ref,
    scale_ref,
    gq_ref, gk_ref, gv_ref, gres_ref, gbo_ref, gah_ref,
    kt_ref, gqt_ref, ga_ref, go_all_ref, guot_ref, uo_ref,
):
    slabs, chunk, group, head_dim, rank, model = dims
    inner = place[0]
    step = pl.program_id(0)

    @pl.when(step < slabs)
    def _():
        here = at_rows(step, chunk)
        grad = res_ref[...] + gm_ref[...].astype(f32) + go_ref[...].astype(f32)
        both = am_ref[...].astype(f32) + ao_ref[...].astype(f32)
        low = both[:, model : model + rank].astype(bf16)
        uo_ref[here, :] = low
        raw = both[:, :model] + nn(low, bo_ref[0, 0])
        raw_inv = inverse_rms(raw)
        unit = raw * raw_inv
        state = h_ref[...].astype(f32)
        rate = rate_ref[0:1, :]
        mixed = state + rate * (unit - state)
        mixed_inv = inverse_rms(mixed)
        out = mixed * mixed_inv
        grad_mixed = mixed_inv * (grad - out * row_mean(grad * out))
        gres_ref[...] = (1.0 - rate) * grad_mixed
        grad_unit = rate * grad_mixed
        ga_ref[here, :] = (raw_inv * (grad_unit - unit * row_mean(grad_unit * unit))).astype(bf16)

    @pl.when(step == slabs)
    def _():
        gbo_ref[...] = nn(uo_ref[...].T, ga_ref[...])
        low_g = nt(ga_ref[...], bo_ref[0, 0]).astype(bf16)
        guot_ref[...] = low_g.T
        go_all_ref[...] = (nt(ga_ref[...], wout_ref[...]) + nn(low_g, ah_ref[...])).astype(bf16)

    @pl.when(step >= slabs)
    def _():
        attend_back_pair(
            dims, inner, step - slabs, start_ref, q_ref, k_ref, v_ref, o_ref, inv_ref,
            qi_ref, ki_ref, cos_ref, sin_ref, scale_ref, gq_ref, gk_ref, gv_ref, gah_ref,
            kt_ref, gqt_ref, go_all_ref, guot_ref,
        )


def attend_back_pair(
    dims, inner, turn, start_ref, q_ref, k_ref, v_ref, o_ref, inv_ref, qi_ref, ki_ref,
    cos_ref, sin_ref, scale_ref, gq_ref, gk_ref, gv_ref, gah_ref, kt_ref, gqt_ref,
    go_all_ref, guot_ref,
):
    slabs, chunk, group, head_dim, rank, model = dims
    block = group * chunk
    kt_ref[...] = k_ref[...].T
    scale = scale_ref[...]
    grad_o = go_all_ref[:, pl.ds(pl.multiple_of(turn * LANES, LANES), LANES)]
    gah_ref[...] = nn(guot_ref[...], o_ref[...])
    pairs_q, pairs_g, deltas, bounds = [], [], [], []
    for m in range(slabs):
        own = slice(m * chunk, (m + 1) * chunk)
        pairs_q.append(spread_pair(q_ref[own, :], head_dim))
        grad = grad_o[own]
        pairs_g.append(spread_pair(grad, head_dim))
        products = (grad.astype(f32) * o_ref[own, :].astype(f32)).T
        deltas.append(
            jnp.concatenate(
                [
                    jnp.sum(products[:head_dim], axis=0, keepdims=True),
                    jnp.sum(products[head_dim:], axis=0, keepdims=True),
                ],
                axis=1,
            )
        )
        bounds.append(query_bounds(start_ref, m, inner, group, chunk))
    for b in range(slabs):
        at = slice(b * block, (b + 1) * block)
        grad_key = jnp.zeros((block, LANES), f32)
        grad_value = jnp.zeros((block, LANES), f32)
        for m in range(b, slabs):
            first, last = bounds[m]
            scores = nt(k_ref[at, :], pairs_q[m])
            mask = allowed_mask(first, last, b * block, block, b == m)
            weights = jnp.exp2(scores * (0.125 * log2e)) * inv_ref[0, m : m + 1, :]
            weights = jnp.where(mask, weights, 0.0)
            grad_value = grad_value + nn(weights.astype(bf16), pairs_g[m])
            grad_weights = nt(v_ref[at, :], pairs_g[m])
            grad_scores = (weights * (grad_weights - deltas[m])).astype(bf16)
            grad_key = grad_key + nn(grad_scores, pairs_q[m])
            part = nn(kt_ref[:, at], grad_scores)
            if b == 0:
                gqt_ref[m] = part
            else:
                gqt_ref[m] += part
        gv_ref[at, :] = grad_value.astype(bf16)
        gk_ref[at, :] = prep_tile_back(
            grad_key * 0.125, k_ref[at, :], ki_ref[at, :], cos_ref[at, :], sin_ref[at, :],
            scale, head_dim,
        )
    upper = row_iota((LANES, chunk)) < head_dim
    for m in range(slabs):
        own = slice(m * chunk, (m + 1) * chunk)
        both = gqt_ref[m]
        grad = jnp.where(upper, both[:, :chunk], both[:, chunk:]).T * 0.125
        there = at_rows(m * group + inner, chunk)
        gq_ref[own, :] = prep_tile_back(
            grad, q_ref[own, :], qi_ref[own, :], cos_ref[there, :], sin_ref[there, :],
            scale, head_dim,
        )


def run_attend_back(
    place, res, gm, go, h_own, am, ao, rates, bm, wout, ah, start, q, k, v, o, inv, qi, ki, cos, sin, scale, slabs, group, head_dim,
):
    rows, model = h_own.shape
    chunk = rows // slabs
    width = q.shape[1]
    length = k.shape[0]
    rank = bm.shape[2]
    pairs = width // LANES
    last = slabs - 1
    wide = row_spec(chunk, model + LANES, last)
    narrow = row_spec(chunk, model, last)
    cols = lambda size: col_spec(size, LANES, slabs)
    out = [
        ((rows, width), bf16, cols(rows)),
        ((length, width), bf16, cols(length)),
        ((length, width), bf16, cols(length)),
        ((rows, model), f32, narrow),
        ((rank, model), f32, whole_spec((rank, model))),
        ((rank, width), f32, cols(rank)),
    ]
    return pl.pallas_call(
        functools.partial(attend_back_kernel, (slabs, chunk, group, head_dim, rank, model)),
        grid_spec=pltpu.PrefetchScalarGridSpec(
            num_scalar_prefetch=1,
            grid=(slabs + pairs,),
            in_specs=[
                narrow,
                narrow,
                narrow,
                narrow,
                wide,
                wide,
                whole_spec((2, model)),
                adapter_spec((2, rank, model)),
                whole_spec((width, model)),
                whole_spec((rank, width)),
                whole_spec((slabs, chunk)),
                cols(rows),
                cols(length),
                cols(length),
                cols(rows),
                pl.BlockSpec(
                    (1, slabs, 2 * chunk), lambda p, s: (lax.max(p - slabs, 0), 0, 0)
                ),
                cols(rows),
                cols(length),
                whole_spec((length, LANES)),
                whole_spec((length, LANES)),
                cols(1),
            ],
            out_specs=[o_[2] for o_ in out],
            scratch_shapes=[
                pltpu.VMEM((LANES, length), bf16),
                pltpu.VMEM((slabs, LANES, 2 * chunk), f32),
                pltpu.VMEM((rows, model), bf16),
                pltpu.VMEM((rows, width), bf16),
                pltpu.VMEM((rank, rows), bf16),
                pltpu.VMEM((rows, rank), bf16),
            ],
        ),
        out_shape=[jax.ShapeDtypeStruct(o_[0], o_[1]) for o_ in out],
        compiler_params=params(),
        cost_estimate=cost(3e10, 4e7),
        name="attend_back",
    )(
        place, res, gm, go, h_own, am, ao, rates, bm, wout, ah, start, q, k, v, o, inv, qi, ki,
        cos, sin, scale,
    )


def apart(blocks):
    none = jnp.zeros_like(blocks[0])
    return jnp.concatenate(
        [
            jnp.concatenate([b if n == m else none for n in range(len(blocks))], axis=1)
            for m, b in enumerate(blocks)
        ],
        axis=0,
    )


def others_kernel(
    place, gk_ref, gv_ref, wk_ref, wv_ref, a_ref, b_ref, keep_ref, send_ref, low_ref
):
    rows, width = keep_ref.shape[1], gk_ref.shape[-1]
    half = keep_ref.shape[2]
    rank = b_ref.shape[1]
    both = jnp.concatenate(
        [gk_ref[...].reshape(rows, width), gv_ref[...].reshape(rows, width)], axis=1
    )
    turn = pl.program_id(1)

    @pl.when(turn == 0)
    def _():
        low_ref[...] = nt(both, apart([b_ref[1], b_ref[2]])).astype(bf16)

    weights = jnp.concatenate([wk_ref[0], wv_ref[0]], axis=1)
    part = nt(both, weights) + nn(low_ref[...], a_ref[0, 1:3].reshape(2 * rank, half))

    @pl.when(turn == 0)
    def _():
        send_ref[0] = part.astype(bf16)

    @pl.when(turn == 1)
    def _():
        keep_ref[0] = part.astype(bf16)


def half_weight(half, width, member):
    return pl.BlockSpec(
        (1, half, width), lambda *a: (member, lax.rem(a[-1][2] + 1 + a[-2], 2), 0)
    )


def half_factors(rank, half):
    return pl.BlockSpec(
        (1, 5, rank, half), lambda *a: (a[-1][4], 0, 0, lax.rem(a[-1][2] + 1 + a[-2], 2))
    )


def run_others(place, gk, gv, w, a, b, slabs, group):
    length, width = gk.shape
    chunk = length // (slabs * group)
    rows = slabs * chunk
    half = w.shape[1] // 2
    rank = b.shape[1]
    shaped = (slabs, group, chunk, width)
    peer = pl.BlockSpec(
        (slabs, 1, chunk, width), lambda g, t, s: (0, lax.rem(s[0] + 1 + g, group), 0, 0)
    )
    return pl.pallas_call(
        others_kernel,
        grid_spec=pltpu.PrefetchScalarGridSpec(
            num_scalar_prefetch=1,
            grid=(group - 1, 2),
            in_specs=[
                peer,
                peer,
                half_weight(half, width, 1),
                half_weight(half, width, 2),
                half_factors(rank, half),
                whole_spec((3, rank, width)),
            ],
            out_specs=[pl.BlockSpec((1, rows, half), lambda g, t, s: (g, 0, 0))] * 2,
            scratch_shapes=[pltpu.VMEM((rows, 2 * rank), bf16)],
        ),
        out_shape=[
            jax.ShapeDtypeStruct((group - 1, rows, half), bf16),
            jax.ShapeDtypeStruct((group - 1, rows, half), bf16),
        ],
        compiler_params=params(),
        cost_estimate=cost(7e9, 1e7),
        name="others",
    )(place, gk.reshape(shaped), gv.reshape(shaped), w, w, a, b)


def own_kernel(
    place, gq_ref, gk_ref, gv_ref, wq_ref, wk_ref, wv_ref, a_ref, b_ref, res_ref, keep_ref,
    send_ref, low_ref,
):
    rows, width = gq_ref.shape
    half = keep_ref.shape[1]
    rank = b_ref.shape[1]
    grads = jnp.concatenate(
        [gq_ref[...], gk_ref[...].reshape(rows, width), gv_ref[...].reshape(rows, width)], axis=1
    )
    turn = pl.program_id(0)

    @pl.when(turn == 0)
    def _():
        low_ref[...] = nt(grads, apart([b_ref[0], b_ref[1], b_ref[2]])).astype(bf16)

    weights = jnp.concatenate([wq_ref[0], wk_ref[0], wv_ref[0]], axis=1)
    part = nt(grads, weights) + nn(low_ref[...], a_ref[0, 0:3].reshape(3 * rank, half))

    @pl.when(turn == 0)
    def _():
        send_ref[...] = part.astype(bf16)

    @pl.when(turn == 1)
    def _():
        keep_ref[...] = (part + res_ref[...]).astype(bf16)


def run_own(place, gq, gk, gv, w, a, b, res, slabs, group):
    length, width = gk.shape
    rows, model = res.shape
    chunk = rows // slabs
    half = model // 2
    rank = b.shape[1]
    shaped = (slabs, group, chunk, width)
    peer = pl.BlockSpec((slabs, 1, chunk, width), lambda t, s: (0, s[0], 0, 0))
    out = [((rows, half), bf16), ((rows, half), bf16)]
    return pl.pallas_call(
        own_kernel,
        grid_spec=pltpu.PrefetchScalarGridSpec(
            num_scalar_prefetch=1,
            grid=(2,),
            in_specs=[
                whole_spec((rows, width)),
                peer,
                peer,
                half_weight(half, width, 0),
                half_weight(half, width, 1),
                half_weight(half, width, 2),
                half_factors(rank, half),
                whole_spec((3, rank, width)),
                pl.BlockSpec((rows, half), lambda t, s: (0, s[2])),
            ],
            out_specs=[whole_spec(o[0]) for o in out],
            scratch_shapes=[pltpu.VMEM((rows, 3 * rank), bf16)],
        ),
        out_shape=[jax.ShapeDtypeStruct(o[0], o[1]) for o in out],
        compiler_params=params(True),
        cost_estimate=cost(7e9, 1e7),
        name="own",
    )(place, gq, gk.reshape(shaped), gv.reshape(shaped), w, w, w, a, b, res)


def grads_kernel(
    dims, place, gq_ref, gk_ref, gv_ref, b_ref, u_ref, h_ref, gbo_ref, gah_ref, table_ref,
    uq_ref, low_ref,
):
    slabs, chunk, group, n_seq, rank, model, head_dim = dims
    inner = place[0]
    width = gq_ref.shape[1]
    heads = width // head_dim
    gq = gq_ref[...]
    both = jnp.concatenate([gk_ref[...], gv_ref[...]], axis=1)
    low_q = nt(gq, b_ref[0]).astype(bf16)
    low_ref[:, : 2 * rank] = nt(both, apart([b_ref[1], b_ref[2]])).astype(bf16)
    low_ref[:, 2 * rank :] = jnp.zeros((low_ref.shape[0], rank), bf16)
    for m in range(slabs):
        there = at_rows(m * group + inner, chunk)
        uq_ref[m * chunk : (m + 1) * chunk, :] = u_ref[there, :]
        low_ref[there, 2 * rank :] = low_q[m * chunk : (m + 1) * chunk]
    products = nn(low_ref[...].T, h_ref[...])
    model_rows = jnp.concatenate(
        [products[2 * rank :], products[: 2 * rank], gbo_ref[...]], axis=0
    ).astype(bf16).astype(f32)
    uqt = uq_ref[...].T
    pair = nn(u_ref[...].T[rank:], both)
    head_rows = jnp.concatenate(
        [gah_ref[...], nn(uqt[:rank], gq), pair[:rank, :width], pair[rank:, width:]], axis=0
    ).astype(bf16)
    owners = n_seq * slabs * group
    cols = model // owners
    each = head_dim // owners
    units = heads * each
    spots = lax.broadcasted_iota(i32, (width, 1), 0)
    owner = spots // units
    inside = spots % units
    source = inside // each * head_dim + owner * each + inside % each
    moved = jnp.where(lane_iota((width, width)) == source, 1.0, 0.0).astype(bf16)
    turned = nt(moved, head_rows)
    for y in range(group):
        for z in range(slabs):
            for x in range(n_seq):
                d = owner_index((y, z, x), group, slabs, n_seq)
                left = model_rows[:, d * cols : (d + 1) * cols]
                heads_part = turned[d * units : (d + 1) * units]
                right = jnp.concatenate(
                    [heads_part[:, rank:], pad_to(heads_part[:, :rank], 3 * rank)], axis=0
                )
                tall = late_rows(rank, units)
                packed = jnp.concatenate(
                    [
                        jnp.pad(left, ((0, tall - left.shape[0]), (0, 0))),
                        jnp.pad(right, ((0, tall - right.shape[0]), (0, 0))),
                    ],
                    axis=1,
                )
                packed = pad_to(packed, LANES)
                table_ref[y, z, x] = fold(packed, table_ref.shape[4] // LANES).astype(bf16)


def run_grads(place, gq, gk, gv, b, u, h, gbo, gah, slabs, group, n_seq, head_dim):
    length, width = gk.shape
    rows, model = gq.shape[0], h.shape[1]
    chunk = rows // slabs
    rank = b.shape[1]
    heads = width // head_dim
    owners = n_seq * slabs * group
    units = heads * (head_dim // owners)
    half = model // 2
    shape = (group, slabs, n_seq, folded_rows(late_rows(rank, units), half // LANES), half)
    operands = (gq, gk, gv, b, u, h, gbo, gah)
    return pl.pallas_call(
        functools.partial(grads_kernel, (slabs, chunk, group, n_seq, rank, model, head_dim)),
        grid_spec=pltpu.PrefetchScalarGridSpec(
            num_scalar_prefetch=1,
            grid=(1,),
            in_specs=[whole_spec(operand.shape) for operand in operands],
            out_specs=whole_spec(shape),
            scratch_shapes=[
                pltpu.VMEM((rows, 3 * rank), bf16),
                pltpu.VMEM((length, 3 * rank), bf16),
            ],
        ),
        out_shape=jax.ShapeDtypeStruct(shape, bf16),
        compiler_params=params(True),
        cost_estimate=cost(1e10, 1e7),
        name="grads",
    )(place, *operands)


def join_kernel(slabs, place, *refs):
    out_ref = refs[-1]
    chunk, half = out_ref.shape[1], refs[0].shape[-1]
    core, slab = place[2], place[1]
    for shift in range(slabs):
        source = lax.rem(slab - shift + slabs, slabs)
        for which, ref in ((core, refs[shift]), (1 - core, refs[slabs + shift])):
            out_ref[source, :, pl.ds(pl.multiple_of(which * half, half), half)] = ref[
                :chunk, :
            ].astype(out_ref.dtype)


def run_join(place, mine, other, chunk, dtype):
    slabs = len(mine)
    half = mine[0].shape[1]
    return pl.pallas_call(
        functools.partial(join_kernel, slabs),
        grid_spec=pltpu.PrefetchScalarGridSpec(
            num_scalar_prefetch=1,
            grid=(1,),
            in_specs=[whole_spec(piece.shape) for piece in (*mine, *other)],
            out_specs=whole_spec((slabs, chunk, 2 * half)),
        ),
        out_shape=jax.ShapeDtypeStruct((slabs, chunk, 2 * half), dtype),
        compiler_params=params(True),
        cost_estimate=cost(1e6, 8e6),
        name="join",
    )(place, *mine, *other)


def for_tables(where, place, index, refs, put):
    n_seq, slabs, chunk, size = where
    home, home_other = refs[:slabs], refs[slabs : 2 * slabs]
    far, far_other = refs[2 * slabs : 2 * slabs + n_seq - 1], refs[2 * slabs + n_seq - 1 :]
    for r in range(slabs):
        at = pl.ds(pl.multiple_of(chunk + place[3] * size, 8), size)
        put(index[0, r], unfold(home[r][at, :]), unfold(home_other[r][at, :]))
    for s in range(1, n_seq):

        def one(r, carry, s=s):
            put(index[s, r], unfold(far[s - 1][r]), unfold(far_other[s - 1][r]))
            return carry

        lax.fori_loop(0, slabs, one, 0)


def unpack_early_kernel(dims, where, place, index, *refs):
    rank, cols, each, hidden_rows, tiles = dims
    am_ref, bm_ref, ad_ref, bd_ref = refs[-4:]
    core = place[2]

    def put(adapter, block, other):
        both = block[: 2 * rank] + other[: 2 * rank]
        am = jnp.where(core == 0, both[:, : cols // 2], both[:, cols // 2 : cols])
        am_ref[adapter] = am.reshape(2, rank, cols // 2)
        bm_ref[adapter] = block[2 * rank : 3 * rank, :cols]
        base = 3 * rank
        wide = jnp.concatenate(
            [block[base + t * each : base + (t + 1) * each] for t in range(tiles)], axis=1
        )
        for k in range(rank):
            ad_ref[adapter, k] = wide[:, k * hidden_rows : (k + 1) * hidden_rows]
        for j in range(2):
            for k in range(rank):
                at = ((j + 1) * rank + k) * hidden_rows
                bd_ref[adapter, j, k] = wide[:, at : at + hidden_rows]

    for_tables(where, place, index, refs[:-4], put)


def unpack_late_kernel(dims, where, place, index, *refs):
    rank, cols, heads, each = dims
    am_gu_ref, bm_down_ref, am_ref, bm_ref, ah_ref, bh_ref = refs[-6:]
    core = place[2]

    def put(adapter, block, other):
        both = block[: 3 * rank] + other[: 3 * rank]
        am = jnp.where(core == 0, both[:, : cols // 2], both[:, cols // 2 : cols])
        am_ref[adapter, 0:3] = am.reshape(3, rank, cols // 2)
        am_ref[adapter, 3:5] = am_gu_ref[adapter]
        bm_ref[adapter, 0] = block[3 * rank : 4 * rank, :cols]
        bm_ref[adapter, 1] = bm_down_ref[adapter]
        units = heads * each
        for n in range(heads):
            at = n * each
            ah_ref[adapter, n] = block[units + at : units + at + each, cols : cols + rank]
            for j in range(3):
                lanes = slice(cols + j * rank, cols + (j + 1) * rank)
                bh_ref[adapter, j, n] = block[at : at + each, lanes]

    for_tables(where, place, index, refs[:-6], put)


def run_unpack(kernel, dims, where, place, index, tables, extra, shapes, name):
    operands = [*tables, *extra]
    return pl.pallas_call(
        functools.partial(kernel, dims, where),
        grid_spec=pltpu.PrefetchScalarGridSpec(
            num_scalar_prefetch=2,
            grid=(1,),
            in_specs=[whole_spec(operand.shape) for operand in operands],
            out_specs=[whole_spec(shape) for shape in shapes],
        ),
        out_shape=[jax.ShapeDtypeStruct(shape, f32) for shape in shapes],
        compiler_params=params(True),
        cost_estimate=cost(1e6, 8e6),
        name=name,
    )(place, index, *operands)


def pick(array, index):
    return lax.dynamic_index_in_dim(array, index, 0, keepdims=False)


def body(
    tokens, segments, adapter_index, w_attn_in, w_attn_out, w_gate_up, w_down, qk_scale,
    mix_rates, mlp_scales, a_model, b_model, a_heads, b_heads, a_hidden, b_hidden, cotangent,
):
    slabs, chunk, model = tokens.shape
    n_seq = lax.axis_size("seq")
    n_ctx = lax.axis_size("ctx")
    group = n_ctx // slabs
    local_width = w_attn_out.shape[0]
    head_dim = a_heads.shape[-1]
    row_width = a_hidden.shape[-1]
    local_hidden = w_down.shape[0]
    local_heads = local_width // head_dim
    rank = a_model.shape[2]
    adapters = a_model.shape[0]
    half = model // 2
    ctx_place = lax.axis_index("ctx")
    slab = ctx_place // group
    inner = ctx_place % group
    core = lax.axis_index("wt")
    seq_place = lax.axis_index("seq")
    owners = n_seq * n_ctx
    rows = slabs * chunk
    length = rows * group
    place = jnp.stack([inner, slab, core, seq_place, pick(adapter_index, slab)]).astype(i32)
    a_heads = jnp.transpose(a_heads, (0, 2, 1, 3))
    b_heads = jnp.transpose(b_heads, (0, 1, 3, 2, 4))
    a_hidden = jnp.transpose(a_hidden, (0, 2, 1, 3))
    b_hidden = jnp.transpose(b_hidden, (0, 1, 3, 2, 4))

    def to_slab(array, shift):
        pairs = [(c, (c + shift * group) % n_ctx) for c in range(n_ctx)]
        return lax.ppermute(array, "ctx", pairs)

    def within_slab(array, shift):
        pairs = [(c, c - c % group + (c % group + shift) % group) for c in range(n_ctx)]
        return lax.ppermute(array, "ctx", pairs)

    def to_seq(array, shift):
        return lax.ppermute(array, "seq", [(c, (c + shift) % n_seq) for c in range(n_seq)])

    def other_core(array):
        return lax.ppermute(array, "wt", [(0, 1), (1, 0)])

    def half_piece(array, index, which):
        return lax.dynamic_slice(array, (index, 0, which * half), (1, chunk, half))[0]

    def token_piece(index):
        seg = jnp.pad(pick(segments, index).astype(bf16), (0, half - chunk))
        return jnp.concatenate(
            [half_piece(tokens, index, core), jnp.broadcast_to(seg, (8, half))], axis=0
        )

    tie = lax.optimization_barrier

    spot = (jnp.arange(LANES, dtype=i32) % (head_dim // 2)).astype(f32)
    frequency = 10000.0 ** (-spot / (head_dim // 2))
    turn = jnp.arange(length, dtype=i32).astype(f32)[:, None] * frequency[None, :]
    cos = jnp.cos(turn)
    lower = jnp.arange(LANES) % head_dim < head_dim // 2
    sin = jnp.sin(turn) * jnp.where(lower, -1.0, 1.0)[None, :]
    scale = qk_scale[None, :]

    own_piece = token_piece(slab)
    got = [own_piece] + [
        to_slab(token_piece((slab + shift) % slabs), shift) for shift in range(1, slabs)
    ]
    index = [adapter_index]
    for shift in range(1, n_seq):
        index.append(to_seq(adapter_index, shift))
    got, cos, sin, place, index = tie((got, cos, sin, place, index))
    near = [within_slab(own_piece, turn) for turn in range(1, group)]
    g_send = [half_piece(cotangent, (slab + shift) % slabs, core) for shift in range(1, slabs)]
    rest, near, g_send = tie((jnp.stack(got[1:]), near, g_send))
    rest_other = other_core(rest)
    peers = [within_slab(rest, turn) for turn in range(1, group)]
    g_mine = [to_slab(g_send[shift - 1], shift) for shift in range(1, slabs)]
    peers, g_mine[0], g_mine[-1] = tie((peers, g_mine[0], g_mine[-1]))
    pieces = [own_piece, rest, rest_other]
    for turn in range(1, group):
        pieces += [
            near[turn - 1], other_core(near[turn - 1]),
            peers[turn - 1], other_core(peers[turn - 1]),
        ]
    if length * model < (1 << 21):
        pieces[2:] = [pltpu.with_memory_space_constraint(p, pltpu.VMEM) for p in pieces[2:]]

    h_full, h_own, u, q, k, v, qi, ki, o, inv, attn_msg, start, bh, ah = run_attend(
        place, tokens, pieces, w_attn_in, a_model, b_heads, a_heads, cos, sin, scale,
        w_attn_out, group, head_dim,
    )
    g_mine, attn_msg = tie((g_mine, attn_msg))
    attn_other = other_core(attn_msg)
    g_mine, attn_msg = tie((jnp.stack(g_mine), attn_msg))
    g_mine, attn_other = tie((g_mine, attn_other))
    g_other = other_core(g_mine)
    mid, u_gu, gate, up, down_msg = run_feed(
        place, attn_msg, pltpu.with_memory_space_constraint(attn_other, pltpu.VMEM), h_own,
        b_model, mix_rates, a_model, w_gate_up, b_hidden,
        w_down, a_hidden, mlp_scales, 512, slabs,
    )
    g_other, down_msg = tie((g_other, down_msg))
    down_other = pltpu.with_memory_space_constraint(other_core(down_msg), pltpu.VMEM)
    out_half, mid_res, mid_msg, early = run_feed_back(
        place, down_msg, down_other, mid, cotangent, g_mine, g_other, b_model, mix_rates,
        a_model, u_gu, gate, up, w_gate_up, b_hidden, w_down, a_hidden, mlp_scales, 512, group,
        n_seq,
    )
    mid_other = pltpu.with_memory_space_constraint(other_core(mid_msg), pltpu.VMEM)

    order = (slab - jnp.arange(slabs, dtype=i32)) % slabs
    index = jnp.stack(index)[:, order]

    def sum_inner(table):
        return pick(table, inner), [
            within_slab(pick(table, (inner + turn) % group), turn) for turn in range(1, group)
        ]

    def add_inner(own, got):
        total = own.astype(f32)
        for piece in got:
            total = total + piece.astype(f32)
        return total.astype(bf16)

    def over_slabs(total):
        return [pick(total, slab)] + [
            to_slab(pick(total, (slab + shift) % slabs), shift) for shift in range(1, slabs)
        ]

    def pack(rows_part, table):
        return jnp.concatenate([rows_part, table.reshape(slabs, -1, half)], axis=1)

    early_size = early.shape[3]
    early_own, early_got = sum_inner(early)
    gq, gk, gv, h_res, gbo, gah = run_attend_back(
        place, mid_res, mid_msg, mid_other, h_own, attn_msg, attn_other, mix_rates, b_model,
        w_attn_out, ah, start, q, k, v, o, inv, qi, ki, cos, sin, scale, slabs, group,
        head_dim,
    )
    early_got, gk, gv = tie((early_got, gk, gv))
    keep, send = run_others(place, gk, gv, w_attn_in, a_model, bh, slabs, group)
    others = (keep.astype(f32) + other_core(send).astype(f32)).astype(bf16)
    others, gq, gk, gv = tie((others, gq, gk, gv))
    waves = [[2, 1], [3, 0]] if slabs == 4 else [list(range(slabs))]
    others = others.reshape(group - 1, slabs, chunk, half)
    others_got = []
    for wave in waves:
        if others_got:
            others_got[-1], others = tie((others_got[-1], others))
        others_got.append(
            [
                within_slab(
                    jnp.stack(
                        [pick(others[turn - 1], (slab + shift) % slabs) for shift in wave]
                    ),
                    turn,
                )
                for turn in range(1, group)
            ]
        )
    home = over_slabs(pack(out_half, add_inner(early_own, early_got)))
    late = run_grads(
        place, gq, gk, gv, bh, u, h_full, gbo, gah, slabs, group, n_seq, head_dim
    )
    late_own, late_got = sum_inner(late)
    late_own, gq, home, others_got[0] = tie((late_own, gq, home, others_got[0]))
    home_other = [other_core(piece) for piece in home]
    early_far = []
    for shift in range(1, n_seq):
        at = chunk + (seq_place + shift) % n_seq * early_size
        sent = [lax.dynamic_slice_in_dim(piece, at, early_size, 0) for piece in home]
        early_far.append(to_seq(jnp.stack(sent), shift))
    own_keep, own_send = run_own(
        place, gq, gk, gv, w_attn_in, a_model, bh, h_res, slabs, group
    )
    late_got, early_far, own_send, others_got = tie(
        (late_got, early_far, own_send, others_got)
    )
    own_got = other_core(own_send)
    late_total = add_inner(late_own, late_got)
    own_sum = (own_keep.astype(f32) + own_got.astype(f32)).reshape(slabs, chunk, half)
    size = late.shape[3]
    result = [None] * slabs
    for wave, got_wave in zip(waves, others_got):
        for n, shift in enumerate(wave):
            target = (slab + shift) % slabs
            total = pick(own_sum, target)
            for got_part in got_wave:
                total = total + got_part[n].astype(f32)
            result[shift] = jnp.concatenate(
                [total.astype(bf16), pick(late_total, target).reshape(n_seq * size, half)],
                axis=0,
            )
    result, home, home_other, early_far = tie((result, home, home_other, early_far))
    result = result[:1] + [to_slab(result[shift], shift) for shift in range(1, slabs)]
    early_tables = [*home, *home_other, *early_far, *(other_core(t) for t in early_far)]
    layer_out = run_join(place, home, home_other, chunk, bf16)
    cols = model // owners
    each = row_width // owners
    hidden_rows = local_hidden // row_width
    grad_am_gu, grad_bm_down, grad_ad, grad_bd = run_unpack(
        unpack_early_kernel,
        (rank, cols, each, hidden_rows, (3 * rank * hidden_rows + LANES - 1) // LANES),
        (n_seq, slabs, chunk, early_size),
        place, index, early_tables, [],
        [
            (adapters, 2, rank, cols // 2),
            (adapters, rank, cols),
            (adapters, rank, each, hidden_rows),
            (adapters, 2, rank, each, hidden_rows),
        ],
        "unpack_early",
    )
    result, layer_out, grad_am_gu, grad_bm_down = tie(
        (result, layer_out, grad_am_gu, grad_bm_down)
    )
    result_other = [other_core(piece) for piece in result]
    far = []
    for shift in range(1, n_seq):
        at = chunk + (seq_place + shift) % n_seq * size
        sent = [lax.dynamic_slice_in_dim(piece, at, size, 0) for piece in result]
        far.append(to_seq(jnp.stack(sent), shift))
    input_grad = run_join(place, result, result_other, chunk, f32)
    far, input_grad = tie((far, input_grad))
    each = head_dim // owners
    grad_am, grad_bm, grad_ah, grad_bh = run_unpack(
        unpack_late_kernel,
        (rank, cols, local_heads, each),
        (n_seq, slabs, chunk, size),
        place, index, [*result, *result_other, *far, *(other_core(piece) for piece in far)],
        [grad_am_gu, grad_bm_down],
        [
            (adapters, 5, rank, cols // 2),
            (adapters, 2, rank, cols),
            (adapters, local_heads, each, rank),
            (adapters, 3, local_heads, each, rank),
        ],
        "unpack_late",
    )
    return (
        layer_out,
        input_grad,
        grad_am,
        grad_bm,
        jnp.transpose(grad_ah, (0, 3, 1, 2)),
        jnp.transpose(grad_bh, (0, 1, 4, 2, 3)),
        jnp.transpose(grad_ad, (0, 1, 3, 2)),
        jnp.transpose(grad_bd, (0, 1, 2, 4, 3)),
    )


def solution(mesh):
    return jax.shard_map(
        body,
        mesh=mesh,
        in_specs=(
            P("seq", "ctx", None),
            P("seq", "ctx"),
            P("seq"),
            P(None, None, "wt"),
            P("wt", None),
            P(None, None, "wt"),
            P("wt", None),
            P("wt"),
            P(),
            P(None, "wt"),
            P(),
            P(),
            P(None, None, "wt", None),
            P(None, None, None, "wt", None),
            P(None, None, "wt", None),
            P(None, None, None, "wt", None),
            P("seq", "ctx", None),
        ),
        out_specs=(
            P("seq", "ctx", None),
            P("seq", "ctx", None),
            P(None, None, None, ("seq", "ctx", "wt")),
            P(None, None, None, ("seq", "ctx")),
            P(None, None, "wt", ("seq", "ctx")),
            P(None, None, None, "wt", ("seq", "ctx")),
            P(None, None, "wt", ("seq", "ctx")),
            P(None, None, None, "wt", ("seq", "ctx")),
        ),
        check_vma=False,
    )
```
